32 devices in a mesh: seq: 8 (over z, core), batch: 4 (over y, x).
Axes of the slice: x: 2, y: 2, z: 4, core: 2. Of those that a mesh axis runs over, the one named last changes fastest.
Arguments:
- tokens: bfloat16 [8, 512, 2048], P('batch', 'seq'), may hold values from -6 to 6
- lengths: int32 [8], P('batch'), may hold values from 256 to 512, as said below
- key_mask: int32 [8, 512], P('batch', 'seq'), may hold values 0 or 1
- top_experts: int32 [8, 512, 4], P('batch', 'seq'), may hold values from 0 to 7, all different within a row
- attn_gain: bfloat16 [2048], P(('seq', 'batch')), may hold values from 0.5 to 2
- query_gain: bfloat16 [2048], P(('seq', 'batch')), may hold values from 0.59765625 to 1.59375
- key_gain: bfloat16 [2048], P(('seq', 'batch')), may hold values from 0.59765625 to 1.59375
- mlp_gain: bfloat16 [2048], P(('seq', 'batch')), may hold values from 0.5 to 2
- w_query: bfloat16 [2048, 2048], P(('seq', 'batch')), may hold values from -0.125 to 0.125
- w_key: bfloat16 [2048, 2048], P(('seq', 'batch')), may hold values from -0.125 to 0.125
- w_value: bfloat16 [2048, 2048], P(('seq', 'batch')), may hold values from -0.125 to 0.125
- w_out: bfloat16 [2048, 2048], P(('seq', 'batch')), may hold values from -1 to 1
- w_router: bfloat16 [2048, 8], P(('seq', 'batch')), may hold values from -0.0625 to 0.0625
- expert_gate: bfloat16 [8, 2048, 1024], P('batch', 'seq'), may hold values from -0.125 to 0.125
- expert_up: bfloat16 [8, 2048, 1024], P('batch', 'seq'), may hold values from -0.125 to 0.125
- expert_down: bfloat16 [8, 1024, 2048], P('batch', 'seq'), may hold values from -1 to 1
- cotangent: bfloat16 [8, 512, 2048], P('batch', 'seq'), may hold values from -6 to 6
Outputs:
- output: bfloat16 [8, 512, 2048], P('batch', 'seq')
- grad_tokens: bfloat16 [8, 512, 2048], P('batch', 'seq')
- grad_attn_gain: float32 [2048], P(('seq', 'batch'))
- grad_query_gain: float32 [2048], P(('seq', 'batch'))
- grad_key_gain: float32 [2048], P(('seq', 'batch'))
- grad_mlp_gain: float32 [2048], P(('seq', 'batch'))
- grad_query: float32 [2048, 2048], P(('seq', 'batch'))
- grad_key: float32 [2048, 2048], P(('seq', 'batch'))
- grad_value: float32 [2048, 2048], P(('seq', 'batch'))
- grad_out: float32 [2048, 2048], P(('seq', 'batch'))
- grad_router: float32 [2048, 8], P(('seq', 'batch'))
- grad_expert_gate: float32 [8, 2048, 1024], P('batch', 'seq')
- grad_expert_up: float32 [8, 2048, 1024], P('batch', 'seq')
- grad_expert_down: float32 [8, 1024, 2048], P('batch', 'seq')
The draws below stay inside these ranges and needn't reach their ends.
Inputs may be any that keep to these rules, and one draw needn't show every extreme that they name: `lengths`: positions at or past a row's length are padding; some row of every draw is full. `top_experts`: each token names 4 different experts.
All inputs are finite; a program needn't handle non-finite values. No bound on the sum of `key_mask` on one device may be relied on, other than what follows from the above.
Results may differ from the reference program's by a relative error of at most 0.038.
Values may be sent and summed in bfloat16 or wider, within the bound.
A program may use at most 320 MiB of HBM per device.

```python
import math
import jax
import jax.numpy as jnp
from jax import lax

D = 2048
HEAD = 128
FF = 1024
EXPERTS = 8
TOP = 4
ROW = 512
ROWS = 8


def draw_lengths(key, part):
    drawn_lengths = jax.random.randint(key, (ROWS,), ROW // 2, ROW + 1, dtype=jnp.int32)
    return drawn_lengths.at[0].set(ROW).astype(jnp.int32)


def with_ends(entries, own_key, low, top_value):
    longest = entries.shape.index(max(entries.shape))
    spots = []
    for shift in (0, 1):
        where = [jax.random.randint(jax.random.fold_in(own_key, axis), (), 0, length) for axis, length in enumerate(entries.shape)]
        where[longest] = (where[longest] + shift) % entries.shape[longest]
        spots.append(tuple(where))
    return entries.at[spots[0]].set(low).at[spots[1]].set(top_value)


def level_of(rng, shape, pieces, low, top_value):
    level = 1.0
    for position, shards_of in pieces:
        draws = jax.random.uniform(jax.random.fold_in(jax.random.fold_in(rng, 6), position), (shards_of,), jnp.float32, low / len(pieces), top_value / len(pieces))
        level = level * jnp.repeat(jnp.exp(draws), shape[position] // shards_of).reshape((-1,) + (1,) * (len(shape) - 1 - position))
    return level


def choose_distinct(key, rows, number_of, top, lift):
    order = jax.random.permutation(jax.random.fold_in(key, 1), number_of)
    boost = order
    for power in range(3):
        boost = boost * boost // number_of
    boost = boost * lift // number_of
    lots = jax.random.randint(jax.random.fold_in(key, 2), (rows, number_of), 0, 4096) + boost
    sure = jax.random.permutation(jax.random.fold_in(key, 3), rows)[jnp.arange(number_of) % rows]
    lots = jnp.where(jnp.arange(rows)[:, None] == sure[None, :], 1 << 14, lots)
    score = lots * number_of + jnp.arange(number_of)
    return lax.top_k(score.astype(jnp.int32), top)[1].astype(jnp.int32)


def scatter_about(rng, dims, spread, bound, pieces=(), kind=jnp.bfloat16):
    drawn = spread * jax.random.normal(rng, dims, jnp.float32)
    if pieces:
        drawn = drawn * level_of(rng, dims, pieces, -0.22, 0.18)
    return jnp.clip(drawn, -bound, bound).astype(kind)


def setup_inputs(seed: int = 0) -> dict:
    arg_keys = jax.random.split(jax.random.key(seed), 18)
    return {
        "tokens": scatter_about(arg_keys[0], (ROWS, ROW, D), 1.0, 6.0, ((0, 4), (1, 8))),
        "lengths": draw_lengths(jax.random.fold_in(arg_keys[17], 71), 0),
        "key_mask": with_ends((jax.random.randint(arg_keys[2], (ROWS, ROW), 0, 4) < 3).astype(jnp.int32), jax.random.fold_in(arg_keys[2], 1), 0, 1),
        "top_experts": choose_distinct(arg_keys[3], ROWS * ROW, EXPERTS, TOP, 4096).reshape((ROWS, ROW, TOP)),
        "attn_gain": jnp.clip(jnp.exp(math.log(2.0) - 1.3862944 * jax.random.uniform(arg_keys[4], (D,), jnp.float32) ** level_of(arg_keys[4], (D,), ((0, 32),), -0.2, 0.2)), 0.5, 2.0).astype(jnp.bfloat16),
        "query_gain": jnp.clip(jnp.exp(math.log(1.59375) - 0.98082925 * jax.random.uniform(arg_keys[5], (D,), jnp.float32) ** level_of(arg_keys[5], (D,), ((0, 32),), -0.2, 0.2)), 0.59765625, 1.59375).astype(jnp.bfloat16),
        "key_gain": jnp.clip(jnp.exp(math.log(1.59375) - 0.98082925 * jax.random.uniform(arg_keys[6], (D,), jnp.float32) ** level_of(arg_keys[6], (D,), ((0, 32),), -0.2, 0.2)), 0.59765625, 1.59375).astype(jnp.bfloat16),
        "mlp_gain": jnp.clip(jnp.exp(math.log(2.0) - 1.3862944 * jax.random.uniform(arg_keys[7], (D,), jnp.float32) ** level_of(arg_keys[7], (D,), ((0, 32),), -0.2, 0.2)), 0.5, 2.0).astype(jnp.bfloat16),
        "w_query": scatter_about(arg_keys[8], (D, D), D ** -0.5, 0.125, ((0, 32),)),
        "w_key": scatter_about(arg_keys[9], (D, D), D ** -0.5, 0.125, ((0, 32),)),
        "w_value": scatter_about(arg_keys[10], (D, D), D ** -0.5, 0.125, ((0, 32),)),
        "w_out": scatter_about(arg_keys[11], (D, D), (D // 64) ** -0.5, 1.0, ((0, 32),)),
        "w_router": scatter_about(arg_keys[12], (D, EXPERTS), (4 * D) ** -0.5, 0.0625, ((0, 32),)),
        "expert_gate": scatter_about(arg_keys[13], (EXPERTS, D, FF), D ** -0.5, 0.125, ((0, 4), (1, 8))),
        "expert_up": scatter_about(arg_keys[14], (EXPERTS, D, FF), D ** -0.5, 0.125, ((0, 4), (1, 8))),
        "expert_down": scatter_about(arg_keys[15], (EXPERTS, FF, D), (FF // 32) ** -0.5, 1.0, ((0, 4), (1, 8))),
        "cotangent": scatter_about(arg_keys[16], (ROWS, ROW, D), 1.0, 6.0, ((0, 4), (1, 8))),
    }


EPS = 1e-05
HIGHEST_PRECISION = lax.Precision.HIGHEST

@jax.custom_vjp
def low(v):
    return lax.optimization_barrier(v.astype(jnp.bfloat16)).astype(jnp.float32)

@jax.custom_vjp
def low_back(v):
    return v

def low_keep(v):
    return (low(v), None)

def low_pass(kept, grad):
    return (grad,)

def back_keep(v):
    return (v, None)

def back_low(kept, grad):
    return (low(grad),)
low.defvjp(low_keep, low_pass)
low_back.defvjp(back_keep, back_low)

def norm_rows(values_in, gain_row):
    return values_in * lax.rsqrt(lax.optimization_barrier(jnp.mean(values_in * values_in, axis=-1, keepdims=True)) + EPS) * gain_row

def rotary_tables(positions):
    half_head = HEAD // 2
    frequency = 10000.0 ** (-2.0 * jnp.arange(half_head, dtype=jnp.float32) / HEAD)
    angles = positions.astype(jnp.float32)[:, None] * frequency[None, :]
    return (jnp.cos(angles), jnp.sin(angles))

def rotate(flat_rows, cos_part, sin_part):
    per_head = flat_rows.reshape(flat_rows.shape[0], -1, HEAD)
    half_head = HEAD // 2
    first_half = per_head[..., :half_head]
    second_half = per_head[..., half_head:]
    cos_wide = cos_part[:, None, :]
    sin_wide = sin_part[:, None, :]
    return jnp.concatenate([first_half * cos_wide - second_half * sin_wide, second_half * cos_wide + first_half * sin_wide], axis=-1)

def product(left_side, right_side):
    return jnp.dot(left_side, right_side, precision=HIGHEST_PRECISION, preferred_element_type=jnp.float32)

def layer_row(inputs, length, key_flags, chosen, params):
    attn_gain, query_gain, key_gain, mlp_gain, w_query, w_key, w_value, w_out, w_router, expert_gate, expert_up, expert_down = params
    row_count = inputs.shape[0]
    positions = jnp.arange(row_count, dtype=jnp.int32)
    cos_part, sin_part = rotary_tables(positions)
    hidden = low(norm_rows(inputs, attn_gain))
    query_pre = low_back(product(hidden, w_query))
    key_pre = low_back(product(hidden, w_key))
    values = low(low_back(product(hidden, w_value))).reshape(row_count, -1, HEAD)
    queries = low(rotate(norm_rows(query_pre, query_gain), cos_part, sin_part))
    key_heads = low(rotate(norm_rows(key_pre, key_gain), cos_part, sin_part))
    usable = (positions < length) & (key_flags == 1)
    block_rows = min(512, row_count)
    score_scale = HEAD ** (-0.5)

    def attend_block(block_data):
        query_block, first_row = block_data
        scores = jnp.einsum('qhd,khd->hqk', query_block, key_heads, precision=HIGHEST_PRECISION) * score_scale
        scores = low_back(scores)
        query_pos = first_row + jnp.arange(block_rows, dtype=jnp.int32)
        allowed = (positions[None, :] <= query_pos[:, None]) & (usable[None, :] | (positions[None, :] == query_pos[:, None]))
        scores = jnp.where(allowed[None], scores, -1e+30)
        weights = low(jax.nn.softmax(scores, axis=-1))
        return jnp.einsum('hqk,khd->qhd', weights, values, precision=HIGHEST_PRECISION)
    blocks = queries.reshape(row_count // block_rows, block_rows, queries.shape[1], HEAD)
    starts = jnp.arange(row_count // block_rows, dtype=jnp.int32) * block_rows
    attended = lax.map(jax.checkpoint(attend_block), (blocks, starts)).reshape(row_count, -1)
    mixed_heads = low(low_back(attended))
    residual = inputs + low_back(product(mixed_heads, w_out))
    normed = low(norm_rows(residual, mlp_gain))
    router_probs = jax.nn.softmax(product(normed, w_router), axis=-1)
    gate_weights = router_probs * chosen
    gate_pre = low_back(jnp.einsum('td,edf->etf', normed, expert_gate, precision=HIGHEST_PRECISION))
    up_pre = low_back(jnp.einsum('td,edf->etf', normed, expert_up, precision=HIGHEST_PRECISION))
    active = low(jax.nn.silu(gate_pre) * up_pre)
    branch = low_back(jnp.einsum('etf,efd->etd', active, expert_down, precision=HIGHEST_PRECISION))
    return residual + jnp.einsum('te,etd->td', gate_weights, branch, precision=HIGHEST_PRECISION)

def reference(tokens, lengths, key_mask, top_experts, attn_gain, query_gain, key_gain, mlp_gain, w_query, w_key, w_value, w_out, w_router, expert_gate, expert_up, expert_down, cotangent):
    params = tuple((weight_array.astype(jnp.float32) for weight_array in (attn_gain, query_gain, key_gain, mlp_gain, w_query, w_key, w_value, w_out, w_router, expert_gate, expert_up, expert_down)))
    chosen_all = jnp.any(top_experts[..., None] == jnp.arange(EXPERTS, dtype=jnp.int32), axis=-2).astype(jnp.float32)

    def one_row(totals, row_data):
        row_in, length, flags, chosen, cot_row = row_data

        def forward(row_values, *weights):
            return layer_row(row_values, length, flags, chosen, weights)
        result, pullback = jax.vjp(forward, row_in.astype(jnp.float32), *params)
        gradients = pullback(cot_row.astype(jnp.float32))
        totals = tuple((total_one + grad_one for total_one, grad_one in zip(totals, gradients[1:])))
        return (totals, (result.astype(jnp.bfloat16), gradients[0].astype(jnp.bfloat16)))
    initial = tuple((jnp.zeros_like(weight_array) for weight_array in params))
    totals, (output, grad_tokens) = lax.scan(one_row, initial, (tokens, lengths, key_mask, chosen_all, cotangent))
    return (output, grad_tokens, totals[0], totals[1], totals[2], totals[3], totals[4], totals[5], totals[6], totals[7], totals[8], totals[9], totals[10], totals[11])
```

```python
import jax
import jax.numpy as jnp
from jax import lax
from jax.sharding import PartitionSpec as P

HEAD = 128
EPS = 1e-05
HIGHEST = lax.Precision.HIGHEST
NEGATIVE = -1e30
BF = jnp.bfloat16
F32 = jnp.float32


def dot(a, b):
    return jnp.dot(a, b, preferred_element_type=F32)


def dot_t(a, b):
    return lax.dot_general(a, b, (((1,), (1,)), ((), ())), preferred_element_type=F32)


def t_dot(a, b):
    return lax.dot_general(a, b, (((0,), (0,)), ((), ())), preferred_element_type=F32)


def rms_scale(v):
    return lax.rsqrt(jnp.mean(v * v, axis=-1, keepdims=True) + EPS)


def rms_back(v, scale, gain, grad):
    normal = v * scale
    weighted = grad * gain
    mean = jnp.mean(weighted * normal, axis=-1, keepdims=True)
    return scale * (weighted - normal * mean), grad * normal


def rotary_tables(positions):
    half_head = HEAD // 2
    frequency = 10000.0 ** (-2.0 * jnp.arange(half_head, dtype=F32) / HEAD)
    angles = positions.astype(F32)[:, None] * frequency[None, :]
    return jnp.cos(angles), jnp.sin(angles)


def rotate(v, cos_part, sin_part):
    first, second = jnp.split(v, 2, axis=-1)
    return jnp.concatenate(
        [first * cos_part - second * sin_part, second * cos_part + first * sin_part], axis=-1
    )


def shards(
    tokens,
    lengths,
    key_mask,
    top_experts,
    attn_gain,
    query_gain,
    key_gain,
    mlp_gain,
    w_query,
    w_key,
    w_value,
    w_out,
    w_router,
    expert_gate,
    expert_up,
    expert_down,
    cotangent,
):
    n_seq = lax.axis_size("seq")
    n_bat = lax.axis_size("batch")
    seq = lax.axis_index("seq")
    bat = lax.axis_index("batch")
    rows, span, dim = tokens.shape
    own = rows * span
    col = n_seq * own
    length = n_seq * span
    shard = w_query.shape[0]
    wide = dim // n_seq
    heads = wide // HEAD
    local_experts, depth, hidden_units = expert_gate.shape
    part = hidden_units // n_seq
    experts = local_experts * n_bat
    every = ("seq", "batch")
    score_scale = HEAD ** (-0.5)

    small = jnp.concatenate(
        [w_router, jnp.stack([attn_gain, query_gain, key_gain, mlp_gain], axis=1)], axis=1
    )
    small_all = lax.all_gather(small, every, axis=0, tiled=True)
    router = small_all[:, :experts]
    gain_attn = small_all[:, experts].astype(F32)
    gain_mlp = small_all[:, experts + 3].astype(F32)
    gain_q = lax.dynamic_slice_in_dim(small_all[:, experts + 1], seq * wide, wide).astype(F32)
    gain_k = lax.dynamic_slice_in_dim(small_all[:, experts + 2], seq * wide, wide).astype(F32)

    qkv_cut = jnp.stack([w_query, w_key, w_value]).reshape(3, shard, n_seq, wide)
    qkv_cut = jnp.transpose(qkv_cut, (2, 1, 0, 3)).reshape(n_seq, shard, 3 * wide)
    qkv_cut = lax.all_to_all(qkv_cut, "seq", 0, 0, tiled=True)
    w_qkv = lax.all_gather(qkv_cut, "batch", axis=1, tiled=True).reshape(dim, 3 * wide)
    w_o = lax.all_gather(w_out, "batch", axis=0, tiled=True)

    gu_cut = jnp.stack([expert_gate, expert_up]).reshape(2, local_experts, depth, n_seq, part)
    gu_cut = jnp.transpose(gu_cut, (3, 2, 0, 1, 4)).reshape(n_seq, depth, 2 * local_experts * part)
    w_gu = lax.all_to_all(gu_cut, "seq", 0, 0, tiled=True).reshape(dim, 2 * local_experts * part)
    w_down = expert_down.reshape(local_experts * part, dim)

    mine = tokens.reshape(own, dim)
    x_col = lax.all_gather(mine, "seq", axis=0, tiled=True).astype(F32)
    scale_x = rms_scale(x_col)
    hidden = (x_col * scale_x * gain_attn).astype(BF)
    qkv = dot(hidden, w_qkv)
    q_pre, k_pre, v_pre = qkv[:, :wide], qkv[:, wide : 2 * wide], qkv[:, 2 * wide :]

    squares = jnp.stack([jnp.sum(q_pre * q_pre, axis=-1), jnp.sum(k_pre * k_pre, axis=-1)])
    squares = lax.psum(squares, "seq")
    scales = lax.rsqrt(squares / dim + EPS)
    scale_q, scale_k = scales[0][:, None], scales[1][:, None]

    def by_row(v):
        v = v.reshape(n_seq, rows, span, heads, HEAD)
        return jnp.transpose(v, (1, 3, 0, 2, 4)).reshape(rows, heads, length, HEAD)

    def by_col(v):
        v = v.reshape(rows, heads, n_seq, span, HEAD)
        return jnp.transpose(v, (2, 0, 3, 1, 4)).reshape(col, wide)

    positions = jnp.arange(length, dtype=jnp.int32)
    cos_part, sin_part = rotary_tables(positions)
    q_norm = by_row(q_pre * scale_q)
    k_norm = by_row(k_pre * scale_k)
    gain_qh = gain_q.reshape(1, heads, 1, HEAD)
    gain_kh = gain_k.reshape(1, heads, 1, HEAD)
    queries = rotate(q_norm * gain_qh, cos_part, sin_part).astype(BF)
    keys = rotate(k_norm * gain_kh, cos_part, sin_part).astype(BF)
    values = by_row(v_pre.astype(BF))

    mask_all = lax.all_gather(key_mask, "seq", axis=1, tiled=True)
    usable = (positions[None, :] < lengths[:, None]) & (mask_all == 1)
    causal = positions[None, :] <= positions[:, None]
    same = positions[None, :] == positions[:, None]
    allowed = (causal[None] & (usable[:, None, :] | same[None]))[:, None]
    scores = jnp.einsum("rhqd,rhkd->rhqk", queries, keys, preferred_element_type=F32) * score_scale
    scores = jnp.where(allowed, scores, NEGATIVE)
    top = jnp.max(scores, axis=-1, keepdims=True)
    raised = jnp.exp(scores - top)
    probs = raised / jnp.sum(raised, axis=-1, keepdims=True)
    probs_low = probs.astype(BF)
    attended = jnp.einsum("rhqk,rhkd->rhqd", probs_low, values, preferred_element_type=F32)
    mixed = by_col(attended.astype(BF))

    mixed_out = lax.psum_scatter(dot(mixed, w_o).astype(BF), "seq", scatter_dimension=0, tiled=True)
    x_own = mine.astype(F32)
    residual = x_own + mixed_out.astype(F32)
    scale_r = rms_scale(residual)
    normed = (residual * scale_r * gain_mlp).astype(BF)
    router_probs = jax.nn.softmax(dot(normed, router), axis=-1)
    expert_ids = jnp.arange(experts, dtype=jnp.int32)
    chosen = jnp.any(top_experts.reshape(own, -1)[:, :, None] == expert_ids, axis=1).astype(F32)
    gates = router_probs * chosen

    normed_all = lax.all_gather(normed, every, axis=0, tiled=True)
    gates_all = lax.all_gather(gates, every, axis=0, tiled=True)
    dy_own = cotangent.reshape(own, dim)
    dy_all = lax.all_gather(dy_own, every, axis=0, tiled=True)
    first_expert = bat * local_experts
    gates_here = lax.dynamic_slice_in_dim(gates_all, first_expert, local_experts, 1)
    units = local_experts * part
    gates_wide = jnp.repeat(gates_here, part, axis=1)
    pre = dot(normed_all, w_gu)
    gate_pre, up_pre = pre[:, :units], pre[:, units:]
    sig = jax.nn.sigmoid(gate_pre)
    silu = gate_pre * sig
    active = (silu * up_pre).astype(BF).astype(F32)
    weighted = (active * gates_wide).astype(BF)
    mixture = dot(weighted, w_down).astype(BF)
    mixture = lax.psum_scatter(mixture, every, scatter_dimension=0, tiled=True)
    output = (residual + mixture.astype(F32)).astype(BF)

    back = dot_t(dy_all, w_down)
    gate_terms = jnp.sum((active * back).reshape(-1, local_experts, part), axis=-1)
    grad_active = back * gates_wide
    grad_gate_pre = (grad_active * up_pre * sig * (1.0 + gate_pre * (1.0 - sig))).astype(BF)
    grad_up_pre = (grad_active * silu).astype(BF)
    grad_pre = jnp.concatenate([grad_gate_pre, grad_up_pre], axis=1)
    grad_down = t_dot(weighted, dy_all)
    grad_gu = t_dot(normed_all, grad_pre).astype(BF)
    grad_normed = dot_t(grad_pre, w_gu).astype(BF)
    grad_normed = lax.psum_scatter(grad_normed, every, scatter_dimension=0, tiled=True).astype(F32)
    grad_gates = lax.dynamic_update_slice_in_dim(
        jnp.zeros((normed_all.shape[0], experts), F32), gate_terms, first_expert, 1
    )
    grad_gates = lax.psum_scatter(grad_gates, every, scatter_dimension=0, tiled=True)

    grad_gu = lax.all_to_all(grad_gu.reshape(n_seq, depth, -1), "seq", 0, 0, tiled=True)
    grad_gu = grad_gu.reshape(n_seq, depth, 2, local_experts, part)
    grad_gu = jnp.transpose(grad_gu, (2, 3, 1, 0, 4)).reshape(2, local_experts, depth, hidden_units)
    grad_gu = grad_gu.astype(F32)
    grad_down = grad_down.reshape(local_experts, part, dim)

    grad_chosen = grad_gates * chosen
    grad_logits = router_probs * (
        grad_chosen - jnp.sum(router_probs * grad_chosen, axis=-1, keepdims=True)
    )
    grad_router = lax.dot_general(
        normed.astype(F32), grad_logits, (((0,), (0,)), ((), ())), precision=HIGHEST
    )
    grad_normed = grad_normed + lax.dot_general(
        grad_logits, router.astype(F32), (((1,), (1,)), ((), ())), precision=HIGHEST
    )
    grad_resid, gain_mlp_terms = rms_back(residual, scale_r, gain_mlp, grad_normed)
    grad_residual = dy_own.astype(F32) + grad_resid
    grad_o = grad_residual.astype(BF)

    grad_o_col = lax.all_gather(grad_o, "seq", axis=0, tiled=True)
    grad_mixed = by_row(dot_t(grad_o_col, w_o).astype(BF))
    grad_w_o = t_dot(mixed, grad_o_col).astype(BF)
    grad_w_o = lax.psum_scatter(grad_w_o, "batch", scatter_dimension=0, tiled=True).astype(F32)
    row_dot = jnp.sum(grad_mixed.astype(F32) * attended, axis=-1, keepdims=True)
    grad_values = jnp.einsum("rhqk,rhqd->rhkd", probs_low, grad_mixed, preferred_element_type=F32)
    grad_probs = jnp.einsum("rhqd,rhkd->rhqk", grad_mixed, values, preferred_element_type=F32)
    grad_scores = (probs * (grad_probs - row_dot)).astype(BF)
    grad_q = score_scale * jnp.einsum(
        "rhqk,rhkd->rhqd", grad_scores, keys, preferred_element_type=F32
    )
    grad_k = score_scale * jnp.einsum(
        "rhqk,rhqd->rhkd", grad_scores, queries, preferred_element_type=F32
    )
    grad_q = rotate(grad_q, cos_part, -sin_part)
    grad_k = rotate(grad_k, cos_part, -sin_part)
    grad_gain_q = jnp.sum(grad_q * q_norm, axis=(0, 2)).reshape(wide)
    grad_gain_k = jnp.sum(grad_k * k_norm, axis=(0, 2)).reshape(wide)
    q_weighted = by_col(grad_q * gain_qh)
    k_weighted = by_col(grad_k * gain_kh)
    q_flat = q_pre * scale_q
    k_flat = k_pre * scale_k
    means = jnp.stack(
        [jnp.sum(q_weighted * q_flat, axis=-1), jnp.sum(k_weighted * k_flat, axis=-1)]
    )
    means = lax.psum(means, "seq") / dim
    grad_q_pre = (scale_q * (q_weighted - q_flat * means[0][:, None])).astype(BF)
    grad_k_pre = (scale_k * (k_weighted - k_flat * means[1][:, None])).astype(BF)
    grad_qkv = jnp.concatenate([grad_q_pre, grad_k_pre, by_col(grad_values).astype(BF)], axis=1)

    grad_hidden = dot_t(grad_qkv, w_qkv).astype(BF)
    grad_hidden = lax.psum_scatter(grad_hidden, "seq", scatter_dimension=0, tiled=True).astype(F32)
    grad_w = t_dot(hidden, grad_qkv).astype(BF).reshape(n_seq, n_bat * shard, 3 * wide)
    grad_w = lax.psum_scatter(grad_w, "batch", scatter_dimension=1, tiled=True)
    grad_w = lax.all_to_all(grad_w, "seq", 0, 0, tiled=True).astype(F32)
    grad_w = grad_w.reshape(n_seq, shard, 3, wide)
    grad_w = jnp.transpose(grad_w, (2, 1, 0, 3)).reshape(3, shard, dim)

    grad_x, gain_attn_terms = rms_back(x_own, rms_scale(x_own), gain_attn, grad_hidden)
    grad_tokens = (grad_residual + grad_x).astype(BF)

    zeros = jnp.zeros((dim,), F32)
    small_grads = jnp.concatenate(
        [
            grad_router,
            jnp.stack(
                [
                    jnp.sum(gain_attn_terms, axis=0),
                    lax.dynamic_update_slice_in_dim(zeros, grad_gain_q, seq * wide, 0),
                    lax.dynamic_update_slice_in_dim(zeros, grad_gain_k, seq * wide, 0),
                    jnp.sum(gain_mlp_terms, axis=0),
                ],
                axis=1,
            ),
        ],
        axis=1,
    )
    small_grads = lax.psum_scatter(small_grads, every, scatter_dimension=0, tiled=True)

    return (
        output.reshape(rows, span, dim),
        grad_tokens.reshape(rows, span, dim),
        small_grads[:, experts],
        small_grads[:, experts + 1],
        small_grads[:, experts + 2],
        small_grads[:, experts + 3],
        grad_w[0],
        grad_w[1],
        grad_w[2],
        grad_w_o,
        small_grads[:, :experts],
        grad_gu[0],
        grad_gu[1],
        grad_down,
    )


def solution(mesh):
    tok = P("batch", "seq", None)
    vec = P(("seq", "batch"))
    mat = P(("seq", "batch"), None)
    in_specs = (tok, P("batch"), P("batch", "seq"), tok) + (vec,) * 4 + (mat,) * 5 + (tok,) * 4
    out_specs = (tok, tok) + (vec,) * 4 + (mat,) * 5 + (tok,) * 3
    return jax.shard_map(shards, mesh=mesh, in_specs=in_specs, out_specs=out_specs, check_vma=False)
```

```python
import functools

import jax
import jax.numpy as jnp
from jax import lax
from jax.experimental import pallas as pl
from jax.experimental.pallas import tpu as pltpu
from jax.sharding import PartitionSpec as P

HEAD = 128
EPS = 1e-05
HIGHEST = lax.Precision.HIGHEST
NEGATIVE = -1e30
BF = jnp.bfloat16
F32 = jnp.float32


def dot(a, b):
    return jnp.dot(a, b, preferred_element_type=F32)


def dot_t(a, b):
    return lax.dot_general(a, b, (((1,), (1,)), ((), ())), preferred_element_type=F32)


def t_dot(a, b):
    return lax.dot_general(a, b, (((0,), (0,)), ((), ())), preferred_element_type=F32)


def rms_scale(v):
    return lax.rsqrt(jnp.mean(v * v, axis=-1, keepdims=True) + EPS)


def rms_back(v, scale, gain, grad):
    normal = v * scale
    weighted = grad * gain
    mean = jnp.mean(weighted * normal, axis=-1, keepdims=True)
    return scale * (weighted - normal * mean), grad * normal


def rotary_tables(positions):
    half_head = HEAD // 2
    frequency = 10000.0 ** (-2.0 * jnp.arange(half_head, dtype=F32) / HEAD)
    angles = positions.astype(F32)[:, None] * frequency[None, :]
    return jnp.cos(angles), jnp.sin(angles)


def rotate(v, cos_part, sin_part):
    first, second = jnp.split(v, 2, axis=-1)
    return jnp.concatenate(
        [first * cos_part - second * sin_part, second * cos_part + first * sin_part], axis=-1
    )

ANY = pl.BlockSpec(memory_space=pl.ANY)
VMEM_LIMIT = 60 * 1024 * 1024


class Place:
    def __init__(self, n_seq, n_bat):
        self.n_seq, self.n_bat, self.half = n_seq, n_bat, n_seq // 2
        self.s = lax.axis_index("seq")
        self.b = lax.axis_index("batch")
        self.twin_s = self.s + 1 - 2 * lax.rem(self.s, 2)

    def seq_at(self, k):
        return lax.rem(self.s + (k + self.n_seq), self.n_seq)

    def twin_at(self, k):
        return lax.rem(self.twin_s + (k + self.n_seq), self.n_seq)

    def bat_at(self, k):
        return lax.rem(self.b + (k + self.n_bat), self.n_bat)

    def seq_peer(self, k):
        return {"seq": self.seq_at(k), "batch": self.b}

    def bat_peer(self, k):
        return {"seq": self.s, "batch": self.bat_at(k)}

    def twin(self):
        return {"seq": self.twin_s, "batch": self.b}

    def greet(self, all_seq=False, batch=True):
        steps = range(1, self.n_seq) if all_seq else range(2, self.n_seq, 2)
        peers = [self.seq_peer(k) for k in steps]
        if not all_seq:
            peers.append(self.twin())
        if batch:
            peers += [self.bat_peer(k) for k in range(1, self.n_bat)]
        barrier = pltpu.get_barrier_semaphore()
        for peer in peers:
            pl.semaphore_signal(
                barrier, inc=1, device_id=peer, device_id_type=pl.DeviceIdType.MESH
            )
        pl.semaphore_wait(barrier, len(peers))


class Wire:
    def __init__(self, send_sems, recv_sems):
        self.send_sems, self.recv_sems = send_sems, recv_sems
        self.copies = []

    def push(self, src, dst, peer):
        slot = len(self.copies)
        copy = pltpu.make_async_remote_copy(
            src_ref=src,
            dst_ref=dst,
            send_sem=self.send_sems.at[slot],
            recv_sem=self.recv_sems.at[slot],
            device_id=peer,
            device_id_type=pl.DeviceIdType.MESH,
        )
        copy.start()
        self.copies.append(copy)
        return copy

    def drain(self):
        for copy in self.copies:
            copy.wait_send()


class SeqGather:
    def __init__(self, place, wire, src, out):
        self.place, self.wire, self.src, self.out = place, wire, src, out
        self.late = []

    def start(self):
        place, mine = self.place, self.out.at[self.place.s]
        self.line = [
            self.wire.push(self.src, mine, place.seq_peer(2 * j)) for j in range(1, place.half)
        ]
        self.late.append(self.wire.push(self.src, mine, place.twin()))

    def step(self, j):
        self.line[j - 1].wait_recv()
        block = self.out.at[self.place.seq_at(-2 * j)]
        self.late.append(self.wire.push(block, block, self.place.twin()))

    def finish(self):
        for copy in self.late:
            copy.wait_recv()


class FullGather:
    def __init__(self, place, wire, src, out):
        self.place, self.wire, self.src, self.out = place, wire, src, out
        self.late = []
        self.across = {}

    def spread(self, j, block):
        place = self.place
        self.across[j] = [
            self.wire.push(block, self.out.at[place.seq_at(-2 * j), place.b], place.bat_peer(k))
            for k in range(1, place.n_bat)
        ]

    def start(self):
        place, mine = self.place, self.out.at[self.place.s, self.place.b]
        self.line = [
            self.wire.push(self.src, mine, place.seq_peer(2 * j)) for j in range(1, place.half)
        ]
        self.spread(0, self.src)
        self.late.append(self.wire.push(self.src, mine, place.twin()))

    def step(self, j):
        self.line[j - 1].wait_recv()
        block = self.out.at[self.place.seq_at(-2 * j), self.place.b]
        self.spread(j, block)
        self.late.append(self.wire.push(block, block, self.place.twin()))

    def collect(self, j):
        place = self.place
        for k in range(1, place.n_bat):
            self.across[j][k - 1].wait_recv()
            block = self.out.at[place.seq_at(-2 * j), place.bat_at(-k)]
            self.late.append(self.wire.push(block, block, place.twin()))

    def finish(self):
        for copy in self.late:
            copy.wait_recv()


def keep_own(src, dst, buffer, sem):
    first = pltpu.make_async_copy(src, buffer, sem)
    first.start()
    first.wait()
    second = pltpu.make_async_copy(buffer, dst, sem)
    second.start()
    return second


def comm_call(kernel, outs, scratch, slots, collective_id, name, in_specs, out_specs=None):
    return pl.pallas_call(
        kernel,
        out_shape=outs,
        in_specs=in_specs,
        out_specs=out_specs if out_specs is not None else jax.tree.map(lambda _: ANY, outs),
        scratch_shapes=list(scratch)
        + [pltpu.SemaphoreType.DMA((slots,)), pltpu.SemaphoreType.DMA((slots,))],
        compiler_params=pltpu.CompilerParams(
            collective_id=collective_id, has_side_effects=True, vmem_limit_bytes=VMEM_LIMIT
        ),
        name=name,
    )


def shape_of(lead, block):
    return jax.ShapeDtypeStruct(tuple(lead) + block.shape, block.dtype)


def gather_seq(block, n_seq, n_bat, collective_id, name):
    def kernel(src, out, buffer, own_sem, send_sems, recv_sems):
        place = Place(n_seq, n_bat)
        place.greet(batch=False)
        gather = SeqGather(place, wire := Wire(send_sems, recv_sems), src, out)
        gather.start()
        own = keep_own(src, out.at[place.s], buffer, own_sem)
        for j in range(1, place.half):
            gather.step(j)
        gather.finish()
        own.wait()
        wire.drain()

    return comm_call(
        kernel,
        shape_of((n_seq,), block),
        [pltpu.VMEM(block.shape, block.dtype), pltpu.SemaphoreType.DMA],
        n_seq,
        collective_id,
        name,
        [ANY],
    )(block)


def gather_all(blocks, n_seq, n_bat, collective_id, name):
    count = len(blocks)

    def kernel(*refs):
        srcs, outs = refs[:count], refs[count : 2 * count]
        buffers = refs[2 * count : 3 * count]
        own_sems, send_sems, recv_sems = refs[3 * count :]
        place = Place(n_seq, n_bat)
        place.greet()
        wire = Wire(send_sems, recv_sems)
        gathers = [FullGather(place, wire, *pair) for pair in zip(srcs, outs)]
        for gather in gathers:
            gather.start()
        own = [
            keep_own(srcs[i], outs[i].at[place.s, place.b], buffers[i], own_sems.at[i])
            for i in range(count)
        ]
        for j in range(1, place.half):
            for gather in gathers:
                gather.step(j)
            for gather in gathers:
                gather.collect(j - 1)
        for gather in gathers:
            gather.collect(place.half - 1)
        for gather in gathers:
            gather.finish()
        for copy in own:
            copy.wait()
        wire.drain()

    return comm_call(
        kernel,
        [shape_of((n_seq, n_bat), block) for block in blocks],
        [pltpu.VMEM(block.shape, block.dtype) for block in blocks]
        + [pltpu.SemaphoreType.DMA((count,))],
        n_seq * n_bat * count,
        collective_id,
        name,
        [ANY] * count,
    )(*blocks)


def add_into(target, *others):
    rows = target.shape[0]
    step = min(rows, 16)

    def body(i, carry):
        at = pl.ds(pl.multiple_of(i * step, step), step)
        total = target[at, :].astype(F32)
        for other in others:
            total = total + other[at, :].astype(F32)
        target[at, :] = total.astype(target.dtype)
        return carry

    lax.fori_loop(0, rows // step, body, 0)


class FullScatter:
    def __init__(self, place, wire, parts, out, mine, twin, across, line, sems, local):
        self.place, self.wire, self.parts, self.out = place, wire, parts, out
        self.mine, self.twin, self.across, self.line = mine, twin, across, line
        self.sems, self.local = sems, local

    @staticmethod
    def scratch(n_seq, n_bat, block):
        half = n_seq // 2
        return [
            pltpu.VMEM((half, n_bat) + block.shape, block.dtype),
            pltpu.VMEM((half, n_bat) + block.shape, block.dtype),
            pltpu.VMEM((half, n_bat) + block.shape, block.dtype),
            pltpu.VMEM((half,) + block.shape, block.dtype),
            pltpu.SemaphoreType.DMA((half, n_bat)),
        ]

    def order(self):
        return list(range(1, self.place.half)) + [0]

    def start(self):
        place = self.place
        self.from_twin, self.loads, self.from_bat, self.from_seq = {}, {}, {}, {}
        for j in self.order():
            for k in list(range(1, place.n_bat)) + [0]:
                to_bat = place.bat_at(k)
                self.from_twin[j, k] = self.wire.push(
                    self.parts.at[place.twin_at(2 * j), to_bat], self.twin.at[j, k], place.twin()
                )
                load = pltpu.make_async_copy(
                    self.parts.at[place.seq_at(2 * j), to_bat],
                    self.mine.at[j, k],
                    self.sems.at[j, k],
                )
                load.start()
                self.loads[j, k] = load

    def pair(self, j):
        place = self.place
        for k in list(range(1, place.n_bat)) + [0]:
            self.from_twin[j, k].wait_recv()
            self.loads[j, k].wait()
            add_into(self.mine.at[j, k], self.twin.at[j, k])
        for k in range(1, place.n_bat):
            self.from_bat[j, k] = self.wire.push(
                self.mine.at[j, k], self.across.at[j, k], place.bat_peer(k)
            )

    def merge(self, j):
        place = self.place
        for k in range(1, place.n_bat):
            self.from_bat[j, k].wait_recv()
        add_into(self.mine.at[j, 0], *[self.across.at[j, k] for k in range(1, place.n_bat)])
        if j:
            self.from_seq[j] = self.wire.push(
                self.mine.at[j, 0], self.line.at[j], place.seq_peer(2 * j)
            )

    def finish(self):
        for j in range(1, self.place.half):
            self.from_seq[j].wait_recv()
        add_into(self.mine.at[0, 0], *[self.line.at[j] for j in range(1, self.place.half)])
        self.out[...] = self.mine[0, 0]


def scatter_all(parts, n_seq, n_bat, collective_id, name):
    blocks = [jax.ShapeDtypeStruct(part.shape[2:], part.dtype) for part in parts]
    count = len(parts)

    def kernel(*refs):
        ins, outs = refs[:count], refs[count : 2 * count]
        rest = refs[2 * count :]
        send_sems, recv_sems = rest[-2:]
        place = Place(n_seq, n_bat)
        place.greet()
        wire = Wire(send_sems, recv_sems)
        works = [
            FullScatter(place, wire, ins[i], outs[i], *rest[5 * i : 5 * i + 5], None)
            for i in range(count)
        ]
        for work in works:
            work.start()
        order = works[0].order()
        for at, j in enumerate(order):
            for work in works:
                work.pair(j)
            if at:
                for work in works:
                    work.merge(order[at - 1])
        for work in works:
            work.merge(order[-1])
        for work in works:
            work.finish()
        wire.drain()

    scratch = []
    for block in blocks:
        scratch += FullScatter.scratch(n_seq, n_bat, block)
    slots = count * (n_seq * n_bat)
    vmem = pl.BlockSpec(memory_space=pltpu.VMEM)
    return comm_call(
        kernel,
        blocks,
        scratch,
        slots,
        collective_id,
        name,
        [ANY] * count,
        [vmem] * count,
    )(*parts)


def scatter_seq(parts, n_seq, n_bat, collective_id, name):
    block = jax.ShapeDtypeStruct(parts.shape[1:], parts.dtype)
    half = n_seq // 2

    def kernel(ref, out, mine, twin, line, sems, send_sems, recv_sems):
        place = Place(n_seq, n_bat)
        place.greet(batch=False)
        wire = Wire(send_sems, recv_sems)
        order = list(range(1, half)) + [0]
        from_twin, loads, from_seq = {}, {}, {}
        for j in order:
            from_twin[j] = wire.push(ref.at[place.twin_at(2 * j)], twin.at[j], place.twin())
            loads[j] = pltpu.make_async_copy(ref.at[place.seq_at(2 * j)], mine.at[j], sems.at[j])
            loads[j].start()
        for j in order:
            from_twin[j].wait_recv()
            loads[j].wait()
            add_into(mine.at[j], twin.at[j])
            if j:
                from_seq[j] = wire.push(mine.at[j], line.at[j], place.seq_peer(2 * j))
        for j in range(1, half):
            from_seq[j].wait_recv()
        add_into(mine.at[0], *[line.at[j] for j in range(1, half)])
        out[...] = mine[0]
        wire.drain()

    scratch = [pltpu.VMEM((half,) + block.shape, block.dtype)] * 3
    return comm_call(
        kernel,
        block,
        scratch + [pltpu.SemaphoreType.DMA((half,))],
        n_seq,
        collective_id,
        name,
        [ANY],
        pl.BlockSpec(memory_space=pltpu.VMEM),
    )(parts)


def pack(values):
    flat = values.astype(F32).reshape(-1)
    tiles = -(-flat.shape[0] // 1024)
    return jnp.pad(flat, (0, tiles * 1024 - flat.shape[0])).reshape(tiles * 8, 128)


def unpack(tiles, lead, shape):
    size = 1
    for extent in shape:
        size *= extent
    return tiles.reshape(tuple(lead) + (-1,))[..., :size].reshape(tuple(lead) + tuple(shape))

def sum_seq(values, n_seq, n_bat, collective_id, name):
    tiles = gather_seq(pack(values), n_seq, n_bat, collective_id, name)
    return unpack(jnp.sum(tiles, axis=0), (), values.shape)


def scatter_blocks(grad_normed, grad_gates, mixture, n_seq, n_bat):
    dim = grad_normed.shape[-1]
    pieces = 1
    while n_seq * n_bat * grad_normed.shape[2] * (dim // pieces) * 4 > 36 * 1024 * 1024:
        pieces *= 2
    size = dim // pieces
    grads, mixtures = [], []
    for i in range(pieces):
        at = slice(i * size, (i + 1) * size)
        parts = [grad_normed[..., at]] + ([grad_gates] if i == 0 else [])
        done = scatter_all(parts, n_seq, n_bat, 16 + 2 * i, "scatter_normed")
        grads.append(done[0])
        if i == 0:
            gates = done[1]
        done = scatter_all([mixture[..., at]], n_seq, n_bat, 17 + 2 * i, "scatter_mixture")
        mixtures.append(done[0])
    return jnp.concatenate(grads, axis=-1), gates, jnp.concatenate(mixtures, axis=-1)


def load_inputs(qkv_cut, w_out, mine, flags, small, gu_cut, dy_own, n_seq, n_bat):
    n_in = 7
    slots = 4 * n_seq * n_bat + 3 * n_seq + 2 * n_bat

    def kernel(*refs):
        cut_ref, wo_ref, x_ref, flag_ref, small_ref, gu_ref, dy_ref = refs[:n_in]
        w_ref, wo_all, x_col, flag_col, small_all, gu_all, dy_all = refs[n_in : 2 * n_in]
        buffers = refs[2 * n_in : 3 * n_in]
        own_sems, send_sems, recv_sems = refs[3 * n_in :]
        place = Place(n_seq, n_bat)
        place.greet(all_seq=True)
        wire = Wire(send_sems, recv_sems)
        small_work = FullGather(place, wire, small_ref, small_all)
        flag_work = SeqGather(place, wire, flag_ref, flag_col)
        x_work = SeqGather(place, wire, x_ref, x_col)
        dy_work = FullGather(place, wire, dy_ref, dy_all)
        small_work.start()
        flag_work.start()
        cuts = [
            wire.push(cut_ref.at[place.seq_at(k)], w_ref.at[place.s, place.b], place.seq_peer(k))
            for k in range(1, n_seq)
        ]
        ends = [
            wire.push(wo_ref, wo_all.at[place.b], place.bat_peer(k)) for k in range(1, n_bat)
        ]
        ends += [
            wire.push(cut_ref.at[place.s], w_ref.at[place.s, place.b], place.bat_peer(k))
            for k in range(1, n_bat)
        ]
        x_work.start()
        own = [
            keep_own(src, dst, buffers[i], own_sems.at[i])
            for i, (src, dst) in enumerate(
                (
                    (cut_ref.at[place.s], w_ref.at[place.s, place.b]),
                    (wo_ref, wo_all.at[place.b]),
                    (x_ref, x_col.at[place.s]),
                    (flag_ref, flag_col.at[place.s]),
                    (small_ref, small_all.at[place.s, place.b]),
                    (gu_ref.at[place.s], gu_all.at[place.s]),
                    (dy_ref, dy_all.at[place.s, place.b]),
                )
            )
        ]
        ends += [
            wire.push(gu_ref.at[place.seq_at(k)], gu_all.at[place.s], place.seq_peer(k))
            for k in range(1, n_seq)
        ]
        dy_work.start()
        for j in range(1, place.half):
            small_work.step(j)
            flag_work.step(j)
        for k in range(1, n_seq):
            cuts[k - 1].wait_recv()
            block = w_ref.at[place.seq_at(-k), place.b]
            ends += [wire.push(block, block, place.bat_peer(m)) for m in range(1, n_bat)]
        for j in range(place.half):
            small_work.collect(j)
        for j in range(1, place.half):
            x_work.step(j)
        for j in range(1, place.half):
            dy_work.step(j)
            dy_work.collect(j - 1)
        dy_work.collect(place.half - 1)
        for work in (small_work, flag_work, x_work, dy_work):
            work.finish()
        for copy in ends:
            copy.wait_recv()
        for copy in own:
            copy.wait()
        wire.drain()

    every = (n_seq, n_bat)
    one = jax.ShapeDtypeStruct(qkv_cut.shape[1:], qkv_cut.dtype)
    gu_one = jax.ShapeDtypeStruct(gu_cut.shape[1:], gu_cut.dtype)
    blocks = (one, w_out, mine, flags, small, gu_one, dy_own)
    leads = (every, (n_bat,), (n_seq,), (n_seq,), every, (n_seq,), every)
    return comm_call(
        kernel,
        [shape_of(lead, block) for lead, block in zip(leads, blocks)],
        [pltpu.VMEM(block.shape, block.dtype) for block in blocks]
        + [pltpu.SemaphoreType.DMA((n_in,))],
        slots,
        1,
        "load_inputs",
        [ANY] * n_in,
    )(qkv_cut, w_out, mine, flags, small, gu_cut, dy_own)


def store_grads(grad_w, grad_wo, grad_gu, small, n_seq, n_bat):
    one = jax.ShapeDtypeStruct(grad_w.shape[2:], grad_w.dtype)
    wo_one = jax.ShapeDtypeStruct(grad_wo.shape[1:], grad_wo.dtype)
    gu_one = jax.ShapeDtypeStruct(grad_gu.shape[1:], grad_gu.dtype)
    small_one = jax.ShapeDtypeStruct(small.shape[2:], small.dtype)
    slots = 2 * n_seq * n_bat + 2 * n_seq + n_bat

    def kernel(*refs):
        w_ref, wo_ref, gu_ref, small_ref = refs[:4]
        w_out_ref, wo_out_ref, gu_out_ref, small_out_ref = refs[4:8]
        w_sum, w_got, wo_sum, wo_got, gu_buf, cut_buf = refs[8:14]
        small_scratch = refs[14:19]
        w_sems, sems, send_sems, recv_sems = refs[19:]
        place = Place(n_seq, n_bat)
        place.greet(all_seq=True)
        wire = Wire(send_sems, recv_sems)
        small_work = FullScatter(
            place, wire, small_ref, small_out_ref, *small_scratch, None
        )
        small_work.start()
        got, loads = {}, {}
        for i in list(range(1, n_seq)) + [0]:
            to_seq = place.seq_at(i)
            for k in range(1, n_bat):
                got[i, k] = wire.push(
                    w_ref.at[to_seq, place.bat_at(k)], w_got.at[i, k - 1], place.bat_peer(k)
                )
            loads[i] = pltpu.make_async_copy(
                w_ref.at[to_seq, place.b], w_sum.at[i], w_sems.at[i]
            )
            loads[i].start()
        wo_pushed = [
            wire.push(wo_ref.at[place.bat_at(k)], wo_got.at[k - 1], place.bat_peer(k))
            for k in range(1, n_bat)
        ]
        wo_load = pltpu.make_async_copy(wo_ref.at[place.b], wo_sum, sems.at[0])
        wo_load.start()
        ends = [
            wire.push(gu_ref.at[place.seq_at(k)], gu_out_ref.at[place.s], place.seq_peer(k))
            for k in range(1, n_seq)
        ]
        gu_own = keep_own(gu_ref.at[place.s], gu_out_ref.at[place.s], gu_buf, sems.at[1])
        order = small_work.order()
        for j in order:
            small_work.pair(j)
        for i in list(range(1, n_seq)) + [0]:
            loads[i].wait()
            for k in range(1, n_bat):
                got[i, k].wait_recv()
            add_into(w_sum.at[i], *[w_got.at[i, k] for k in range(n_bat - 1)])
            if i:
                ends.append(
                    wire.push(w_sum.at[i], w_out_ref.at[place.s], place.seq_peer(i))
                )
        w_own = pltpu.make_async_copy(w_sum.at[0], w_out_ref.at[place.s], sems.at[2])
        w_own.start()
        for j in order:
            small_work.merge(j)
        wo_load.wait()
        for copy in wo_pushed:
            copy.wait_recv()
        add_into(wo_sum, *[wo_got.at[k] for k in range(n_bat - 1)])
        wo_out_ref[...] = wo_sum[...].astype(F32)
        small_work.finish()
        for copy in ends:
            copy.wait_recv()
        gu_own.wait()
        w_own.wait()
        wire.drain()

    vmem = pl.BlockSpec(memory_space=pltpu.VMEM)
    return comm_call(
        kernel,
        [
            shape_of((n_seq,), one),
            jax.ShapeDtypeStruct(wo_one.shape, F32),
            shape_of((n_seq,), gu_one),
            small_one,
        ],
        [
            pltpu.VMEM((n_seq,) + one.shape, one.dtype),
            pltpu.VMEM((n_seq, n_bat - 1) + one.shape, one.dtype),
            pltpu.VMEM(wo_one.shape, wo_one.dtype),
            pltpu.VMEM((n_bat - 1,) + wo_one.shape, wo_one.dtype),
            pltpu.VMEM(gu_one.shape, gu_one.dtype),
            pltpu.VMEM(one.shape, one.dtype),
        ]
        + FullScatter.scratch(n_seq, n_bat, small_one)
        + [pltpu.SemaphoreType.DMA((n_seq,)), pltpu.SemaphoreType.DMA((3,))],
        slots,
        8,
        "store_grads",
        [ANY] * 4,
        [ANY, vmem, ANY, vmem],
    )(grad_w, grad_wo, grad_gu, small)


def shards(
    tokens,
    lengths,
    key_mask,
    top_experts,
    attn_gain,
    query_gain,
    key_gain,
    mlp_gain,
    w_query,
    w_key,
    w_value,
    w_out,
    w_router,
    expert_gate,
    expert_up,
    expert_down,
    cotangent,
):
    n_seq = lax.axis_size("seq")
    n_bat = lax.axis_size("batch")
    seq = lax.axis_index("seq")
    bat = lax.axis_index("batch")
    rows, span, dim = tokens.shape
    own = rows * span
    col = n_seq * own
    length = n_seq * span
    shard = w_query.shape[0]
    wide = dim // n_seq
    heads = wide // HEAD
    local_experts, depth, hidden_units = expert_gate.shape
    part = hidden_units // n_seq
    experts = local_experts * n_bat
    score_scale = HEAD ** (-0.5)

    mine = tokens.reshape(own, dim)
    dy_own = cotangent.reshape(own, dim)
    small = jnp.concatenate(
        [w_router.T, jnp.stack([attn_gain, query_gain, key_gain, mlp_gain])], axis=0
    )
    positions_own = seq * span + jnp.arange(span, dtype=jnp.int32)
    flags = pack((positions_own[None, :] < lengths[:, None]) & (key_mask == 1))
    qkv_cut = jnp.stack([w_query, w_key, w_value]).reshape(3, shard, n_seq, wide)
    qkv_cut = jnp.transpose(qkv_cut, (2, 1, 0, 3)).reshape(n_seq, shard, 3 * wide)
    gu_cut = jnp.stack([expert_gate, expert_up]).reshape(2, local_experts, depth, n_seq, part)
    gu_cut = jnp.transpose(gu_cut, (3, 2, 0, 1, 4)).reshape(n_seq, depth, 2 * local_experts * part)
    w_qkv, w_o, x_col, flag_col, small_all, w_gu, dy_all = load_inputs(
        qkv_cut, w_out, mine, flags, pack(small), gu_cut, dy_own, n_seq, n_bat
    )
    w_qkv = w_qkv.reshape(dim, 3 * wide)
    w_o = w_o.reshape(wide, dim)
    w_gu = w_gu.reshape(dim, 2 * local_experts * part)
    w_down = expert_down.reshape(local_experts * part, dim)
    dy_all = dy_all.reshape(-1, dim)
    small_all = unpack(small_all, (n_seq, n_bat), small.shape)
    small_all = jnp.transpose(small_all, (2, 0, 1, 3)).reshape(-1, dim)
    router = small_all[:experts].T.astype(BF)
    gain_attn, gain_mlp = small_all[experts], small_all[experts + 3]
    gain_q = lax.dynamic_slice_in_dim(small_all[experts + 1], seq * wide, wide)
    gain_k = lax.dynamic_slice_in_dim(small_all[experts + 2], seq * wide, wide)
    usable = unpack(flag_col, (n_seq,), key_mask.shape)
    usable = jnp.transpose(usable, (1, 0, 2)).reshape(rows, length) > 0

    x_col = x_col.reshape(col, dim).astype(F32)
    scale_x = rms_scale(x_col)
    hidden = (x_col * scale_x * gain_attn).astype(BF)
    qkv = dot(hidden, w_qkv)
    q_pre, k_pre, v_pre = qkv[:, :wide], qkv[:, wide : 2 * wide], qkv[:, 2 * wide :]

    squares = jnp.stack([jnp.sum(q_pre * q_pre, axis=-1), jnp.sum(k_pre * k_pre, axis=-1)])
    squares = sum_seq(squares, n_seq, n_bat, 2, "sum_squares")
    scales = lax.rsqrt(squares / dim + EPS)
    scale_q, scale_k = scales[0][:, None], scales[1][:, None]

    def by_row(v):
        v = v.reshape(n_seq, rows, span, heads, HEAD)
        return jnp.transpose(v, (1, 3, 0, 2, 4)).reshape(rows, heads, length, HEAD)

    def by_col(v):
        v = v.reshape(rows, heads, n_seq, span, HEAD)
        return jnp.transpose(v, (2, 0, 3, 1, 4)).reshape(col, wide)

    positions = jnp.arange(length, dtype=jnp.int32)
    cos_part, sin_part = rotary_tables(positions)
    q_norm = by_row(q_pre * scale_q)
    k_norm = by_row(k_pre * scale_k)
    gain_qh = gain_q.reshape(1, heads, 1, HEAD)
    gain_kh = gain_k.reshape(1, heads, 1, HEAD)
    queries = rotate(q_norm * gain_qh, cos_part, sin_part).astype(BF)
    keys = rotate(k_norm * gain_kh, cos_part, sin_part).astype(BF)
    values = by_row(v_pre.astype(BF))

    causal = positions[None, :] <= positions[:, None]
    same = positions[None, :] == positions[:, None]
    allowed = (causal[None] & (usable[:, None, :] | same[None]))[:, None]
    scores = jnp.einsum("rhqd,rhkd->rhqk", queries, keys, preferred_element_type=F32) * score_scale
    scores = jnp.where(allowed, scores, NEGATIVE)
    top = jnp.max(scores, axis=-1, keepdims=True)
    raised = jnp.exp(scores - top)
    probs = raised / jnp.sum(raised, axis=-1, keepdims=True)
    probs_low = probs.astype(BF)
    attended = jnp.einsum("rhqk,rhkd->rhqd", probs_low, values, preferred_element_type=F32)
    mixed = by_col(attended.astype(BF))

    mixed_out = scatter_seq(
        dot(mixed, w_o).astype(BF).reshape(n_seq, own, dim), n_seq, n_bat, 3, "scatter_mixed"
    )
    x_own = mine.astype(F32)
    residual = x_own + mixed_out.astype(F32)
    scale_r = rms_scale(residual)
    normed = (residual * scale_r * gain_mlp).astype(BF)
    router_probs = jax.nn.softmax(dot(normed, router), axis=-1)
    expert_ids = jnp.arange(experts, dtype=jnp.int32)
    chosen = jnp.any(top_experts.reshape(own, -1)[:, :, None] == expert_ids, axis=1).astype(F32)
    gates = router_probs * chosen

    normed_all, gates_all = gather_all([normed, pack(gates.T)], n_seq, n_bat, 4, "gather_normed")
    normed_all = normed_all.reshape(-1, dim)
    gates_all = unpack(gates_all, (n_seq, n_bat), (experts, own))
    gates_all = jnp.transpose(gates_all, (0, 1, 3, 2)).reshape(-1, experts)
    first_expert = bat * local_experts
    gates_here = lax.dynamic_slice_in_dim(gates_all, first_expert, local_experts, 1)
    units = local_experts * part
    gates_wide = jnp.repeat(gates_here, part, axis=1)
    pre = dot(normed_all, w_gu)
    gate_pre, up_pre = pre[:, :units], pre[:, units:]
    sig = jax.nn.sigmoid(gate_pre)
    silu = gate_pre * sig
    active = (silu * up_pre).astype(BF).astype(F32)
    weighted = (active * gates_wide).astype(BF)
    mixture = dot(weighted, w_down).astype(BF)
    mixture = mixture.reshape(n_seq, n_bat, own, dim)
    back = dot_t(dy_all, w_down)
    gate_terms = jnp.sum((active * back).reshape(-1, local_experts, part), axis=-1)
    grad_active = back * gates_wide
    grad_gate_pre = (grad_active * up_pre * sig * (1.0 + gate_pre * (1.0 - sig))).astype(BF)
    grad_up_pre = (grad_active * silu).astype(BF)
    grad_pre = jnp.concatenate([grad_gate_pre, grad_up_pre], axis=1)
    grad_down = t_dot(weighted, dy_all)
    grad_gu = t_dot(normed_all, grad_pre).astype(BF)
    grad_normed = dot_t(grad_pre, w_gu).astype(BF)
    gate_terms = gate_terms.reshape(n_seq, n_bat, own, local_experts)
    grad_gates = lax.dynamic_update_slice_in_dim(
        jnp.zeros((n_seq, n_bat, experts, own), F32),
        jnp.transpose(gate_terms, (0, 1, 3, 2)),
        first_expert,
        2,
    )
    grad_gates = jax.vmap(jax.vmap(pack))(grad_gates)
    grad_normed = grad_normed.reshape(n_seq, n_bat, own, dim)
    grad_normed, grad_gates, mixture = scatter_blocks(
        grad_normed, grad_gates, mixture, n_seq, n_bat
    )
    grad_normed = grad_normed.astype(F32)
    grad_gates = unpack(grad_gates, (), (experts, own)).T
    output = (residual + mixture.astype(F32)).astype(BF)
    grad_down = grad_down.reshape(local_experts, part, dim)

    grad_chosen = grad_gates * chosen
    grad_logits = router_probs * (
        grad_chosen - jnp.sum(router_probs * grad_chosen, axis=-1, keepdims=True)
    )
    grad_router = lax.dot_general(
        normed.astype(F32), grad_logits, (((0,), (0,)), ((), ())), precision=HIGHEST
    )
    grad_normed = grad_normed + lax.dot_general(
        grad_logits, router.astype(F32), (((1,), (1,)), ((), ())), precision=HIGHEST
    )
    grad_resid, gain_mlp_terms = rms_back(residual, scale_r, gain_mlp, grad_normed)
    grad_residual = dy_own.astype(F32) + grad_resid
    grad_o = grad_residual.astype(BF)

    grad_o_col = gather_seq(grad_o, n_seq, n_bat, 6, "gather_grad_o").reshape(col, dim)
    grad_mixed = by_row(dot_t(grad_o_col, w_o).astype(BF))
    grad_w_o = t_dot(mixed, grad_o_col).astype(BF).reshape(n_bat, shard, dim)
    row_dot = jnp.sum(grad_mixed.astype(F32) * attended, axis=-1, keepdims=True)
    grad_values = jnp.einsum("rhqk,rhqd->rhkd", probs_low, grad_mixed, preferred_element_type=F32)
    grad_probs = jnp.einsum("rhqd,rhkd->rhqk", grad_mixed, values, preferred_element_type=F32)
    grad_scores = (probs * (grad_probs - row_dot)).astype(BF)
    grad_q = score_scale * jnp.einsum(
        "rhqk,rhkd->rhqd", grad_scores, keys, preferred_element_type=F32
    )
    grad_k = score_scale * jnp.einsum(
        "rhqk,rhqd->rhkd", grad_scores, queries, preferred_element_type=F32
    )
    grad_q = rotate(grad_q, cos_part, -sin_part)
    grad_k = rotate(grad_k, cos_part, -sin_part)
    grad_gain_q = jnp.sum(grad_q * q_norm, axis=(0, 2)).reshape(wide)
    grad_gain_k = jnp.sum(grad_k * k_norm, axis=(0, 2)).reshape(wide)
    q_weighted = by_col(grad_q * gain_qh)
    k_weighted = by_col(grad_k * gain_kh)
    q_flat = q_pre * scale_q
    k_flat = k_pre * scale_k
    means = jnp.stack(
        [jnp.sum(q_weighted * q_flat, axis=-1), jnp.sum(k_weighted * k_flat, axis=-1)]
    )
    means = sum_seq(means, n_seq, n_bat, 9, "sum_means") / dim
    grad_q_pre = (scale_q * (q_weighted - q_flat * means[0][:, None])).astype(BF)
    grad_k_pre = (scale_k * (k_weighted - k_flat * means[1][:, None])).astype(BF)
    grad_qkv = jnp.concatenate([grad_q_pre, grad_k_pre, by_col(grad_values).astype(BF)], axis=1)

    grad_hidden = dot_t(grad_qkv, w_qkv).astype(BF)
    grad_hidden = grad_hidden.reshape(n_seq, own, dim)
    grad_hidden = scatter_seq(grad_hidden, n_seq, n_bat, 7, "scatter_hidden").astype(F32)
    grad_w = t_dot(hidden, grad_qkv).astype(BF).reshape(n_seq, n_bat, shard, 3 * wide)

    grad_x, gain_attn_terms = rms_back(x_own, rms_scale(x_own), gain_attn, grad_hidden)
    grad_tokens = (grad_residual + grad_x).astype(BF)

    zeros = jnp.zeros((dim,), F32)
    small_grads = jnp.concatenate(
        [
            grad_router.T,
            jnp.stack(
                [
                    jnp.sum(gain_attn_terms, axis=0),
                    lax.dynamic_update_slice_in_dim(zeros, grad_gain_q, seq * wide, 0),
                    lax.dynamic_update_slice_in_dim(zeros, grad_gain_k, seq * wide, 0),
                    jnp.sum(gain_mlp_terms, axis=0),
                ]
            ),
        ],
        axis=0,
    )
    small_grads = jnp.transpose(small_grads.reshape(-1, n_seq, n_bat, shard), (1, 2, 0, 3))
    small_grads = jax.vmap(jax.vmap(pack))(small_grads)
    grad_gu = grad_gu.reshape(n_seq, depth, -1)
    grad_w, grad_w_o, grad_gu, small_grads = store_grads(
        grad_w, grad_w_o, grad_gu, small_grads, n_seq, n_bat
    )
    grad_w = grad_w.astype(F32).reshape(n_seq, shard, 3, wide)
    grad_w = jnp.transpose(grad_w, (2, 1, 0, 3)).reshape(3, shard, dim)
    grad_gu = grad_gu.reshape(n_seq, depth, 2, local_experts, part)
    grad_gu = jnp.transpose(grad_gu, (2, 3, 1, 0, 4)).reshape(2, local_experts, depth, hidden_units)
    grad_gu = grad_gu.astype(F32)
    small_grads = unpack(small_grads, (), (experts + 4, shard))

    return (
        output.reshape(rows, span, dim),
        grad_tokens.reshape(rows, span, dim),
        small_grads[experts],
        small_grads[experts + 1],
        small_grads[experts + 2],
        small_grads[experts + 3],
        grad_w[0],
        grad_w[1],
        grad_w[2],
        grad_w_o,
        small_grads[:experts].T,
        grad_gu[0],
        grad_gu[1],
        grad_down,
    )


def solution(mesh):
    tok = P("batch", "seq", None)
    vec = P(("seq", "batch"))
    mat = P(("seq", "batch"), None)
    in_specs = (tok, P("batch"), P("batch", "seq"), tok) + (vec,) * 4 + (mat,) * 5 + (tok,) * 4
    out_specs = (tok, tok) + (vec,) * 4 + (mat,) * 5 + (tok,) * 3
    return jax.shard_map(shards, mesh=mesh, in_specs=in_specs, out_specs=out_specs, check_vma=False)
```

```python
import functools

import jax
import jax.numpy as jnp
from jax import lax
from jax.experimental import pallas as pl
from jax.experimental.pallas import tpu as pltpu
from jax.sharding import PartitionSpec as P

HEAD = 128
EPS = 1e-05
HIGHEST = lax.Precision.HIGHEST
NEGATIVE = -1e30
BF = jnp.bfloat16
F32 = jnp.float32


def dot(a, b):
    return jnp.dot(a, b, preferred_element_type=F32)


def dot_t(a, b):
    return lax.dot_general(a, b, (((1,), (1,)), ((), ())), preferred_element_type=F32)


def t_dot(a, b):
    return lax.dot_general(a, b, (((0,), (0,)), ((), ())), preferred_element_type=F32)


def rms_scale(v):
    return lax.rsqrt(jnp.mean(v * v, axis=-1, keepdims=True) + EPS)


def rms_back(v, scale, gain, grad):
    normal = v * scale
    weighted = grad * gain
    mean = jnp.mean(weighted * normal, axis=-1, keepdims=True)
    return scale * (weighted - normal * mean), grad * normal


def rotary_tables(positions):
    half_head = HEAD // 2
    frequency = 10000.0 ** (-2.0 * jnp.arange(half_head, dtype=F32) / HEAD)
    angles = positions.astype(F32)[:, None] * frequency[None, :]
    return jnp.cos(angles), jnp.sin(angles)


ANY = pl.BlockSpec(memory_space=pl.ANY)
VMEM_LIMIT = 60 * 1024 * 1024


class Place:
    def __init__(self, n_seq, n_bat):
        self.n_seq, self.n_bat, self.half = n_seq, n_bat, n_seq // 2
        self.s = lax.axis_index("seq")
        self.b = lax.axis_index("batch")
        self.twin_s = self.s + 1 - 2 * lax.rem(self.s, 2)

    def seq_at(self, k):
        return lax.rem(self.s + (k + self.n_seq), self.n_seq)

    def twin_at(self, k):
        return lax.rem(self.twin_s + (k + self.n_seq), self.n_seq)

    def bat_at(self, k):
        return lax.rem(self.b + (k + self.n_bat), self.n_bat)

    def seq_peer(self, k):
        return {"seq": self.seq_at(k), "batch": self.b}

    def bat_peer(self, k):
        return {"seq": self.s, "batch": self.bat_at(k)}

    def twin(self):
        return {"seq": self.twin_s, "batch": self.b}

    def greet(self, all_seq=False, batch=True):
        steps = range(1, self.n_seq) if all_seq else range(2, self.n_seq, 2)
        peers = [self.seq_peer(k) for k in steps]
        if not all_seq:
            peers.append(self.twin())
        if batch:
            peers += [self.bat_peer(k) for k in range(1, self.n_bat)]
        barrier = pltpu.get_barrier_semaphore()
        for peer in peers:
            pl.semaphore_signal(
                barrier, inc=1, device_id=peer, device_id_type=pl.DeviceIdType.MESH
            )
        pl.semaphore_wait(barrier, len(peers))


class Wire:
    def __init__(self, send_sems, recv_sems):
        self.send_sems, self.recv_sems = send_sems, recv_sems
        self.copies = []

    def push(self, src, dst, peer):
        slot = len(self.copies)
        copy = pltpu.make_async_remote_copy(
            src_ref=src,
            dst_ref=dst,
            send_sem=self.send_sems.at[slot],
            recv_sem=self.recv_sems.at[slot],
            device_id=peer,
            device_id_type=pl.DeviceIdType.MESH,
        )
        copy.start()
        self.copies.append(copy)
        return copy

    def drain(self):
        for copy in self.copies:
            copy.wait_send()


class SeqGather:
    def __init__(self, place, wire, src, out):
        self.place, self.wire, self.src, self.out = place, wire, src, out
        self.late = []

    def start(self):
        place, mine = self.place, self.out.at[self.place.s]
        self.line = [
            self.wire.push(self.src, mine, place.seq_peer(2 * j)) for j in range(1, place.half)
        ]
        self.late.append(self.wire.push(self.src, mine, place.twin()))

    def step(self, j):
        self.line[j - 1].wait_recv()
        block = self.out.at[self.place.seq_at(-2 * j)]
        self.late.append(self.wire.push(block, block, self.place.twin()))

    def finish(self):
        for copy in self.late:
            copy.wait_recv()


class FullGather:
    def __init__(self, place, wire, src, out):
        self.place, self.wire, self.src, self.out = place, wire, src, out
        self.late = []
        self.across = {}

    def spread(self, j, block):
        place = self.place
        self.across[j] = [
            self.wire.push(block, self.out.at[place.seq_at(-2 * j), place.b], place.bat_peer(k))
            for k in range(1, place.n_bat)
        ]

    def start(self):
        place, mine = self.place, self.out.at[self.place.s, self.place.b]
        self.line = [
            self.wire.push(self.src, mine, place.seq_peer(2 * j)) for j in range(1, place.half)
        ]
        self.spread(0, self.src)
        self.late.append(self.wire.push(self.src, mine, place.twin()))

    def step(self, j):
        self.line[j - 1].wait_recv()
        block = self.out.at[self.place.seq_at(-2 * j), self.place.b]
        self.spread(j, block)
        self.late.append(self.wire.push(block, block, self.place.twin()))

    def collect(self, j):
        place = self.place
        for k in range(1, place.n_bat):
            self.across[j][k - 1].wait_recv()
            block = self.out.at[place.seq_at(-2 * j), place.bat_at(-k)]
            self.late.append(self.wire.push(block, block, place.twin()))

    def finish(self):
        for copy in self.late:
            copy.wait_recv()


def keep_own(src, dst, buffer, sem):
    first = pltpu.make_async_copy(src, buffer, sem)
    first.start()
    first.wait()
    second = pltpu.make_async_copy(buffer, dst, sem)
    second.start()
    return second


def comm_call(kernel, outs, scratch, slots, collective_id, name, in_specs, out_specs=None):
    return pl.pallas_call(
        kernel,
        out_shape=outs,
        in_specs=in_specs,
        out_specs=out_specs if out_specs is not None else jax.tree.map(lambda _: ANY, outs),
        scratch_shapes=list(scratch)
        + [pltpu.SemaphoreType.DMA((slots,)), pltpu.SemaphoreType.DMA((slots,))],
        compiler_params=pltpu.CompilerParams(
            collective_id=collective_id, has_side_effects=True, vmem_limit_bytes=VMEM_LIMIT
        ),
        name=name,
    )


def shape_of(lead, block):
    return jax.ShapeDtypeStruct(tuple(lead) + block.shape, block.dtype)


def gather_all(blocks, n_seq, n_bat, collective_id, name):
    count = len(blocks)

    def kernel(*refs):
        srcs, outs = refs[:count], refs[count : 2 * count]
        buffers = refs[2 * count : 3 * count]
        own_sems, send_sems, recv_sems = refs[3 * count :]
        place = Place(n_seq, n_bat)
        place.greet()
        wire = Wire(send_sems, recv_sems)
        gathers = [FullGather(place, wire, *pair) for pair in zip(srcs, outs)]
        for gather in gathers:
            gather.start()
        own = [
            keep_own(srcs[i], outs[i].at[place.s, place.b], buffers[i], own_sems.at[i])
            for i in range(count)
        ]
        for j in range(1, place.half):
            for gather in gathers:
                gather.step(j)
            for gather in gathers:
                gather.collect(j - 1)
        for gather in gathers:
            gather.collect(place.half - 1)
        for gather in gathers:
            gather.finish()
        for copy in own:
            copy.wait()
        wire.drain()

    return comm_call(
        kernel,
        [shape_of((n_seq, n_bat), block) for block in blocks],
        [pltpu.VMEM(block.shape, block.dtype) for block in blocks]
        + [pltpu.SemaphoreType.DMA((count,))],
        n_seq * n_bat * count,
        collective_id,
        name,
        [ANY] * count,
    )(*blocks)


def add_into(target, *others):
    rows = target.shape[0]
    step = min(rows, 16)

    def body(i, carry):
        at = pl.ds(pl.multiple_of(i * step, step), step)
        total = target[at, :].astype(F32)
        for other in others:
            total = total + other[at, :].astype(F32)
        target[at, :] = total.astype(target.dtype)
        return carry

    lax.fori_loop(0, rows // step, body, 0)


class FullScatter:
    def __init__(self, place, wire, parts, out, mine, twin, across, line, sems, local):
        self.place, self.wire, self.parts, self.out = place, wire, parts, out
        self.mine, self.twin, self.across, self.line = mine, twin, across, line
        self.sems, self.local = sems, local

    @staticmethod
    def scratch(n_seq, n_bat, block):
        half = n_seq // 2
        return [
            pltpu.VMEM((half, n_bat) + block.shape, block.dtype),
            pltpu.VMEM((half, n_bat) + block.shape, block.dtype),
            pltpu.VMEM((half, n_bat) + block.shape, block.dtype),
            pltpu.VMEM((half,) + block.shape, block.dtype),
            pltpu.SemaphoreType.DMA((half, n_bat)),
        ]

    def order(self):
        return list(range(1, self.place.half)) + [0]

    def start(self):
        place = self.place
        self.from_twin, self.loads, self.from_bat, self.from_seq = {}, {}, {}, {}
        for j in self.order():
            for k in list(range(1, place.n_bat)) + [0]:
                to_bat = place.bat_at(k)
                self.from_twin[j, k] = self.wire.push(
                    self.parts.at[place.twin_at(2 * j), to_bat], self.twin.at[j, k], place.twin()
                )
                load = pltpu.make_async_copy(
                    self.parts.at[place.seq_at(2 * j), to_bat],
                    self.mine.at[j, k],
                    self.sems.at[j, k],
                )
                load.start()
                self.loads[j, k] = load

    def pair(self, j):
        place = self.place
        for k in list(range(1, place.n_bat)) + [0]:
            self.from_twin[j, k].wait_recv()
            self.loads[j, k].wait()
            add_into(self.mine.at[j, k], self.twin.at[j, k])
        for k in range(1, place.n_bat):
            self.from_bat[j, k] = self.wire.push(
                self.mine.at[j, k], self.across.at[j, k], place.bat_peer(k)
            )

    def merge(self, j):
        place = self.place
        for k in range(1, place.n_bat):
            self.from_bat[j, k].wait_recv()
        add_into(self.mine.at[j, 0], *[self.across.at[j, k] for k in range(1, place.n_bat)])
        if j:
            self.from_seq[j] = self.wire.push(
                self.mine.at[j, 0], self.line.at[j], place.seq_peer(2 * j)
            )

    def finish(self):
        for j in range(1, self.place.half):
            self.from_seq[j].wait_recv()
        add_into(self.mine.at[0, 0], *[self.line.at[j] for j in range(1, self.place.half)])
        self.out[...] = self.mine[0, 0]


def scatter_all(parts, n_seq, n_bat, collective_id, name):
    blocks = [jax.ShapeDtypeStruct(part.shape[2:], part.dtype) for part in parts]
    count = len(parts)

    def kernel(*refs):
        ins, outs = refs[:count], refs[count : 2 * count]
        rest = refs[2 * count :]
        send_sems, recv_sems = rest[-2:]
        place = Place(n_seq, n_bat)
        place.greet()
        wire = Wire(send_sems, recv_sems)
        works = [
            FullScatter(place, wire, ins[i], outs[i], *rest[5 * i : 5 * i + 5], None)
            for i in range(count)
        ]
        for work in works:
            work.start()
        order = works[0].order()
        for at, j in enumerate(order):
            for work in works:
                work.pair(j)
            if at:
                for work in works:
                    work.merge(order[at - 1])
        for work in works:
            work.merge(order[-1])
        for work in works:
            work.finish()
        wire.drain()

    scratch = []
    for block in blocks:
        scratch += FullScatter.scratch(n_seq, n_bat, block)
    slots = count * (n_seq * n_bat)
    vmem = pl.BlockSpec(memory_space=pltpu.VMEM)
    return comm_call(
        kernel,
        blocks,
        scratch,
        slots,
        collective_id,
        name,
        [ANY] * count,
        [vmem] * count,
    )(*parts)


def pack(values):
    flat = values.astype(F32).reshape(-1)
    tiles = -(-flat.shape[0] // 1024)
    return jnp.pad(flat, (0, tiles * 1024 - flat.shape[0])).reshape(tiles * 8, 128)


def unpack(tiles, lead, shape):
    size = 1
    for extent in shape:
        size *= extent
    return tiles.reshape(tuple(lead) + (-1,))[..., :size].reshape(tuple(lead) + tuple(shape))


def scatter_blocks(grad_normed, grad_gates, mixture, n_seq, n_bat):
    dim = grad_normed.shape[-1]
    pieces = 1
    while n_seq * n_bat * grad_normed.shape[2] * (dim // pieces) * 4 > 36 * 1024 * 1024:
        pieces *= 2
    size = dim // pieces
    grads, mixtures = [], []
    for i in range(pieces):
        at = slice(i * size, (i + 1) * size)
        parts = [grad_normed[..., at]] + ([grad_gates] if i == 0 else [])
        done = scatter_all(parts, n_seq, n_bat, 16 + 2 * i, "scatter_normed")
        grads.append(done[0])
        if i == 0:
            gates = done[1]
        done = scatter_all([mixture[..., at]], n_seq, n_bat, 17 + 2 * i, "scatter_mixture")
        mixtures.append(done[0])
    return jnp.concatenate(grads, axis=-1), gates, jnp.concatenate(mixtures, axis=-1)


class SeqScatter:
    def __init__(self, place, wire, away, mine, twin, line):
        self.place, self.wire = place, wire
        self.away, self.mine, self.twin, self.line = away, mine, twin, line
        self.from_twin, self.from_seq = {}, {}
        self.order = list(range(1, place.half)) + [0]

    @staticmethod
    def scratch(n_seq, block):
        return [pltpu.VMEM((n_seq // 2,) + block.shape, block.dtype)] * 4

    def run(self, compute, out):
        place, wire = self.place, self.wire
        waiting = None
        for j in self.order:
            self.away[j] = compute(place.twin_at(2 * j)).astype(self.away.dtype)
            if waiting is not None:
                self.send(waiting)
            waiting = j
        for j in self.order:
            self.mine[j] = compute(place.seq_at(2 * j)).astype(self.mine.dtype)
            if waiting is not None:
                self.send(waiting)
                waiting = None
        waiting = None
        for j in self.order:
            self.from_twin[j].wait_recv()
            add_into(self.mine.at[j], self.twin.at[j])
            if waiting:
                self.pass_on(waiting)
            waiting = j

    def send(self, j):
        self.from_twin[j] = self.wire.push(self.away.at[j], self.twin.at[j], self.place.twin())

    def pass_on(self, j):
        self.from_seq[j] = self.wire.push(
            self.mine.at[j], self.line.at[j], self.place.seq_peer(2 * j)
        )

    def finish(self, out):
        for j in range(1, self.place.half):
            self.from_seq[j].wait_recv()
        add_into(self.mine.at[0], *[self.line.at[j] for j in range(1, self.place.half)])
        out[...] = self.mine[0]


def turn(v, cos_wide, sin_wide):
    return v * cos_wide + pltpu.roll(v, HEAD // 2, axis=1) * sin_wide


def exchange_rows(place, wire, local, got):
    copies = [
        wire.push(local, got.at[k - 1], place.seq_peer(k)) for k in range(1, place.n_seq)
    ]
    for copy in copies:
        copy.wait_recv()
    total = local[...]
    for k in range(place.n_seq - 1):
        total = total + got[k]
    return total


def lane_sums(v):
    ones = jnp.ones((8, v.shape[1]), F32)
    sums = lax.dot_general(
        ones, v, (((1,), (1,)), ((), ())), precision=HIGHEST, preferred_element_type=F32
    )
    return sums[0:1]


def allowed_block(use, first, count, keys):
    at_query = first + lax.broadcasted_iota(jnp.int32, (count, keys), 0)
    at_key = lax.broadcasted_iota(jnp.int32, (count, keys), 1)
    return (at_key == at_query) | ((at_key < at_query) & (use > 0))


def attend_forward(qkv, usable, w_o, gain_q, gain_k, cos_wide, sin_wide, n_seq, n_bat, span):
    col, three = qkv.shape
    wide = three // 3
    heads = wide // HEAD
    own = col // n_seq
    rows = own // span
    length = n_seq * span
    dim = w_o.shape[1]
    chunk = min(256, length)
    scale = HEAD ** (-0.5)
    block = jax.ShapeDtypeStruct((own, dim), BF)

    def kernel(*refs):
        qkv_ref, use_ref, wo_ref, gq_ref, gk_ref, cos_ref, sin_ref = refs[:7]
        q_ref, k_ref, v_ref, mix_ref, stat_ref, out_ref = refs[7:13]
        local, got, away, mine, twin, line, send_sems, recv_sems = refs[13:]
        place = Place(n_seq, n_bat)
        place.greet(all_seq=True, batch=False)
        wire = Wire(send_sems, recv_sems)
        for i in range(n_seq):
            for which in range(2):
                v = qkv_ref[i * own : (i + 1) * own, which * wide : (which + 1) * wide]
                local[which * n_seq + i : which * n_seq + i + 1, :] = lane_sums(v * v)
        for i in range(n_seq):
            for r in range(rows):
                for h in range(heads):
                    at = slice(i * own + r * span, i * own + (r + 1) * span)
                    lanes = slice(2 * wide + h * HEAD, 2 * wide + (h + 1) * HEAD)
                    v_ref[r, h, i * span : (i + 1) * span, :] = qkv_ref[at, lanes].astype(BF)
        total = exchange_rows(place, wire, local, got)
        stat_ref[...] = total
        columns = lax.rsqrt(total / dim + EPS).T
        for which, gain_ref, target in ((0, gq_ref, q_ref), (1, gk_ref, k_ref)):
            for i in range(n_seq):
                at_pos = slice(i * span, (i + 1) * span)
                for r in range(rows):
                    at = slice(i * own + r * span, i * own + (r + 1) * span)
                    factor = columns[
                        r * span : (r + 1) * span, which * n_seq + i : which * n_seq + i + 1
                    ]
                    for h in range(heads):
                        lanes = slice(which * wide + h * HEAD, which * wide + (h + 1) * HEAD)
                        gain = gain_ref[0:1, h * HEAD : (h + 1) * HEAD]
                        v = qkv_ref[at, lanes] * factor * gain
                        target[r, h, at_pos, :] = turn(
                            v, cos_ref[at_pos, :], sin_ref[at_pos, :]
                        ).astype(BF)
        for r in range(rows):
            for c in range(length // chunk):
                keys = (c + 1) * chunk
                allowed = allowed_block(use_ref[r : r + 1, :keys], c * chunk, chunk, keys)
                for h in range(heads):
                    query = q_ref[r, h, c * chunk : keys, :]
                    scores = dot_t(query, k_ref[r, h, :keys, :]) * scale
                    scores = jnp.where(allowed, scores, NEGATIVE)
                    raised = jnp.exp(scores - jnp.max(scores, axis=-1, keepdims=True))
                    probs = raised / jnp.sum(raised, axis=-1, keepdims=True)
                    mixed = dot(probs.astype(BF), v_ref[r, h, :keys, :]).astype(BF)
                    for p in range(chunk // span):
                        i = c * (chunk // span) + p
                        mix_ref[
                            i * own + r * span : i * own + (r + 1) * span,
                            h * HEAD : (h + 1) * HEAD,
                        ] = mixed[p * span : (p + 1) * span, :]
        scatter = SeqScatter(place, wire, away, mine, twin, line)

        def project(i):
            rows_at = pl.ds(pl.multiple_of(i * own, own), own)
            return dot(mix_ref[rows_at, :], wo_ref[...])

        scatter.run(project, out_ref)
        scatter.finish(out_ref)
        wire.drain()

    vmem = pl.BlockSpec(memory_space=pltpu.VMEM)
    head_block = jax.ShapeDtypeStruct((rows, heads, length, HEAD), BF)
    stats = jax.ShapeDtypeStruct((2 * n_seq, own), F32)
    return comm_call(
        kernel,
        [head_block] * 3 + [jax.ShapeDtypeStruct((col, wide), BF), stats, block],
        [pltpu.VMEM(stats.shape, F32), pltpu.VMEM((n_seq - 1,) + stats.shape, F32)]
        + SeqScatter.scratch(n_seq, block),
        3 * n_seq,
        2,
        "attend_forward",
        [vmem] * 7,
        [vmem] * 6,
    )(qkv, usable, w_o, gain_q, gain_k, cos_wide, sin_wide)


def attend_backward(
    grad_o, q, k, v, mixed, qkv, stats, hidden, usable, w_o, w_qkv, gain_q, gain_k,
    cos_wide, sin_wide, n_seq, n_bat,
):
    rows, heads, length, _ = q.shape
    own, dim = grad_o.shape
    span = own // rows
    col, three = qkv.shape
    wide = three // 3
    chunk = min(256, length)
    scale = HEAD ** (-0.5)

    def kernel(*refs):
        (go_ref, q_ref, k_ref, v_ref, mix_ref, qkv_ref, stat_ref, hid_ref, use_ref, wo_ref,
         w_ref, gq_ref, gk_ref, cos_ref, sin_ref) = refs[:15]
        gwo_ref, gw_ref, gain_ref, out_ref = refs[15:19]
        go_all, gm, dq, dk, dv, dqkv, local, got = refs[19:27]
        away, mine, twin, line, send_sems, recv_sems = refs[27:]
        place = Place(n_seq, n_bat)
        place.greet(all_seq=True, batch=False)
        wire = Wire(send_sems, recv_sems)
        gather = SeqGather(place, wire, go_ref, go_all)
        gather.start()
        go_all[place.s] = go_ref[...]
        for j in range(1, place.half):
            gather.step(j)
        gather.finish()
        for i in range(n_seq):
            part = dot_t(go_all[i], wo_ref[...]).astype(BF)
            for r in range(rows):
                gm[r, i * span : (i + 1) * span, :] = part[r * span : (r + 1) * span, :]
        dk[...] = jnp.zeros_like(dk)
        dv[...] = jnp.zeros_like(dv)
        for r in range(rows):
            for c in range(length // chunk):
                keys = (c + 1) * chunk
                now = slice(c * chunk, keys)
                allowed = allowed_block(use_ref[r : r + 1, :keys], c * chunk, chunk, keys)
                for h in range(heads):
                    lanes = slice(h * HEAD, (h + 1) * HEAD)
                    query = q_ref[r, h, now, :]
                    key = k_ref[r, h, :keys, :]
                    scores = jnp.where(allowed, dot_t(query, key) * scale, NEGATIVE)
                    raised = jnp.exp(scores - jnp.max(scores, axis=-1, keepdims=True))
                    probs = raised / jnp.sum(raised, axis=-1, keepdims=True)
                    low = probs.astype(BF)
                    grad_mix = gm[r, now, lanes]
                    grad_probs = dot_t(grad_mix, v_ref[r, h, :keys, :])
                    row_dot = jnp.sum(low.astype(F32) * grad_probs, axis=-1, keepdims=True)
                    grad_scores = (probs * (grad_probs - row_dot)).astype(BF)
                    dq[r, now, lanes] = scale * dot(grad_scores, key)
                    dk[r, :keys, lanes] += scale * t_dot(grad_scores, query)
                    dv[r, :keys, lanes] += t_dot(low, grad_mix)
        columns = lax.rsqrt(stat_ref[...] / dim + EPS).T
        for which, g_ref, grads in ((0, gq_ref, dq), (1, gk_ref, dk)):
            sums = [jnp.zeros((1, HEAD), F32) for _ in range(heads)]
            for i in range(n_seq):
                at_pos = slice(i * span, (i + 1) * span)
                products = []
                for r in range(rows):
                    at = slice(i * own + r * span, i * own + (r + 1) * span)
                    factor = columns[
                        r * span : (r + 1) * span, which * n_seq + i : which * n_seq + i + 1
                    ]
                    parts = []
                    for h in range(heads):
                        lanes = slice(h * HEAD, (h + 1) * HEAD)
                        flat = qkv_ref[at, which * wide + h * HEAD : which * wide + (h + 1) * HEAD]
                        flat = flat * factor
                        back = turn(
                            grads[r, at_pos, lanes], cos_ref[at_pos, :], -sin_ref[at_pos, :]
                        )
                        sums[h] = sums[h] + jnp.sum(back * flat, axis=0, keepdims=True)
                        weighted = back * g_ref[0:1, lanes]
                        grads[r, at_pos, lanes] = weighted
                        parts.append(weighted * flat)
                    products.append(sum(parts))
                local[which * n_seq + i : which * n_seq + i + 1, :] = lane_sums(
                    jnp.concatenate(products, axis=0)
                )
            for h in range(heads):
                gain_ref[which : which + 1, h * HEAD : (h + 1) * HEAD] = sums[h]
        for i in range(n_seq):
            for r in range(rows):
                at = slice(i * own + r * span, i * own + (r + 1) * span)
                dqkv[at, 2 * wide :] = dv[r, i * span : (i + 1) * span, :].astype(BF)
        means = (exchange_rows(place, wire, local, got) / dim).T
        for which, grads in ((0, dq), (1, dk)):
            for i in range(n_seq):
                at_pos = slice(i * span, (i + 1) * span)
                column = which * n_seq + i
                for r in range(rows):
                    at = slice(i * own + r * span, i * own + (r + 1) * span)
                    inside = slice(r * span, (r + 1) * span)
                    factor = columns[inside, column : column + 1]
                    mean = means[inside, column : column + 1]
                    lanes = slice(which * wide, (which + 1) * wide)
                    flat = qkv_ref[at, lanes] * factor
                    dqkv[at, lanes] = (factor * (grads[r, at_pos, :] - flat * mean)).astype(BF)
        scatter = SeqScatter(place, wire, away, mine, twin, line)

        def project(i):
            rows_at = pl.ds(pl.multiple_of(i * own, own), own)
            return dot_t(dqkv[rows_at, :], w_ref[...])

        scatter.run(project, out_ref)
        for part in range(dim // 256):
            at = slice(part * 256, (part + 1) * 256)
            gw_ref[at, :] = t_dot(hid_ref[:, at], dqkv[...]).astype(BF)
            total = t_dot(mix_ref[0:own, :], go_all[0, :, at])
            for i in range(1, n_seq):
                total = total + t_dot(mix_ref[i * own : (i + 1) * own, :], go_all[i, :, at])
            gwo_ref[:, at] = total.astype(BF)
        scatter.finish(out_ref)
        wire.drain()

    vmem = pl.BlockSpec(memory_space=pltpu.VMEM)
    block = jax.ShapeDtypeStruct((own, dim), BF)
    stat_shape = (2 * n_seq, own)
    return comm_call(
        kernel,
        [
            jax.ShapeDtypeStruct((wide, dim), BF),
            jax.ShapeDtypeStruct((dim, three), BF),
            jax.ShapeDtypeStruct((2, wide), F32),
            block,
        ],
        [
            pltpu.VMEM((n_seq, own, dim), BF),
            pltpu.VMEM((rows, length, wide), BF),
            pltpu.VMEM((rows, length, wide), F32),
            pltpu.VMEM((rows, length, wide), F32),
            pltpu.VMEM((rows, length, wide), F32),
            pltpu.VMEM((col, three), BF),
            pltpu.VMEM(stat_shape, F32),
            pltpu.VMEM((n_seq - 1,) + stat_shape, F32),
        ]
        + SeqScatter.scratch(n_seq, block),
        4 * n_seq,
        6,
        "attend_backward",
        [vmem] * 15,
        [vmem] * 4,
    )(grad_o, q, k, v, mixed, qkv, stats, hidden, usable, w_o, w_qkv, gain_q, gain_k,
      cos_wide, sin_wide)


def load_inputs(qkv_cut, w_out, mine, flags, small, gu_cut, dy_own, n_seq, n_bat):
    n_in = 7
    slots = 4 * n_seq * n_bat + 3 * n_seq + 2 * n_bat

    def kernel(*refs):
        cut_ref, wo_ref, x_ref, flag_ref, small_ref, gu_ref, dy_ref = refs[:n_in]
        w_ref, wo_all, x_col, flag_col, small_all, gu_all, dy_all = refs[n_in : 2 * n_in]
        buffers = refs[2 * n_in : 3 * n_in]
        own_sems, send_sems, recv_sems = refs[3 * n_in :]
        place = Place(n_seq, n_bat)
        place.greet(all_seq=True)
        wire = Wire(send_sems, recv_sems)
        small_work = FullGather(place, wire, small_ref, small_all)
        flag_work = SeqGather(place, wire, flag_ref, flag_col)
        x_work = SeqGather(place, wire, x_ref, x_col)
        dy_work = FullGather(place, wire, dy_ref, dy_all)
        small_work.start()
        flag_work.start()
        cuts = [
            wire.push(cut_ref.at[place.seq_at(k)], w_ref.at[place.s, place.b], place.seq_peer(k))
            for k in range(1, n_seq)
        ]
        ends = [
            wire.push(wo_ref, wo_all.at[place.b], place.bat_peer(k)) for k in range(1, n_bat)
        ]
        ends += [
            wire.push(cut_ref.at[place.s], w_ref.at[place.s, place.b], place.bat_peer(k))
            for k in range(1, n_bat)
        ]
        x_work.start()
        own = [
            keep_own(src, dst, buffers[i], own_sems.at[i])
            for i, (src, dst) in enumerate(
                (
                    (cut_ref.at[place.s], w_ref.at[place.s, place.b]),
                    (wo_ref, wo_all.at[place.b]),
                    (x_ref, x_col.at[place.s]),
                    (flag_ref, flag_col.at[place.s]),
                    (small_ref, small_all.at[place.s, place.b]),
                    (gu_ref.at[place.s], gu_all.at[place.s]),
                    (dy_ref, dy_all.at[place.s, place.b]),
                )
            )
        ]
        ends += [
            wire.push(gu_ref.at[place.seq_at(k)], gu_all.at[place.s], place.seq_peer(k))
            for k in range(1, n_seq)
        ]
        dy_work.start()
        for j in range(1, place.half):
            small_work.step(j)
            flag_work.step(j)
        for k in range(1, n_seq):
            cuts[k - 1].wait_recv()
            block = w_ref.at[place.seq_at(-k), place.b]
            ends += [wire.push(block, block, place.bat_peer(m)) for m in range(1, n_bat)]
        for j in range(place.half):
            small_work.collect(j)
        for j in range(1, place.half):
            x_work.step(j)
        for j in range(1, place.half):
            dy_work.step(j)
            dy_work.collect(j - 1)
        dy_work.collect(place.half - 1)
        for work in (small_work, flag_work, x_work, dy_work):
            work.finish()
        for copy in ends:
            copy.wait_recv()
        for copy in own:
            copy.wait()
        wire.drain()

    every = (n_seq, n_bat)
    one = jax.ShapeDtypeStruct(qkv_cut.shape[1:], qkv_cut.dtype)
    gu_one = jax.ShapeDtypeStruct(gu_cut.shape[1:], gu_cut.dtype)
    blocks = (one, w_out, mine, flags, small, gu_one, dy_own)
    leads = (every, (n_bat,), (n_seq,), (n_seq,), every, (n_seq,), every)
    return comm_call(
        kernel,
        [shape_of(lead, block) for lead, block in zip(leads, blocks)],
        [pltpu.VMEM(block.shape, block.dtype) for block in blocks]
        + [pltpu.SemaphoreType.DMA((n_in,))],
        slots,
        1,
        "load_inputs",
        [ANY] * n_in,
    )(qkv_cut, w_out, mine, flags, small, gu_cut, dy_own)


def store_grads(grad_w, grad_wo, grad_gu, small, n_seq, n_bat):
    one = jax.ShapeDtypeStruct(grad_w.shape[2:], grad_w.dtype)
    wo_one = jax.ShapeDtypeStruct(grad_wo.shape[1:], grad_wo.dtype)
    gu_one = jax.ShapeDtypeStruct(grad_gu.shape[1:], grad_gu.dtype)
    small_one = jax.ShapeDtypeStruct(small.shape[2:], small.dtype)
    slots = 2 * n_seq * n_bat + 2 * n_seq + n_bat

    def kernel(*refs):
        w_ref, wo_ref, gu_ref, small_ref = refs[:4]
        w_out_ref, wo_out_ref, gu_out_ref, small_out_ref = refs[4:8]
        w_sum, w_got, wo_sum, wo_got, gu_buf, cut_buf = refs[8:14]
        small_scratch = refs[14:19]
        w_sems, sems, send_sems, recv_sems = refs[19:]
        place = Place(n_seq, n_bat)
        place.greet(all_seq=True)
        wire = Wire(send_sems, recv_sems)
        small_work = FullScatter(
            place, wire, small_ref, small_out_ref, *small_scratch, None
        )
        small_work.start()
        got, loads = {}, {}
        for i in list(range(1, n_seq)) + [0]:
            to_seq = place.seq_at(i)
            for k in range(1, n_bat):
                got[i, k] = wire.push(
                    w_ref.at[to_seq, place.bat_at(k)], w_got.at[i, k - 1], place.bat_peer(k)
                )
            loads[i] = pltpu.make_async_copy(
                w_ref.at[to_seq, place.b], w_sum.at[i], w_sems.at[i]
            )
            loads[i].start()
        wo_pushed = [
            wire.push(wo_ref.at[place.bat_at(k)], wo_got.at[k - 1], place.bat_peer(k))
            for k in range(1, n_bat)
        ]
        wo_load = pltpu.make_async_copy(wo_ref.at[place.b], wo_sum, sems.at[0])
        wo_load.start()
        ends = [
            wire.push(gu_ref.at[place.seq_at(k)], gu_out_ref.at[place.s], place.seq_peer(k))
            for k in range(1, n_seq)
        ]
        gu_own = keep_own(gu_ref.at[place.s], gu_out_ref.at[place.s], gu_buf, sems.at[1])
        order = small_work.order()
        for j in order:
            small_work.pair(j)
        for i in list(range(1, n_seq)) + [0]:
            loads[i].wait()
            for k in range(1, n_bat):
                got[i, k].wait_recv()
            add_into(w_sum.at[i], *[w_got.at[i, k] for k in range(n_bat - 1)])
            if i:
                ends.append(
                    wire.push(w_sum.at[i], w_out_ref.at[place.s], place.seq_peer(i))
                )
        w_own = pltpu.make_async_copy(w_sum.at[0], w_out_ref.at[place.s], sems.at[2])
        w_own.start()
        for j in order:
            small_work.merge(j)
        wo_load.wait()
        for copy in wo_pushed:
            copy.wait_recv()
        add_into(wo_sum, *[wo_got.at[k] for k in range(n_bat - 1)])
        wo_out_ref[...] = wo_sum[...].astype(F32)
        small_work.finish()
        for copy in ends:
            copy.wait_recv()
        gu_own.wait()
        w_own.wait()
        wire.drain()

    vmem = pl.BlockSpec(memory_space=pltpu.VMEM)
    return comm_call(
        kernel,
        [
            shape_of((n_seq,), one),
            jax.ShapeDtypeStruct(wo_one.shape, F32),
            shape_of((n_seq,), gu_one),
            small_one,
        ],
        [
            pltpu.VMEM((n_seq,) + one.shape, one.dtype),
            pltpu.VMEM((n_seq, n_bat - 1) + one.shape, one.dtype),
            pltpu.VMEM(wo_one.shape, wo_one.dtype),
            pltpu.VMEM((n_bat - 1,) + wo_one.shape, wo_one.dtype),
            pltpu.VMEM(gu_one.shape, gu_one.dtype),
            pltpu.VMEM(one.shape, one.dtype),
        ]
        + FullScatter.scratch(n_seq, n_bat, small_one)
        + [pltpu.SemaphoreType.DMA((n_seq,)), pltpu.SemaphoreType.DMA((3,))],
        slots,
        8,
        "store_grads",
        [ANY] * 4,
        [ANY, vmem, ANY, vmem],
    )(grad_w, grad_wo, grad_gu, small)


def shards(
    tokens,
    lengths,
    key_mask,
    top_experts,
    attn_gain,
    query_gain,
    key_gain,
    mlp_gain,
    w_query,
    w_key,
    w_value,
    w_out,
    w_router,
    expert_gate,
    expert_up,
    expert_down,
    cotangent,
):
    n_seq = lax.axis_size("seq")
    n_bat = lax.axis_size("batch")
    seq = lax.axis_index("seq")
    bat = lax.axis_index("batch")
    rows, span, dim = tokens.shape
    own = rows * span
    col = n_seq * own
    length = n_seq * span
    shard = w_query.shape[0]
    wide = dim // n_seq
    heads = wide // HEAD
    local_experts, depth, hidden_units = expert_gate.shape
    part = hidden_units // n_seq
    experts = local_experts * n_bat

    mine = tokens.reshape(own, dim)
    dy_own = cotangent.reshape(own, dim)
    small = jnp.concatenate(
        [w_router.T, jnp.stack([attn_gain, query_gain, key_gain, mlp_gain])], axis=0
    )
    positions_own = seq * span + jnp.arange(span, dtype=jnp.int32)
    flags = pack((positions_own[None, :] < lengths[:, None]) & (key_mask == 1))
    qkv_cut = jnp.stack([w_query, w_key, w_value]).reshape(3, shard, n_seq, wide)
    qkv_cut = jnp.transpose(qkv_cut, (2, 1, 0, 3)).reshape(n_seq, shard, 3 * wide)
    gu_cut = jnp.stack([expert_gate, expert_up]).reshape(2, local_experts, depth, n_seq, part)
    gu_cut = jnp.transpose(gu_cut, (3, 2, 0, 1, 4)).reshape(n_seq, depth, 2 * local_experts * part)
    w_qkv, w_o, x_col, flag_col, small_all, w_gu, dy_all = load_inputs(
        qkv_cut, w_out, mine, flags, pack(small), gu_cut, dy_own, n_seq, n_bat
    )
    w_qkv = w_qkv.reshape(dim, 3 * wide)
    w_o = w_o.reshape(wide, dim)
    w_gu = w_gu.reshape(dim, 2 * local_experts * part)
    w_down = expert_down.reshape(local_experts * part, dim)
    dy_all = dy_all.reshape(-1, dim)
    small_all = unpack(small_all, (n_seq, n_bat), small.shape)
    small_all = jnp.transpose(small_all, (2, 0, 1, 3)).reshape(-1, dim)
    router = small_all[:experts].T.astype(BF)
    gain_attn, gain_mlp = small_all[experts], small_all[experts + 3]
    gain_q = lax.dynamic_slice_in_dim(small_all[experts + 1], seq * wide, wide)
    gain_k = lax.dynamic_slice_in_dim(small_all[experts + 2], seq * wide, wide)
    usable = unpack(flag_col, (n_seq,), key_mask.shape)
    usable = jnp.transpose(usable, (1, 0, 2)).reshape(rows, length)

    x_col = x_col.reshape(col, dim).astype(F32)
    scale_x = rms_scale(x_col)
    hidden = (x_col * scale_x * gain_attn).astype(BF)
    qkv = dot(hidden, w_qkv)
    cos_part, sin_part = rotary_tables(jnp.arange(length, dtype=jnp.int32))
    cos_wide = jnp.concatenate([cos_part, cos_part], axis=1)
    sin_wide = jnp.concatenate([-sin_part, sin_part], axis=1)
    gain_q, gain_k = gain_q[None, :], gain_k[None, :]
    q, k, v, mixed, stats, mixed_out = attend_forward(
        qkv, usable, w_o, gain_q, gain_k, cos_wide, sin_wide, n_seq, n_bat, span
    )
    x_own = mine.astype(F32)
    residual = x_own + mixed_out.astype(F32)
    scale_r = rms_scale(residual)
    normed = (residual * scale_r * gain_mlp).astype(BF)
    router_probs = jax.nn.softmax(dot(normed, router), axis=-1)
    expert_ids = jnp.arange(experts, dtype=jnp.int32)
    chosen = jnp.any(top_experts.reshape(own, -1)[:, :, None] == expert_ids, axis=1).astype(F32)
    gates = router_probs * chosen

    normed_all, gates_all = gather_all([normed, pack(gates.T)], n_seq, n_bat, 4, "gather_normed")
    normed_all = normed_all.reshape(-1, dim)
    gates_all = unpack(gates_all, (n_seq, n_bat), (experts, own))
    gates_all = jnp.transpose(gates_all, (0, 1, 3, 2)).reshape(-1, experts)
    first_expert = bat * local_experts
    gates_here = lax.dynamic_slice_in_dim(gates_all, first_expert, local_experts, 1)
    units = local_experts * part
    gates_wide = jnp.repeat(gates_here, part, axis=1)
    pre = dot(normed_all, w_gu)
    gate_pre, up_pre = pre[:, :units], pre[:, units:]
    sig = jax.nn.sigmoid(gate_pre)
    silu = gate_pre * sig
    active = (silu * up_pre).astype(BF).astype(F32)
    weighted = (active * gates_wide).astype(BF)
    mixture = dot(weighted, w_down).astype(BF)
    mixture = mixture.reshape(n_seq, n_bat, own, dim)
    back = dot_t(dy_all, w_down)
    gate_terms = jnp.sum((active * back).reshape(-1, local_experts, part), axis=-1)
    grad_active = back * gates_wide
    grad_gate_pre = (grad_active * up_pre * sig * (1.0 + gate_pre * (1.0 - sig))).astype(BF)
    grad_up_pre = (grad_active * silu).astype(BF)
    grad_pre = jnp.concatenate([grad_gate_pre, grad_up_pre], axis=1)
    grad_down = t_dot(weighted, dy_all)
    grad_gu = t_dot(normed_all, grad_pre).astype(BF)
    grad_normed = dot_t(grad_pre, w_gu).astype(BF)
    gate_terms = gate_terms.reshape(n_seq, n_bat, own, local_experts)
    grad_gates = lax.dynamic_update_slice_in_dim(
        jnp.zeros((n_seq, n_bat, experts, own), F32),
        jnp.transpose(gate_terms, (0, 1, 3, 2)),
        first_expert,
        2,
    )
    grad_gates = jax.vmap(jax.vmap(pack))(grad_gates)
    grad_normed = grad_normed.reshape(n_seq, n_bat, own, dim)
    grad_normed, grad_gates, mixture = scatter_blocks(
        grad_normed, grad_gates, mixture, n_seq, n_bat
    )
    grad_normed = grad_normed.astype(F32)
    grad_gates = unpack(grad_gates, (), (experts, own)).T
    output = (residual + mixture.astype(F32)).astype(BF)
    grad_down = grad_down.reshape(local_experts, part, dim)

    grad_chosen = grad_gates * chosen
    grad_logits = router_probs * (
        grad_chosen - jnp.sum(router_probs * grad_chosen, axis=-1, keepdims=True)
    )
    grad_router = lax.dot_general(
        normed.astype(F32), grad_logits, (((0,), (0,)), ((), ())), precision=HIGHEST
    )
    grad_normed = grad_normed + lax.dot_general(
        grad_logits, router.astype(F32), (((1,), (1,)), ((), ())), precision=HIGHEST
    )
    grad_resid, gain_mlp_terms = rms_back(residual, scale_r, gain_mlp, grad_normed)
    grad_residual = dy_own.astype(F32) + grad_resid
    grad_o = grad_residual.astype(BF)

    grad_w_o, grad_w, grad_gains, grad_hidden = attend_backward(
        grad_o, q, k, v, mixed, qkv, stats, hidden, usable, w_o, w_qkv, gain_q, gain_k,
        cos_wide, sin_wide, n_seq, n_bat,
    )
    grad_w_o = grad_w_o.reshape(n_bat, shard, dim)
    grad_w = grad_w.reshape(n_seq, n_bat, shard, 3 * wide)
    grad_hidden = grad_hidden.astype(F32)
    grad_x, gain_attn_terms = rms_back(x_own, rms_scale(x_own), gain_attn, grad_hidden)
    grad_tokens = (grad_residual + grad_x).astype(BF)

    zeros = jnp.zeros((dim,), F32)
    small_grads = jnp.concatenate(
        [
            grad_router.T,
            jnp.stack(
                [
                    jnp.sum(gain_attn_terms, axis=0),
                    lax.dynamic_update_slice_in_dim(zeros, grad_gains[0], seq * wide, 0),
                    lax.dynamic_update_slice_in_dim(zeros, grad_gains[1], seq * wide, 0),
                    jnp.sum(gain_mlp_terms, axis=0),
                ]
            ),
        ],
        axis=0,
    )
    small_grads = jnp.transpose(small_grads.reshape(-1, n_seq, n_bat, shard), (1, 2, 0, 3))
    small_grads = jax.vmap(jax.vmap(pack))(small_grads)
    grad_gu = grad_gu.reshape(n_seq, depth, -1)
    grad_w, grad_w_o, grad_gu, small_grads = store_grads(
        grad_w, grad_w_o, grad_gu, small_grads, n_seq, n_bat
    )
    grad_w = grad_w.astype(F32).reshape(n_seq, shard, 3, wide)
    grad_w = jnp.transpose(grad_w, (2, 1, 0, 3)).reshape(3, shard, dim)
    grad_gu = grad_gu.reshape(n_seq, depth, 2, local_experts, part)
    grad_gu = jnp.transpose(grad_gu, (2, 3, 1, 0, 4)).reshape(2, local_experts, depth, hidden_units)
    grad_gu = grad_gu.astype(F32)
    small_grads = unpack(small_grads, (), (experts + 4, shard))

    return (
        output.reshape(rows, span, dim),
        grad_tokens.reshape(rows, span, dim),
        small_grads[experts],
        small_grads[experts + 1],
        small_grads[experts + 2],
        small_grads[experts + 3],
        grad_w[0],
        grad_w[1],
        grad_w[2],
        grad_w_o,
        small_grads[:experts].T,
        grad_gu[0],
        grad_gu[1],
        grad_down,
    )


def solution(mesh):
    tok = P("batch", "seq", None)
    vec = P(("seq", "batch"))
    mat = P(("seq", "batch"), None)
    in_specs = (tok, P("batch"), P("batch", "seq"), tok) + (vec,) * 4 + (mat,) * 5 + (tok,) * 4
    out_specs = (tok, tok) + (vec,) * 4 + (mat,) * 5 + (tok,) * 3
    return jax.shard_map(shards, mesh=mesh, in_specs=in_specs, out_specs=out_specs, check_vma=False)
```

```python
import functools

import jax
import jax.numpy as jnp
from jax import lax
from jax.experimental import pallas as pl
from jax.experimental.pallas import tpu as pltpu
from jax.sharding import PartitionSpec as P

HEAD = 128
EPS = 1e-05
HIGHEST = lax.Precision.HIGHEST
NEGATIVE = -1e30
BF = jnp.bfloat16
F32 = jnp.float32


def dot(a, b):
    return jnp.dot(a, b, preferred_element_type=F32)


def dot_t(a, b):
    return lax.dot_general(a, b, (((1,), (1,)), ((), ())), preferred_element_type=F32)


def t_dot(a, b):
    return lax.dot_general(a, b, (((0,), (0,)), ((), ())), preferred_element_type=F32)


def rms_scale(v):
    return lax.rsqrt(jnp.mean(v * v, axis=-1, keepdims=True) + EPS)


def rms_back(v, scale, gain, grad):
    normal = v * scale
    weighted = grad * gain
    mean = jnp.mean(weighted * normal, axis=-1, keepdims=True)
    return scale * (weighted - normal * mean), grad * normal


def rotary_tables(positions):
    half_head = HEAD // 2
    frequency = 10000.0 ** (-2.0 * jnp.arange(half_head, dtype=F32) / HEAD)
    angles = positions.astype(F32)[:, None] * frequency[None, :]
    return jnp.cos(angles), jnp.sin(angles)


ANY = pl.BlockSpec(memory_space=pl.ANY)
VMEM_LIMIT = 67043328


class Place:
    def __init__(self, n_seq, n_bat):
        self.n_seq, self.n_bat, self.half = n_seq, n_bat, n_seq // 2
        self.s = lax.axis_index("seq")
        self.b = lax.axis_index("batch")
        self.twin_s = self.s + 1 - 2 * lax.rem(self.s, 2)
        self.bat_x = self.b + 1 - 2 * lax.rem(self.b, 2)
        self.bat_y = lax.rem(self.b + 2, 4)
        self.bat_d = lax.rem(self.bat_x + 2, 4)

    def seq_at(self, k):
        return lax.rem(self.s + (k + self.n_seq), self.n_seq)

    def twin_at(self, k):
        return lax.rem(self.twin_s + (k + self.n_seq), self.n_seq)

    def bat_at(self, k):
        return lax.rem(self.b + (k + self.n_bat), self.n_bat)

    def seq_peer(self, k):
        return {"seq": self.seq_at(k), "batch": self.b}

    def bat_peer(self, k):
        return {"seq": self.s, "batch": self.bat_at(k)}

    def x_peer(self):
        return {"seq": self.s, "batch": self.bat_x}

    def y_peer(self):
        return {"seq": self.s, "batch": self.bat_y}

    def twin(self):
        return {"seq": self.twin_s, "batch": self.b}

    def greet(self, all_seq=False, batch=True):
        steps = range(1, self.n_seq) if all_seq else range(2, self.n_seq, 2)
        peers = [self.seq_peer(k) for k in steps]
        if not all_seq:
            peers.append(self.twin())
        if batch:
            peers += [self.bat_peer(k) for k in range(1, self.n_bat)]
        barrier = pltpu.get_barrier_semaphore()
        for peer in peers:
            pl.semaphore_signal(
                barrier, inc=1, device_id=peer, device_id_type=pl.DeviceIdType.MESH
            )
        pl.semaphore_wait(barrier, len(peers))


class Wire:
    def __init__(self, send_sems, recv_sems):
        self.send_sems, self.recv_sems = send_sems, recv_sems
        self.copies, self.used = [], 0

    def push(self, src, dst, peer):
        slot = self.used
        self.used += 1
        copy = pltpu.make_async_remote_copy(
            src_ref=src,
            dst_ref=dst,
            send_sem=self.send_sems.at[slot],
            recv_sem=self.recv_sems.at[slot],
            device_id=peer,
            device_id_type=pl.DeviceIdType.MESH,
        )
        copy.start()
        self.copies.append(copy)
        return copy

    def settle(self, copy):
        copy.wait_send()
        self.copies = [other for other in self.copies if other is not copy]

    def drain(self):
        for copy in self.copies:
            copy.wait_send()


class SeqGather:
    def __init__(self, place, wire, src, out):
        self.place, self.wire, self.src, self.out = place, wire, src, out
        self.late = []

    def start(self):
        place, mine = self.place, self.out.at[self.place.s]
        self.line = [
            self.wire.push(self.src, mine, place.seq_peer(2 * j)) for j in range(1, place.half)
        ]
        self.late.append(self.wire.push(self.src, mine, place.twin()))

    def step(self, j):
        self.line[j - 1].wait_recv()
        block = self.out.at[self.place.seq_at(-2 * j)]
        self.late.append(self.wire.push(block, block, self.place.twin()))

    def finish(self):
        for copy in self.late:
            copy.wait_recv()


class FullGather:
    def __init__(self, place, wire, src, out):
        self.place, self.wire, self.src, self.out = place, wire, src, out
        self.late = []
        self.across = {}

    def spread(self, j, block):
        place = self.place
        self.across[j] = [
            self.wire.push(block, self.out.at[place.seq_at(-2 * j), place.b], place.bat_peer(k))
            for k in range(1, place.n_bat)
        ]

    def start(self):
        place, mine = self.place, self.out.at[self.place.s, self.place.b]
        self.line = [
            self.wire.push(self.src, mine, place.seq_peer(2 * j)) for j in range(1, place.half)
        ]
        self.spread(0, self.src)
        self.late.append(self.wire.push(self.src, mine, place.twin()))

    def step(self, j):
        self.line[j - 1].wait_recv()
        block = self.out.at[self.place.seq_at(-2 * j), self.place.b]
        self.spread(j, block)
        self.late.append(self.wire.push(block, block, self.place.twin()))

    def collect(self, j):
        place = self.place
        for k in range(1, place.n_bat):
            self.across[j][k - 1].wait_recv()
            block = self.out.at[place.seq_at(-2 * j), place.bat_at(-k)]
            self.late.append(self.wire.push(block, block, place.twin()))

    def finish(self):
        for copy in self.late:
            copy.wait_recv()


def keep_own(src, dst, buffer, sem):
    first = pltpu.make_async_copy(src, buffer, sem)
    first.start()
    first.wait()
    second = pltpu.make_async_copy(buffer, dst, sem)
    second.start()
    return second


def comm_call(
    kernel, outs, scratch, slots, collective_id, name, in_specs, out_specs=None, aliases=None
):
    return pl.pallas_call(
        kernel,
        out_shape=outs,
        in_specs=in_specs,
        out_specs=out_specs if out_specs is not None else jax.tree.map(lambda _: ANY, outs),
        scratch_shapes=list(scratch)
        + [pltpu.SemaphoreType.DMA((slots,)), pltpu.SemaphoreType.DMA((slots,))],
        compiler_params=pltpu.CompilerParams(
            collective_id=collective_id, has_side_effects=True, vmem_limit_bytes=VMEM_LIMIT
        ),
        name=name,
        input_output_aliases=aliases or {},
    )


def shape_of(lead, block):
    return jax.ShapeDtypeStruct(tuple(lead) + block.shape, block.dtype)


def gather_all(blocks, n_seq, n_bat, collective_id, name):
    count = len(blocks)

    def kernel(*refs):
        srcs, outs = refs[:count], refs[count : 2 * count]
        buffers = refs[2 * count : 3 * count]
        own_sems, send_sems, recv_sems = refs[3 * count :]
        place = Place(n_seq, n_bat)
        place.greet()
        wire = Wire(send_sems, recv_sems)
        gathers = [FullGather(place, wire, *pair) for pair in zip(srcs, outs)]
        for gather in gathers:
            gather.start()
        own = [
            keep_own(srcs[i], outs[i].at[place.s, place.b], buffers[i], own_sems.at[i])
            for i in range(count)
        ]
        for j in range(1, place.half):
            for gather in gathers:
                gather.step(j)
            for gather in gathers:
                gather.collect(j - 1)
        for gather in gathers:
            gather.collect(place.half - 1)
        for gather in gathers:
            gather.finish()
        for copy in own:
            copy.wait()
        wire.drain()

    return comm_call(
        kernel,
        [shape_of((n_seq, n_bat), block) for block in blocks],
        [pltpu.VMEM(block.shape, block.dtype) for block in blocks]
        + [pltpu.SemaphoreType.DMA((count,))],
        n_seq * n_bat * count,
        collective_id,
        name,
        [ANY] * count,
    )(*blocks)


def add_into(target, *others):
    rows = target.shape[0]
    step = min(rows, 16)

    def body(i, carry):
        at = pl.ds(pl.multiple_of(i * step, step), step)
        total = target[at, :].astype(F32)
        for other in others:
            total = total + other[at, :].astype(F32)
        target[at, :] = total.astype(target.dtype)
        return carry

    lax.fori_loop(0, rows // step, body, 0)


class FullScatter:
    def __init__(self, place, wire, parts, out, mine, twin, across, line, sems, local):
        self.place, self.wire, self.parts, self.out = place, wire, parts, out
        self.mine, self.twin, self.across, self.line = mine, twin, across, line
        self.sems, self.local = sems, local

    @staticmethod
    def scratch(n_seq, n_bat, block):
        half = n_seq // 2
        return [
            pltpu.VMEM((half, n_bat) + block.shape, block.dtype),
            pltpu.VMEM((half, n_bat) + block.shape, block.dtype),
            pltpu.VMEM((half, n_bat) + block.shape, block.dtype),
            pltpu.VMEM((half,) + block.shape, block.dtype),
            pltpu.SemaphoreType.DMA((half, n_bat)),
        ]

    def order(self):
        return list(range(1, self.place.half)) + [0]

    def start(self):
        place = self.place
        self.from_twin, self.loads, self.from_bat, self.from_seq = {}, {}, {}, {}
        for j in self.order():
            for k in list(range(1, place.n_bat)) + [0]:
                to_bat = place.bat_at(k)
                self.from_twin[j, k] = self.wire.push(
                    self.parts.at[place.twin_at(2 * j), to_bat], self.twin.at[j, k], place.twin()
                )
                load = pltpu.make_async_copy(
                    self.parts.at[place.seq_at(2 * j), to_bat],
                    self.mine.at[j, k],
                    self.sems.at[j, k],
                )
                load.start()
                self.loads[j, k] = load

    def pair(self, j):
        place = self.place
        for k in list(range(1, place.n_bat)) + [0]:
            self.from_twin[j, k].wait_recv()
            self.loads[j, k].wait()
            add_into(self.mine.at[j, k], self.twin.at[j, k])
        for k in range(1, place.n_bat):
            self.from_bat[j, k] = self.wire.push(
                self.mine.at[j, k], self.across.at[j, k], place.bat_peer(k)
            )

    def merge(self, j):
        place = self.place
        for k in range(1, place.n_bat):
            self.from_bat[j, k].wait_recv()
        add_into(self.mine.at[j, 0], *[self.across.at[j, k] for k in range(1, place.n_bat)])
        if j:
            self.from_seq[j] = self.wire.push(
                self.mine.at[j, 0], self.line.at[j], place.seq_peer(2 * j)
            )

    def finish(self):
        for j in range(1, self.place.half):
            self.from_seq[j].wait_recv()
        add_into(self.mine.at[0, 0], *[self.line.at[j] for j in range(1, self.place.half)])
        self.out[...] = self.mine[0, 0]


def scatter_all(parts, n_seq, n_bat, collective_id, name):
    blocks = [jax.ShapeDtypeStruct(part.shape[2:], part.dtype) for part in parts]
    count = len(parts)

    def kernel(*refs):
        ins, outs = refs[:count], refs[count : 2 * count]
        rest = refs[2 * count :]
        send_sems, recv_sems = rest[-2:]
        place = Place(n_seq, n_bat)
        place.greet()
        wire = Wire(send_sems, recv_sems)
        works = [
            FullScatter(place, wire, ins[i], outs[i], *rest[5 * i : 5 * i + 5], None)
            for i in range(count)
        ]
        for work in works:
            work.start()
        order = works[0].order()
        for at, j in enumerate(order):
            for work in works:
                work.pair(j)
            if at:
                for work in works:
                    work.merge(order[at - 1])
        for work in works:
            work.merge(order[-1])
        for work in works:
            work.finish()
        wire.drain()

    scratch = []
    for block in blocks:
        scratch += FullScatter.scratch(n_seq, n_bat, block)
    slots = count * (n_seq * n_bat)
    vmem = pl.BlockSpec(memory_space=pltpu.VMEM)
    return comm_call(
        kernel,
        blocks,
        scratch,
        slots,
        collective_id,
        name,
        [ANY] * count,
        [vmem] * count,
    )(*parts)


def pack(values):
    flat = values.astype(F32).reshape(-1)
    tiles = -(-flat.shape[0] // 1024)
    return jnp.pad(flat, (0, tiles * 1024 - flat.shape[0])).reshape(tiles * 8, 128)


def unpack(tiles, lead, shape):
    size = 1
    for extent in shape:
        size *= extent
    return tiles.reshape(tuple(lead) + (-1,))[..., :size].reshape(tuple(lead) + tuple(shape))


def scatter_blocks(grad_normed, grad_gates, mixture, n_seq, n_bat):
    dim = grad_normed.shape[-1]
    pieces = 1
    while n_seq * n_bat * grad_normed.shape[2] * (dim // pieces) * 4 > 36 * 1024 * 1024:
        pieces *= 2
    size = dim // pieces
    grads, mixtures = [], []
    for i in range(pieces):
        at = slice(i * size, (i + 1) * size)
        parts = [grad_normed[..., at]] + ([grad_gates] if i == 0 else [])
        done = scatter_all(parts, n_seq, n_bat, 16 + 2 * i, "scatter_normed")
        grads.append(done[0])
        if i == 0:
            gates = done[1]
        done = scatter_all([mixture[..., at]], n_seq, n_bat, 17 + 2 * i, "scatter_mixture")
        mixtures.append(done[0])
    return jnp.concatenate(grads, axis=-1), gates, jnp.concatenate(mixtures, axis=-1)


class SeqScatter:
    def __init__(self, place, wire, away, mine, twin, line):
        self.place, self.wire = place, wire
        self.away, self.mine, self.twin, self.line = away, mine, twin, line
        self.from_twin, self.from_seq = {}, {}
        self.order = list(range(1, place.half)) + [0]

    @staticmethod
    def scratch(n_seq, block):
        return [pltpu.VMEM((n_seq // 2,) + block.shape, block.dtype)] * 4

    def run(self, compute, out):
        place, wire = self.place, self.wire
        waiting = None
        for j in self.order:
            self.away[j] = compute(place.twin_at(2 * j)).astype(self.away.dtype)
            if waiting is not None:
                self.send(waiting)
            waiting = j
        for j in self.order:
            self.mine[j] = compute(place.seq_at(2 * j)).astype(self.mine.dtype)
            if waiting is not None:
                self.send(waiting)
                waiting = None
        waiting = None
        for j in self.order:
            self.from_twin[j].wait_recv()
            add_into(self.mine.at[j], self.twin.at[j])
            if waiting:
                self.pass_on(waiting)
            waiting = j

    def send(self, j):
        self.from_twin[j] = self.wire.push(self.away.at[j], self.twin.at[j], self.place.twin())

    def pass_on(self, j):
        self.from_seq[j] = self.wire.push(
            self.mine.at[j], self.line.at[j], self.place.seq_peer(2 * j)
        )

    def finish(self, out):
        for j in range(1, self.place.half):
            self.from_seq[j].wait_recv()
        add_into(self.mine.at[0], *[self.line.at[j] for j in range(1, self.place.half)])
        out[...] = self.mine[0]


def turn(v, cos_wide, sin_wide):
    return v * cos_wide + pltpu.roll(v, HEAD // 2, axis=1) * sin_wide


def exchange_rows(place, wire, local, got, between=None):
    copies = [
        wire.push(local, got.at[k - 1], place.seq_peer(k)) for k in range(1, place.n_seq)
    ]
    if between is not None:
        between()
    for copy in copies:
        copy.wait_recv()
    total = local[...]
    for k in range(place.n_seq - 1):
        total = total + got[k]
    return total


def lane_sums(v):
    ones = jnp.ones((8, v.shape[1]), F32)
    sums = lax.dot_general(
        ones, v, (((1,), (1,)), ((), ())), precision=HIGHEST, preferred_element_type=F32
    )
    return sums[0:1]


def allowed_block(use, first, count, keys):
    at_query = first + lax.broadcasted_iota(jnp.int32, (count, keys), 0)
    at_key = lax.broadcasted_iota(jnp.int32, (count, keys), 1)
    return (at_key == at_query) | ((at_key < at_query) & (use > 0))


def attend_forward(
    qkv, usable, w_o, gain_q, gain_k, cos_wide, sin_wide, n_seq, n_bat, span, side=None
):
    col, three = qkv.shape
    wide = three // 3
    heads = wide // HEAD
    own = col // n_seq
    rows = own // span
    length = n_seq * span
    dim = w_o.shape[1]
    chunk = min(256, length)
    scale = HEAD ** (-0.5)
    block = jax.ShapeDtypeStruct((own, dim), BF)

    def kernel(*refs):
        qkv_ref, use_ref, wo_ref, gq_ref, gk_ref, cos_ref, sin_ref = refs[:7]
        refs = refs[7:]
        if side:
            _, gate_ref, up_ref = refs[:3]
            refs = refs[3:]
        q_ref, k_ref, v_ref, mix_ref, stat_ref, out_ref = refs[:6]
        refs = refs[6:]
        if side:
            dy_all, gu_all = refs[:2]
            gu_own, gu_sems = refs[-4:-2]
            refs = refs[2:-4] + refs[-2:]
        local, got, away, mine, twin, line, send_sems, recv_sems = refs
        place = Place(n_seq, n_bat)
        place.greet(all_seq=True, batch=bool(side))
        wire = Wire(send_sems, recv_sems)
        dy_works, gu_copies, gu_here = [], [], []
        if side:
            for j in range(place.half):
                at_seq = place.seq_at(-2 * j)
                dy_works.append(
                    Across(
                        place,
                        wire,
                        dy_all.at[at_seq, place.b],
                        lambda i, at_seq=at_seq: dy_all.at[at_seq, i],
                    )
                )
                dy_works[-1].start()

        def send_experts():
            if not side:
                return
            count, _, hidden = gate_ref.shape
            part = hidden // n_seq
            for k in list(range(1, n_seq)) + [0]:
                lanes = pl.ds(pl.multiple_of(place.seq_at(k) * part, part), part)
                for m, ref in enumerate((gate_ref, up_ref)):
                    for e in range(count):
                        to = pl.ds((m * count + e) * part, part)
                        if k:
                            gu_copies.append(
                                wire.push(
                                    ref.at[e, :, lanes],
                                    gu_all.at[place.s, :, to],
                                    place.seq_peer(k),
                                )
                            )
                        else:
                            copy = pltpu.make_async_copy(
                                ref.at[e, :, lanes], gu_own.at[:, to], gu_sems.at[m * count + e]
                            )
                            copy.start()
                            gu_here.append(copy)

        for i in range(n_seq):
            for which in range(2):
                v = qkv_ref[i * own : (i + 1) * own, which * wide : (which + 1) * wide]
                local[which * n_seq + i : which * n_seq + i + 1, :] = lane_sums(v * v)
        for i in range(n_seq):
            for r in range(rows):
                for h in range(heads):
                    at = slice(i * own + r * span, i * own + (r + 1) * span)
                    lanes = slice(2 * wide + h * HEAD, 2 * wide + (h + 1) * HEAD)
                    v_ref[r, h, i * span : (i + 1) * span, :] = qkv_ref[at, lanes].astype(BF)
        total = exchange_rows(place, wire, local, got, send_experts)
        stat_ref[...] = total
        columns = lax.rsqrt(total / dim + EPS).T
        for which, gain_ref, target in ((0, gq_ref, q_ref), (1, gk_ref, k_ref)):
            for i in range(n_seq):
                at_pos = slice(i * span, (i + 1) * span)
                for r in range(rows):
                    at = slice(i * own + r * span, i * own + (r + 1) * span)
                    factor = columns[
                        r * span : (r + 1) * span, which * n_seq + i : which * n_seq + i + 1
                    ]
                    for h in range(heads):
                        lanes = slice(which * wide + h * HEAD, which * wide + (h + 1) * HEAD)
                        gain = gain_ref[0:1, h * HEAD : (h + 1) * HEAD]
                        v = qkv_ref[at, lanes] * factor * gain
                        target[r, h, at_pos, :] = turn(
                            v, cos_ref[at_pos, :], sin_ref[at_pos, :]
                        ).astype(BF)
        for r in range(rows):
            for c in range(length // chunk):
                keys = (c + 1) * chunk
                allowed = allowed_block(use_ref[r : r + 1, :keys], c * chunk, chunk, keys)
                for h in range(heads):
                    query = q_ref[r, h, c * chunk : keys, :]
                    scores = dot_t(query, k_ref[r, h, :keys, :]) * scale
                    scores = jnp.where(allowed, scores, NEGATIVE)
                    raised = jnp.exp(scores - jnp.max(scores, axis=-1, keepdims=True))
                    probs = raised / jnp.sum(raised, axis=-1, keepdims=True)
                    mixed = dot(probs.astype(BF), v_ref[r, h, :keys, :]).astype(BF)
                    for p in range(chunk // span):
                        i = c * (chunk // span) + p
                        mix_ref[
                            i * own + r * span : i * own + (r + 1) * span,
                            h * HEAD : (h + 1) * HEAD,
                        ] = mixed[p * span : (p + 1) * span, :]
        scatter = SeqScatter(place, wire, away, mine, twin, line)

        def project(i):
            rows_at = pl.ds(pl.multiple_of(i * own, own), own)
            return dot(mix_ref[rows_at, :], wo_ref[...])

        scatter.run(project, out_ref)
        if side:
            for copy in gu_here:
                copy.wait()
            gu_store = pltpu.make_async_copy(gu_own, gu_all.at[place.s], gu_sems.at[0])
            gu_store.start()
            for work in dy_works:
                work.relay()
            passed = []
            for j, work in enumerate(dy_works):
                work.finish()
                group = dy_all.at[place.seq_at(-2 * j)]
                passed.append(wire.push(group, group, place.twin()))
        scatter.finish(out_ref)
        if side:
            for copy in passed + gu_copies:
                copy.wait_recv()
            gu_store.wait()
        wire.drain()

    vmem = pl.BlockSpec(memory_space=pltpu.VMEM)
    side_in, side_out, side_scratch, aliases = [], [], [], {}
    slots = 3 * n_seq
    if side:
        dy_part, gate, up = side
        count, depth, hidden = gate.shape
        lanes = 2 * count * (hidden // n_seq)
        side_in = [ANY] * 3
        side_out = [
            jax.ShapeDtypeStruct(dy_part.shape, dy_part.dtype),
            jax.ShapeDtypeStruct((n_seq, depth, lanes), gate.dtype),
        ]
        side_scratch = [
            pltpu.VMEM((depth, lanes), gate.dtype),
            pltpu.SemaphoreType.DMA((2 * count,)),
        ]
        aliases = {7: 6}
        slots += 3 * n_seq + 2 * count * n_seq
    head_block = jax.ShapeDtypeStruct((rows, heads, length, HEAD), BF)
    stats = jax.ShapeDtypeStruct((2 * n_seq, own), F32)
    return comm_call(
        kernel,
        [head_block] * 3 + [jax.ShapeDtypeStruct((col, wide), BF), stats, block] + side_out,
        [pltpu.VMEM(stats.shape, F32), pltpu.VMEM((n_seq - 1,) + stats.shape, F32)]
        + SeqScatter.scratch(n_seq, block)
        + side_scratch,
        slots,
        2,
        "attend_forward",
        [vmem] * 7 + side_in,
        [vmem] * 6 + [ANY] * len(side_out),
        aliases,
    )(qkv, usable, w_o, gain_q, gain_k, cos_wide, sin_wide, *(side or ()))


def attend_backward(
    grad_o, q, k, v, mixed, qkv, stats, hidden, usable, w_o, w_qkv, gain_q, gain_k,
    cos_wide, sin_wide, n_seq, n_bat, side=None,
):
    rows, heads, length, _ = q.shape
    own, dim = grad_o.shape
    span = own // rows
    col, three = qkv.shape
    wide = three // 3
    chunk = min(256, length)
    scale = HEAD ** (-0.5)

    def kernel(*refs):
        (go_ref, q_ref, k_ref, v_ref, mix_ref, qkv_ref, stat_ref, hid_ref, use_ref, wo_ref,
         w_ref, gq_ref, gk_ref, cos_ref, sin_ref) = refs[:15]
        refs = refs[15:]
        if side:
            weighted_ref, down_ref = refs[:2]
            refs = refs[2:]
        gwo_ref, gw_ref, gain_ref, out_ref = refs[:4]
        refs = refs[4:]
        if side:
            mixture_ref = refs[0]
            mix_away, mix_twin, mix_halves, mix_full = refs[-6:-2]
            refs = refs[1:-6] + refs[-2:]
        go_all, gm, dq, dk, dv, dqkv, local, got, hid_buf, hid_sems = refs[:10]
        away, mine, twin, line, send_sems, recv_sems = refs[10:]
        place = Place(n_seq, n_bat)
        place.greet(all_seq=True, batch=bool(side))
        wire = Wire(send_sems, recv_sems)
        gather = SeqGather(place, wire, go_ref, go_all)
        gather.start()
        go_all[place.s] = go_ref[...]
        order = list(range(1, place.half)) + [0]
        works, from_twin = {}, {}

        def mixture_of(i):
            group = n_bat * own
            at = pl.ds(pl.multiple_of(i * group, group), group)
            return dot(weighted_ref[at, :], down_ref[...])

        if side:
            waiting = None
            for n, j in enumerate(order):
                if n >= 2:
                    wire.settle(from_twin[order[n - 2]])
                mix_away[n % 2] = (
                    mixture_of(place.twin_at(2 * j)).astype(BF).reshape(n_bat, own, dim)
                )
                total = mixture_of(place.seq_at(2 * j))
                from_twin[j] = wire.push(mix_away.at[n % 2], mix_twin.at[j], place.twin())
                from_twin[j].wait_recv()
                mix_twin[j] = (
                    (total + mix_twin[j].reshape(n_bat * own, dim).astype(F32))
                    .astype(BF)
                    .reshape(n_bat, own, dim)
                )
                works[j] = AcrossSum(
                    place, wire, mix_twin.at[j], mix_halves.at[j], mix_full.at[j]
                )
                if waiting is not None:
                    works[waiting].start()
                waiting = j
                if j:
                    gather.step(j)
            works[waiting].start()
        else:
            for j in range(1, place.half):
                gather.step(j)
        gather.finish()
        for i in range(n_seq):
            part = dot_t(go_all[i], wo_ref[...]).astype(BF)
            for r in range(rows):
                gm[r, i * span : (i + 1) * span, :] = part[r * span : (r + 1) * span, :]
        for j in works:
            works[j].middle()
        dk[...] = jnp.zeros_like(dk)
        dv[...] = jnp.zeros_like(dv)
        for r in range(rows):
            for c in range(length // chunk):
                keys = (c + 1) * chunk
                now = slice(c * chunk, keys)
                allowed = allowed_block(use_ref[r : r + 1, :keys], c * chunk, chunk, keys)
                for h in range(heads):
                    lanes = slice(h * HEAD, (h + 1) * HEAD)
                    query = q_ref[r, h, now, :]
                    key = k_ref[r, h, :keys, :]
                    scores = jnp.where(allowed, dot_t(query, key) * scale, NEGATIVE)
                    raised = jnp.exp(scores - jnp.max(scores, axis=-1, keepdims=True))
                    probs = raised / jnp.sum(raised, axis=-1, keepdims=True)
                    low = probs.astype(BF)
                    grad_mix = gm[r, now, lanes]
                    grad_probs = dot_t(grad_mix, v_ref[r, h, :keys, :])
                    row_dot = jnp.sum(low.astype(F32) * grad_probs, axis=-1, keepdims=True)
                    grad_scores = (probs * (grad_probs - row_dot)).astype(BF)
                    dq[r, now, lanes] = scale * dot(grad_scores, key)
                    dk[r, :keys, lanes] += scale * t_dot(grad_scores, query)
                    dv[r, :keys, lanes] += t_dot(low, grad_mix)
        columns = lax.rsqrt(stat_ref[...] / dim + EPS).T
        for which, g_ref, grads in ((0, gq_ref, dq), (1, gk_ref, dk)):
            sums = [jnp.zeros((1, HEAD), F32) for _ in range(heads)]
            for i in range(n_seq):
                at_pos = slice(i * span, (i + 1) * span)
                products = []
                for r in range(rows):
                    at = slice(i * own + r * span, i * own + (r + 1) * span)
                    factor = columns[
                        r * span : (r + 1) * span, which * n_seq + i : which * n_seq + i + 1
                    ]
                    parts = []
                    for h in range(heads):
                        lanes = slice(h * HEAD, (h + 1) * HEAD)
                        flat = qkv_ref[at, which * wide + h * HEAD : which * wide + (h + 1) * HEAD]
                        flat = flat * factor
                        back = turn(
                            grads[r, at_pos, lanes], cos_ref[at_pos, :], -sin_ref[at_pos, :]
                        )
                        sums[h] = sums[h] + jnp.sum(back * flat, axis=0, keepdims=True)
                        weighted = back * g_ref[0:1, lanes]
                        grads[r, at_pos, lanes] = weighted
                        parts.append(weighted * flat)
                    products.append(sum(parts))
                local[which * n_seq + i : which * n_seq + i + 1, :] = lane_sums(
                    jnp.concatenate(products, axis=0)
                )
            for h in range(heads):
                gain_ref[which : which + 1, h * HEAD : (h + 1) * HEAD] = sums[h]
        for i in range(n_seq):
            for r in range(rows):
                at = slice(i * own + r * span, i * own + (r + 1) * span)
                dqkv[at, 2 * wide :] = dv[r, i * span : (i + 1) * span, :].astype(BF)
        means = (exchange_rows(place, wire, local, got) / dim).T
        for which, grads in ((0, dq), (1, dk)):
            for i in range(n_seq):
                at_pos = slice(i * span, (i + 1) * span)
                column = which * n_seq + i
                for r in range(rows):
                    at = slice(i * own + r * span, i * own + (r + 1) * span)
                    inside = slice(r * span, (r + 1) * span)
                    factor = columns[inside, column : column + 1]
                    mean = means[inside, column : column + 1]
                    lanes = slice(which * wide, (which + 1) * wide)
                    flat = qkv_ref[at, lanes] * factor
                    dqkv[at, lanes] = (factor * (grads[r, at_pos, :] - flat * mean)).astype(BF)
        scatter = SeqScatter(place, wire, away, mine, twin, line)

        def project(i):
            rows_at = pl.ds(pl.multiple_of(i * own, own), own)
            return dot_t(dqkv[rows_at, :], w_ref[...])

        def hidden_load(part):
            return pltpu.make_async_copy(
                hid_ref.at[:, pl.ds(part * 256, 256)], hid_buf.at[part % 2], hid_sems.at[part % 2]
            )

        hidden_load(0).start()
        scatter.run(project, out_ref)
        for part in range(dim // 256):
            at = slice(part * 256, (part + 1) * 256)
            if part + 1 < dim // 256:
                hidden_load(part + 1).start()
            hidden_load(part).wait()
            gw_ref[at, :] = t_dot(hid_buf[part % 2], dqkv[...]).astype(BF)
            total = t_dot(mix_ref[0:own, :], go_all[0, :, at])
            for i in range(1, n_seq):
                total = total + t_dot(mix_ref[i * own : (i + 1) * own, :], go_all[i, :, at])
            gwo_ref[:, at] = total.astype(BF)
        for j in works:
            works[j].finish()
            mixture_ref[j] = mix_twin[j, place.b]
        scatter.finish(out_ref)
        wire.drain()

    vmem = pl.BlockSpec(memory_space=pltpu.VMEM)
    block = jax.ShapeDtypeStruct((own, dim), BF)
    stat_shape = (2 * n_seq, own)
    side_out, side_scratch = [], []
    if side:
        half = n_seq // 2
        side_out = [jax.ShapeDtypeStruct((half, own, dim), BF)]
        side_scratch = [
            pltpu.VMEM((2, n_bat, own, dim), BF),
            pltpu.VMEM((half, n_bat, own, dim), BF),
            pltpu.VMEM((half, 2, own // 2, dim), BF),
            pltpu.VMEM((half, 2, own, dim), BF),
        ]
    return comm_call(
        kernel,
        [
            jax.ShapeDtypeStruct((wide, dim), BF),
            jax.ShapeDtypeStruct((dim, three), BF),
            jax.ShapeDtypeStruct((2, wide), F32),
            block,
        ]
        + side_out,
        [
            pltpu.VMEM((n_seq, own, dim), BF),
            pltpu.VMEM((rows, length, wide), BF),
            pltpu.VMEM((rows, length, wide), F32),
            pltpu.VMEM((rows, length, wide), F32),
            pltpu.VMEM((rows, length, wide), F32),
            pltpu.VMEM((col, three), BF),
            pltpu.VMEM(stat_shape, F32),
            pltpu.VMEM((n_seq - 1,) + stat_shape, F32),
            pltpu.VMEM((2, col, 256), BF),
            pltpu.SemaphoreType.DMA((2,)),
        ]
        + SeqScatter.scratch(n_seq, block)
        + side_scratch,
        4 * n_seq + (3 * n_seq if side else 0),
        6,
        "attend_backward",
        [vmem] * 7 + [ANY] + [vmem] * (7 + len(side or ())),
        [vmem] * (4 + len(side_out)),
    )(grad_o, q, k, v, mixed, qkv, stats, hidden, usable, w_o, w_qkv, gain_q, gain_k,
      cos_wide, sin_wide, *(side or ()))


class Across:
    def __init__(self, place, wire, src, at):
        self.place, self.wire, self.src, self.at = place, wire, src, at
        self.half = src.shape[0] // 2

    def start(self):
        place, own = self.place, self.at(self.place.b)
        self.to_x = self.wire.push(self.src, own, place.x_peer())
        self.to_y = self.wire.push(self.src, own, place.y_peer())

    def relay(self):
        place, half = self.place, self.half
        self.to_x.wait_recv()
        top = self.at(place.bat_x).at[pl.ds(0, half)]
        self.top = self.wire.push(top, top, place.y_peer())
        self.to_y.wait_recv()
        low = self.at(place.bat_y).at[pl.ds(half, half)]
        self.low = self.wire.push(low, low, place.x_peer())

    def finish(self):
        self.top.wait_recv()
        self.low.wait_recv()


class AcrossSum:
    def __init__(self, place, wire, group, halves, full):
        self.place, self.wire = place, wire
        self.group, self.halves, self.full = group, halves, full
        self.half = halves.shape[1]

    def start(self):
        place, half = self.place, self.half
        far = self.group.at[place.bat_d]
        self.top = self.wire.push(far.at[pl.ds(0, half)], self.halves.at[0], place.x_peer())
        self.low = self.wire.push(far.at[pl.ds(half, half)], self.halves.at[1], place.y_peer())

    def middle(self):
        place, half = self.place, self.half
        self.top.wait_recv()
        add_into(self.group.at[place.bat_y].at[pl.ds(0, half)], self.halves.at[0])
        self.low.wait_recv()
        add_into(self.group.at[place.bat_x].at[pl.ds(half, half)], self.halves.at[1])
        self.y = self.wire.push(self.group.at[place.bat_y], self.full.at[0], place.y_peer())
        self.x = self.wire.push(self.group.at[place.bat_x], self.full.at[1], place.x_peer())

    def finish(self):
        self.y.wait_recv()
        self.x.wait_recv()
        add_into(self.group.at[self.place.b], self.full.at[0], self.full.at[1])


def load_first(weights, w_out, mine, flags, small, dy_own, n_seq, n_bat):
    shard, dim = weights[0].shape
    wide = dim // n_seq
    own = mine.shape[0]
    slots = 12 * n_seq + n_seq * n_bat

    def kernel(*refs):
        parts = refs[:3]
        wo_ref, x_ref, flag_ref, small_ref, dy_ref = refs[3:8]
        w_ref, wo_all, x_col, flag_col, small_all, dy_all = refs[8:14]
        buffers = refs[14:20]
        own_sems, cut_sems, send_sems, recv_sems = refs[20:]
        place = Place(n_seq, n_bat)
        place.greet(all_seq=True)
        wire = Wire(send_sems, recv_sems)
        small_work = FullGather(place, wire, small_ref, small_all)
        flag_work = SeqGather(place, wire, flag_ref, flag_col)
        x_work = SeqGather(place, wire, x_ref, x_col)
        small_work.start()
        flag_work.start()

        def cut(k):
            return pl.ds(pl.multiple_of(place.seq_at(k) * wide, wide), wide)

        def columns(m):
            return pl.ds(m * wide, wide)

        own_cuts = []
        for m in range(3):
            copy = pltpu.make_async_copy(
                parts[m].at[:, cut(0)], buffers[0].at[:, columns(m)], cut_sems.at[m]
            )
            copy.start()
            own_cuts.append(copy)
        cuts = {}
        for k in range(1, n_seq):
            for m in range(3):
                cuts[k, m] = wire.push(
                    parts[m].at[:, cut(k)],
                    w_ref.at[place.s, place.b, :, columns(m)],
                    place.seq_peer(k),
                )
        wo_work = Across(place, wire, wo_ref, lambda i: wo_all.at[i])
        wo_work.start()
        x_work.start()
        line = [
            wire.push(dy_ref, dy_all.at[place.s, place.b], place.seq_peer(2 * j))
            for j in range(1, place.half)
        ]
        for copy in own_cuts:
            copy.wait()
        spreads = []

        def spread(src, from_seq):
            work = Across(place, wire, src, lambda i: w_ref.at[from_seq, i])
            work.start()
            spreads.append(work)

        spread(buffers[0], place.s)
        own_w = pltpu.make_async_copy(buffers[0], w_ref.at[place.s, place.b], own_sems.at[0])
        own_w.start()
        copies = [own_w] + [
            keep_own(src, dst, buffers[i + 1], own_sems.at[i + 1])
            for i, (src, dst) in enumerate(
                (
                    (wo_ref, wo_all.at[place.b]),
                    (x_ref, x_col.at[place.s]),
                    (flag_ref, flag_col.at[place.s]),
                    (small_ref, small_all.at[place.s, place.b]),
                    (dy_ref, dy_all.at[place.s, place.b]),
                )
            )
        ]
        for j in range(1, place.half):
            small_work.step(j)
            flag_work.step(j)
        for k in range(1, n_seq):
            for m in range(3):
                cuts[k, m].wait_recv()
            spread(w_ref.at[place.seq_at(-k), place.b], place.seq_at(-k))
        for j in range(place.half):
            small_work.collect(j)
        wo_work.relay()
        for work in spreads:
            work.relay()
        for j in range(1, place.half):
            x_work.step(j)
        wo_work.finish()
        for work in spreads:
            work.finish()
        for work in (small_work, flag_work, x_work):
            work.finish()
        for copy in line:
            copy.wait_recv()
        for copy in copies:
            copy.wait()
        wire.drain()

    every = (n_seq, n_bat)
    one = jax.ShapeDtypeStruct((shard, 3 * wide), BF)
    blocks = (one, w_out, mine, flags, small, dy_own)
    leads = (every, (n_bat,), (n_seq,), (n_seq,), every, every)
    return comm_call(
        kernel,
        [shape_of(lead, block) for lead, block in zip(leads, blocks)],
        [pltpu.VMEM(block.shape, block.dtype) for block in blocks]
        + [pltpu.SemaphoreType.DMA((6,)), pltpu.SemaphoreType.DMA((3,))],
        slots,
        1,
        "load_first",
        [ANY] * 8,
    )(*weights, w_out, mine, flags, small, dy_own)


def pick_units(first, experts, units, part):
    at_expert = lax.broadcasted_iota(jnp.int32, (experts, units), 0)
    at_unit = lax.broadcasted_iota(jnp.int32, (experts, units), 1)
    low = (at_expert - first) * part
    return jnp.where((at_unit >= low) & (at_unit < low + part), 1.0, 0.0).astype(F32)


def experts_forward(normed, gates, dy_all, w_gu, w_down, local_experts, n_seq, n_bat):
    own, dim = normed.shape
    units = w_down.shape[0]
    part = units // local_experts
    group = n_bat * own
    tokens = n_seq * group
    experts = gates.shape[0]
    slots = 64 + 2 * n_seq * n_bat

    def kernel(*refs):
        x_ref, gate_ref, dy_ref, gu_ref, down_ref = refs[:5]
        x_all, weighted_ref, grad_ref, term_ref = refs[5:9]
        gates_all, back, x_buf, dy_buf, keep, own_sems, x_sems, dy_sems = refs[9:17]
        send_sems, recv_sems = refs[17:]
        place = Place(n_seq, n_bat)
        place.greet()
        wire = Wire(send_sems, recv_sems)
        gate_work = FullGather(place, wire, gate_ref, gates_all)
        gate_work.start()
        gates_all[place.s, place.b] = gate_ref[...]
        line = [
            wire.push(x_ref, x_all.at[place.s, place.b], place.seq_peer(2 * j))
            for j in range(1, place.half)
        ]
        works = []
        for j in range(place.half):
            at_seq = place.seq_at(-2 * j)
            src = x_ref if j == 0 else x_all.at[at_seq, place.b]
            works.append(
                Across(place, wire, src, lambda i, at_seq=at_seq: x_all.at[at_seq, i])
            )
        works[0].start()
        own = keep_own(x_ref, x_all.at[place.s, place.b], keep, own_sems.at[0])
        selected = pick_units(place.b * local_experts, experts, units, part)

        def dy_load(g, slot):
            return pltpu.make_async_copy(dy_ref.at[g], dy_buf.at[slot], dy_sems.at[slot])

        def rows_of(g):
            return pl.ds(pl.multiple_of(g * group, group), group)

        def backs(first, count):
            dy_load(first, first % 2).start()
            for g in range(first, first + count):
                if g + 1 < first + count:
                    dy_load(g + 1, (g + 1) % 2).start()
                dy_load(g, g % 2).wait()
                block = dy_buf[g % 2].reshape(group, dim)
                back[g * group : (g + 1) * group, :] = dot_t(block, down_ref[...])

        passed = []

        def hand_over(j):
            at_seq = place.seq_at(-2 * j)
            works[j].finish()
            if j == 0:
                own.wait()
            passed.append(wire.push(x_all.at[at_seq], x_all.at[at_seq], place.twin()))

        loads = {}

        def fetch(g, slot):
            loads[slot] = pltpu.make_async_copy(x_all.at[g], x_buf.at[slot], x_sems.at[slot])
            loads[slot].start()

        def units_on(g, slot):
            loads[slot].wait()
            at = rows_of(g)
            pre = dot(x_buf[slot].reshape(group, dim), gu_ref[...])
            gate_pre, up_pre = pre[:, :units], pre[:, units:]
            sig = jax.nn.sigmoid(gate_pre)
            silu = gate_pre * sig
            active = (silu * up_pre).astype(BF).astype(F32)
            grad_back = back[at, :]
            product = active * grad_back
            wide_gates = []
            for i in range(n_bat):
                inside = slice(i * x_ref.shape[0], (i + 1) * x_ref.shape[0])
                wide_gates.append(
                    lax.dot_general(
                        gates_all[g, i],
                        selected,
                        (((0,), (0,)), ((), ())),
                        precision=HIGHEST,
                        preferred_element_type=F32,
                    )
                )
                term_ref[g, i] = lax.dot_general(
                    selected,
                    product[inside, :],
                    (((1,), (1,)), ((), ())),
                    precision=HIGHEST,
                    preferred_element_type=F32,
                )
            wide_gate = jnp.concatenate(wide_gates, axis=0)
            weighted_ref[at, :] = (active * wide_gate).astype(BF)
            grad_active = grad_back * wide_gate
            grad_ref[at, :units] = (
                grad_active * up_pre * sig * (1.0 + gate_pre * (1.0 - sig))
            ).astype(BF)
            grad_ref[at, units:] = (grad_active * silu).astype(BF)

        half = place.half
        per = n_seq // half
        for j in range(1, half):
            backs((j - 1) * per, per)
            gate_work.step(j)
            gate_work.collect(j - 1)
            line[j - 1].wait_recv()
            works[j].start()
            works[j - 1].relay()
        backs((half - 1) * per, per)
        gate_work.collect(half - 1)
        gate_work.finish()
        hand_over(0)
        fetch(place.seq_at(0), 0)
        for j in range(half):
            units_on(place.seq_at(-2 * j), (2 * j) % 4)
            passed[j].wait_recv()
            fetch(place.twin_at(-2 * j), (2 * j + 1) % 4)
            if j + 1 < half:
                hand_over(j + 1)
                fetch(place.seq_at(-2 * (j + 1)), (2 * j + 2) % 4)
            units_on(place.twin_at(-2 * j), (2 * j + 1) % 4)
            if j == max(0, half - 4):
                works[half - 1].relay()
        wire.drain()

    vmem = pl.BlockSpec(memory_space=pltpu.VMEM)
    return comm_call(
        kernel,
        [
            shape_of((n_seq, n_bat), normed),
            jax.ShapeDtypeStruct((tokens, units), BF),
            jax.ShapeDtypeStruct((tokens, 2 * units), BF),
            shape_of((n_seq, n_bat), gates),
        ],
        [
            pltpu.VMEM((n_seq, n_bat) + gates.shape, F32),
            pltpu.VMEM((tokens, units), F32),
            pltpu.VMEM((4, n_bat, own, dim), BF),
            pltpu.VMEM((2, n_bat, own, dim), BF),
            pltpu.VMEM((own, dim), BF),
            pltpu.SemaphoreType.DMA((1,)),
            pltpu.SemaphoreType.DMA((4,)),
            pltpu.SemaphoreType.DMA((2,)),
        ],
        slots,
        4,
        "experts_forward",
        [ANY, vmem, ANY, vmem, vmem],
        [ANY, vmem, vmem, vmem],
    )(normed, gates, dy_all, w_gu, w_down)


def experts_backward(
    grad_pre, weighted, w_gu, terms, x_all, dy_all, local_experts, n_seq, n_bat, own
):
    tokens, dim = x_all.shape
    units = weighted.shape[1]
    part = units // local_experts
    group = n_bat * own
    depth = dim // n_seq
    hidden = n_seq * part
    half = n_seq // 2
    slots = 128 + 2 * n_seq * n_bat
    block = jax.ShapeDtypeStruct((own, dim), BF)
    term = jax.ShapeDtypeStruct(terms.shape[2:], F32)

    def kernel(*refs):
        grad_ref, weighted_ref, gu_ref, term_in, x_ref, dy_ref = refs[:6]
        out_ref, term_out, gate_out, up_out, down_out = refs[6:11]
        away, twin, halves, full, line = refs[11:16]
        columns, sent, got, column_sems = refs[16:20]
        term_scratch = refs[20:25]
        send_sems, recv_sems = refs[25:]
        place = Place(n_seq, n_bat)
        place.greet(all_seq=True)
        wire = Wire(send_sems, recv_sems)
        term_work = FullScatter(place, wire, term_in, term_out, *term_scratch, None)
        term_work.start()

        def product(i):
            at = pl.ds(pl.multiple_of(i * group, group), group)
            return dot_t(grad_ref[at, :], gu_ref[...])

        order = list(range(1, half)) + [0]
        from_twin, from_seq, works = {}, {}, {}

        def send(j):
            from_twin[j] = wire.push(away.at[j], twin.at[j], place.twin())

        waiting = None
        for j in order:
            away[j] = product(place.twin_at(2 * j)).astype(BF).reshape(n_bat, own, dim)
            if waiting is not None:
                send(waiting)
            waiting = j
        chunks = [("x", k) for k in list(range(1, n_seq)) + [0]] + [
            ("y", k) for k in range(dim // 256)
        ]

        def chunk_load(n):
            kind, k = chunks[n]
            if kind == "x":
                src = x_ref.at[:, pl.ds(pl.multiple_of(place.seq_at(k) * depth, depth), depth)]
            else:
                src = dy_ref.at[:, pl.ds(k * 256, 256)]
            return pltpu.make_async_copy(src, columns.at[n % 2], column_sems.at[n % 2])

        chunk_load(0).start()
        for j in order:
            part_sum = product(place.seq_at(2 * j))
            if waiting is not None:
                send(waiting)
                waiting = None
            from_twin[j].wait_recv()
            twin[j] = (
                (part_sum + twin[j].reshape(group, dim).astype(F32))
                .astype(BF)
                .reshape(n_bat, own, dim)
            )
            works[j] = AcrossSum(place, wire, twin.at[j], halves.at[j], full.at[j])
            if len(works) > 1:
                works[order[len(works) - 2]].start()
        term_order = term_work.order()
        for j in term_order:
            term_work.pair(j)
        works[order[-1]].start()

        arrivals = []
        done = [0]

        def work_chunk():
            n = done[0]
            if n >= len(chunks):
                return
            done[0] = n + 1
            if n + 1 < len(chunks):
                chunk_load(n + 1).start()
            chunk_load(n).wait()
            kind, k = chunks[n]
            if kind == "y":
                down_out[:, k * 256 : (k + 1) * 256] = t_dot(weighted_ref[...], columns[n % 2])
                return
            value = t_dot(columns[n % 2], grad_ref[...]).astype(BF)
            if k == 0:
                got[place.s] = value
            else:
                sent[k] = value
            if n:
                push_chunk(chunks[n - 1][1])

        def push_chunk(k):
            if k:
                arrivals.append(wire.push(sent.at[k], got.at[place.s], place.seq_peer(k)))

        def pass_on(j):
            works[j].finish()
            if j:
                from_seq[j] = wire.push(twin.at[j, place.b], line.at[j], place.seq_peer(2 * j))

        steps = []
        for n, j in enumerate(order):
            steps.append(("middle", j))
            if n:
                steps.append(("finish", order[n - 1]))
        steps.append(("finish", order[-1]))
        share = -(-len(chunks) // len(steps))
        for kind, j in steps:
            for _ in range(share):
                work_chunk()
            if kind == "middle":
                works[j].middle()
            else:
                pass_on(j)
        for j in term_order:
            term_work.merge(j)
        while done[0] < len(chunks):
            work_chunk()
        for copy in arrivals:
            copy.wait_recv()
        for i in range(n_seq):
            lanes = slice(i * part, (i + 1) * part)
            for e in range(local_experts):
                gate_out[e, :, lanes] = got[i, :, e * part : (e + 1) * part].astype(F32)
                up_out[e, :, lanes] = got[i, :, units + e * part : units + (e + 1) * part].astype(
                    F32
                )
        term_work.finish()
        for j in range(1, half):
            from_seq[j].wait_recv()
        total = twin[0, place.b].astype(F32)
        for j in range(1, half):
            total = total + line[j].astype(F32)
        out_ref[...] = total
        wire.drain()

    vmem = pl.BlockSpec(memory_space=pltpu.VMEM)
    expert = jax.ShapeDtypeStruct((local_experts, depth, hidden), F32)
    return comm_call(
        kernel,
        [
            jax.ShapeDtypeStruct((own, dim), F32),
            term,
            expert,
            expert,
            jax.ShapeDtypeStruct((units, dim), F32),
        ],
        [
            pltpu.VMEM((half, n_bat, own, dim), BF),
            pltpu.VMEM((half, n_bat, own, dim), BF),
            pltpu.VMEM((half, 2, own // 2, dim), BF),
            pltpu.VMEM((half, 2, own, dim), BF),
            pltpu.VMEM((half, own, dim), BF),
            pltpu.VMEM((2, tokens, 256), BF),
            pltpu.VMEM((n_seq, depth, 2 * units), BF),
            pltpu.VMEM((n_seq, depth, 2 * units), BF),
            pltpu.SemaphoreType.DMA((2,)),
        ]
        + FullScatter.scratch(n_seq, n_bat, term),
        slots,
        5,
        "experts_backward",
        [vmem] * 3 + [ANY] * 3,
        [vmem] * 5,
    )(grad_pre, weighted, w_gu, terms, x_all, dy_all)


def store_last(grad_w, grad_wo, small, mixture, n_seq, n_bat):
    one = jax.ShapeDtypeStruct(grad_w.shape[2:], grad_w.dtype)
    shard, three = one.shape
    wide = three // 3
    wo_one = jax.ShapeDtypeStruct(grad_wo.shape[1:], grad_wo.dtype)
    small_one = jax.ShapeDtypeStruct(small.shape[2:], small.dtype)
    half = n_seq // 2
    dim = wo_one.shape[1]
    slots = 64 + n_seq * n_bat + 5 * n_seq

    def kernel(*refs):
        w_ref, wo_ref, small_ref, mix_ref = refs[:4]
        q_out, k_out, v_out, wo_out, small_out, mix_out = refs[4:10]
        w_sum, w_halves, w_full, w_got, wo_sum, wo_halves, wo_full, line = refs[10:18]
        small_scratch = refs[18:23]
        w_sems, wo_sem, send_sems, recv_sems = refs[23:]
        place = Place(n_seq, n_bat)
        place.greet(all_seq=True)
        wire = Wire(send_sems, recv_sems)
        small_work = FullScatter(place, wire, small_ref, small_out, *small_scratch, None)
        small_work.start()
        order = list(range(1, n_seq)) + [0]
        loads = {}
        for k in order:
            loads[k] = pltpu.make_async_copy(
                w_ref.at[place.seq_at(k)], w_sum.at[k], w_sems.at[k]
            )
            loads[k].start()
        wo_load = pltpu.make_async_copy(wo_ref, wo_sum, wo_sem.at[0])
        wo_load.start()
        works = {}
        for k in order:
            loads[k].wait()
            works[k] = AcrossSum(place, wire, w_sum.at[k], w_halves.at[k], w_full.at[k])
            works[k].start()
        wo_load.wait()
        wo_work = AcrossSum(place, wire, wo_sum, wo_halves, wo_full)
        wo_work.start()
        term_order = small_work.order()
        for j in term_order:
            small_work.pair(j)
        mix_line = {
            j: wire.push(mix_ref.at[j], line.at[j], place.seq_peer(2 * j)) for j in range(1, half)
        }
        arrivals = []
        ready = None

        def ship(k):
            if k:
                arrivals.append(
                    wire.push(w_sum.at[k, place.b], w_got.at[place.s], place.seq_peer(k))
                )

        for k in order:
            works[k].middle()
        wo_work.middle()
        for j in term_order:
            small_work.merge(j)
        for k in order:
            works[k].finish()
            if ready is not None:
                ship(ready)
            ready = k
        w_got[place.s] = w_sum[0, place.b]
        wo_work.finish()
        wo_out[...] = wo_sum[place.b].astype(F32)
        small_work.finish()
        for copy in arrivals:
            copy.wait_recv()
        for i in range(n_seq):
            at = slice(i * wide, (i + 1) * wide)
            for m, out in enumerate((q_out, k_out, v_out)):
                out[:, at] = w_got[i, :, m * wide : (m + 1) * wide].astype(F32)
        for copy in mix_line.values():
            copy.wait_recv()
        total = mix_ref[0].astype(F32)
        for j in range(1, half):
            total = total + line[j].astype(F32)
        mix_out[...] = total
        wire.drain()

    vmem = pl.BlockSpec(memory_space=pltpu.VMEM)
    matrix = jax.ShapeDtypeStruct((shard, dim), F32)
    return comm_call(
        kernel,
        [matrix] * 4 + [small_one, jax.ShapeDtypeStruct(mixture.shape[1:], F32)],
        [
            pltpu.VMEM((n_seq, n_bat, shard, three), BF),
            pltpu.VMEM((n_seq, 2, shard // 2, three), BF),
            pltpu.VMEM((n_seq, 2, shard, three), BF),
            pltpu.VMEM((n_seq, shard, three), BF),
            pltpu.VMEM((n_bat, shard, dim), BF),
            pltpu.VMEM((2, shard // 2, dim), BF),
            pltpu.VMEM((2, shard, dim), BF),
            pltpu.VMEM(mixture.shape, BF),
        ]
        + FullScatter.scratch(n_seq, n_bat, small_one)
        + [pltpu.SemaphoreType.DMA((n_seq,)), pltpu.SemaphoreType.DMA((1,))],
        slots,
        8,
        "store_last",
        [ANY] * 3 + [vmem],
        [vmem] * 6,
    )(grad_w, grad_wo, small, mixture)


def load_inputs(qkv_cut, w_out, mine, flags, small, gu_cut, dy_own, n_seq, n_bat):
    n_in = 7
    slots = 4 * n_seq * n_bat + 3 * n_seq + 2 * n_bat

    def kernel(*refs):
        cut_ref, wo_ref, x_ref, flag_ref, small_ref, gu_ref, dy_ref = refs[:n_in]
        w_ref, wo_all, x_col, flag_col, small_all, gu_all, dy_all = refs[n_in : 2 * n_in]
        buffers = refs[2 * n_in : 3 * n_in]
        own_sems, send_sems, recv_sems = refs[3 * n_in :]
        place = Place(n_seq, n_bat)
        place.greet(all_seq=True)
        wire = Wire(send_sems, recv_sems)
        small_work = FullGather(place, wire, small_ref, small_all)
        flag_work = SeqGather(place, wire, flag_ref, flag_col)
        x_work = SeqGather(place, wire, x_ref, x_col)
        dy_work = FullGather(place, wire, dy_ref, dy_all)
        small_work.start()
        flag_work.start()
        cuts = [
            wire.push(cut_ref.at[place.seq_at(k)], w_ref.at[place.s, place.b], place.seq_peer(k))
            for k in range(1, n_seq)
        ]
        ends = [
            wire.push(wo_ref, wo_all.at[place.b], place.bat_peer(k)) for k in range(1, n_bat)
        ]
        ends += [
            wire.push(cut_ref.at[place.s], w_ref.at[place.s, place.b], place.bat_peer(k))
            for k in range(1, n_bat)
        ]
        x_work.start()
        own = [
            keep_own(src, dst, buffers[i], own_sems.at[i])
            for i, (src, dst) in enumerate(
                (
                    (cut_ref.at[place.s], w_ref.at[place.s, place.b]),
                    (wo_ref, wo_all.at[place.b]),
                    (x_ref, x_col.at[place.s]),
                    (flag_ref, flag_col.at[place.s]),
                    (small_ref, small_all.at[place.s, place.b]),
                    (gu_ref.at[place.s], gu_all.at[place.s]),
                    (dy_ref, dy_all.at[place.s, place.b]),
                )
            )
        ]
        ends += [
            wire.push(gu_ref.at[place.seq_at(k)], gu_all.at[place.s], place.seq_peer(k))
            for k in range(1, n_seq)
        ]
        dy_work.start()
        for j in range(1, place.half):
            small_work.step(j)
            flag_work.step(j)
        for k in range(1, n_seq):
            cuts[k - 1].wait_recv()
            block = w_ref.at[place.seq_at(-k), place.b]
            ends += [wire.push(block, block, place.bat_peer(m)) for m in range(1, n_bat)]
        for j in range(place.half):
            small_work.collect(j)
        for j in range(1, place.half):
            x_work.step(j)
        for j in range(1, place.half):
            dy_work.step(j)
            dy_work.collect(j - 1)
        dy_work.collect(place.half - 1)
        for work in (small_work, flag_work, x_work, dy_work):
            work.finish()
        for copy in ends:
            copy.wait_recv()
        for copy in own:
            copy.wait()
        wire.drain()

    every = (n_seq, n_bat)
    one = jax.ShapeDtypeStruct(qkv_cut.shape[1:], qkv_cut.dtype)
    gu_one = jax.ShapeDtypeStruct(gu_cut.shape[1:], gu_cut.dtype)
    blocks = (one, w_out, mine, flags, small, gu_one, dy_own)
    leads = (every, (n_bat,), (n_seq,), (n_seq,), every, (n_seq,), every)
    return comm_call(
        kernel,
        [shape_of(lead, block) for lead, block in zip(leads, blocks)],
        [pltpu.VMEM(block.shape, block.dtype) for block in blocks]
        + [pltpu.SemaphoreType.DMA((n_in,))],
        slots,
        1,
        "load_inputs",
        [ANY] * n_in,
    )(qkv_cut, w_out, mine, flags, small, gu_cut, dy_own)


def store_grads(grad_w, grad_wo, grad_gu, small, n_seq, n_bat):
    one = jax.ShapeDtypeStruct(grad_w.shape[2:], grad_w.dtype)
    wo_one = jax.ShapeDtypeStruct(grad_wo.shape[1:], grad_wo.dtype)
    gu_one = jax.ShapeDtypeStruct(grad_gu.shape[1:], grad_gu.dtype)
    small_one = jax.ShapeDtypeStruct(small.shape[2:], small.dtype)
    slots = 2 * n_seq * n_bat + 2 * n_seq + n_bat

    def kernel(*refs):
        w_ref, wo_ref, gu_ref, small_ref = refs[:4]
        w_out_ref, wo_out_ref, gu_out_ref, small_out_ref = refs[4:8]
        w_sum, w_got, wo_sum, wo_got, gu_buf, cut_buf = refs[8:14]
        small_scratch = refs[14:19]
        w_sems, sems, send_sems, recv_sems = refs[19:]
        place = Place(n_seq, n_bat)
        place.greet(all_seq=True)
        wire = Wire(send_sems, recv_sems)
        small_work = FullScatter(
            place, wire, small_ref, small_out_ref, *small_scratch, None
        )
        small_work.start()
        got, loads = {}, {}
        for i in list(range(1, n_seq)) + [0]:
            to_seq = place.seq_at(i)
            for k in range(1, n_bat):
                got[i, k] = wire.push(
                    w_ref.at[to_seq, place.bat_at(k)], w_got.at[i, k - 1], place.bat_peer(k)
                )
            loads[i] = pltpu.make_async_copy(
                w_ref.at[to_seq, place.b], w_sum.at[i], w_sems.at[i]
            )
            loads[i].start()
        wo_pushed = [
            wire.push(wo_ref.at[place.bat_at(k)], wo_got.at[k - 1], place.bat_peer(k))
            for k in range(1, n_bat)
        ]
        wo_load = pltpu.make_async_copy(wo_ref.at[place.b], wo_sum, sems.at[0])
        wo_load.start()
        ends = [
            wire.push(gu_ref.at[place.seq_at(k)], gu_out_ref.at[place.s], place.seq_peer(k))
            for k in range(1, n_seq)
        ]
        gu_own = keep_own(gu_ref.at[place.s], gu_out_ref.at[place.s], gu_buf, sems.at[1])
        order = small_work.order()
        for j in order:
            small_work.pair(j)
        for i in list(range(1, n_seq)) + [0]:
            loads[i].wait()
            for k in range(1, n_bat):
                got[i, k].wait_recv()
            add_into(w_sum.at[i], *[w_got.at[i, k] for k in range(n_bat - 1)])
            if i:
                ends.append(
                    wire.push(w_sum.at[i], w_out_ref.at[place.s], place.seq_peer(i))
                )
        w_own = pltpu.make_async_copy(w_sum.at[0], w_out_ref.at[place.s], sems.at[2])
        w_own.start()
        for j in order:
            small_work.merge(j)
        wo_load.wait()
        for copy in wo_pushed:
            copy.wait_recv()
        add_into(wo_sum, *[wo_got.at[k] for k in range(n_bat - 1)])
        wo_out_ref[...] = wo_sum[...].astype(F32)
        small_work.finish()
        for copy in ends:
            copy.wait_recv()
        gu_own.wait()
        w_own.wait()
        wire.drain()

    vmem = pl.BlockSpec(memory_space=pltpu.VMEM)
    return comm_call(
        kernel,
        [
            shape_of((n_seq,), one),
            jax.ShapeDtypeStruct(wo_one.shape, F32),
            shape_of((n_seq,), gu_one),
            small_one,
        ],
        [
            pltpu.VMEM((n_seq,) + one.shape, one.dtype),
            pltpu.VMEM((n_seq, n_bat - 1) + one.shape, one.dtype),
            pltpu.VMEM(wo_one.shape, wo_one.dtype),
            pltpu.VMEM((n_bat - 1,) + wo_one.shape, wo_one.dtype),
            pltpu.VMEM(gu_one.shape, gu_one.dtype),
            pltpu.VMEM(one.shape, one.dtype),
        ]
        + FullScatter.scratch(n_seq, n_bat, small_one)
        + [pltpu.SemaphoreType.DMA((n_seq,)), pltpu.SemaphoreType.DMA((3,))],
        slots,
        8,
        "store_grads",
        [ANY] * 4,
        [ANY, vmem, ANY, vmem],
    )(grad_w, grad_wo, grad_gu, small)


def shards(
    tokens,
    lengths,
    key_mask,
    top_experts,
    attn_gain,
    query_gain,
    key_gain,
    mlp_gain,
    w_query,
    w_key,
    w_value,
    w_out,
    w_router,
    expert_gate,
    expert_up,
    expert_down,
    cotangent,
):
    n_seq = lax.axis_size("seq")
    n_bat = lax.axis_size("batch")
    seq = lax.axis_index("seq")
    bat = lax.axis_index("batch")
    rows, span, dim = tokens.shape
    own = rows * span
    col = n_seq * own
    length = n_seq * span
    shard = w_query.shape[0]
    wide = dim // n_seq
    heads = wide // HEAD
    local_experts, depth, hidden_units = expert_gate.shape
    part = hidden_units // n_seq
    experts = local_experts * n_bat

    mine = tokens.reshape(own, dim)
    dy_own = cotangent.reshape(own, dim)
    small = jnp.concatenate(
        [w_router.T, jnp.stack([attn_gain, query_gain, key_gain, mlp_gain])], axis=0
    )
    positions_own = seq * span + jnp.arange(span, dtype=jnp.int32)
    flags = pack((positions_own[None, :] < lengths[:, None]) & (key_mask == 1))
    units = local_experts * part
    fused = (
        n_bat == 4
        and part % 128 == 0
        and own == 128
        and shard % 32 == 0
        and n_seq * n_bat * own * dim <= 8 * 1024 * 1024
    )
    if fused:
        w_qkv, w_o, x_col, flag_col, small_all, dy_part = load_first(
            (w_query, w_key, w_value), w_out, mine, flags, pack(small), dy_own, n_seq, n_bat
        )
    else:
        qkv_cut = jnp.stack([w_query, w_key, w_value]).reshape(3, shard, n_seq, wide)
        qkv_cut = jnp.transpose(qkv_cut, (2, 1, 0, 3)).reshape(n_seq, shard, 3 * wide)
        gu_cut = jnp.stack([expert_gate, expert_up]).reshape(2, local_experts, depth, n_seq, part)
        gu_cut = jnp.transpose(gu_cut, (3, 2, 0, 1, 4)).reshape(n_seq, depth, 2 * units)
        w_qkv, w_o, x_col, flag_col, small_all, w_gu, dy_all = load_inputs(
            qkv_cut, w_out, mine, flags, pack(small), gu_cut, dy_own, n_seq, n_bat
        )
        w_gu = w_gu.reshape(dim, 2 * units)
        dy_all = dy_all.reshape(-1, dim)
    w_qkv = w_qkv.reshape(dim, 3 * wide)
    w_o = w_o.reshape(wide, dim)
    w_down = expert_down.reshape(local_experts * part, dim)
    small_all = unpack(small_all, (n_seq, n_bat), small.shape)
    small_all = jnp.transpose(small_all, (2, 0, 1, 3)).reshape(-1, dim)
    router = small_all[:experts].T.astype(BF)
    gain_attn, gain_mlp = small_all[experts], small_all[experts + 3]
    gain_q = lax.dynamic_slice_in_dim(small_all[experts + 1], seq * wide, wide)
    gain_k = lax.dynamic_slice_in_dim(small_all[experts + 2], seq * wide, wide)
    usable = unpack(flag_col, (n_seq,), key_mask.shape)
    usable = jnp.transpose(usable, (1, 0, 2)).reshape(rows, length)

    x_col = x_col.reshape(col, dim).astype(F32)
    scale_x = rms_scale(x_col)
    hidden = (x_col * scale_x * gain_attn).astype(BF)
    qkv = dot(hidden, w_qkv)
    cos_part, sin_part = rotary_tables(jnp.arange(length, dtype=jnp.int32))
    cos_wide = jnp.concatenate([cos_part, cos_part], axis=1)
    sin_wide = jnp.concatenate([-sin_part, sin_part], axis=1)
    gain_q, gain_k = gain_q[None, :], gain_k[None, :]
    q, k, v, mixed, stats, mixed_out, *extra = attend_forward(
        qkv, usable, w_o, gain_q, gain_k, cos_wide, sin_wide, n_seq, n_bat, span,
        (dy_part, expert_gate, expert_up) if fused else None,
    )
    x_own = mine.astype(F32)
    residual = x_own + mixed_out.astype(F32)
    scale_r = rms_scale(residual)
    normed = (residual * scale_r * gain_mlp).astype(BF)
    router_probs = jax.nn.softmax(dot(normed, router), axis=-1)
    expert_ids = jnp.arange(experts, dtype=jnp.int32)
    chosen = jnp.any(top_experts.reshape(own, -1)[:, :, None] == expert_ids, axis=1).astype(F32)
    gates = router_probs * chosen

    if fused:
        dy_all, w_gu = extra[0], extra[1].reshape(dim, 2 * units)
        normed_all, weighted, grad_pre, gate_terms = experts_forward(
            normed, gates.T, dy_all, w_gu, w_down, local_experts, n_seq, n_bat
        )
        grad_normed, grad_gates, grad_gate, grad_up, grad_down = experts_backward(
            grad_pre,
            weighted,
            w_gu,
            gate_terms,
            normed_all.reshape(-1, dim),
            dy_all.reshape(-1, dim),
            local_experts,
            n_seq,
            n_bat,
            own,
        )
        grad_gates = grad_gates.T
        grad_down = grad_down.reshape(local_experts, part, dim)
    else:
        normed_all, gates_all = gather_all([normed, pack(gates.T)], n_seq, n_bat, 4, "gather_normed")
        normed_all = normed_all.reshape(-1, dim)
        gates_all = unpack(gates_all, (n_seq, n_bat), (experts, own))
        gates_all = jnp.transpose(gates_all, (0, 1, 3, 2)).reshape(-1, experts)
        first_expert = bat * local_experts
        gates_here = lax.dynamic_slice_in_dim(gates_all, first_expert, local_experts, 1)
        gates_wide = jnp.repeat(gates_here, part, axis=1)
        pre = dot(normed_all, w_gu)
        gate_pre, up_pre = pre[:, :units], pre[:, units:]
        sig = jax.nn.sigmoid(gate_pre)
        silu = gate_pre * sig
        active = (silu * up_pre).astype(BF).astype(F32)
        weighted = (active * gates_wide).astype(BF)
        mixture = dot(weighted, w_down).astype(BF)
        mixture = mixture.reshape(n_seq, n_bat, own, dim)
        back = dot_t(dy_all, w_down)
        gate_terms = jnp.sum((active * back).reshape(-1, local_experts, part), axis=-1)
        grad_active = back * gates_wide
        grad_gate_pre = (grad_active * up_pre * sig * (1.0 + gate_pre * (1.0 - sig))).astype(BF)
        grad_up_pre = (grad_active * silu).astype(BF)
        grad_pre = jnp.concatenate([grad_gate_pre, grad_up_pre], axis=1)
        grad_down = t_dot(weighted, dy_all)
        grad_gu = t_dot(normed_all, grad_pre).astype(BF)
        grad_normed = dot_t(grad_pre, w_gu).astype(BF)
        gate_terms = gate_terms.reshape(n_seq, n_bat, own, local_experts)
        grad_gates = lax.dynamic_update_slice_in_dim(
            jnp.zeros((n_seq, n_bat, experts, own), F32),
            jnp.transpose(gate_terms, (0, 1, 3, 2)),
            first_expert,
            2,
        )
        grad_gates = jax.vmap(jax.vmap(pack))(grad_gates)
        grad_normed = grad_normed.reshape(n_seq, n_bat, own, dim)
        grad_normed, grad_gates, mixture = scatter_blocks(
            grad_normed, grad_gates, mixture, n_seq, n_bat
        )
        grad_normed = grad_normed.astype(F32)
        grad_gates = unpack(grad_gates, (), (experts, own)).T
        output = (residual + mixture.astype(F32)).astype(BF)
        grad_down = grad_down.reshape(local_experts, part, dim)

    grad_chosen = grad_gates * chosen
    grad_logits = router_probs * (
        grad_chosen - jnp.sum(router_probs * grad_chosen, axis=-1, keepdims=True)
    )
    grad_router = lax.dot_general(
        normed.astype(F32), grad_logits, (((0,), (0,)), ((), ())), precision=HIGHEST
    )
    grad_normed = grad_normed + lax.dot_general(
        grad_logits, router.astype(F32), (((1,), (1,)), ((), ())), precision=HIGHEST
    )
    grad_resid, gain_mlp_terms = rms_back(residual, scale_r, gain_mlp, grad_normed)
    grad_residual = dy_own.astype(F32) + grad_resid
    grad_o = grad_residual.astype(BF)

    grad_w_o, grad_w, grad_gains, grad_hidden, *extra = attend_backward(
        grad_o, q, k, v, mixed, qkv, stats, hidden, usable, w_o, w_qkv, gain_q, gain_k,
        cos_wide, sin_wide, n_seq, n_bat, (weighted, w_down) if fused else None,
    )
    grad_w_o = grad_w_o.reshape(n_bat, shard, dim)
    grad_w = grad_w.reshape(n_seq, n_bat, shard, 3 * wide)
    grad_hidden = grad_hidden.astype(F32)
    grad_x, gain_attn_terms = rms_back(x_own, rms_scale(x_own), gain_attn, grad_hidden)
    grad_tokens = (grad_residual + grad_x).astype(BF)

    zeros = jnp.zeros((dim,), F32)
    small_grads = jnp.concatenate(
        [
            grad_router.T,
            jnp.stack(
                [
                    jnp.sum(gain_attn_terms, axis=0),
                    lax.dynamic_update_slice_in_dim(zeros, grad_gains[0], seq * wide, 0),
                    lax.dynamic_update_slice_in_dim(zeros, grad_gains[1], seq * wide, 0),
                    jnp.sum(gain_mlp_terms, axis=0),
                ]
            ),
        ],
        axis=0,
    )
    small_grads = jnp.transpose(small_grads.reshape(-1, n_seq, n_bat, shard), (1, 2, 0, 3))
    small_grads = jax.vmap(jax.vmap(pack))(small_grads)
    if fused:
        *grad_w, grad_w_o, small_grads, mixture = store_last(
            grad_w, grad_w_o, small_grads, extra[0], n_seq, n_bat
        )
        output = (residual + mixture).astype(BF)
    else:
        grad_gu = grad_gu.reshape(n_seq, depth, -1)
        grad_w, grad_w_o, grad_gu, small_grads = store_grads(
            grad_w, grad_w_o, grad_gu, small_grads, n_seq, n_bat
        )
        grad_w = grad_w.astype(F32).reshape(n_seq, shard, 3, wide)
        grad_w = jnp.transpose(grad_w, (2, 1, 0, 3)).reshape(3, shard, dim)
        grad_gu = grad_gu.reshape(n_seq, depth, 2, local_experts, part)
        grad_gu = jnp.transpose(grad_gu, (2, 3, 1, 0, 4)).reshape(2, local_experts, depth, hidden_units)
        grad_gu = grad_gu.astype(F32)
        grad_gate, grad_up = grad_gu[0], grad_gu[1]
    small_grads = unpack(small_grads, (), (experts + 4, shard))

    return (
        output.reshape(rows, span, dim),
        grad_tokens.reshape(rows, span, dim),
        small_grads[experts],
        small_grads[experts + 1],
        small_grads[experts + 2],
        small_grads[experts + 3],
        grad_w[0],
        grad_w[1],
        grad_w[2],
        grad_w_o,
        small_grads[:experts].T,
        grad_gate,
        grad_up,
        grad_down,
    )


def solution(mesh):
    tok = P("batch", "seq", None)
    vec = P(("seq", "batch"))
    mat = P(("seq", "batch"), None)
    in_specs = (tok, P("batch"), P("batch", "seq"), tok) + (vec,) * 4 + (mat,) * 5 + (tok,) * 4
    out_specs = (tok, tok) + (vec,) * 4 + (mat,) * 5 + (tok,) * 3
    return jax.shard_map(shards, mesh=mesh, in_specs=in_specs, out_specs=out_specs, check_vma=False)
```

```python
import functools

import jax
import jax.numpy as jnp
from jax import lax
from jax.experimental import pallas as pl
from jax.experimental.pallas import tpu as pltpu
from jax.sharding import PartitionSpec as P

HEAD = 128
EPS = 1e-05
HIGHEST = lax.Precision.HIGHEST
NEGATIVE = -1e30
BF = jnp.bfloat16
F32 = jnp.float32


def dot(a, b):
    return jnp.dot(a, b, preferred_element_type=F32)


def dot_t(a, b):
    return lax.dot_general(a, b, (((1,), (1,)), ((), ())), preferred_element_type=F32)


def t_dot(a, b):
    return lax.dot_general(a, b, (((0,), (0,)), ((), ())), preferred_element_type=F32)


def rms_scale(v):
    return lax.rsqrt(jnp.mean(v * v, axis=-1, keepdims=True) + EPS)


def rms_back(v, scale, gain, grad):
    normal = v * scale
    weighted = grad * gain
    mean = jnp.mean(weighted * normal, axis=-1, keepdims=True)
    return scale * (weighted - normal * mean), grad * normal


def rotary_tables(positions):
    half_head = HEAD // 2
    frequency = 10000.0 ** (-2.0 * jnp.arange(half_head, dtype=F32) / HEAD)
    angles = positions.astype(F32)[:, None] * frequency[None, :]
    return jnp.cos(angles), jnp.sin(angles)


ANY = pl.BlockSpec(memory_space=pl.ANY)
VMEM_LIMIT = 67043328


class Place:
    def __init__(self, n_seq, n_bat):
        self.n_seq, self.n_bat, self.half = n_seq, n_bat, n_seq // 2
        self.s = lax.axis_index("seq")
        self.b = lax.axis_index("batch")
        self.core = lax.rem(self.s, 2)
        self.z = lax.div(self.s, 2)
        self.twin_s = self.s + 1 - 2 * self.core
        self.bat_x = self.b + 1 - 2 * lax.rem(self.b, 2)
        self.bat_y = lax.rem(self.b + 2, 4)
        self.bat_d = lax.rem(self.bat_x + 2, 4)

    def chip(self, i):
        return 2 * i + self.core

    def chip_twin(self, i):
        return 2 * i + 1 - self.core

    def chip_peer(self, i):
        return {"seq": self.chip(lax.rem(i + self.half, self.half)), "batch": self.b}

    def origin(self, m):
        if m == 0:
            return self.z
        last = self.half - 1
        upper = lax.div(2 * self.z, self.half)
        mirrored = self.z + upper * (last - 2 * self.z)
        place = m - 1 + lax.div(m - mirrored + last, self.half)
        return place + upper * (last - 2 * place)

    def seq_at(self, k):
        return lax.rem(self.s + (k + self.n_seq), self.n_seq)

    def twin_at(self, k):
        return lax.rem(self.twin_s + (k + self.n_seq), self.n_seq)

    def bat_at(self, k):
        return lax.rem(self.b + (k + self.n_bat), self.n_bat)

    def seq_peer(self, k):
        return {"seq": self.seq_at(k), "batch": self.b}

    def bat_peer(self, k):
        return {"seq": self.s, "batch": self.bat_at(k)}

    def x_peer(self):
        return {"seq": self.s, "batch": self.bat_x}

    def y_peer(self):
        return {"seq": self.s, "batch": self.bat_y}

    def twin(self):
        return {"seq": self.twin_s, "batch": self.b}

    def greet(self, all_seq=False, batch=True):
        steps = range(1, self.n_seq) if all_seq else range(2, self.n_seq, 2)
        peers = [self.seq_peer(k) for k in steps]
        if not all_seq:
            peers.append(self.twin())
        if batch:
            peers += [self.bat_peer(k) for k in range(1, self.n_bat)]
        barrier = pltpu.get_barrier_semaphore()
        for peer in peers:
            pl.semaphore_signal(
                barrier, inc=1, device_id=peer, device_id_type=pl.DeviceIdType.MESH
            )
        pl.semaphore_wait(barrier, len(peers))


class Wire:
    def __init__(self, send_sems, recv_sems):
        self.send_sems, self.recv_sems = send_sems, recv_sems
        self.copies, self.used = [], 0

    def reserve(self, count):
        first = self.used
        self.used += count
        return first

    def make(self, src, dst, peer, send_slot, recv_slot):
        return pltpu.make_async_remote_copy(
            src_ref=src,
            dst_ref=dst,
            send_sem=self.send_sems.at[send_slot],
            recv_sem=self.recv_sems.at[recv_slot],
            device_id=peer,
            device_id_type=pl.DeviceIdType.MESH,
        )

    def push(self, src, dst, peer):
        slot = self.reserve(1)
        copy = self.make(src, dst, peer, slot, slot)
        copy.start()
        self.copies.append((copy, None))
        return copy

    def push_if(self, there, copy):
        pl.when(there)(copy.start)
        self.copies.append((copy, there))

    def settle(self, copy):
        copy.wait_send()
        self.copies = [other for other in self.copies if other[0] is not copy]

    def drain(self):
        for copy, there in self.copies:
            if there is None:
                copy.wait_send()
            else:
                pl.when(there)(copy.wait_send)


class Line:
    def __init__(self, place, wire, src, at):
        self.place, self.wire, self.src, self.at = place, wire, src, at
        self.base = wire.reserve(place.half + 2)
        self.sends = 0

    def copy(self, src, origin, peer):
        return self.wire.make(
            src, self.at(origin), peer, self.base + self.sends, self.base + origin
        )

    def send(self, there, src, origin, to):
        copy = self.copy(src, origin, self.place.chip_peer(to))
        self.sends += 1
        self.wire.push_if(there, copy)

    def start(self):
        place = self.place
        self.send(place.z < place.half - 1, self.src, place.z, place.z + 1)
        self.send(place.z > 0, self.src, place.z, place.z - 1)

    def step(self, m):
        place = self.place
        origin = place.origin(m)
        self.copy(self.at(origin), origin, place.chip_peer(place.z)).wait_recv()
        from_left = lax.div(place.z - origin - 1 + place.half, place.half)
        to = place.z + 2 * from_left - 1
        self.send((to >= 0) & (to < place.half), self.at(origin), origin, to)
        return origin


class SeqGather:
    def __init__(self, place, wire, src, out):
        self.place, self.wire, self.src, self.out = place, wire, src, out
        self.late = []

    def start(self):
        place = self.place
        self.line = Line(place, self.wire, self.src, lambda i: self.out.at[place.chip(i)])
        self.line.start()
        self.late.append(self.wire.push(self.src, self.out.at[place.s], place.twin()))

    def step(self, j):
        block = self.out.at[self.place.chip(self.line.step(j))]
        self.late.append(self.wire.push(block, block, self.place.twin()))

    def finish(self):
        for copy in self.late:
            copy.wait_recv()


class FullGather:
    def __init__(self, place, wire, src, out):
        self.place, self.wire, self.src, self.out = place, wire, src, out
        self.late = []
        self.across = {}

    def spread(self, j, block):
        place = self.place
        self.across[j] = [
            self.wire.push(block, self.out.at[place.seq_at(-2 * j), place.b], place.bat_peer(k))
            for k in range(1, place.n_bat)
        ]

    def start(self):
        place, mine = self.place, self.out.at[self.place.s, self.place.b]
        self.line = [
            self.wire.push(self.src, mine, place.seq_peer(2 * j)) for j in range(1, place.half)
        ]
        self.spread(0, self.src)
        self.late.append(self.wire.push(self.src, mine, place.twin()))

    def step(self, j):
        self.line[j - 1].wait_recv()
        block = self.out.at[self.place.seq_at(-2 * j), self.place.b]
        self.spread(j, block)
        self.late.append(self.wire.push(block, block, self.place.twin()))

    def collect(self, j):
        place = self.place
        for k in range(1, place.n_bat):
            self.across[j][k - 1].wait_recv()
            block = self.out.at[place.seq_at(-2 * j), place.bat_at(-k)]
            self.late.append(self.wire.push(block, block, place.twin()))

    def finish(self):
        for copy in self.late:
            copy.wait_recv()


def keep_own(src, dst, buffer, sem):
    first = pltpu.make_async_copy(src, buffer, sem)
    first.start()
    first.wait()
    second = pltpu.make_async_copy(buffer, dst, sem)
    second.start()
    return second


def comm_call(
    kernel, outs, scratch, slots, collective_id, name, in_specs, out_specs=None, aliases=None
):
    return pl.pallas_call(
        kernel,
        out_shape=outs,
        in_specs=in_specs,
        out_specs=out_specs if out_specs is not None else jax.tree.map(lambda _: ANY, outs),
        scratch_shapes=list(scratch)
        + [pltpu.SemaphoreType.DMA((slots,)), pltpu.SemaphoreType.DMA((slots,))],
        compiler_params=pltpu.CompilerParams(
            collective_id=collective_id, has_side_effects=True, vmem_limit_bytes=VMEM_LIMIT
        ),
        name=name,
        input_output_aliases=aliases or {},
    )


def shape_of(lead, block):
    return jax.ShapeDtypeStruct(tuple(lead) + block.shape, block.dtype)


def gather_all(blocks, n_seq, n_bat, collective_id, name):
    count = len(blocks)

    def kernel(*refs):
        srcs, outs = refs[:count], refs[count : 2 * count]
        buffers = refs[2 * count : 3 * count]
        own_sems, send_sems, recv_sems = refs[3 * count :]
        place = Place(n_seq, n_bat)
        place.greet()
        wire = Wire(send_sems, recv_sems)
        gathers = [FullGather(place, wire, *pair) for pair in zip(srcs, outs)]
        for gather in gathers:
            gather.start()
        own = [
            keep_own(srcs[i], outs[i].at[place.s, place.b], buffers[i], own_sems.at[i])
            for i in range(count)
        ]
        for j in range(1, place.half):
            for gather in gathers:
                gather.step(j)
            for gather in gathers:
                gather.collect(j - 1)
        for gather in gathers:
            gather.collect(place.half - 1)
        for gather in gathers:
            gather.finish()
        for copy in own:
            copy.wait()
        wire.drain()

    return comm_call(
        kernel,
        [shape_of((n_seq, n_bat), block) for block in blocks],
        [pltpu.VMEM(block.shape, block.dtype) for block in blocks]
        + [pltpu.SemaphoreType.DMA((count,))],
        n_seq * n_bat * count,
        collective_id,
        name,
        [ANY] * count,
    )(*blocks)


def add_into(target, *others):
    rows = target.shape[0]
    step = min(rows, 16)

    def body(i, carry):
        at = pl.ds(pl.multiple_of(i * step, step), step)
        total = target[at, :].astype(F32)
        for other in others:
            total = total + other[at, :].astype(F32)
        target[at, :] = total.astype(target.dtype)
        return carry

    lax.fori_loop(0, rows // step, body, 0)


class FullScatter:
    def __init__(self, place, wire, parts, out, mine, twin, across, line, sems, local):
        self.place, self.wire, self.parts, self.out = place, wire, parts, out
        self.mine, self.twin, self.across, self.line = mine, twin, across, line
        self.sems, self.local = sems, local

    @staticmethod
    def scratch(n_seq, n_bat, block):
        half = n_seq // 2
        return [
            pltpu.VMEM((half, n_bat) + block.shape, block.dtype),
            pltpu.VMEM((half, n_bat) + block.shape, block.dtype),
            pltpu.VMEM((half, n_bat) + block.shape, block.dtype),
            pltpu.VMEM((half,) + block.shape, block.dtype),
            pltpu.SemaphoreType.DMA((half, n_bat)),
        ]

    def order(self):
        return list(range(1, self.place.half)) + [0]

    def start(self):
        place = self.place
        self.from_twin, self.loads, self.from_bat, self.from_seq = {}, {}, {}, {}
        for j in self.order():
            for k in list(range(1, place.n_bat)) + [0]:
                to_bat = place.bat_at(k)
                self.from_twin[j, k] = self.wire.push(
                    self.parts.at[place.twin_at(2 * j), to_bat], self.twin.at[j, k], place.twin()
                )
                load = pltpu.make_async_copy(
                    self.parts.at[place.seq_at(2 * j), to_bat],
                    self.mine.at[j, k],
                    self.sems.at[j, k],
                )
                load.start()
                self.loads[j, k] = load

    def pair(self, j):
        place = self.place
        for k in list(range(1, place.n_bat)) + [0]:
            self.from_twin[j, k].wait_recv()
            self.loads[j, k].wait()
            add_into(self.mine.at[j, k], self.twin.at[j, k])
        for k in range(1, place.n_bat):
            self.from_bat[j, k] = self.wire.push(
                self.mine.at[j, k], self.across.at[j, k], place.bat_peer(k)
            )

    def merge(self, j):
        place = self.place
        for k in range(1, place.n_bat):
            self.from_bat[j, k].wait_recv()
        add_into(self.mine.at[j, 0], *[self.across.at[j, k] for k in range(1, place.n_bat)])
        if j:
            self.from_seq[j] = self.wire.push(
                self.mine.at[j, 0], self.line.at[j], place.seq_peer(2 * j)
            )

    def finish(self):
        for j in range(1, self.place.half):
            self.from_seq[j].wait_recv()
        add_into(self.mine.at[0, 0], *[self.line.at[j] for j in range(1, self.place.half)])
        self.out[...] = self.mine[0, 0]


def scatter_all(parts, n_seq, n_bat, collective_id, name):
    blocks = [jax.ShapeDtypeStruct(part.shape[2:], part.dtype) for part in parts]
    count = len(parts)

    def kernel(*refs):
        ins, outs = refs[:count], refs[count : 2 * count]
        rest = refs[2 * count :]
        send_sems, recv_sems = rest[-2:]
        place = Place(n_seq, n_bat)
        place.greet()
        wire = Wire(send_sems, recv_sems)
        works = [
            FullScatter(place, wire, ins[i], outs[i], *rest[5 * i : 5 * i + 5], None)
            for i in range(count)
        ]
        for work in works:
            work.start()
        order = works[0].order()
        for at, j in enumerate(order):
            for work in works:
                work.pair(j)
            if at:
                for work in works:
                    work.merge(order[at - 1])
        for work in works:
            work.merge(order[-1])
        for work in works:
            work.finish()
        wire.drain()

    scratch = []
    for block in blocks:
        scratch += FullScatter.scratch(n_seq, n_bat, block)
    slots = count * (n_seq * n_bat)
    vmem = pl.BlockSpec(memory_space=pltpu.VMEM)
    return comm_call(
        kernel,
        blocks,
        scratch,
        slots,
        collective_id,
        name,
        [ANY] * count,
        [vmem] * count,
    )(*parts)


def pack(values):
    flat = values.astype(F32).reshape(-1)
    tiles = -(-flat.shape[0] // 1024)
    return jnp.pad(flat, (0, tiles * 1024 - flat.shape[0])).reshape(tiles * 8, 128)


def unpack(tiles, lead, shape):
    size = 1
    for extent in shape:
        size *= extent
    return tiles.reshape(tuple(lead) + (-1,))[..., :size].reshape(tuple(lead) + tuple(shape))


def scatter_blocks(grad_normed, grad_gates, mixture, n_seq, n_bat):
    dim = grad_normed.shape[-1]
    pieces = 1
    while n_seq * n_bat * grad_normed.shape[2] * (dim // pieces) * 4 > 36 * 1024 * 1024:
        pieces *= 2
    size = dim // pieces
    grads, mixtures = [], []
    for i in range(pieces):
        at = slice(i * size, (i + 1) * size)
        parts = [grad_normed[..., at]] + ([grad_gates] if i == 0 else [])
        done = scatter_all(parts, n_seq, n_bat, 16 + 2 * i, "scatter_normed")
        grads.append(done[0])
        if i == 0:
            gates = done[1]
        done = scatter_all([mixture[..., at]], n_seq, n_bat, 17 + 2 * i, "scatter_mixture")
        mixtures.append(done[0])
    return jnp.concatenate(grads, axis=-1), gates, jnp.concatenate(mixtures, axis=-1)


class SeqScatter:
    def __init__(self, place, wire, full, twin, line):
        self.place, self.wire = place, wire
        self.full, self.twin, self.line = full, twin, line
        self.order = list(range(1, place.half)) + [0]

    @staticmethod
    def scratch(rows, n_seq, block):
        lead = ((rows, n_seq), (rows, n_seq // 2), (rows, n_seq // 2))
        return [pltpu.VMEM(extent + block.shape, block.dtype) for extent in lead]

    def start(self):
        place = self.place
        self.from_twin = {
            j: self.wire.push(self.full.at[place.twin_at(2 * j)], self.twin.at[j], place.twin())
            for j in self.order
        }

    def pass_on(self):
        place = self.place
        self.from_seq = {}
        for j in self.order:
            self.from_twin[j].wait_recv()
            block = self.full.at[place.seq_at(2 * j)]
            add_into(block, self.twin.at[j])
            if j:
                self.from_seq[j] = self.wire.push(block, self.line.at[j], place.seq_peer(2 * j))

    def finish(self, out, at):
        for copy in self.from_seq.values():
            copy.wait_recv()
        own = self.full.at[self.place.s]
        add_into(own, *[self.line.at[j] for j in range(1, self.place.half)])
        out[at, :] = own[...]


def turn(v, cos_wide, sin_wide):
    return v * cos_wide + pltpu.roll(v, HEAD // 2, axis=1) * sin_wide


class Exchange:
    def __init__(self, place, wire, local, got):
        self.local, self.got, self.count = local, got, place.n_seq - 1
        self.copies = [
            wire.push(local, got.at[k - 1], place.seq_peer(k)) for k in range(1, place.n_seq)
        ]

    def total(self):
        for copy in self.copies:
            copy.wait_recv()
        total = self.local[...]
        for k in range(self.count):
            total = total + self.got[k]
        return total


def lane_sums(v):
    ones = jnp.ones((8, v.shape[1]), F32)
    sums = lax.dot_general(
        ones, v, (((1,), (1,)), ((), ())), precision=HIGHEST, preferred_element_type=F32
    )
    return sums[0:1]


def allowed_block(use, first, count, keys):
    at_query = first + lax.broadcasted_iota(jnp.int32, (count, keys), 0)
    at_key = lax.broadcasted_iota(jnp.int32, (count, keys), 1)
    return (at_key == at_query) | ((at_key < at_query) & (use > 0))


STEP = 128


def attend_forward(
    x_col, w_qkv, gain_attn, usable, w_o, gain_q, gain_k, cos_wide, sin_wide, n_seq, n_bat, rows,
    side=None,
):
    col, dim = x_col.shape
    three = w_qkv.shape[1]
    wide = three // 3
    heads = wide // HEAD
    length = col // rows
    span = length // n_seq
    own = rows * span
    steps = length // STEP
    chunk = min(256, length)
    scale = HEAD ** (-0.5)
    block = jax.ShapeDtypeStruct((span, dim), BF)

    def kernel(*refs):
        (x_ref, w_ref, ga_ref, use_ref, wo_ref, gq_ref, gk_ref, cos_ref, sin_ref) = refs[:9]
        refs = refs[9:]
        if side:
            _, gate_ref, up_ref = refs[:3]
            refs = refs[3:]
        hid_ref, qkv_ref, q_ref, k_ref, v_ref, mix_ref, stat_ref, out_ref = refs[:8]
        refs = refs[8:]
        if side:
            dy_all, gu_all = refs[:2]
            gu_own, gu_sems = refs[-4:-2]
            refs = refs[2:-4] + refs[-2:]
        local, got, full, twin, line, send_sems, recv_sems = refs
        place = Place(n_seq, n_bat)
        place.greet(all_seq=True, batch=bool(side))
        wire = Wire(send_sems, recv_sems)
        dy_works, gu_copies, gu_here = [], [], []
        if side:
            for j in range(place.half):
                at_seq = place.seq_at(-2 * j)
                dy_works.append(
                    Across(
                        place,
                        wire,
                        dy_all.at[at_seq, place.b],
                        lambda i, at_seq=at_seq: dy_all.at[at_seq, i],
                    )
                )
                dy_works[-1].start()

        def send_experts(steps_of):
            if not side:
                return
            count, _, hidden = gate_ref.shape
            part = hidden // n_seq
            for k in steps_of:
                lanes = pl.ds(pl.multiple_of(place.seq_at(k) * part, part), part)
                for m, ref in enumerate((gate_ref, up_ref)):
                    for e in range(count):
                        to = pl.ds((m * count + e) * part, part)
                        if k:
                            gu_copies.append(
                                wire.push(
                                    ref.at[e, :, lanes],
                                    gu_all.at[place.s, :, to],
                                    place.seq_peer(k),
                                )
                            )
                        else:
                            copy = pltpu.make_async_copy(
                                ref.at[e, :, lanes], gu_own.at[:, to], gu_sems.at[m * count + e]
                            )
                            copy.start()
                            gu_here.append(copy)

        send_experts([0, 2, 3])
        for first in range(0, col, chunk):
            at = slice(first, first + chunk)
            x = x_ref[at, :].astype(F32)
            hidden = (x * rms_scale(x) * ga_ref[...]).astype(BF)
            hid_ref[at, :] = hidden
            qkv_ref[at, :] = dot(hidden, w_ref[...])
        for r in range(rows):
            for c in range(steps):
                at = slice(r * length + c * STEP, r * length + (c + 1) * STEP)
                for which in range(2):
                    v = qkv_ref[at, which * wide : (which + 1) * wide]
                    row = (r * 2 + which) * steps + c
                    local[row : row + 1, :] = lane_sums(v * v)
        for r in range(rows):
            for h in range(heads):
                lanes = slice(2 * wide + h * HEAD, 2 * wide + (h + 1) * HEAD)
                v_ref[r, h] = qkv_ref[r * length : (r + 1) * length, lanes].astype(BF)
        exchange = Exchange(place, wire, local, got)
        send_experts([k for k in range(1, n_seq) if k not in (2, 3)])
        total = exchange.total()
        stat_ref[...] = total
        columns = lax.rsqrt(total / dim + EPS).T
        scatters = [
            SeqScatter(place, wire, full.at[r], twin.at[r], line.at[r]) for r in range(rows)
        ]
        for r in range(rows):
            for c in range(steps):
                inside = slice(c * STEP, (c + 1) * STEP)
                at = slice(r * length + c * STEP, r * length + (c + 1) * STEP)
                for which, gain_ref, target in ((0, gq_ref, q_ref), (1, gk_ref, k_ref)):
                    row = (r * 2 + which) * steps + c
                    factor = columns[:, row : row + 1]
                    for h in range(heads):
                        lanes = slice(which * wide + h * HEAD, which * wide + (h + 1) * HEAD)
                        gain = gain_ref[0:1, h * HEAD : (h + 1) * HEAD]
                        v = qkv_ref[at, lanes] * factor * gain
                        target[r, h, inside, :] = turn(
                            v, cos_ref[inside, :], sin_ref[inside, :]
                        ).astype(BF)
            for c in range(length // chunk):
                keys = (c + 1) * chunk
                allowed = allowed_block(use_ref[r : r + 1, :keys], c * chunk, chunk, keys)
                for h in range(heads):
                    query = q_ref[r, h, c * chunk : keys, :]
                    scores = dot_t(query, k_ref[r, h, :keys, :]) * scale
                    scores = jnp.where(allowed, scores, NEGATIVE)
                    raised = jnp.exp(scores - jnp.max(scores, axis=-1, keepdims=True))
                    probs = raised / jnp.sum(raised, axis=-1, keepdims=True)
                    mixed = dot(probs.astype(BF), v_ref[r, h, :keys, :]).astype(BF)
                    mix_ref[r, c * chunk : keys, h * HEAD : (h + 1) * HEAD] = mixed
                if r and c == 0:
                    scatters[r - 1].pass_on()
            full[r] = dot(mix_ref[r], wo_ref[...]).astype(BF).reshape(n_seq, span, dim)
            if side and r == 0:
                for work in dy_works:
                    work.relay()
            scatters[r].start()
        if side:
            for copy in gu_here:
                copy.wait()
            gu_store = pltpu.make_async_copy(gu_own, gu_all.at[place.s], gu_sems.at[0])
            gu_store.start()
        scatters[-1].pass_on()
        passed = []
        for j, work in enumerate(dy_works):
            work.finish()
            group = dy_all.at[place.seq_at(-2 * j)]
            passed.append(wire.push(group, group, place.twin()))
        for r in range(rows):
            scatters[r].finish(out_ref, slice(r * span, (r + 1) * span))
        if side:
            for copy in passed + gu_copies:
                copy.wait_recv()
            gu_store.wait()
        wire.drain()

    vmem = pl.BlockSpec(memory_space=pltpu.VMEM)
    side_in, side_out, side_scratch, aliases = [], [], [], {}
    slots = (1 + rows) * n_seq
    if side:
        dy_part, gate, up = side
        count, depth, hidden = gate.shape
        lanes = 2 * count * (hidden // n_seq)
        side_in = [ANY] * 3
        side_out = [
            jax.ShapeDtypeStruct(dy_part.shape, dy_part.dtype),
            jax.ShapeDtypeStruct((n_seq, depth, lanes), gate.dtype),
        ]
        side_scratch = [
            pltpu.VMEM((depth, lanes), gate.dtype),
            pltpu.SemaphoreType.DMA((2 * count,)),
        ]
        aliases = {9: 8}
        slots += 3 * n_seq + 2 * count * n_seq
    head_block = jax.ShapeDtypeStruct((rows, heads, length, HEAD), BF)
    stats = jax.ShapeDtypeStruct((2 * rows * steps, STEP), F32)
    outs = [
        jax.ShapeDtypeStruct((col, dim), BF),
        jax.ShapeDtypeStruct((col, three), F32),
        head_block,
        head_block,
        head_block,
        jax.ShapeDtypeStruct((rows, length, wide), BF),
        stats,
        jax.ShapeDtypeStruct((own, dim), BF),
    ]
    return comm_call(
        kernel,
        outs + side_out,
        [pltpu.VMEM(stats.shape, F32), pltpu.VMEM((n_seq - 1,) + stats.shape, F32)]
        + SeqScatter.scratch(rows, n_seq, block)
        + side_scratch,
        slots,
        2,
        "attend_forward",
        [vmem] * 9 + side_in,
        [vmem] * 8 + [ANY] * len(side_out),
        aliases,
    )(x_col, w_qkv, gain_attn, usable, w_o, gain_q, gain_k, cos_wide, sin_wide, *(side or ()))


def attend_backward(
    grad_o, q, k, v, mixed, qkv, stats, hidden, usable, w_o, w_qkv, gain_q, gain_k,
    cos_wide, sin_wide, n_seq, n_bat, side=None,
):
    rows, heads, length, _ = q.shape
    own, dim = grad_o.shape
    span = own // rows
    col, three = qkv.shape
    wide = three // 3
    steps = length // STEP
    chunk = min(256, length)
    scale = HEAD ** (-0.5)
    group = n_bat * own

    def kernel(*refs):
        (go_ref, q_ref, k_ref, v_ref, mix_ref, qkv_ref, stat_ref, hid_ref, use_ref, wo_ref,
         w_ref, gq_ref, gk_ref, cos_ref, sin_ref) = refs[:15]
        refs = refs[15:]
        if side:
            weighted_ref, down_ref = refs[:2]
            refs = refs[2:]
        gwo_ref, gw_ref, gain_ref, out_ref = refs[:4]
        refs = refs[4:]
        if side:
            mixture_ref = refs[0]
            mix_away, mix_twin, mix_halves, mix_full = refs[-6:-2]
            refs = refs[1:-6] + refs[-2:]
        go_all, gm, dq, dk, dv, dqkv, local, got, hid_buf, hid_sems = refs[:10]
        full, twin, line, send_sems, recv_sems = refs[10:]
        place = Place(n_seq, n_bat)
        place.greet(all_seq=True, batch=bool(side))
        wire = Wire(send_sems, recv_sems)
        gathers = [
            SeqGather(place, wire, go_ref.at[pl.ds(r * span, span)], go_all.at[r])
            for r in range(rows)
        ]
        for gather in gathers:
            gather.start()
        for r in range(rows):
            go_all[r, place.s] = go_ref[r * span : (r + 1) * span, :]
        order = list(range(1, place.half)) + [0]
        works, from_twin = {}, {}

        def mixture_of(i):
            at = pl.ds(pl.multiple_of(i * group, group), group)
            return dot(weighted_ref[at, :], down_ref[...])

        todo = [(gather, m) for gather in gathers for m in range(1, place.half)]

        def forward(count):
            for _ in range(min(count, len(todo))):
                gather, m = todo.pop(0)
                gather.step(m)

        if side:
            waiting = None
            for n, j in enumerate(order):
                if n >= 2:
                    wire.settle(from_twin[order[n - 2]])
                mix_away[n % 2] = (
                    mixture_of(place.twin_at(2 * j)).astype(BF).reshape(n_bat, own, dim)
                )
                total = mixture_of(place.seq_at(2 * j))
                from_twin[j] = wire.push(mix_away.at[n % 2], mix_twin.at[j], place.twin())
                from_twin[j].wait_recv()
                mix_twin[j] = (
                    (total + mix_twin[j].reshape(group, dim).astype(F32))
                    .astype(BF)
                    .reshape(n_bat, own, dim)
                )
                works[j] = AcrossSum(
                    place, wire, mix_twin.at[j], mix_halves.at[j], mix_full.at[j]
                )
                if waiting is not None:
                    works[waiting].start()
                waiting = j
                forward(1)
            works[waiting].start()
        forward(max(0, len(todo) - (rows - 1) * (place.half - 1)))
        columns = lax.rsqrt(stat_ref[...] / dim + EPS).T
        scatters = [
            SeqScatter(place, wire, full.at[r], twin.at[r], line.at[r]) for r in range(rows)
        ]
        gain_sums = [[jnp.zeros((1, HEAD), F32) for _ in range(heads)] for _ in range(2)]
        middles = [works[j] for j in works]

        def attend(r, c, h):
            keys = (c + 1) * chunk
            now = slice(c * chunk, keys)
            allowed = allowed_block(use_ref[r : r + 1, :keys], c * chunk, chunk, keys)
            lanes = slice(h * HEAD, (h + 1) * HEAD)
            query = q_ref[r, h, now, :]
            key = k_ref[r, h, :keys, :]
            scores = jnp.where(allowed, dot_t(query, key) * scale, NEGATIVE)
            raised = jnp.exp(scores - jnp.max(scores, axis=-1, keepdims=True))
            probs = raised / jnp.sum(raised, axis=-1, keepdims=True)
            low = probs.astype(BF)
            grad_mix = gm[now, lanes]
            grad_probs = dot_t(grad_mix, v_ref[r, h, :keys, :])
            row_dot = jnp.sum(low.astype(F32) * grad_probs, axis=-1, keepdims=True)
            grad_scores = (probs * (grad_probs - row_dot)).astype(BF)
            dq[now, lanes] = scale * dot(grad_scores, key)
            dk[:keys, lanes] += scale * t_dot(grad_scores, query)
            dv[:keys, lanes] += t_dot(low, grad_mix)

        for r in range(rows):
            gathers[r].finish()
            gm[...] = dot_t(go_all[r].reshape(length, dim), wo_ref[...]).astype(BF)
            if r:
                scatters[r - 1].pass_on()
            dk[...] = jnp.zeros_like(dk)
            dv[...] = jnp.zeros_like(dv)
            for h in range(heads):
                for c in range(length // chunk):
                    attend(r, c, h)
                    forward(1)
                    if middles:
                        middles.pop(0).middle()
            if r == 0:
                forward(len(todo))
                while middles:
                    middles.pop(0).middle()
            for which, g_ref, grads in ((0, gq_ref, dq), (1, gk_ref, dk)):
                for c in range(steps):
                    inside = slice(c * STEP, (c + 1) * STEP)
                    at = slice(r * length + c * STEP, r * length + (c + 1) * STEP)
                    row = (r * 2 + which) * steps + c
                    factor = columns[:, row : row + 1]
                    products = None
                    for h in range(heads):
                        lanes = slice(h * HEAD, (h + 1) * HEAD)
                        flat = qkv_ref[at, which * wide + h * HEAD : which * wide + (h + 1) * HEAD]
                        flat = flat * factor
                        back = turn(grads[inside, lanes], cos_ref[inside, :], -sin_ref[inside, :])
                        gain_sums[which][h] = gain_sums[which][h] + jnp.sum(
                            back * flat, axis=0, keepdims=True
                        )
                        weighted = back * g_ref[0:1, lanes]
                        grads[inside, lanes] = weighted
                        product = weighted * flat
                        products = product if products is None else products + product
                    row = which * steps + c
                    local[r, row : row + 1, :] = lane_sums(products)
            exchange = Exchange(place, wire, local.at[r], got.at[r])
            dqkv[r, :, 2 * wide :] = dv[...].astype(BF)
            means = (exchange.total() / dim).T
            for which, grads in ((0, dq), (1, dk)):
                lanes = slice(which * wide, (which + 1) * wide)
                for c in range(steps):
                    inside = slice(c * STEP, (c + 1) * STEP)
                    at = slice(r * length + c * STEP, r * length + (c + 1) * STEP)
                    row = (r * 2 + which) * steps + c
                    factor = columns[:, row : row + 1]
                    mean = means[:, which * steps + c : which * steps + c + 1]
                    flat = qkv_ref[at, lanes] * factor
                    dqkv[r, inside, lanes] = (factor * (grads[inside, :] - flat * mean)).astype(BF)
            full[r] = dot_t(dqkv[r], w_ref[...]).astype(BF).reshape(n_seq, span, dim)
            scatters[r].start()
        for which in range(2):
            for h in range(heads):
                gain_ref[which : which + 1, h * HEAD : (h + 1) * HEAD] = gain_sums[which][h]

        def hidden_load(part):
            return pltpu.make_async_copy(
                hid_ref.at[:, pl.ds(part * 256, 256)], hid_buf.at[part % 2], hid_sems.at[part % 2]
            )

        hidden_load(0).start()
        scatters[-1].pass_on()
        for part in range(dim // 256):
            at = slice(part * 256, (part + 1) * 256)
            if part + 1 < dim // 256:
                hidden_load(part + 1).start()
            hidden_load(part).wait()
            gw_ref[at, :] = t_dot(hid_buf[part % 2], dqkv[...].reshape(col, three)).astype(BF)
            total = t_dot(mix_ref[0], go_all[0, :, :, at].reshape(length, 256))
            for r in range(1, rows):
                total = total + t_dot(mix_ref[r], go_all[r, :, :, at].reshape(length, 256))
            gwo_ref[:, at] = total.astype(BF)
        for j in works:
            works[j].finish()
            mixture_ref[j] = mix_twin[j, place.b]
        for r in range(rows):
            scatters[r].finish(out_ref, slice(r * span, (r + 1) * span))
        wire.drain()

    vmem = pl.BlockSpec(memory_space=pltpu.VMEM)
    block = jax.ShapeDtypeStruct((span, dim), BF)
    stat_shape = (2 * steps, STEP)
    side_out, side_scratch = [], []
    if side:
        half = n_seq // 2
        side_out = [jax.ShapeDtypeStruct((half, own, dim), BF)]
        side_scratch = [
            pltpu.VMEM((2, n_bat, own, dim), BF),
            pltpu.VMEM((half, n_bat, own, dim), BF),
            pltpu.VMEM((half, 2, own // 2, dim), BF),
            pltpu.VMEM((half, 2, own, dim), BF),
        ]
    return comm_call(
        kernel,
        [
            jax.ShapeDtypeStruct((wide, dim), BF),
            jax.ShapeDtypeStruct((dim, three), BF),
            jax.ShapeDtypeStruct((2, wide), F32),
            jax.ShapeDtypeStruct((own, dim), BF),
        ]
        + side_out,
        [
            pltpu.VMEM((rows, n_seq, span, dim), BF),
            pltpu.VMEM((length, wide), BF),
            pltpu.VMEM((length, wide), F32),
            pltpu.VMEM((length, wide), F32),
            pltpu.VMEM((length, wide), F32),
            pltpu.VMEM((rows, length, three), BF),
            pltpu.VMEM((rows,) + stat_shape, F32),
            pltpu.VMEM((rows, n_seq - 1) + stat_shape, F32),
            pltpu.VMEM((2, col, 256), BF),
            pltpu.SemaphoreType.DMA((2,)),
        ]
        + SeqScatter.scratch(rows, n_seq, block)
        + side_scratch,
        5 * rows * n_seq + (3 * n_seq if side else 0),
        6,
        "attend_backward",
        [vmem] * 7 + [ANY] + [vmem] * (7 + len(side or ())),
        [vmem] * (4 + len(side_out)),
    )(grad_o, q, k, v, mixed, qkv, stats, hidden, usable, w_o, w_qkv, gain_q, gain_k,
      cos_wide, sin_wide, *(side or ()))


class Across:
    def __init__(self, place, wire, src, at):
        self.place, self.wire, self.src, self.at = place, wire, src, at
        self.half = src.shape[0] // 2

    def start(self):
        place, own = self.place, self.at(self.place.b)
        self.to_x = self.wire.push(self.src, own, place.x_peer())
        self.to_y = self.wire.push(self.src, own, place.y_peer())

    def relay(self):
        place, half = self.place, self.half
        self.to_x.wait_recv()
        top = self.at(place.bat_x).at[pl.ds(0, half)]
        self.top = self.wire.push(top, top, place.y_peer())
        self.to_y.wait_recv()
        low = self.at(place.bat_y).at[pl.ds(half, half)]
        self.low = self.wire.push(low, low, place.x_peer())

    def finish(self):
        self.top.wait_recv()
        self.low.wait_recv()


class AcrossSum:
    def __init__(self, place, wire, group, halves, full):
        self.place, self.wire = place, wire
        self.group, self.halves, self.full = group, halves, full
        self.half = halves.shape[1]

    def start(self):
        place, half = self.place, self.half
        far = self.group.at[place.bat_d]
        self.top = self.wire.push(far.at[pl.ds(0, half)], self.halves.at[0], place.x_peer())
        self.low = self.wire.push(far.at[pl.ds(half, half)], self.halves.at[1], place.y_peer())

    def middle(self):
        place, half = self.place, self.half
        self.top.wait_recv()
        add_into(self.group.at[place.bat_y].at[pl.ds(0, half)], self.halves.at[0])
        self.low.wait_recv()
        add_into(self.group.at[place.bat_x].at[pl.ds(half, half)], self.halves.at[1])
        self.y = self.wire.push(self.group.at[place.bat_y], self.full.at[0], place.y_peer())
        self.x = self.wire.push(self.group.at[place.bat_x], self.full.at[1], place.x_peer())

    def finish(self):
        self.y.wait_recv()
        self.x.wait_recv()
        add_into(self.group.at[self.place.b], self.full.at[0], self.full.at[1])


def load_first(weights, w_out, mine, flags, small, dy_own, rows, n_seq, n_bat):
    shard, dim = weights[0].shape
    wide = dim // n_seq
    own = mine.shape[0]
    span = own // rows
    slots = 15 * n_seq + n_seq * n_bat

    def kernel(*refs):
        parts = refs[:3]
        wo_ref, x_ref, flag_ref, small_ref, dy_ref = refs[3:8]
        w_ref, wo_all, x_col, flag_col, small_all, dy_all = refs[8:14]
        buffers = refs[14:20]
        own_sems, cut_sems, x_sems, send_sems, recv_sems = refs[20:]
        place = Place(n_seq, n_bat)
        place.greet(all_seq=True)
        wire = Wire(send_sems, recv_sems)
        small_work = FullGather(place, wire, small_ref, small_all)
        flag_work = SeqGather(place, wire, flag_ref, flag_col)
        x_works = [
            SeqGather(place, wire, x_ref.at[pl.ds(r * span, span)], x_col.at[r])
            for r in range(rows)
        ]
        small_work.start()
        flag_work.start()

        def cut(k):
            return pl.ds(pl.multiple_of(place.seq_at(k) * wide, wide), wide)

        def columns(m):
            return pl.ds(m * wide, wide)

        own_cuts = []
        for m in range(3):
            copy = pltpu.make_async_copy(
                parts[m].at[:, cut(0)], buffers[0].at[:, columns(m)], cut_sems.at[m]
            )
            copy.start()
            own_cuts.append(copy)
        cuts = {}
        for k in range(1, n_seq):
            for m in range(3):
                cuts[k, m] = wire.push(
                    parts[m].at[:, cut(k)],
                    w_ref.at[place.s, place.b, :, columns(m)],
                    place.seq_peer(k),
                )
        wo_work = Across(place, wire, wo_ref, lambda i: wo_all.at[i])
        wo_work.start()
        for work in x_works:
            work.start()
        dy_line = Line(place, wire, dy_ref, lambda i: dy_all.at[place.chip(i), place.b])
        dy_line.start()
        for copy in own_cuts:
            copy.wait()
        spreads = []

        def spread(src, from_seq):
            work = Across(place, wire, src, lambda i: w_ref.at[from_seq, i])
            work.start()
            spreads.append(work)

        spread(buffers[0], place.s)
        own_w = pltpu.make_async_copy(buffers[0], w_ref.at[place.s, place.b], own_sems.at[0])
        own_w.start()
        copies = [own_w]
        fetched = pltpu.make_async_copy(x_ref, buffers[5], own_sems.at[5])
        fetched.start()
        fetched.wait()
        for r in range(rows):
            copy = pltpu.make_async_copy(
                buffers[5].at[pl.ds(r * span, span)], x_col.at[r, place.s], x_sems.at[r]
            )
            copy.start()
            copies.append(copy)
        copies += [
            keep_own(src, dst, buffers[i + 1], own_sems.at[i + 1])
            for i, (src, dst) in enumerate(
                (
                    (wo_ref, wo_all.at[place.b]),
                    (flag_ref, flag_col.at[place.s]),
                    (small_ref, small_all.at[place.s, place.b]),
                    (dy_ref, dy_all.at[place.s, place.b]),
                )
            )
        ]
        for j in range(1, place.half):
            small_work.step(j)
            flag_work.step(j)
        for k in range(1, n_seq):
            for m in range(3):
                cuts[k, m].wait_recv()
            spread(w_ref.at[place.seq_at(-k), place.b], place.seq_at(-k))
        for j in range(place.half):
            small_work.collect(j)
        todo = [(work, m) for work in x_works for m in range(1, place.half)]

        def forward(count):
            for _ in range(min(count, len(todo))):
                work, m = todo.pop(0)
                work.step(m)

        forward(1)
        wo_work.relay()
        for work in spreads:
            work.relay()
            forward(1)
        forward(len(todo))
        for j in range(1, place.half):
            dy_line.step(j)
        wo_work.finish()
        for work in spreads:
            work.finish()
        for work in [small_work, flag_work] + x_works:
            work.finish()
        for copy in copies:
            copy.wait()
        wire.drain()

    every = (n_seq, n_bat)
    one = jax.ShapeDtypeStruct((shard, 3 * wide), BF)
    x_one = jax.ShapeDtypeStruct((span, dim), BF)
    blocks = (one, w_out, x_one, flags, small, dy_own)
    leads = (every, (n_bat,), (rows, n_seq), (n_seq,), every, every)
    held = (one, w_out, flags, small, dy_own, mine)
    return comm_call(
        kernel,
        [shape_of(lead, block) for lead, block in zip(leads, blocks)],
        [pltpu.VMEM(block.shape, block.dtype) for block in held]
        + [pltpu.SemaphoreType.DMA((n,)) for n in (6, 3, rows)],
        slots,
        1,
        "load_first",
        [ANY] * 8,
    )(*weights, w_out, mine, flags, small, dy_own)


def pick_units(first, experts, units, part):
    at_expert = lax.broadcasted_iota(jnp.int32, (experts, units), 0)
    at_unit = lax.broadcasted_iota(jnp.int32, (experts, units), 1)
    low = (at_expert - first) * part
    return jnp.where((at_unit >= low) & (at_unit < low + part), 1.0, 0.0).astype(F32)


def experts_forward(normed, gates, dy_all, w_gu, w_down, local_experts, n_seq, n_bat):
    own, dim = normed.shape
    units = w_down.shape[0]
    part = units // local_experts
    group = n_bat * own
    tokens = n_seq * group
    experts = gates.shape[0]
    slots = 64 + 2 * n_seq * n_bat

    def kernel(*refs):
        x_ref, gate_ref, dy_ref, gu_ref, down_ref = refs[:5]
        x_all, weighted_ref, grad_ref, term_ref = refs[5:9]
        gates_all, back, x_buf, dy_buf, keep, own_sems, x_sems, dy_sems = refs[9:17]
        send_sems, recv_sems = refs[17:]
        place = Place(n_seq, n_bat)
        place.greet()
        wire = Wire(send_sems, recv_sems)
        gate_work = FullGather(place, wire, gate_ref, gates_all)
        gate_work.start()
        gates_all[place.s, place.b] = gate_ref[...]
        line = Line(place, wire, x_ref, lambda i: x_all.at[place.chip(i), place.b])
        line.start()
        works = []
        here = [place.chip(place.origin(m)) for m in range(place.half)]
        there = [place.chip_twin(place.origin(m)) for m in range(place.half)]
        for j in range(place.half):
            at_seq = here[j]
            src = x_ref if j == 0 else x_all.at[at_seq, place.b]
            works.append(
                Across(place, wire, src, lambda i, at_seq=at_seq: x_all.at[at_seq, i])
            )
        works[0].start()
        own = keep_own(x_ref, x_all.at[place.s, place.b], keep, own_sems.at[0])
        selected = pick_units(place.b * local_experts, experts, units, part)

        def dy_load(g, slot):
            return pltpu.make_async_copy(dy_ref.at[g], dy_buf.at[slot], dy_sems.at[slot])

        def rows_of(g):
            return pl.ds(pl.multiple_of(g * group, group), group)

        def backs(first, count):
            dy_load(first, first % 2).start()
            for g in range(first, first + count):
                if g + 1 < first + count:
                    dy_load(g + 1, (g + 1) % 2).start()
                dy_load(g, g % 2).wait()
                block = dy_buf[g % 2].reshape(group, dim)
                back[g * group : (g + 1) * group, :] = dot_t(block, down_ref[...])

        passed = []

        def hand_over(j):
            at_seq = here[j]
            works[j].finish()
            if j == 0:
                own.wait()
            passed.append(wire.push(x_all.at[at_seq], x_all.at[at_seq], place.twin()))

        loads = {}

        def fetch(g, slot):
            loads[slot] = pltpu.make_async_copy(x_all.at[g], x_buf.at[slot], x_sems.at[slot])
            loads[slot].start()

        def units_on(g, slot):
            loads[slot].wait()
            at = rows_of(g)
            pre = dot(x_buf[slot].reshape(group, dim), gu_ref[...])
            gate_pre, up_pre = pre[:, :units], pre[:, units:]
            sig = jax.nn.sigmoid(gate_pre)
            silu = gate_pre * sig
            active = (silu * up_pre).astype(BF).astype(F32)
            grad_back = back[at, :]
            product = active * grad_back
            wide_gates = []
            for i in range(n_bat):
                inside = slice(i * x_ref.shape[0], (i + 1) * x_ref.shape[0])
                wide_gates.append(
                    lax.dot_general(
                        gates_all[g, i],
                        selected,
                        (((0,), (0,)), ((), ())),
                        precision=HIGHEST,
                        preferred_element_type=F32,
                    )
                )
                term_ref[g, i] = lax.dot_general(
                    selected,
                    product[inside, :],
                    (((1,), (1,)), ((), ())),
                    precision=HIGHEST,
                    preferred_element_type=F32,
                )
            wide_gate = jnp.concatenate(wide_gates, axis=0)
            weighted_ref[at, :] = (active * wide_gate).astype(BF)
            grad_active = grad_back * wide_gate
            grad_ref[at, :units] = (
                grad_active * up_pre * sig * (1.0 + gate_pre * (1.0 - sig))
            ).astype(BF)
            grad_ref[at, units:] = (grad_active * silu).astype(BF)

        half = place.half
        per = n_seq // half
        for j in range(1, half):
            backs((j - 1) * per, per)
            gate_work.step(j)
            gate_work.collect(j - 1)
            line.step(j)
            works[j].start()
            works[j - 1].relay()
        backs((half - 1) * per, per)
        gate_work.collect(half - 1)
        gate_work.finish()
        hand_over(0)
        fetch(here[0], 0)
        for j in range(half):
            units_on(here[j], (2 * j) % 4)
            passed[j].wait_recv()
            fetch(there[j], (2 * j + 1) % 4)
            if j + 1 < half:
                hand_over(j + 1)
                fetch(here[j + 1], (2 * j + 2) % 4)
            units_on(there[j], (2 * j + 1) % 4)
            if j == max(0, half - 4):
                works[half - 1].relay()
        wire.drain()

    vmem = pl.BlockSpec(memory_space=pltpu.VMEM)
    return comm_call(
        kernel,
        [
            shape_of((n_seq, n_bat), normed),
            jax.ShapeDtypeStruct((tokens, units), BF),
            jax.ShapeDtypeStruct((tokens, 2 * units), BF),
            shape_of((n_seq, n_bat), gates),
        ],
        [
            pltpu.VMEM((n_seq, n_bat) + gates.shape, F32),
            pltpu.VMEM((tokens, units), F32),
            pltpu.VMEM((4, n_bat, own, dim), BF),
            pltpu.VMEM((2, n_bat, own, dim), BF),
            pltpu.VMEM((own, dim), BF),
            pltpu.SemaphoreType.DMA((1,)),
            pltpu.SemaphoreType.DMA((4,)),
            pltpu.SemaphoreType.DMA((2,)),
        ],
        slots,
        4,
        "experts_forward",
        [ANY, vmem, ANY, vmem, vmem],
        [ANY, vmem, vmem, vmem],
    )(normed, gates, dy_all, w_gu, w_down)


def experts_backward(
    grad_pre, weighted, w_gu, terms, x_all, dy_all, local_experts, n_seq, n_bat, own
):
    tokens, dim = x_all.shape
    units = weighted.shape[1]
    part = units // local_experts
    group = n_bat * own
    depth = dim // n_seq
    hidden = n_seq * part
    half = n_seq // 2
    slots = 128 + 2 * n_seq * n_bat
    block = jax.ShapeDtypeStruct((own, dim), BF)
    term = jax.ShapeDtypeStruct(terms.shape[2:], F32)

    def kernel(*refs):
        grad_ref, weighted_ref, gu_ref, term_in, x_ref, dy_ref = refs[:6]
        out_ref, term_out, gate_out, up_out, down_out = refs[6:11]
        away, twin, halves, full, line = refs[11:16]
        columns, sent, got, column_sems = refs[16:20]
        term_scratch = refs[20:25]
        send_sems, recv_sems = refs[25:]
        place = Place(n_seq, n_bat)
        place.greet(all_seq=True)
        wire = Wire(send_sems, recv_sems)
        term_work = FullScatter(place, wire, term_in, term_out, *term_scratch, None)
        term_work.start()

        def product(i):
            at = pl.ds(pl.multiple_of(i * group, group), group)
            return dot_t(grad_ref[at, :], gu_ref[...])

        order = list(range(1, half)) + [0]
        from_twin, from_seq, works = {}, {}, {}

        def send(j):
            from_twin[j] = wire.push(away.at[j], twin.at[j], place.twin())

        waiting = None
        for j in order:
            away[j] = product(place.twin_at(2 * j)).astype(BF).reshape(n_bat, own, dim)
            if waiting is not None:
                send(waiting)
            waiting = j
        chunks = [("x", k) for k in list(range(1, n_seq)) + [0]] + [
            ("y", k) for k in range(dim // 256)
        ]

        def chunk_load(n):
            kind, k = chunks[n]
            if kind == "x":
                src = x_ref.at[:, pl.ds(pl.multiple_of(place.seq_at(k) * depth, depth), depth)]
            else:
                src = dy_ref.at[:, pl.ds(k * 256, 256)]
            return pltpu.make_async_copy(src, columns.at[n % 2], column_sems.at[n % 2])

        chunk_load(0).start()

        def pair(j):
            part_sum = product(place.seq_at(2 * j))
            from_twin[j].wait_recv()
            twin[j] = (
                (part_sum + twin[j].reshape(group, dim).astype(F32))
                .astype(BF)
                .reshape(n_bat, own, dim)
            )
            works[j] = AcrossSum(place, wire, twin.at[j], halves.at[j], full.at[j])

        arrivals = []
        done = [0]

        def work_chunks(count):
            for n in range(done[0], min(done[0] + count, len(chunks))):
                done[0] = n + 1
                if n + 1 < len(chunks):
                    chunk_load(n + 1).start()
                chunk_load(n).wait()
                kind, k = chunks[n]
                if kind == "y":
                    down_out[:, k * 256 : (k + 1) * 256] = t_dot(
                        weighted_ref[...], columns[n % 2]
                    )
                else:
                    value = t_dot(columns[n % 2], grad_ref[...]).astype(BF)
                    if k == 0:
                        got[place.s] = value
                    else:
                        sent[k] = value
                if n and chunks[n - 1][0] == "x" and chunks[n - 1][1]:
                    k = chunks[n - 1][1]
                    arrivals.append(wire.push(sent.at[k], got.at[place.s], place.seq_peer(k)))

        def pass_on(j):
            works[j].finish()
            if j:
                from_seq[j] = wire.push(twin.at[j, place.b], line.at[j], place.seq_peer(2 * j))

        first, rest = order[:2], order[2:]
        pair(order[0])
        send(waiting)
        for j in first[1:]:
            pair(j)
            works[first[0]].start()
        works[first[-1]].start()
        for j in rest:
            pair(j)
        term_order = term_work.order()
        for j in term_order:
            term_work.pair(j)
        works[first[0]].middle()
        work_chunks(1)
        for j in first[1:]:
            works[j].middle()
        for j in rest:
            works[j].start()
        for j in term_order:
            term_work.merge(j)
        for j in first:
            work_chunks(3)
            pass_on(j)
        for j in rest:
            work_chunks(1)
            works[j].middle()
        for j in rest:
            work_chunks(4)
            pass_on(j)
        work_chunks(len(chunks))
        for copy in arrivals:
            copy.wait_recv()
        for i in range(n_seq):
            lanes = slice(i * part, (i + 1) * part)
            for e in range(local_experts):
                gate_out[e, :, lanes] = got[i, :, e * part : (e + 1) * part].astype(F32)
                up_out[e, :, lanes] = got[i, :, units + e * part : units + (e + 1) * part].astype(
                    F32
                )
        term_work.finish()
        for j in range(1, half):
            from_seq[j].wait_recv()
        total = twin[0, place.b].astype(F32)
        for j in range(1, half):
            total = total + line[j].astype(F32)
        out_ref[...] = total
        wire.drain()

    vmem = pl.BlockSpec(memory_space=pltpu.VMEM)
    expert = jax.ShapeDtypeStruct((local_experts, depth, hidden), F32)
    return comm_call(
        kernel,
        [
            jax.ShapeDtypeStruct((own, dim), F32),
            term,
            expert,
            expert,
            jax.ShapeDtypeStruct((units, dim), F32),
        ],
        [
            pltpu.VMEM((half, n_bat, own, dim), BF),
            pltpu.VMEM((half, n_bat, own, dim), BF),
            pltpu.VMEM((half, 2, own // 2, dim), BF),
            pltpu.VMEM((half, 2, own, dim), BF),
            pltpu.VMEM((half, own, dim), BF),
            pltpu.VMEM((2, tokens, 256), BF),
            pltpu.VMEM((n_seq, depth, 2 * units), BF),
            pltpu.VMEM((n_seq, depth, 2 * units), BF),
            pltpu.SemaphoreType.DMA((2,)),
        ]
        + FullScatter.scratch(n_seq, n_bat, term),
        slots,
        5,
        "experts_backward",
        [vmem] * 3 + [ANY] * 3,
        [vmem] * 5,
    )(grad_pre, weighted, w_gu, terms, x_all, dy_all)


def store_last(grad_w, grad_wo, small, mixture, n_seq, n_bat):
    one = jax.ShapeDtypeStruct(grad_w.shape[2:], grad_w.dtype)
    shard, three = one.shape
    wide = three // 3
    wo_one = jax.ShapeDtypeStruct(grad_wo.shape[1:], grad_wo.dtype)
    small_one = jax.ShapeDtypeStruct(small.shape[2:], small.dtype)
    half = n_seq // 2
    dim = wo_one.shape[1]
    slots = 64 + n_seq * n_bat + 5 * n_seq

    def kernel(*refs):
        w_ref, wo_ref, small_ref, mix_ref = refs[:4]
        q_out, k_out, v_out, wo_out, small_out, mix_out = refs[4:10]
        w_sum, w_halves, w_full, w_got, wo_sum, wo_halves, wo_full, line = refs[10:18]
        small_scratch = refs[18:23]
        w_sems, wo_sem, send_sems, recv_sems = refs[23:]
        place = Place(n_seq, n_bat)
        place.greet(all_seq=True)
        wire = Wire(send_sems, recv_sems)
        small_work = FullScatter(place, wire, small_ref, small_out, *small_scratch, None)
        small_work.start()
        order = list(range(1, n_seq)) + [0]
        loads = {}
        for k in order:
            loads[k] = pltpu.make_async_copy(
                w_ref.at[place.seq_at(k)], w_sum.at[k], w_sems.at[k]
            )
            loads[k].start()
        wo_load = pltpu.make_async_copy(wo_ref, wo_sum, wo_sem.at[0])
        wo_load.start()
        works = {}
        for k in order:
            loads[k].wait()
            works[k] = AcrossSum(place, wire, w_sum.at[k], w_halves.at[k], w_full.at[k])
            works[k].start()
        wo_load.wait()
        wo_work = AcrossSum(place, wire, wo_sum, wo_halves, wo_full)
        wo_work.start()
        term_order = small_work.order()
        for j in term_order:
            small_work.pair(j)
        mix_line = {
            j: wire.push(mix_ref.at[j], line.at[j], place.seq_peer(2 * j)) for j in range(1, half)
        }
        arrivals = []
        ready = None

        def ship(k):
            if k:
                arrivals.append(
                    wire.push(w_sum.at[k, place.b], w_got.at[place.s], place.seq_peer(k))
                )

        for k in order:
            works[k].middle()
        wo_work.middle()
        for j in term_order:
            small_work.merge(j)
        for k in order:
            works[k].finish()
            if ready is not None:
                ship(ready)
            ready = k
        w_got[place.s] = w_sum[0, place.b]
        wo_work.finish()
        wo_out[...] = wo_sum[place.b].astype(F32)
        small_work.finish()
        for copy in arrivals:
            copy.wait_recv()
        for i in range(n_seq):
            at = slice(i * wide, (i + 1) * wide)
            for m, out in enumerate((q_out, k_out, v_out)):
                out[:, at] = w_got[i, :, m * wide : (m + 1) * wide].astype(F32)
        for copy in mix_line.values():
            copy.wait_recv()
        total = mix_ref[0].astype(F32)
        for j in range(1, half):
            total = total + line[j].astype(F32)
        mix_out[...] = total
        wire.drain()

    vmem = pl.BlockSpec(memory_space=pltpu.VMEM)
    matrix = jax.ShapeDtypeStruct((shard, dim), F32)
    return comm_call(
        kernel,
        [matrix] * 4 + [small_one, jax.ShapeDtypeStruct(mixture.shape[1:], F32)],
        [
            pltpu.VMEM((n_seq, n_bat, shard, three), BF),
            pltpu.VMEM((n_seq, 2, shard // 2, three), BF),
            pltpu.VMEM((n_seq, 2, shard, three), BF),
            pltpu.VMEM((n_seq, shard, three), BF),
            pltpu.VMEM((n_bat, shard, dim), BF),
            pltpu.VMEM((2, shard // 2, dim), BF),
            pltpu.VMEM((2, shard, dim), BF),
            pltpu.VMEM(mixture.shape, BF),
        ]
        + FullScatter.scratch(n_seq, n_bat, small_one)
        + [pltpu.SemaphoreType.DMA((n_seq,)), pltpu.SemaphoreType.DMA((1,))],
        slots,
        8,
        "store_last",
        [ANY] * 3 + [vmem],
        [vmem] * 6,
    )(grad_w, grad_wo, small, mixture)


def load_inputs(qkv_cut, w_out, mine, flags, small, gu_cut, dy_own, n_seq, n_bat):
    n_in = 7
    slots = 4 * n_seq * n_bat + 5 * n_seq + 2 * n_bat

    def kernel(*refs):
        cut_ref, wo_ref, x_ref, flag_ref, small_ref, gu_ref, dy_ref = refs[:n_in]
        w_ref, wo_all, x_col, flag_col, small_all, gu_all, dy_all = refs[n_in : 2 * n_in]
        buffers = refs[2 * n_in : 3 * n_in]
        own_sems, send_sems, recv_sems = refs[3 * n_in :]
        place = Place(n_seq, n_bat)
        place.greet(all_seq=True)
        wire = Wire(send_sems, recv_sems)
        small_work = FullGather(place, wire, small_ref, small_all)
        flag_work = SeqGather(place, wire, flag_ref, flag_col)
        x_work = SeqGather(place, wire, x_ref, x_col)
        dy_work = FullGather(place, wire, dy_ref, dy_all)
        small_work.start()
        flag_work.start()
        cuts = [
            wire.push(cut_ref.at[place.seq_at(k)], w_ref.at[place.s, place.b], place.seq_peer(k))
            for k in range(1, n_seq)
        ]
        ends = [
            wire.push(wo_ref, wo_all.at[place.b], place.bat_peer(k)) for k in range(1, n_bat)
        ]
        ends += [
            wire.push(cut_ref.at[place.s], w_ref.at[place.s, place.b], place.bat_peer(k))
            for k in range(1, n_bat)
        ]
        x_work.start()
        own = [
            keep_own(src, dst, buffers[i], own_sems.at[i])
            for i, (src, dst) in enumerate(
                (
                    (cut_ref.at[place.s], w_ref.at[place.s, place.b]),
                    (wo_ref, wo_all.at[place.b]),
                    (x_ref, x_col.at[place.s]),
                    (flag_ref, flag_col.at[place.s]),
                    (small_ref, small_all.at[place.s, place.b]),
                    (gu_ref.at[place.s], gu_all.at[place.s]),
                    (dy_ref, dy_all.at[place.s, place.b]),
                )
            )
        ]
        ends += [
            wire.push(gu_ref.at[place.seq_at(k)], gu_all.at[place.s], place.seq_peer(k))
            for k in range(1, n_seq)
        ]
        dy_work.start()
        for j in range(1, place.half):
            small_work.step(j)
            flag_work.step(j)
        for k in range(1, n_seq):
            cuts[k - 1].wait_recv()
            block = w_ref.at[place.seq_at(-k), place.b]
            ends += [wire.push(block, block, place.bat_peer(m)) for m in range(1, n_bat)]
        for j in range(place.half):
            small_work.collect(j)
        for j in range(1, place.half):
            x_work.step(j)
        for j in range(1, place.half):
            dy_work.step(j)
            dy_work.collect(j - 1)
        dy_work.collect(place.half - 1)
        for work in (small_work, flag_work, x_work, dy_work):
            work.finish()
        for copy in ends:
            copy.wait_recv()
        for copy in own:
            copy.wait()
        wire.drain()

    every = (n_seq, n_bat)
    one = jax.ShapeDtypeStruct(qkv_cut.shape[1:], qkv_cut.dtype)
    gu_one = jax.ShapeDtypeStruct(gu_cut.shape[1:], gu_cut.dtype)
    blocks = (one, w_out, mine, flags, small, gu_one, dy_own)
    leads = (every, (n_bat,), (n_seq,), (n_seq,), every, (n_seq,), every)
    return comm_call(
        kernel,
        [shape_of(lead, block) for lead, block in zip(leads, blocks)],
        [pltpu.VMEM(block.shape, block.dtype) for block in blocks]
        + [pltpu.SemaphoreType.DMA((n_in,))],
        slots,
        1,
        "load_inputs",
        [ANY] * n_in,
    )(qkv_cut, w_out, mine, flags, small, gu_cut, dy_own)


def store_grads(grad_w, grad_wo, grad_gu, small, n_seq, n_bat):
    one = jax.ShapeDtypeStruct(grad_w.shape[2:], grad_w.dtype)
    wo_one = jax.ShapeDtypeStruct(grad_wo.shape[1:], grad_wo.dtype)
    gu_one = jax.ShapeDtypeStruct(grad_gu.shape[1:], grad_gu.dtype)
    small_one = jax.ShapeDtypeStruct(small.shape[2:], small.dtype)
    slots = 2 * n_seq * n_bat + 2 * n_seq + n_bat

    def kernel(*refs):
        w_ref, wo_ref, gu_ref, small_ref = refs[:4]
        w_out_ref, wo_out_ref, gu_out_ref, small_out_ref = refs[4:8]
        w_sum, w_got, wo_sum, wo_got, gu_buf, cut_buf = refs[8:14]
        small_scratch = refs[14:19]
        w_sems, sems, send_sems, recv_sems = refs[19:]
        place = Place(n_seq, n_bat)
        place.greet(all_seq=True)
        wire = Wire(send_sems, recv_sems)
        small_work = FullScatter(
            place, wire, small_ref, small_out_ref, *small_scratch, None
        )
        small_work.start()
        got, loads = {}, {}
        for i in list(range(1, n_seq)) + [0]:
            to_seq = place.seq_at(i)
            for k in range(1, n_bat):
                got[i, k] = wire.push(
                    w_ref.at[to_seq, place.bat_at(k)], w_got.at[i, k - 1], place.bat_peer(k)
                )
            loads[i] = pltpu.make_async_copy(
                w_ref.at[to_seq, place.b], w_sum.at[i], w_sems.at[i]
            )
            loads[i].start()
        wo_pushed = [
            wire.push(wo_ref.at[place.bat_at(k)], wo_got.at[k - 1], place.bat_peer(k))
            for k in range(1, n_bat)
        ]
        wo_load = pltpu.make_async_copy(wo_ref.at[place.b], wo_sum, sems.at[0])
        wo_load.start()
        ends = [
            wire.push(gu_ref.at[place.seq_at(k)], gu_out_ref.at[place.s], place.seq_peer(k))
            for k in range(1, n_seq)
        ]
        gu_own = keep_own(gu_ref.at[place.s], gu_out_ref.at[place.s], gu_buf, sems.at[1])
        order = small_work.order()
        for j in order:
            small_work.pair(j)
        for i in list(range(1, n_seq)) + [0]:
            loads[i].wait()
            for k in range(1, n_bat):
                got[i, k].wait_recv()
            add_into(w_sum.at[i], *[w_got.at[i, k] for k in range(n_bat - 1)])
            if i:
                ends.append(
                    wire.push(w_sum.at[i], w_out_ref.at[place.s], place.seq_peer(i))
                )
        w_own = pltpu.make_async_copy(w_sum.at[0], w_out_ref.at[place.s], sems.at[2])
        w_own.start()
        for j in order:
            small_work.merge(j)
        wo_load.wait()
        for copy in wo_pushed:
            copy.wait_recv()
        add_into(wo_sum, *[wo_got.at[k] for k in range(n_bat - 1)])
        wo_out_ref[...] = wo_sum[...].astype(F32)
        small_work.finish()
        for copy in ends:
            copy.wait_recv()
        gu_own.wait()
        w_own.wait()
        wire.drain()

    vmem = pl.BlockSpec(memory_space=pltpu.VMEM)
    return comm_call(
        kernel,
        [
            shape_of((n_seq,), one),
            jax.ShapeDtypeStruct(wo_one.shape, F32),
            shape_of((n_seq,), gu_one),
            small_one,
        ],
        [
            pltpu.VMEM((n_seq,) + one.shape, one.dtype),
            pltpu.VMEM((n_seq, n_bat - 1) + one.shape, one.dtype),
            pltpu.VMEM(wo_one.shape, wo_one.dtype),
            pltpu.VMEM((n_bat - 1,) + wo_one.shape, wo_one.dtype),
            pltpu.VMEM(gu_one.shape, gu_one.dtype),
            pltpu.VMEM(one.shape, one.dtype),
        ]
        + FullScatter.scratch(n_seq, n_bat, small_one)
        + [pltpu.SemaphoreType.DMA((n_seq,)), pltpu.SemaphoreType.DMA((3,))],
        slots,
        8,
        "store_grads",
        [ANY] * 4,
        [ANY, vmem, ANY, vmem],
    )(grad_w, grad_wo, grad_gu, small)


def shards(
    tokens,
    lengths,
    key_mask,
    top_experts,
    attn_gain,
    query_gain,
    key_gain,
    mlp_gain,
    w_query,
    w_key,
    w_value,
    w_out,
    w_router,
    expert_gate,
    expert_up,
    expert_down,
    cotangent,
):
    n_seq = lax.axis_size("seq")
    n_bat = lax.axis_size("batch")
    seq = lax.axis_index("seq")
    bat = lax.axis_index("batch")
    rows, span, dim = tokens.shape
    own = rows * span
    col = n_seq * own
    length = n_seq * span
    shard = w_query.shape[0]
    wide = dim // n_seq
    heads = wide // HEAD
    local_experts, depth, hidden_units = expert_gate.shape
    part = hidden_units // n_seq
    experts = local_experts * n_bat

    mine = tokens.reshape(own, dim)
    dy_own = cotangent.reshape(own, dim)
    small = jnp.concatenate(
        [w_router.T, jnp.stack([attn_gain, query_gain, key_gain, mlp_gain])], axis=0
    )
    positions_own = seq * span + jnp.arange(span, dtype=jnp.int32)
    flags = pack((positions_own[None, :] < lengths[:, None]) & (key_mask == 1))
    units = local_experts * part
    fused = (
        n_bat == 4
        and part % 128 == 0
        and own == 128
        and shard % 32 == 0
        and n_seq * n_bat * own * dim <= 8 * 1024 * 1024
    )
    if fused:
        w_qkv, w_o, x_col, flag_col, small_all, dy_part = load_first(
            (w_query, w_key, w_value), w_out, mine, flags, pack(small), dy_own, rows, n_seq, n_bat
        )
    else:
        qkv_cut = jnp.stack([w_query, w_key, w_value]).reshape(3, shard, n_seq, wide)
        qkv_cut = jnp.transpose(qkv_cut, (2, 1, 0, 3)).reshape(n_seq, shard, 3 * wide)
        gu_cut = jnp.stack([expert_gate, expert_up]).reshape(2, local_experts, depth, n_seq, part)
        gu_cut = jnp.transpose(gu_cut, (3, 2, 0, 1, 4)).reshape(n_seq, depth, 2 * units)
        w_qkv, w_o, x_col, flag_col, small_all, w_gu, dy_all = load_inputs(
            qkv_cut, w_out, mine, flags, pack(small), gu_cut, dy_own, n_seq, n_bat
        )
        w_gu = w_gu.reshape(dim, 2 * units)
        dy_all = dy_all.reshape(-1, dim)
        x_col = jnp.transpose(x_col.reshape(n_seq, rows, span, dim), (1, 0, 2, 3))
    w_qkv = w_qkv.reshape(dim, 3 * wide)
    w_o = w_o.reshape(wide, dim)
    w_down = expert_down.reshape(local_experts * part, dim)
    small_all = unpack(small_all, (n_seq, n_bat), small.shape)
    small_all = jnp.transpose(small_all, (2, 0, 1, 3)).reshape(-1, dim)
    router = small_all[:experts].T.astype(BF)
    gain_attn, gain_mlp = small_all[experts], small_all[experts + 3]
    gain_q = lax.dynamic_slice_in_dim(small_all[experts + 1], seq * wide, wide)
    gain_k = lax.dynamic_slice_in_dim(small_all[experts + 2], seq * wide, wide)
    usable = unpack(flag_col, (n_seq,), key_mask.shape)
    usable = jnp.transpose(usable, (1, 0, 2)).reshape(rows, length)

    cos_part, sin_part = rotary_tables(jnp.arange(length, dtype=jnp.int32))
    cos_wide = jnp.concatenate([cos_part, cos_part], axis=1)
    sin_wide = jnp.concatenate([-sin_part, sin_part], axis=1)
    gain_q, gain_k = gain_q[None, :], gain_k[None, :]
    hidden, qkv, q, k, v, mixed, stats, mixed_out, *extra = attend_forward(
        x_col.reshape(col, dim), w_qkv, gain_attn[None, :], usable, w_o, gain_q, gain_k,
        cos_wide, sin_wide, n_seq, n_bat, rows,
        (dy_part, expert_gate, expert_up) if fused else None,
    )
    x_own = mine.astype(F32)
    residual = x_own + mixed_out.astype(F32)
    scale_r = rms_scale(residual)
    normed = (residual * scale_r * gain_mlp).astype(BF)
    router_probs = jax.nn.softmax(dot(normed, router), axis=-1)
    expert_ids = jnp.arange(experts, dtype=jnp.int32)
    chosen = jnp.any(top_experts.reshape(own, -1)[:, :, None] == expert_ids, axis=1).astype(F32)
    gates = router_probs * chosen

    if fused:
        dy_all, w_gu = extra[0], extra[1].reshape(dim, 2 * units)
        normed_all, weighted, grad_pre, gate_terms = experts_forward(
            normed, gates.T, dy_all, w_gu, w_down, local_experts, n_seq, n_bat
        )
        grad_normed, grad_gates, grad_gate, grad_up, grad_down = experts_backward(
            grad_pre,
            weighted,
            w_gu,
            gate_terms,
            normed_all.reshape(-1, dim),
            dy_all.reshape(-1, dim),
            local_experts,
            n_seq,
            n_bat,
            own,
        )
        grad_gates = grad_gates.T
        grad_down = grad_down.reshape(local_experts, part, dim)
    else:
        normed_all, gates_all = gather_all([normed, pack(gates.T)], n_seq, n_bat, 4, "gather_normed")
        normed_all = normed_all.reshape(-1, dim)
        gates_all = unpack(gates_all, (n_seq, n_bat), (experts, own))
        gates_all = jnp.transpose(gates_all, (0, 1, 3, 2)).reshape(-1, experts)
        first_expert = bat * local_experts
        gates_here = lax.dynamic_slice_in_dim(gates_all, first_expert, local_experts, 1)
        gates_wide = jnp.repeat(gates_here, part, axis=1)
        pre = dot(normed_all, w_gu)
        gate_pre, up_pre = pre[:, :units], pre[:, units:]
        sig = jax.nn.sigmoid(gate_pre)
        silu = gate_pre * sig
        active = (silu * up_pre).astype(BF).astype(F32)
        weighted = (active * gates_wide).astype(BF)
        mixture = dot(weighted, w_down).astype(BF)
        mixture = mixture.reshape(n_seq, n_bat, own, dim)
        back = dot_t(dy_all, w_down)
        gate_terms = jnp.sum((active * back).reshape(-1, local_experts, part), axis=-1)
        grad_active = back * gates_wide
        grad_gate_pre = (grad_active * up_pre * sig * (1.0 + gate_pre * (1.0 - sig))).astype(BF)
        grad_up_pre = (grad_active * silu).astype(BF)
        grad_pre = jnp.concatenate([grad_gate_pre, grad_up_pre], axis=1)
        grad_down = t_dot(weighted, dy_all)
        grad_gu = t_dot(normed_all, grad_pre).astype(BF)
        grad_normed = dot_t(grad_pre, w_gu).astype(BF)
        gate_terms = gate_terms.reshape(n_seq, n_bat, own, local_experts)
        grad_gates = lax.dynamic_update_slice_in_dim(
            jnp.zeros((n_seq, n_bat, experts, own), F32),
            jnp.transpose(gate_terms, (0, 1, 3, 2)),
            first_expert,
            2,
        )
        grad_gates = jax.vmap(jax.vmap(pack))(grad_gates)
        grad_normed = grad_normed.reshape(n_seq, n_bat, own, dim)
        grad_normed, grad_gates, mixture = scatter_blocks(
            grad_normed, grad_gates, mixture, n_seq, n_bat
        )
        grad_normed = grad_normed.astype(F32)
        grad_gates = unpack(grad_gates, (), (experts, own)).T
        output = (residual + mixture.astype(F32)).astype(BF)
        grad_down = grad_down.reshape(local_experts, part, dim)

    grad_chosen = grad_gates * chosen
    grad_logits = router_probs * (
        grad_chosen - jnp.sum(router_probs * grad_chosen, axis=-1, keepdims=True)
    )
    grad_router = lax.dot_general(
        normed.astype(F32), grad_logits, (((0,), (0,)), ((), ())), precision=HIGHEST
    )
    grad_normed = grad_normed + lax.dot_general(
        grad_logits, router.astype(F32), (((1,), (1,)), ((), ())), precision=HIGHEST
    )
    grad_resid, gain_mlp_terms = rms_back(residual, scale_r, gain_mlp, grad_normed)
    grad_residual = dy_own.astype(F32) + grad_resid
    grad_o = grad_residual.astype(BF)

    grad_w_o, grad_w, grad_gains, grad_hidden, *extra = attend_backward(
        grad_o, q, k, v, mixed, qkv, stats, hidden, usable, w_o, w_qkv, gain_q, gain_k,
        cos_wide, sin_wide, n_seq, n_bat, (weighted, w_down) if fused else None,
    )
    grad_w_o = grad_w_o.reshape(n_bat, shard, dim)
    grad_w = grad_w.reshape(n_seq, n_bat, shard, 3 * wide)
    grad_hidden = grad_hidden.astype(F32)
    grad_x, gain_attn_terms = rms_back(x_own, rms_scale(x_own), gain_attn, grad_hidden)
    grad_tokens = (grad_residual + grad_x).astype(BF)

    zeros = jnp.zeros((dim,), F32)
    small_grads = jnp.concatenate(
        [
            grad_router.T,
            jnp.stack(
                [
                    jnp.sum(gain_attn_terms, axis=0),
                    lax.dynamic_update_slice_in_dim(zeros, grad_gains[0], seq * wide, 0),
                    lax.dynamic_update_slice_in_dim(zeros, grad_gains[1], seq * wide, 0),
                    jnp.sum(gain_mlp_terms, axis=0),
                ]
            ),
        ],
        axis=0,
    )
    small_grads = jnp.transpose(small_grads.reshape(-1, n_seq, n_bat, shard), (1, 2, 0, 3))
    small_grads = jax.vmap(jax.vmap(pack))(small_grads)
    if fused:
        *grad_w, grad_w_o, small_grads, mixture = store_last(
            grad_w, grad_w_o, small_grads, extra[0], n_seq, n_bat
        )
        output = (residual + mixture).astype(BF)
    else:
        grad_gu = grad_gu.reshape(n_seq, depth, -1)
        grad_w, grad_w_o, grad_gu, small_grads = store_grads(
            grad_w, grad_w_o, grad_gu, small_grads, n_seq, n_bat
        )
        grad_w = grad_w.astype(F32).reshape(n_seq, shard, 3, wide)
        grad_w = jnp.transpose(grad_w, (2, 1, 0, 3)).reshape(3, shard, dim)
        grad_gu = grad_gu.reshape(n_seq, depth, 2, local_experts, part)
        grad_gu = jnp.transpose(grad_gu, (2, 3, 1, 0, 4)).reshape(2, local_experts, depth, hidden_units)
        grad_gu = grad_gu.astype(F32)
        grad_gate, grad_up = grad_gu[0], grad_gu[1]
    small_grads = unpack(small_grads, (), (experts + 4, shard))

    return (
        output.reshape(rows, span, dim),
        grad_tokens.reshape(rows, span, dim),
        small_grads[experts],
        small_grads[experts + 1],
        small_grads[experts + 2],
        small_grads[experts + 3],
        grad_w[0],
        grad_w[1],
        grad_w[2],
        grad_w_o,
        small_grads[:experts].T,
        grad_gate,
        grad_up,
        grad_down,
    )


def solution(mesh):
    tok = P("batch", "seq", None)
    vec = P(("seq", "batch"))
    mat = P(("seq", "batch"), None)
    in_specs = (tok, P("batch"), P("batch", "seq"), tok) + (vec,) * 4 + (mat,) * 5 + (tok,) * 4
    out_specs = (tok, tok) + (vec,) * 4 + (mat,) * 5 + (tok,) * 3
    return jax.shard_map(shards, mesh=mesh, in_specs=in_specs, out_specs=out_specs, check_vma=False)
```

```python
import functools

import jax
import jax.numpy as jnp
from jax import lax
from jax.experimental import pallas as pl
from jax.experimental.pallas import tpu as pltpu
from jax.sharding import PartitionSpec as P

HEAD = 128
EPS = 1e-05
HIGHEST = lax.Precision.HIGHEST
NEGATIVE = -1e30
BF = jnp.bfloat16
F32 = jnp.float32


def dot(a, b):
    return jnp.dot(a, b, preferred_element_type=F32)


def dot_t(a, b):
    return lax.dot_general(a, b, (((1,), (1,)), ((), ())), preferred_element_type=F32)


def t_dot(a, b):
    return lax.dot_general(a, b, (((0,), (0,)), ((), ())), preferred_element_type=F32)


def rms_scale(v):
    return lax.rsqrt(jnp.mean(v * v, axis=-1, keepdims=True) + EPS)


def rms_back(v, scale, gain, grad):
    normal = v * scale
    weighted = grad * gain
    mean = jnp.mean(weighted * normal, axis=-1, keepdims=True)
    return scale * (weighted - normal * mean), grad * normal


def rotary_tables(positions):
    half_head = HEAD // 2
    frequency = 10000.0 ** (-2.0 * jnp.arange(half_head, dtype=F32) / HEAD)
    angles = positions.astype(F32)[:, None] * frequency[None, :]
    return jnp.cos(angles), jnp.sin(angles)


ANY = pl.BlockSpec(memory_space=pl.ANY)
VMEM_LIMIT = 67043328


class Place:
    def __init__(self, n_seq, n_bat):
        self.n_seq, self.n_bat, self.half = n_seq, n_bat, n_seq // 2
        self.s = lax.axis_index("seq")
        self.b = lax.axis_index("batch")
        self.core = lax.rem(self.s, 2)
        self.z = lax.div(self.s, 2)
        self.twin_s = self.s + 1 - 2 * self.core
        self.bat_x = self.b + 1 - 2 * lax.rem(self.b, 2)
        self.bat_y = lax.rem(self.b + 2, 4)
        self.bat_d = lax.rem(self.bat_x + 2, 4)

    def chip(self, i):
        return 2 * i + self.core

    def chip_twin(self, i):
        return 2 * i + 1 - self.core

    def chip_peer(self, i):
        return {"seq": self.chip(lax.rem(i + self.half, self.half)), "batch": self.b}

    def origin(self, m):
        if m == 0:
            return self.z
        last = self.half - 1
        upper = lax.div(2 * self.z, self.half)
        mirrored = self.z + upper * (last - 2 * self.z)
        place = m - 1 + lax.div(m - mirrored + last, self.half)
        return place + upper * (last - 2 * place)

    def seq_at(self, k):
        return lax.rem(self.s + (k + self.n_seq), self.n_seq)

    def twin_at(self, k):
        return lax.rem(self.twin_s + (k + self.n_seq), self.n_seq)

    def bat_at(self, k):
        return lax.rem(self.b + (k + self.n_bat), self.n_bat)

    def seq_peer(self, k):
        return {"seq": self.seq_at(k), "batch": self.b}

    def bat_peer(self, k):
        return {"seq": self.s, "batch": self.bat_at(k)}

    def x_peer(self):
        return {"seq": self.s, "batch": self.bat_x}

    def y_peer(self):
        return {"seq": self.s, "batch": self.bat_y}

    def twin(self):
        return {"seq": self.twin_s, "batch": self.b}

    def greet(self, all_seq=False, batch=True):
        steps = range(1, self.n_seq) if all_seq else range(2, self.n_seq, 2)
        peers = [self.seq_peer(k) for k in steps]
        if not all_seq:
            peers.append(self.twin())
        if batch:
            peers += [self.bat_peer(k) for k in range(1, self.n_bat)]
        barrier = pltpu.get_barrier_semaphore()
        for peer in peers:
            pl.semaphore_signal(
                barrier, inc=1, device_id=peer, device_id_type=pl.DeviceIdType.MESH
            )
        pl.semaphore_wait(barrier, len(peers))


class Wire:
    def __init__(self, send_sems, recv_sems):
        self.send_sems, self.recv_sems = send_sems, recv_sems
        self.copies, self.used = [], 0

    def reserve(self, count):
        first = self.used
        self.used += count
        return first

    def make(self, src, dst, peer, send_slot, recv_slot):
        return pltpu.make_async_remote_copy(
            src_ref=src,
            dst_ref=dst,
            send_sem=self.send_sems.at[send_slot],
            recv_sem=self.recv_sems.at[recv_slot],
            device_id=peer,
            device_id_type=pl.DeviceIdType.MESH,
        )

    def push(self, src, dst, peer):
        slot = self.reserve(1)
        copy = self.make(src, dst, peer, slot, slot)
        copy.start()
        self.copies.append((copy, None))
        return copy

    def push_if(self, there, copy):
        pl.when(there)(copy.start)
        self.copies.append((copy, there))

    def settle(self, copy):
        copy.wait_send()
        self.copies = [other for other in self.copies if other[0] is not copy]

    def drain(self):
        for copy, there in self.copies:
            if there is None:
                copy.wait_send()
            else:
                pl.when(there)(copy.wait_send)


class Line:
    def __init__(self, place, wire, src, at):
        self.place, self.wire, self.src, self.at = place, wire, src, at
        self.base = wire.reserve(place.half + 2)
        self.sends = 0

    def copy(self, src, origin, peer):
        return self.wire.make(
            src, self.at(origin), peer, self.base + self.sends, self.base + origin
        )

    def send(self, there, src, origin, to):
        copy = self.copy(src, origin, self.place.chip_peer(to))
        self.sends += 1
        self.wire.push_if(there, copy)

    def start(self):
        place = self.place
        self.send(place.z < place.half - 1, self.src, place.z, place.z + 1)
        self.send(place.z > 0, self.src, place.z, place.z - 1)

    def step(self, m):
        place = self.place
        origin = place.origin(m)
        self.copy(self.at(origin), origin, place.chip_peer(place.z)).wait_recv()
        from_left = lax.div(place.z - origin - 1 + place.half, place.half)
        to = place.z + 2 * from_left - 1
        self.send((to >= 0) & (to < place.half), self.at(origin), origin, to)
        return origin


class SeqGather:
    def __init__(self, place, wire, src, out):
        self.place, self.wire, self.src, self.out = place, wire, src, out
        self.late = []

    def start(self):
        place = self.place
        self.line = Line(place, self.wire, self.src, lambda i: self.out.at[place.chip(i)])
        self.line.start()
        self.late.append(self.wire.push(self.src, self.out.at[place.s], place.twin()))

    def step(self, j):
        block = self.out.at[self.place.chip(self.line.step(j))]
        self.late.append(self.wire.push(block, block, self.place.twin()))

    def finish(self):
        for copy in self.late:
            copy.wait_recv()


class FullGather:
    def __init__(self, place, wire, src, out):
        self.place, self.wire, self.src, self.out = place, wire, src, out
        self.late = []
        self.across = {}

    def spread(self, j, block):
        place = self.place
        self.across[j] = [
            self.wire.push(block, self.out.at[place.seq_at(-2 * j), place.b], place.bat_peer(k))
            for k in range(1, place.n_bat)
        ]

    def start(self):
        place, mine = self.place, self.out.at[self.place.s, self.place.b]
        self.line = [
            self.wire.push(self.src, mine, place.seq_peer(2 * j)) for j in range(1, place.half)
        ]
        self.spread(0, self.src)
        self.late.append(self.wire.push(self.src, mine, place.twin()))

    def step(self, j):
        self.line[j - 1].wait_recv()
        block = self.out.at[self.place.seq_at(-2 * j), self.place.b]
        self.spread(j, block)
        self.late.append(self.wire.push(block, block, self.place.twin()))

    def collect(self, j):
        place = self.place
        for k in range(1, place.n_bat):
            self.across[j][k - 1].wait_recv()
            block = self.out.at[place.seq_at(-2 * j), place.bat_at(-k)]
            self.late.append(self.wire.push(block, block, place.twin()))

    def finish(self):
        for copy in self.late:
            copy.wait_recv()


def keep_own(src, dst, buffer, sem):
    first = pltpu.make_async_copy(src, buffer, sem)
    first.start()
    first.wait()
    second = pltpu.make_async_copy(buffer, dst, sem)
    second.start()
    return second


def comm_call(
    kernel, outs, scratch, slots, collective_id, name, in_specs, out_specs=None, aliases=None
):
    return pl.pallas_call(
        kernel,
        out_shape=outs,
        in_specs=in_specs,
        out_specs=out_specs if out_specs is not None else jax.tree.map(lambda _: ANY, outs),
        scratch_shapes=list(scratch)
        + [pltpu.SemaphoreType.DMA((slots,)), pltpu.SemaphoreType.DMA((slots,))],
        compiler_params=pltpu.CompilerParams(
            collective_id=collective_id, has_side_effects=True, vmem_limit_bytes=VMEM_LIMIT
        ),
        name=name,
        input_output_aliases=aliases or {},
    )


def shape_of(lead, block):
    return jax.ShapeDtypeStruct(tuple(lead) + block.shape, block.dtype)


def gather_all(blocks, n_seq, n_bat, collective_id, name):
    count = len(blocks)

    def kernel(*refs):
        srcs, outs = refs[:count], refs[count : 2 * count]
        buffers = refs[2 * count : 3 * count]
        own_sems, send_sems, recv_sems = refs[3 * count :]
        place = Place(n_seq, n_bat)
        place.greet()
        wire = Wire(send_sems, recv_sems)
        gathers = [FullGather(place, wire, *pair) for pair in zip(srcs, outs)]
        for gather in gathers:
            gather.start()
        own = [
            keep_own(srcs[i], outs[i].at[place.s, place.b], buffers[i], own_sems.at[i])
            for i in range(count)
        ]
        for j in range(1, place.half):
            for gather in gathers:
                gather.step(j)
            for gather in gathers:
                gather.collect(j - 1)
        for gather in gathers:
            gather.collect(place.half - 1)
        for gather in gathers:
            gather.finish()
        for copy in own:
            copy.wait()
        wire.drain()

    return comm_call(
        kernel,
        [shape_of((n_seq, n_bat), block) for block in blocks],
        [pltpu.VMEM(block.shape, block.dtype) for block in blocks]
        + [pltpu.SemaphoreType.DMA((count,))],
        n_seq * n_bat * count,
        collective_id,
        name,
        [ANY] * count,
    )(*blocks)


def add_into(target, *others):
    rows = target.shape[0]
    step = min(rows, 16)

    def body(i, carry):
        at = pl.ds(pl.multiple_of(i * step, step), step)
        total = target[at, :].astype(F32)
        for other in others:
            total = total + other[at, :].astype(F32)
        target[at, :] = total.astype(target.dtype)
        return carry

    lax.fori_loop(0, rows // step, body, 0)


class FullScatter:
    def __init__(self, place, wire, parts, out, mine, twin, across, line, sems, pick=None):
        self.place, self.wire, self.out = place, wire, out
        self.mine, self.twin, self.across, self.line = mine, twin, across, line
        self.sems = sems
        self.pick = pick or (lambda i, j: parts.at[i, j])

    @staticmethod
    def scratch(n_seq, n_bat, block):
        half = n_seq // 2
        return [
            pltpu.VMEM((half, n_bat) + block.shape, block.dtype),
            pltpu.VMEM((half, n_bat) + block.shape, block.dtype),
            pltpu.VMEM((half, n_bat) + block.shape, block.dtype),
            pltpu.VMEM((half,) + block.shape, block.dtype),
            pltpu.SemaphoreType.DMA((half, n_bat)),
        ]

    def order(self):
        return list(range(1, self.place.half)) + [0]

    def start(self):
        place = self.place
        self.from_twin, self.loads, self.from_bat, self.from_seq = {}, {}, {}, {}
        for j in self.order():
            for k in list(range(1, place.n_bat)) + [0]:
                to_bat = place.bat_at(k)
                self.from_twin[j, k] = self.wire.push(
                    self.pick(place.twin_at(2 * j), to_bat), self.twin.at[j, k], place.twin()
                )
                load = pltpu.make_async_copy(
                    self.pick(place.seq_at(2 * j), to_bat),
                    self.mine.at[j, k],
                    self.sems.at[j, k],
                )
                load.start()
                self.loads[j, k] = load

    def pair(self, j):
        place = self.place
        for k in list(range(1, place.n_bat)) + [0]:
            self.from_twin[j, k].wait_recv()
            self.loads[j, k].wait()
            add_into(self.mine.at[j, k], self.twin.at[j, k])
        for k in range(1, place.n_bat):
            self.from_bat[j, k] = self.wire.push(
                self.mine.at[j, k], self.across.at[j, k], place.bat_peer(k)
            )

    def merge(self, j):
        place = self.place
        for k in range(1, place.n_bat):
            self.from_bat[j, k].wait_recv()
        add_into(self.mine.at[j, 0], *[self.across.at[j, k] for k in range(1, place.n_bat)])
        if j:
            self.from_seq[j] = self.wire.push(
                self.mine.at[j, 0], self.line.at[j], place.seq_peer(2 * j)
            )

    def finish(self):
        for j in range(1, self.place.half):
            self.from_seq[j].wait_recv()
        add_into(self.mine.at[0, 0], *[self.line.at[j] for j in range(1, self.place.half)])
        self.out[...] = self.mine[0, 0]


def scatter_all(parts, n_seq, n_bat, collective_id, name):
    blocks = [jax.ShapeDtypeStruct(part.shape[2:], part.dtype) for part in parts]
    count = len(parts)

    def kernel(*refs):
        ins, outs = refs[:count], refs[count : 2 * count]
        rest = refs[2 * count :]
        send_sems, recv_sems = rest[-2:]
        place = Place(n_seq, n_bat)
        place.greet()
        wire = Wire(send_sems, recv_sems)
        works = [
            FullScatter(place, wire, ins[i], outs[i], *rest[5 * i : 5 * i + 5])
            for i in range(count)
        ]
        for work in works:
            work.start()
        order = works[0].order()
        for at, j in enumerate(order):
            for work in works:
                work.pair(j)
            if at:
                for work in works:
                    work.merge(order[at - 1])
        for work in works:
            work.merge(order[-1])
        for work in works:
            work.finish()
        wire.drain()

    scratch = []
    for block in blocks:
        scratch += FullScatter.scratch(n_seq, n_bat, block)
    slots = count * (n_seq * n_bat)
    vmem = pl.BlockSpec(memory_space=pltpu.VMEM)
    return comm_call(
        kernel,
        blocks,
        scratch,
        slots,
        collective_id,
        name,
        [ANY] * count,
        [vmem] * count,
    )(*parts)


def pack(values):
    flat = values.astype(F32).reshape(-1)
    tiles = -(-flat.shape[0] // 1024)
    return jnp.pad(flat, (0, tiles * 1024 - flat.shape[0])).reshape(tiles * 8, 128)


def unpack(tiles, lead, shape):
    size = 1
    for extent in shape:
        size *= extent
    return tiles.reshape(tuple(lead) + (-1,))[..., :size].reshape(tuple(lead) + tuple(shape))


def scatter_blocks(grad_normed, grad_gates, mixture, n_seq, n_bat):
    dim = grad_normed.shape[-1]
    pieces = 1
    while n_seq * n_bat * grad_normed.shape[2] * (dim // pieces) * 4 > 36 * 1024 * 1024:
        pieces *= 2
    size = dim // pieces
    grads, mixtures = [], []
    for i in range(pieces):
        at = slice(i * size, (i + 1) * size)
        parts = [grad_normed[..., at]] + ([grad_gates] if i == 0 else [])
        done = scatter_all(parts, n_seq, n_bat, 16 + 2 * i, "scatter_normed")
        grads.append(done[0])
        if i == 0:
            gates = done[1]
        done = scatter_all([mixture[..., at]], n_seq, n_bat, 17 + 2 * i, "scatter_mixture")
        mixtures.append(done[0])
    return jnp.concatenate(grads, axis=-1), gates, jnp.concatenate(mixtures, axis=-1)


class SeqScatter:
    def __init__(self, place, wire, full, twin, line):
        self.place, self.wire = place, wire
        self.full, self.twin, self.line = full, twin, line
        self.order = list(range(1, place.half)) + [0]

    @staticmethod
    def scratch(rows, n_seq, block):
        lead = ((rows, n_seq), (rows, n_seq // 2), (rows, n_seq // 2))
        return [pltpu.VMEM(extent + block.shape, block.dtype) for extent in lead]

    def start(self):
        place = self.place
        self.from_twin = {
            j: self.wire.push(self.full.at[place.twin_at(2 * j)], self.twin.at[j], place.twin())
            for j in self.order
        }

    def pass_on(self):
        place = self.place
        self.from_seq = {}
        for j in self.order:
            self.from_twin[j].wait_recv()
            block = self.full.at[place.seq_at(2 * j)]
            add_into(block, self.twin.at[j])
            if j:
                self.from_seq[j] = self.wire.push(block, self.line.at[j], place.seq_peer(2 * j))

    def total(self):
        for copy in self.from_seq.values():
            copy.wait_recv()
        total = self.full[self.place.s].astype(F32)
        for j in range(1, self.place.half):
            total = total + self.line[j].astype(F32)
        return total

    def finish(self, out, at):
        for copy in self.from_seq.values():
            copy.wait_recv()
        own = self.full.at[self.place.s]
        add_into(own, *[self.line.at[j] for j in range(1, self.place.half)])
        out[at, :] = own[...]


def turn(v, cos_wide, sin_wide):
    return v * cos_wide + pltpu.roll(v, HEAD // 2, axis=1) * sin_wide


class Exchange:
    def __init__(self, place, wire, local, got):
        self.local, self.got, self.count = local, got, place.n_seq - 1
        self.copies = [
            wire.push(local, got.at[k - 1], place.seq_peer(k)) for k in range(1, place.n_seq)
        ]

    def total(self):
        for copy in self.copies:
            copy.wait_recv()
        total = self.local[...]
        for k in range(self.count):
            total = total + self.got[k]
        return total


def lane_sums(v):
    ones = jnp.ones((8, v.shape[1]), F32)
    sums = lax.dot_general(
        ones, v, (((1,), (1,)), ((), ())), precision=HIGHEST, preferred_element_type=F32
    )
    return sums[0:1]


def allowed_block(use, first, count, keys):
    at_query = first + lax.broadcasted_iota(jnp.int32, (count, keys), 0)
    at_key = lax.broadcasted_iota(jnp.int32, (count, keys), 1)
    return (at_key == at_query) | ((at_key < at_query) & (use > 0))


STEP = 128


def attend_forward(
    x_col, w_qkv, gain_attn, usable, w_o, gain_q, gain_k, cos_wide, sin_wide, n_seq, n_bat, rows,
    side=None,
):
    col, dim = x_col.shape
    three = w_qkv.shape[1]
    wide = three // 3
    heads = wide // HEAD
    length = col // rows
    span = length // n_seq
    own = rows * span
    steps = length // STEP
    chunk = min(256, length)
    scale = HEAD ** (-0.5)
    block = jax.ShapeDtypeStruct((span, dim), BF)

    def kernel(*refs):
        (x_ref, w_ref, ga_ref, use_ref, wo_ref, gq_ref, gk_ref, cos_ref, sin_ref) = refs[:9]
        refs = refs[9:]
        if side is not None:
            dy_ref, own_ref, gm_ref, router_ref, chosen_ref = refs[:5]
            refs = refs[5:]
        hid_ref, qkv_ref, q_ref, k_ref, v_ref, mix_ref, stat_ref, out_ref = refs[:8]
        refs = refs[8:]
        if side is not None:
            dy_all, res_ref, normed_ref, probs_ref, gates_ref = refs[:5]
            dy_keep, dy_sem = refs[-4:-2]
            refs = refs[5:-4] + refs[-2:]
        local, got, full, twin, line, send_sems, recv_sems = refs
        place = Place(n_seq, n_bat)
        place.greet(all_seq=True, batch=side is not None)
        wire = Wire(send_sems, recv_sems)
        dy_works, dy_here = [], [place.chip(place.origin(m)) for m in range(place.half)]

        def dy_spread(m):
            if side is None:
                return
            if m:
                dy_line.step(m)
            src = dy_all.at[dy_here[m], place.b] if m else dy_ref
            work = Across(place, wire, src, lambda i: dy_all.at[dy_here[m], i])
            work.start()
            dy_works.append(work)

        if side is not None:
            dy_line = Line(place, wire, dy_ref, lambda i: dy_all.at[place.chip(i), place.b])
            dy_line.start()
            dy_spread(0)
            dy_own = keep_own(dy_ref, dy_all.at[place.s, place.b], dy_keep, dy_sem)
        for first in range(0, col, chunk):
            at = slice(first, first + chunk)
            x = x_ref[at, :].astype(F32)
            hidden = (x * rms_scale(x) * ga_ref[...]).astype(BF)
            hid_ref[at, :] = hidden
            qkv_ref[at, :] = dot(hidden, w_ref[...])
        for r in range(rows):
            for c in range(steps):
                at = slice(r * length + c * STEP, r * length + (c + 1) * STEP)
                for which in range(2):
                    v = qkv_ref[at, which * wide : (which + 1) * wide]
                    row = (r * 2 + which) * steps + c
                    local[row : row + 1, :] = lane_sums(v * v)
        for r in range(rows):
            for h in range(heads):
                lanes = slice(2 * wide + h * HEAD, 2 * wide + (h + 1) * HEAD)
                v_ref[r, h] = qkv_ref[r * length : (r + 1) * length, lanes].astype(BF)
        exchange = Exchange(place, wire, local, got)
        dy_spread(1)
        total = exchange.total()
        stat_ref[...] = total
        columns = lax.rsqrt(total / dim + EPS).T
        scatters = [
            SeqScatter(place, wire, full.at[r], twin.at[r], line.at[r]) for r in range(rows)
        ]
        for r in range(rows):
            for c in range(steps):
                inside = slice(c * STEP, (c + 1) * STEP)
                at = slice(r * length + c * STEP, r * length + (c + 1) * STEP)
                for which, gain_ref, target in ((0, gq_ref, q_ref), (1, gk_ref, k_ref)):
                    row = (r * 2 + which) * steps + c
                    factor = columns[:, row : row + 1]
                    for h in range(heads):
                        lanes = slice(which * wide + h * HEAD, which * wide + (h + 1) * HEAD)
                        gain = gain_ref[0:1, h * HEAD : (h + 1) * HEAD]
                        v = qkv_ref[at, lanes] * factor * gain
                        target[r, h, inside, :] = turn(
                            v, cos_ref[inside, :], sin_ref[inside, :]
                        ).astype(BF)
            for c in range(length // chunk):
                keys = (c + 1) * chunk
                allowed = allowed_block(use_ref[r : r + 1, :keys], c * chunk, chunk, keys)
                for h in range(heads):
                    query = q_ref[r, h, c * chunk : keys, :]
                    scores = dot_t(query, k_ref[r, h, :keys, :]) * scale
                    scores = jnp.where(allowed, scores, NEGATIVE)
                    raised = jnp.exp(scores - jnp.max(scores, axis=-1, keepdims=True))
                    probs = raised / jnp.sum(raised, axis=-1, keepdims=True)
                    mixed = dot(probs.astype(BF), v_ref[r, h, :keys, :]).astype(BF)
                    mix_ref[r, c * chunk : keys, h * HEAD : (h + 1) * HEAD] = mixed
                if r and c == 0:
                    scatters[r - 1].pass_on()
                if r == 0 and c == 0 and side is not None:
                    dy_works[0].relay()
                    dy_spread(2)
            full[r] = dot(mix_ref[r], wo_ref[...]).astype(BF).reshape(n_seq, span, dim)
            scatters[r].start()
            if r == 0 and side is not None:
                dy_works[1].relay()
                for m in range(3, place.half):
                    dy_spread(m)
        scatters[-1].pass_on()
        for work in dy_works[2:]:
            work.relay()
        passed = []
        if side is not None:
            dy_own.wait()
        for m, work in enumerate(dy_works):
            work.finish()
            group = dy_all.at[dy_here[m]]
            passed.append(wire.push(group, group, place.twin()))
        for r in range(rows):
            at = slice(r * span, (r + 1) * span)
            if side is None:
                scatters[r].finish(out_ref, at)
                continue
            residual = own_ref[at, :].astype(F32) + scatters[r].total()
            res_ref[at, :] = residual
            normed_ref[at, :] = (residual * rms_scale(residual) * gm_ref[...]).astype(BF)
        if side is not None:
            out_ref[...] = jnp.zeros_like(out_ref)
            logits = dot_t(router_ref[...].astype(BF), normed_ref[...])
            raised = jnp.exp(logits - jnp.max(logits, axis=0, keepdims=True))
            probs = raised / jnp.sum(raised, axis=0, keepdims=True)
            probs_ref[...] = probs
            gates_ref[...] = probs * chosen_ref[...]
        for copy in passed:
            copy.wait_recv()
        wire.drain()

    vmem = pl.BlockSpec(memory_space=pltpu.VMEM)
    side_in, side_out, side_scratch = [], [], []
    slots = (1 + rows) * n_seq
    if side is not None:
        dy, _, _, router, _ = side
        side_in = list(side)
        side_out = [
            shape_of((n_seq, n_bat), dy),
            jax.ShapeDtypeStruct((own, dim), F32),
            jax.ShapeDtypeStruct((own, dim), BF),
            jax.ShapeDtypeStruct((router.shape[0], own), F32),
            jax.ShapeDtypeStruct((router.shape[0], own), F32),
        ]
        side_scratch = [pltpu.VMEM(dy.shape, dy.dtype), pltpu.SemaphoreType.DMA]
        slots += 4 * n_seq
    head_block = jax.ShapeDtypeStruct((rows, heads, length, HEAD), BF)
    stats = jax.ShapeDtypeStruct((2 * rows * steps, STEP), F32)
    outs = [
        jax.ShapeDtypeStruct((col, dim), BF),
        jax.ShapeDtypeStruct((col, three), F32),
        head_block,
        head_block,
        head_block,
        jax.ShapeDtypeStruct((rows, length, wide), BF),
        stats,
        jax.ShapeDtypeStruct((own, dim) if side is None else (8, HEAD), BF),
    ]
    return comm_call(
        kernel,
        outs + side_out,
        [pltpu.VMEM(stats.shape, F32), pltpu.VMEM((n_seq - 1,) + stats.shape, F32)]
        + SeqScatter.scratch(rows, n_seq, block)
        + side_scratch,
        slots,
        2,
        "attend_forward",
        [vmem] * 9 + ([ANY] + [vmem] * 4 if side_in else []),
        [vmem] * 8 + ([ANY] + [vmem] * 4 if side_in else []),
    )(x_col, w_qkv, gain_attn, usable, w_o, gain_q, gain_k, cos_wide, sin_wide, *side_in)


def attend_backward(
    grad_o, q, k, v, mixed, qkv, stats, hidden, usable, w_o, w_qkv, gain_q, gain_k,
    cos_wide, sin_wide, n_seq, n_bat, side=None,
):
    rows, heads, length, _ = q.shape
    own, dim = grad_o.shape
    span = own // rows
    col, three = qkv.shape
    wide = three // 3
    steps = length // STEP
    chunk = min(256, length)
    scale = HEAD ** (-0.5)
    group = n_bat * own

    def kernel(*refs):
        (go_ref, q_ref, k_ref, v_ref, mix_ref, qkv_ref, stat_ref, hid_ref, use_ref, wo_ref,
         w_ref, gq_ref, gk_ref, cos_ref, sin_ref) = refs[:15]
        refs = refs[15:]
        if side:
            weighted_ref, down_ref, own_ref, res_ref, ga_ref, small_in = refs[:6]
            refs = refs[6:]
        gwo_ref, gw_ref, gain_ref, out_ref = refs[:4]
        refs = refs[4:]
        if side:
            mixture_ref, small_ref = refs[:2]
            mix_away, mix_twin, mix_halves, mix_full = refs[-6:-2]
            refs = refs[2:-6] + refs[-2:]
        go_all, gm, dq, dk, dv, dqkv, local, got, hid_buf, hid_sems = refs[:10]
        full, twin, line, send_sems, recv_sems = refs[10:]
        place = Place(n_seq, n_bat)
        place.greet(all_seq=True, batch=bool(side))
        wire = Wire(send_sems, recv_sems)
        gathers = [
            SeqGather(place, wire, go_ref.at[pl.ds(r * span, span)], go_all.at[r])
            for r in range(rows)
        ]
        for gather in gathers:
            gather.start()
        for r in range(rows):
            go_all[r, place.s] = go_ref[r * span : (r + 1) * span, :]
        order = list(range(1, place.half)) + [0]
        works, from_twin = {}, {}

        def mixture_of(i):
            at = pl.ds(pl.multiple_of(i * group, group), group)
            return dot(weighted_ref[at, :], down_ref[...])

        todo = [(gather, m) for gather in gathers for m in range(1, place.half)]

        def forward(count):
            for _ in range(min(count, len(todo))):
                gather, m = todo.pop(0)
                gather.step(m)

        if side:

            def send_mixture(n):
                j = order[n]
                if n >= 2:
                    wire.settle(from_twin[order[n - 2]])
                mix_away[n % 2] = (
                    mixture_of(place.twin_at(2 * j)).astype(BF).reshape(n_bat, own, dim)
                )

            def push_mixture(n):
                j = order[n]
                from_twin[j] = wire.push(mix_away.at[n % 2], mix_twin.at[j], place.twin())

            waiting = None
            send_mixture(0)
            push_mixture(0)
            for n, j in enumerate(order):
                if n + 1 < len(order):
                    send_mixture(n + 1)
                total = mixture_of(place.seq_at(2 * j))
                if n + 1 < len(order):
                    push_mixture(n + 1)
                from_twin[j].wait_recv()
                mix_twin[j] = (
                    (total + mix_twin[j].reshape(group, dim).astype(F32))
                    .astype(BF)
                    .reshape(n_bat, own, dim)
                )
                works[j] = AcrossSum(
                    place, wire, mix_twin.at[j], mix_halves.at[j], mix_full.at[j]
                )
                if waiting is not None:
                    works[waiting].start()
                waiting = j
                forward(1)
            works[waiting].start()
        forward(max(0, len(todo) - (rows - 1) * (place.half - 1)))
        columns = lax.rsqrt(stat_ref[...] / dim + EPS).T
        scatters = [
            SeqScatter(place, wire, full.at[r], twin.at[r], line.at[r]) for r in range(rows)
        ]
        gain_sums = [[jnp.zeros((1, HEAD), F32) for _ in range(heads)] for _ in range(2)]
        middles = [works[j] for j in works]

        def attend(r, c, h):
            keys = (c + 1) * chunk
            now = slice(c * chunk, keys)
            allowed = allowed_block(use_ref[r : r + 1, :keys], c * chunk, chunk, keys)
            lanes = slice(h * HEAD, (h + 1) * HEAD)
            query = q_ref[r, h, now, :]
            key = k_ref[r, h, :keys, :]
            scores = jnp.where(allowed, dot_t(query, key) * scale, NEGATIVE)
            raised = jnp.exp(scores - jnp.max(scores, axis=-1, keepdims=True))
            probs = raised / jnp.sum(raised, axis=-1, keepdims=True)
            low = probs.astype(BF)
            grad_mix = gm[r, now, lanes]
            grad_probs = dot_t(grad_mix, v_ref[r, h, :keys, :])
            row_dot = jnp.sum(low.astype(F32) * grad_probs, axis=-1, keepdims=True)
            grad_scores = (probs * (grad_probs - row_dot)).astype(BF)
            dq[now, lanes] = scale * dot(grad_scores, key)
            dk[:keys, lanes] += scale * t_dot(grad_scores, query)
            dv[:keys, lanes] += t_dot(low, grad_mix)

        def take(r):
            gathers[r].finish()
            gm[r] = dot_t(go_all[r].reshape(length, dim), wo_ref[...]).astype(BF)

        take(0)
        for r in range(rows):
            if r:
                scatters[r - 1].pass_on()
            dk[...] = jnp.zeros_like(dk)
            dv[...] = jnp.zeros_like(dv)
            for h in range(heads):
                for c in range(length // chunk):
                    attend(r, c, h)
                    forward(1)
                    if middles:
                        middles.pop(0).middle()
            if r == 0:
                forward(len(todo))
                while middles:
                    middles.pop(0).middle()
            for which, g_ref, grads in ((0, gq_ref, dq), (1, gk_ref, dk)):
                for c in range(steps):
                    inside = slice(c * STEP, (c + 1) * STEP)
                    at = slice(r * length + c * STEP, r * length + (c + 1) * STEP)
                    row = (r * 2 + which) * steps + c
                    factor = columns[:, row : row + 1]
                    products = None
                    for h in range(heads):
                        lanes = slice(h * HEAD, (h + 1) * HEAD)
                        flat = qkv_ref[at, which * wide + h * HEAD : which * wide + (h + 1) * HEAD]
                        flat = flat * factor
                        back = turn(grads[inside, lanes], cos_ref[inside, :], -sin_ref[inside, :])
                        gain_sums[which][h] = gain_sums[which][h] + jnp.sum(
                            back * flat, axis=0, keepdims=True
                        )
                        weighted = back * g_ref[0:1, lanes]
                        grads[inside, lanes] = weighted
                        product = weighted * flat
                        products = product if products is None else products + product
                    row = which * steps + c
                    local[r, row : row + 1, :] = lane_sums(products)
            exchange = Exchange(place, wire, local.at[r], got.at[r])
            dqkv[r, :, 2 * wide :] = dv[...].astype(BF)
            if r + 1 < rows:
                take(r + 1)
            means = (exchange.total() / dim).T
            for which, grads in ((0, dq), (1, dk)):
                lanes = slice(which * wide, (which + 1) * wide)
                for c in range(steps):
                    inside = slice(c * STEP, (c + 1) * STEP)
                    at = slice(r * length + c * STEP, r * length + (c + 1) * STEP)
                    row = (r * 2 + which) * steps + c
                    factor = columns[:, row : row + 1]
                    mean = means[:, which * steps + c : which * steps + c + 1]
                    flat = qkv_ref[at, lanes] * factor
                    dqkv[r, inside, lanes] = (factor * (grads[inside, :] - flat * mean)).astype(BF)
            full[r] = dot_t(dqkv[r], w_ref[...]).astype(BF).reshape(n_seq, span, dim)
            scatters[r].start()
        for which in range(2):
            for h in range(heads):
                gain_ref[which : which + 1, h * HEAD : (h + 1) * HEAD] = gain_sums[which][h]

        def hidden_load(part):
            return pltpu.make_async_copy(
                hid_ref.at[:, pl.ds(part * 256, 256)], hid_buf.at[part % 2], hid_sems.at[part % 2]
            )

        hidden_load(0).start()
        scatters[-1].pass_on()
        for part in range(dim // 256):
            at = slice(part * 256, (part + 1) * 256)
            if part + 1 < dim // 256:
                hidden_load(part + 1).start()
            hidden_load(part).wait()
            gw_ref[at, :] = t_dot(hid_buf[part % 2], dqkv[...].reshape(col, three)).astype(BF)
            total = t_dot(mix_ref[0], go_all[0, :, :, at].reshape(length, 256))
            for r in range(1, rows):
                total = total + t_dot(mix_ref[r], go_all[r, :, :, at].reshape(length, 256))
            gwo_ref[:, at] = total.astype(BF)
        for j in works:
            works[j].finish()
            mixture_ref[j] = mix_twin[j, place.b]
        sums = jnp.zeros((1, dim), F32)
        for r in range(rows):
            at = slice(r * span, (r + 1) * span)
            if not side:
                scatters[r].finish(out_ref, at)
                continue
            x = own_ref[at, :].astype(F32)
            grad, terms = rms_back(x, rms_scale(x), ga_ref[...], scatters[r].total())
            sums = sums + jnp.sum(terms, axis=0, keepdims=True)
            out_ref[at, :] = (res_ref[at, :] + grad).astype(BF)
        if side:
            small_ref[...] = small_in[...]
            small_ref[8:9, :] = sums
            lanes = pl.ds(pl.multiple_of(place.s * wide, wide), wide)
            for which in range(2):
                small_ref[9 + which : 10 + which, lanes] = gain_ref[which : which + 1, :]
        wire.drain()

    vmem = pl.BlockSpec(memory_space=pltpu.VMEM)
    block = jax.ShapeDtypeStruct((span, dim), BF)
    stat_shape = (2 * steps, STEP)
    side_out, side_scratch = [], []
    if side:
        half = n_seq // 2
        side_out = [
            jax.ShapeDtypeStruct((half, own, dim), BF),
            jax.ShapeDtypeStruct((16, dim), F32),
        ]
        side_scratch = [
            pltpu.VMEM((2, n_bat, own, dim), BF),
            pltpu.VMEM((half, n_bat, own, dim), BF),
            pltpu.VMEM((half, 2, own // 2, dim), BF),
            pltpu.VMEM((half, 2, own, dim), BF),
        ]
    return comm_call(
        kernel,
        [
            jax.ShapeDtypeStruct((wide, dim), BF),
            jax.ShapeDtypeStruct((dim, three), BF),
            jax.ShapeDtypeStruct((2, wide), F32),
            jax.ShapeDtypeStruct((own, dim), BF),
        ]
        + side_out,
        [
            pltpu.VMEM((rows, n_seq, span, dim), BF),
            pltpu.VMEM((rows, length, wide), BF),
            pltpu.VMEM((length, wide), F32),
            pltpu.VMEM((length, wide), F32),
            pltpu.VMEM((length, wide), F32),
            pltpu.VMEM((rows, length, three), BF),
            pltpu.VMEM((rows,) + stat_shape, F32),
            pltpu.VMEM((rows, n_seq - 1) + stat_shape, F32),
            pltpu.VMEM((2, col, 256), BF),
            pltpu.SemaphoreType.DMA((2,)),
        ]
        + SeqScatter.scratch(rows, n_seq, block)
        + side_scratch,
        5 * rows * n_seq + (3 * n_seq if side else 0),
        6,
        "attend_backward",
        [vmem] * 7 + [ANY] + [vmem] * (7 + len(side or ())),
        [vmem] * (4 + len(side_out)),
    )(grad_o, q, k, v, mixed, qkv, stats, hidden, usable, w_o, w_qkv, gain_q, gain_k,
      cos_wide, sin_wide, *(side or ()))


class Across:
    def __init__(self, place, wire, src, at):
        self.place, self.wire, self.src, self.at = place, wire, src, at
        self.half = src.shape[0] // 2

    def start(self):
        place, own = self.place, self.at(self.place.b)
        self.to_x = self.wire.push(self.src, own, place.x_peer())
        self.to_y = self.wire.push(self.src, own, place.y_peer())

    def relay(self):
        place, half = self.place, self.half
        self.to_x.wait_recv()
        top = self.at(place.bat_x).at[pl.ds(0, half)]
        self.top = self.wire.push(top, top, place.y_peer())
        self.to_y.wait_recv()
        low = self.at(place.bat_y).at[pl.ds(half, half)]
        self.low = self.wire.push(low, low, place.x_peer())

    def finish(self):
        self.top.wait_recv()
        self.low.wait_recv()


class AcrossSum:
    def __init__(self, place, wire, group, halves, full):
        self.place, self.wire = place, wire
        self.group, self.halves, self.full = group, halves, full
        self.half = halves.shape[1]

    def start(self):
        place, half = self.place, self.half
        far = self.group.at[place.bat_d]
        self.top = self.wire.push(far.at[pl.ds(0, half)], self.halves.at[0], place.x_peer())
        self.low = self.wire.push(far.at[pl.ds(half, half)], self.halves.at[1], place.y_peer())

    def middle(self):
        place, half = self.place, self.half
        self.top.wait_recv()
        add_into(self.group.at[place.bat_y].at[pl.ds(0, half)], self.halves.at[0])
        self.low.wait_recv()
        add_into(self.group.at[place.bat_x].at[pl.ds(half, half)], self.halves.at[1])
        self.y = self.wire.push(self.group.at[place.bat_y], self.full.at[0], place.y_peer())
        self.x = self.wire.push(self.group.at[place.bat_x], self.full.at[1], place.x_peer())

    def finish(self):
        self.y.wait_recv()
        self.x.wait_recv()
        add_into(self.group.at[self.place.b], self.full.at[0], self.full.at[1])


def load_first(weights, w_out, mine, flags, small, rows, n_seq, n_bat):
    shard, dim = weights[0].shape
    wide = dim // n_seq
    own = mine.shape[0]
    span = own // rows
    slots = 15 * n_seq + n_seq * n_bat

    def kernel(*refs):
        parts = refs[:3]
        wo_ref, x_ref, flag_ref, small_ref = refs[3:7]
        w_ref, wo_all, x_col, flag_col, small_all = refs[7:12]
        buffers = refs[12:17]
        own_sems, cut_sems, x_sems, send_sems, recv_sems = refs[17:]
        place = Place(n_seq, n_bat)
        place.greet(all_seq=True)
        wire = Wire(send_sems, recv_sems)
        small_work = FullGather(place, wire, small_ref, small_all)
        flag_work = SeqGather(place, wire, flag_ref, flag_col)
        x_works = [
            SeqGather(place, wire, x_ref.at[pl.ds(r * span, span)], x_col.at[r])
            for r in range(rows)
        ]
        small_work.start()
        flag_work.start()

        def cut(k):
            return pl.ds(pl.multiple_of(place.seq_at(k) * wide, wide), wide)

        def columns(m):
            return pl.ds(m * wide, wide)

        own_cuts = []
        for m in range(3):
            copy = pltpu.make_async_copy(
                parts[m].at[:, cut(0)], buffers[0].at[:, columns(m)], cut_sems.at[m]
            )
            copy.start()
            own_cuts.append(copy)
        cuts = {}
        for k in range(1, n_seq):
            for m in range(3):
                cuts[k, m] = wire.push(
                    parts[m].at[:, cut(k)],
                    w_ref.at[place.s, place.b, :, columns(m)],
                    place.seq_peer(k),
                )
        wo_work = Across(place, wire, wo_ref, lambda i: wo_all.at[i])
        wo_work.start()
        for work in x_works:
            work.start()
        for copy in own_cuts:
            copy.wait()
        spreads = []

        def spread(src, from_seq):
            work = Across(place, wire, src, lambda i: w_ref.at[from_seq, i])
            work.start()
            spreads.append(work)

        spread(buffers[0], place.s)
        own_w = pltpu.make_async_copy(buffers[0], w_ref.at[place.s, place.b], own_sems.at[0])
        own_w.start()
        copies = [own_w]
        fetched = pltpu.make_async_copy(x_ref, buffers[4], own_sems.at[4])
        fetched.start()
        fetched.wait()
        for r in range(rows):
            copy = pltpu.make_async_copy(
                buffers[4].at[pl.ds(r * span, span)], x_col.at[r, place.s], x_sems.at[r]
            )
            copy.start()
            copies.append(copy)
        copies += [
            keep_own(src, dst, buffers[i + 1], own_sems.at[i + 1])
            for i, (src, dst) in enumerate(
                (
                    (wo_ref, wo_all.at[place.b]),
                    (flag_ref, flag_col.at[place.s]),
                    (small_ref, small_all.at[place.s, place.b]),
                )
            )
        ]
        for j in range(1, place.half):
            small_work.step(j)
            flag_work.step(j)
        for k in range(1, n_seq):
            for m in range(3):
                cuts[k, m].wait_recv()
            spread(w_ref.at[place.seq_at(-k), place.b], place.seq_at(-k))
        for j in range(place.half):
            small_work.collect(j)
        todo = [(work, m) for work in x_works for m in range(1, place.half)]

        def forward(count):
            for _ in range(min(count, len(todo))):
                work, m = todo.pop(0)
                work.step(m)

        forward(1)
        wo_work.relay()
        for work in spreads:
            work.relay()
            forward(1)
        forward(len(todo))
        wo_work.finish()
        for work in spreads:
            work.finish()
        for work in [small_work, flag_work] + x_works:
            work.finish()
        for copy in copies:
            copy.wait()
        wire.drain()

    every = (n_seq, n_bat)
    one = jax.ShapeDtypeStruct((shard, 3 * wide), BF)
    x_one = jax.ShapeDtypeStruct((span, dim), BF)
    blocks = (one, w_out, x_one, flags, small)
    leads = (every, (n_bat,), (rows, n_seq), (n_seq,), every)
    held = (one, w_out, flags, small, mine)
    return comm_call(
        kernel,
        [shape_of(lead, block) for lead, block in zip(leads, blocks)],
        [pltpu.VMEM(block.shape, block.dtype) for block in held]
        + [pltpu.SemaphoreType.DMA((n,)) for n in (5, 3, rows)],
        slots,
        1,
        "load_first",
        [ANY] * 7,
    )(*weights, w_out, mine, flags, small)


def pick_units(first, experts, units, part):
    at_expert = lax.broadcasted_iota(jnp.int32, (experts, units), 0)
    at_unit = lax.broadcasted_iota(jnp.int32, (experts, units), 1)
    low = (at_expert - first) * part
    return jnp.where((at_unit >= low) & (at_unit < low + part), 1.0, 0.0).astype(F32)


def experts_forward(normed, gates, dy_all, gate, up, w_down, n_seq, n_bat):
    own, dim = normed.shape
    local_experts, depth, hidden = gate.shape
    units = w_down.shape[0]
    part = hidden // n_seq
    group = n_bat * own
    tokens = n_seq * group
    experts = gates.shape[0]
    slots = 64 + 2 * n_seq * n_bat + 2 * local_experts * n_seq

    def kernel(*refs):
        x_ref, gate_ref, dy_ref, wg_ref, wu_ref, down_ref = refs[:6]
        x_all, weighted_ref, grad_ref, term_ref, gu_ref = refs[6:11]
        gates_all, back, gate_buf, x_buf, dy_buf, keep = refs[11:17]
        own_sems, x_sems, dy_sems, gu_sems, send_sems, recv_sems = refs[17:]
        place = Place(n_seq, n_bat)
        place.greet(all_seq=True)
        wire = Wire(send_sems, recv_sems)
        gate_work = FullGather(place, wire, gate_ref, gates_all)
        gate_work.start()
        gates_all[place.s, place.b] = gate_ref[...]
        line = Line(place, wire, x_ref, lambda i: x_all.at[place.chip(i), place.b])
        line.start()
        works = []
        here = [place.chip(place.origin(m)) for m in range(place.half)]
        there = [place.chip_twin(place.origin(m)) for m in range(place.half)]
        for j in range(place.half):
            at_seq = here[j]
            src = x_ref if j == 0 else x_all.at[at_seq, place.b]
            works.append(
                Across(place, wire, src, lambda i, at_seq=at_seq: x_all.at[at_seq, i])
            )
        works[0].start()
        own = keep_own(x_ref, x_all.at[place.s, place.b], keep, own_sems.at[0])
        selected = pick_units(place.b * local_experts, experts, units, part)

        def dy_load(g, slot):
            return pltpu.make_async_copy(dy_ref.at[g], dy_buf.at[slot], dy_sems.at[slot])

        def rows_of(g):
            return pl.ds(pl.multiple_of(g * group, group), group)

        def backs(first, count):
            dy_load(first, first % 2).start()
            for g in range(first, first + count):
                if g + 1 < first + count:
                    dy_load(g + 1, (g + 1) % 2).start()
                dy_load(g, g % 2).wait()
                block = dy_buf[g % 2].reshape(group, dim)
                back[g * group : (g + 1) * group, :] = dot_t(block, down_ref[...])

        gu_copies = ([], [])

        def send_units(m, ref, offsets):
            for k in offsets:
                lanes = pl.ds(pl.multiple_of(place.seq_at(k) * part, part), part)
                for e in range(local_experts):
                    src = ref.at[e, :, lanes]
                    dst = gu_ref.at[place.s, :, pl.ds(m * units + e * part, part)]
                    if k:
                        gu_copies[m].append(wire.push(src, dst, place.seq_peer(k)).wait_recv)
                    else:
                        copy = pltpu.make_async_copy(src, dst, gu_sems.at[m, e])
                        copy.start()
                        gu_copies[m].append(copy.wait)

        passed = []

        def hand_over(j):
            at_seq = here[j]
            works[j].finish()
            if j == 0:
                own.wait()
            passed.append(wire.push(x_all.at[at_seq], x_all.at[at_seq], place.twin()))

        loads = {}

        def fetch(g, slot):
            loads[slot] = pltpu.make_async_copy(x_all.at[g], x_buf.at[slot], x_sems.at[slot])
            loads[slot].start()

        def weight(m):
            return gu_ref[:, :, m * units : (m + 1) * units].reshape(dim, units)

        def gate_on(g, slot):
            loads[slot].wait()
            gate_buf[rows_of(g), :] = dot(x_buf[slot].reshape(group, dim), weight(0))

        def units_on(g, slot, gated=False):
            if not gated:
                loads[slot].wait()
            at = rows_of(g)
            block = x_buf[slot].reshape(group, dim)
            gate_pre = gate_buf[at, :] if gated else dot(block, weight(0))
            up_pre = dot(block, weight(1))
            sig = jax.nn.sigmoid(gate_pre)
            silu = gate_pre * sig
            active = (silu * up_pre).astype(BF).astype(F32)
            grad_back = back[at, :]
            product = active * grad_back
            wide_gates = []
            for i in range(n_bat):
                inside = slice(i * x_ref.shape[0], (i + 1) * x_ref.shape[0])
                wide_gates.append(
                    lax.dot_general(
                        gates_all[g, i],
                        selected,
                        (((0,), (0,)), ((), ())),
                        precision=HIGHEST,
                        preferred_element_type=F32,
                    )
                )
                term_ref[g, i] = lax.dot_general(
                    selected,
                    product[inside, :],
                    (((1,), (1,)), ((), ())),
                    precision=HIGHEST,
                    preferred_element_type=F32,
                )
            wide_gate = jnp.concatenate(wide_gates, axis=0)
            weighted_ref[at, :] = (active * wide_gate).astype(BF)
            grad_active = grad_back * wide_gate
            grad_ref[at, :units] = (
                grad_active * up_pre * sig * (1.0 + gate_pre * (1.0 - sig))
            ).astype(BF)
            grad_ref[at, units:] = (grad_active * silu).astype(BF)

        half = place.half
        per = n_seq // half
        offsets = list(range(1, n_seq)) + [0]
        for j in range(1, half):
            backs((j - 1) * per, per)
            gate_work.step(j)
            gate_work.collect(j - 1)
            line.step(j)
            works[j].start()
            works[j - 1].relay()
            if j < half - 1:
                send_units(0, wg_ref, offsets[2 * j - 2 : 2 * j])
            else:
                send_units(0, wg_ref, offsets[2 * j - 2 :])
                send_units(1, wu_ref, offsets)
        backs((half - 1) * per, per)
        gate_work.collect(half - 1)
        gate_work.finish()
        hand_over(0)
        fetch(here[0], 0)
        for wait in gu_copies[0]:
            wait()
        gate_on(here[0], 0)
        passed[0].wait_recv()
        fetch(there[0], 1)
        hand_over(1)
        fetch(here[1], 2)
        gate_on(there[0], 1)
        gate_on(here[1], 2)
        works[half - 1].relay()
        passed[1].wait_recv()
        fetch(there[1], 3)
        gate_on(there[1], 3)
        for wait in gu_copies[1]:
            wait()
        for j in range(half):
            units_on(here[j], (2 * j) % 4, j < 2)
            if j + 2 < half:
                hand_over(j + 2)
                fetch(here[j + 2], (2 * j) % 4)
            units_on(there[j], (2 * j + 1) % 4, j < 2)
            if j + 2 < half:
                passed[j + 2].wait_recv()
                fetch(there[j + 2], (2 * j + 1) % 4)
        wire.drain()

    vmem = pl.BlockSpec(memory_space=pltpu.VMEM)
    return comm_call(
        kernel,
        [
            shape_of((n_seq, n_bat), normed),
            jax.ShapeDtypeStruct((tokens, units), BF),
            jax.ShapeDtypeStruct((tokens, 2 * units), BF),
            shape_of((n_seq, n_bat), gates),
            jax.ShapeDtypeStruct((n_seq, depth, 2 * units), BF),
        ],
        [
            pltpu.VMEM((n_seq, n_bat) + gates.shape, F32),
            pltpu.VMEM((tokens, units), F32),
            pltpu.VMEM((tokens, units), F32),
            pltpu.VMEM((4, n_bat, own, dim), BF),
            pltpu.VMEM((2, n_bat, own, dim), BF),
            pltpu.VMEM((own, dim), BF),
            pltpu.SemaphoreType.DMA((1,)),
            pltpu.SemaphoreType.DMA((4,)),
            pltpu.SemaphoreType.DMA((2,)),
            pltpu.SemaphoreType.DMA((2, local_experts)),
        ],
        slots,
        4,
        "experts_forward",
        [ANY, vmem, ANY, ANY, ANY, vmem],
        [ANY, vmem, vmem, vmem, vmem],
    )(normed, gates, dy_all, gate, up, w_down)


def experts_backward(
    grad_pre, weighted, w_gu, terms, x_all, dy_all, residual, dy_own, gain_mlp, router, probs, chosen,
    local_experts, n_seq, n_bat,
):
    own = residual.shape[0]
    tokens, dim = x_all.shape
    units = weighted.shape[1]
    part = units // local_experts
    group = n_bat * own
    depth = dim // n_seq
    hidden = n_seq * part
    half = n_seq // 2
    slots = 128 + 2 * n_seq * n_bat
    block = jax.ShapeDtypeStruct((own, dim), BF)
    term = jax.ShapeDtypeStruct(terms.shape[2:], F32)

    def kernel(*refs):
        grad_ref, weighted_ref, gu_ref, term_in, x_ref, dy_ref = refs[:6]
        res_ref, own_dy_ref, gm_ref, router_ref, probs_ref, chosen_ref = refs[6:12]
        out_ref, low_ref, small_ref, gate_out, up_out, down_out = refs[12:18]
        refs = refs[18:]
        away, twin, halves, full, line = refs[:5]
        columns, sent, got, column_sems, term_out = refs[5:10]
        term_scratch = refs[10:15]
        send_sems, recv_sems = refs[15:]
        place = Place(n_seq, n_bat)
        place.greet(all_seq=True)
        wire = Wire(send_sems, recv_sems)
        term_work = FullScatter(place, wire, term_in, term_out, *term_scratch)
        term_work.start()

        def product(i):
            at = pl.ds(pl.multiple_of(i * group, group), group)
            return dot_t(grad_ref[at, :], gu_ref[...])

        order = list(range(1, half)) + [0]
        from_twin, from_seq, works = {}, {}, {}

        def send(j):
            from_twin[j] = wire.push(away.at[j], twin.at[j], place.twin())

        chunks = [("x", k) for k in list(range(1, n_seq)) + [0]] + [
            ("y", k) for k in range(dim // 256)
        ]

        def chunk_load(n):
            kind, k = chunks[n]
            if kind == "x":
                src = x_ref.at[:, pl.ds(pl.multiple_of(place.seq_at(k) * depth, depth), depth)]
            else:
                src = dy_ref.at[:, pl.ds(k * 256, 256)]
            return pltpu.make_async_copy(src, columns.at[n % 2], column_sems.at[n % 2])

        chunk_load(0).start()

        def pair(j):
            part_sum = product(place.seq_at(2 * j))
            from_twin[j].wait_recv()
            twin[j] = (
                (part_sum + twin[j].reshape(group, dim).astype(F32))
                .astype(BF)
                .reshape(n_bat, own, dim)
            )
            works[j] = AcrossSum(place, wire, twin.at[j], halves.at[j], full.at[j])

        arrivals = []
        done = [0]

        def work_chunks(count):
            for n in range(done[0], min(done[0] + count, len(chunks))):
                done[0] = n + 1
                if n + 1 < len(chunks):
                    chunk_load(n + 1).start()
                chunk_load(n).wait()
                kind, k = chunks[n]
                if kind == "y":
                    down_out[:, k * 256 : (k + 1) * 256] = t_dot(
                        weighted_ref[...], columns[n % 2]
                    )
                else:
                    value = t_dot(columns[n % 2], grad_ref[...]).astype(BF)
                    if k == 0:
                        got[place.s] = value
                    else:
                        sent[k] = value
                if n and chunks[n - 1][0] == "x" and chunks[n - 1][1]:
                    k = chunks[n - 1][1]
                    arrivals.append(wire.push(sent.at[k], got.at[place.s], place.seq_peer(k)))

        def pass_on(j):
            works[j].finish()
            if j:
                from_seq[j] = wire.push(twin.at[j, place.b], line.at[j], place.seq_peer(2 * j))

        work_chunks(1)
        waiting = None
        for j in order:
            away[j] = product(place.twin_at(2 * j)).astype(BF).reshape(n_bat, own, dim)
            if waiting is not None:
                send(waiting)
            waiting = j
            work_chunks(1)
        first, rest = order[:2], order[2:]
        pair(order[0])
        send(waiting)
        for j in first[1:]:
            pair(j)
            works[first[0]].start()
        works[first[-1]].start()
        for j in rest:
            pair(j)
        term_order = term_work.order()
        for j in term_order:
            term_work.pair(j)
        works[first[0]].middle()
        work_chunks(1)
        for j in first[1:]:
            works[j].middle()
        for j in rest:
            works[j].start()
        for j in term_order:
            term_work.merge(j)
        for j in first:
            work_chunks(3)
            pass_on(j)
        for j in rest:
            work_chunks(1)
            works[j].middle()
        for j in rest:
            work_chunks(4)
            pass_on(j)
        work_chunks(len(chunks))
        for copy in arrivals:
            copy.wait_recv()
        for i in range(n_seq):
            lanes = slice(i * part, (i + 1) * part)
            for e in range(local_experts):
                gate_out[e, :, lanes] = got[i, :, e * part : (e + 1) * part].astype(F32)
                up_out[e, :, lanes] = got[i, :, units + e * part : units + (e + 1) * part].astype(
                    F32
                )
        term_work.finish()
        for j in range(1, half):
            from_seq[j].wait_recv()
        total = twin[0, place.b].astype(F32)
        for j in range(1, half):
            total = total + line[j].astype(F32)
        grad_chosen = term_out[...] * chosen_ref[...]
        probs = probs_ref[...]
        grad_logits = probs * (
            grad_chosen - jnp.sum(probs * grad_chosen, axis=0, keepdims=True)
        )
        small_ref[...] = jnp.zeros_like(small_ref)
        residual = res_ref[...]
        scale = rms_scale(residual)
        normal = residual * scale
        normed = (normal * gm_ref[...]).astype(BF).astype(F32)
        experts = probs.shape[0]
        small_ref[0:experts, :] = lax.dot_general(
            grad_logits, normed, (((1,), (0,)), ((), ())), precision=HIGHEST,
            preferred_element_type=F32,
        )
        total = total + lax.dot_general(
            grad_logits, router_ref[...], (((0,), (0,)), ((), ())), precision=HIGHEST,
            preferred_element_type=F32,
        )
        grad, terms_of = rms_back(residual, scale, gm_ref[...], total)
        small_ref[experts + 3 : experts + 4, :] = jnp.sum(terms_of, axis=0, keepdims=True)
        grad = own_dy_ref[...].astype(F32) + grad
        out_ref[...] = grad
        low_ref[...] = grad.astype(BF)
        wire.drain()

    vmem = pl.BlockSpec(memory_space=pltpu.VMEM)
    expert = jax.ShapeDtypeStruct((local_experts, depth, hidden), F32)
    return comm_call(
        kernel,
        [
            jax.ShapeDtypeStruct((own, dim), F32),
            jax.ShapeDtypeStruct((own, dim), BF),
            jax.ShapeDtypeStruct((16, dim), F32),
            expert,
            expert,
            jax.ShapeDtypeStruct((units, dim), F32),
        ],
        [
            pltpu.VMEM((half, n_bat, own, dim), BF),
            pltpu.VMEM((half, n_bat, own, dim), BF),
            pltpu.VMEM((half, 2, own // 2, dim), BF),
            pltpu.VMEM((half, 2, own, dim), BF),
            pltpu.VMEM((half, own, dim), BF),
            pltpu.VMEM((2, tokens, 256), BF),
            pltpu.VMEM((n_seq, depth, 2 * units), BF),
            pltpu.VMEM((n_seq, depth, 2 * units), BF),
            pltpu.SemaphoreType.DMA((2,)),
            pltpu.VMEM(term.shape, F32),
        ]
        + FullScatter.scratch(n_seq, n_bat, term),
        slots,
        5,
        "experts_backward",
        [vmem] * 3 + [ANY] * 3 + [vmem] * 6,
        [vmem] * 6,
    )(grad_pre, weighted, w_gu, terms, x_all, dy_all, residual, dy_own, gain_mlp, router, probs, chosen)


def store_last(grad_w, grad_wo, small, mixture, n_seq, n_bat):
    one = jax.ShapeDtypeStruct(grad_w.shape[2:], grad_w.dtype)
    shard, three = one.shape
    wide = three // 3
    wo_one = jax.ShapeDtypeStruct(grad_wo.shape[1:], grad_wo.dtype)
    small_one = jax.ShapeDtypeStruct((16, 2 * shard), small.dtype)
    half = n_seq // 2
    dim = wo_one.shape[1]
    slots = 64 + n_seq * n_bat + 5 * n_seq

    def kernel(*refs):
        w_ref, wo_ref, small_ref, mix_ref = refs[:4]
        q_out, k_out, v_out, wo_out, small_out, mix_out = refs[4:10]
        w_sum, w_halves, w_full, w_got, wo_sum, wo_halves, wo_full, line = refs[10:18]
        small_scratch = refs[18:23]
        w_sems, wo_sem, send_sems, recv_sems = refs[23:]
        place = Place(n_seq, n_bat)
        place.greet(all_seq=True)
        wire = Wire(send_sems, recv_sems)

        def pick(i, m):
            tile = i * (n_bat // 2) + lax.div(m, 2)
            return small_ref.at[:, pl.ds(pl.multiple_of(tile * 2 * shard, 128), 2 * shard)]

        small_work = FullScatter(place, wire, small_ref, small_out, *small_scratch, pick)
        small_work.start()
        order = list(range(1, n_seq)) + [0]
        loads = {}
        for k in order:
            loads[k] = pltpu.make_async_copy(
                w_ref.at[place.seq_at(k)], w_sum.at[k], w_sems.at[k]
            )
            loads[k].start()
        wo_load = pltpu.make_async_copy(wo_ref, wo_sum, wo_sem.at[0])
        wo_load.start()
        works = {}
        for k in order:
            loads[k].wait()
            works[k] = AcrossSum(place, wire, w_sum.at[k], w_halves.at[k], w_full.at[k])
            works[k].start()
        wo_load.wait()
        wo_work = AcrossSum(place, wire, wo_sum, wo_halves, wo_full)
        wo_work.start()
        term_order = small_work.order()
        for j in term_order:
            small_work.pair(j)
        mix_line = {
            j: wire.push(mix_ref.at[j], line.at[j], place.seq_peer(2 * j)) for j in range(1, half)
        }
        arrivals = []
        ready = None

        def ship(k):
            if k:
                arrivals.append(
                    wire.push(w_sum.at[k, place.b], w_got.at[place.s], place.seq_peer(k))
                )

        for k in order:
            works[k].middle()
        wo_work.middle()
        for j in term_order:
            small_work.merge(j)
        for k in order:
            works[k].finish()
            if ready is not None:
                ship(ready)
            ready = k
        w_got[place.s] = w_sum[0, place.b]
        wo_work.finish()
        wo_out[...] = wo_sum[place.b].astype(F32)
        small_work.finish()
        for copy in arrivals:
            copy.wait_recv()
        for i in range(n_seq):
            at = slice(i * wide, (i + 1) * wide)
            for m, out in enumerate((q_out, k_out, v_out)):
                out[:, at] = w_got[i, :, m * wide : (m + 1) * wide].astype(F32)
        for copy in mix_line.values():
            copy.wait_recv()
        total = mix_ref[0].astype(F32)
        for j in range(1, half):
            total = total + line[j].astype(F32)
        mix_out[...] = total
        wire.drain()

    vmem = pl.BlockSpec(memory_space=pltpu.VMEM)
    matrix = jax.ShapeDtypeStruct((shard, dim), F32)
    return comm_call(
        kernel,
        [matrix] * 4 + [small_one, jax.ShapeDtypeStruct(mixture.shape[1:], F32)],
        [
            pltpu.VMEM((n_seq, n_bat, shard, three), BF),
            pltpu.VMEM((n_seq, 2, shard // 2, three), BF),
            pltpu.VMEM((n_seq, 2, shard, three), BF),
            pltpu.VMEM((n_seq, shard, three), BF),
            pltpu.VMEM((n_bat, shard, dim), BF),
            pltpu.VMEM((2, shard // 2, dim), BF),
            pltpu.VMEM((2, shard, dim), BF),
            pltpu.VMEM(mixture.shape, BF),
        ]
        + FullScatter.scratch(n_seq, n_bat, small_one)
        + [pltpu.SemaphoreType.DMA((n_seq,)), pltpu.SemaphoreType.DMA((1,))],
        slots,
        8,
        "store_last",
        [ANY] * 3 + [vmem],
        [vmem] * 6,
    )(grad_w, grad_wo, small, mixture)


def finish(residual, mixture, grads):
    count = len(grads)

    def kernel(*refs):
        res_ref, mix_ref = refs[:2]
        ins, out_ref, outs = refs[2 : 2 + count], refs[2 + count], refs[3 + count : 3 + 2 * count]
        buffers, sems = refs[3 + 2 * count : 3 + 3 * count], refs[-1]
        loads = []
        for i in range(count):
            copy = pltpu.make_async_copy(ins[i], buffers[i], sems.at[0, i])
            copy.start()
            loads.append(copy)
        out_ref[...] = (res_ref[...] + mix_ref[...]).astype(BF)
        stores = []
        for i in range(count):
            loads[i].wait()
            copy = pltpu.make_async_copy(buffers[i], outs[i], sems.at[1, i])
            copy.start()
            stores.append(copy)
        for copy in stores:
            copy.wait()

    vmem = pl.BlockSpec(memory_space=pltpu.VMEM)
    return pl.pallas_call(
        kernel,
        out_shape=[jax.ShapeDtypeStruct(residual.shape, BF)]
        + [jax.ShapeDtypeStruct(grad.shape, grad.dtype) for grad in grads],
        in_specs=[vmem] * 2 + [ANY] * count,
        out_specs=[vmem] + [ANY] * count,
        scratch_shapes=[pltpu.VMEM(grad.shape, grad.dtype) for grad in grads]
        + [pltpu.SemaphoreType.DMA((2, count))],
        compiler_params=pltpu.CompilerParams(vmem_limit_bytes=VMEM_LIMIT),
        name="finish",
    )(residual, mixture, *grads)


def load_inputs(qkv_cut, w_out, mine, flags, small, gu_cut, dy_own, n_seq, n_bat):
    n_in = 7
    slots = 4 * n_seq * n_bat + 5 * n_seq + 2 * n_bat

    def kernel(*refs):
        cut_ref, wo_ref, x_ref, flag_ref, small_ref, gu_ref, dy_ref = refs[:n_in]
        w_ref, wo_all, x_col, flag_col, small_all, gu_all, dy_all = refs[n_in : 2 * n_in]
        buffers = refs[2 * n_in : 3 * n_in]
        own_sems, send_sems, recv_sems = refs[3 * n_in :]
        place = Place(n_seq, n_bat)
        place.greet(all_seq=True)
        wire = Wire(send_sems, recv_sems)
        small_work = FullGather(place, wire, small_ref, small_all)
        flag_work = SeqGather(place, wire, flag_ref, flag_col)
        x_work = SeqGather(place, wire, x_ref, x_col)
        dy_work = FullGather(place, wire, dy_ref, dy_all)
        small_work.start()
        flag_work.start()
        cuts = [
            wire.push(cut_ref.at[place.seq_at(k)], w_ref.at[place.s, place.b], place.seq_peer(k))
            for k in range(1, n_seq)
        ]
        ends = [
            wire.push(wo_ref, wo_all.at[place.b], place.bat_peer(k)) for k in range(1, n_bat)
        ]
        ends += [
            wire.push(cut_ref.at[place.s], w_ref.at[place.s, place.b], place.bat_peer(k))
            for k in range(1, n_bat)
        ]
        x_work.start()
        own = [
            keep_own(src, dst, buffers[i], own_sems.at[i])
            for i, (src, dst) in enumerate(
                (
                    (cut_ref.at[place.s], w_ref.at[place.s, place.b]),
                    (wo_ref, wo_all.at[place.b]),
                    (x_ref, x_col.at[place.s]),
                    (flag_ref, flag_col.at[place.s]),
                    (small_ref, small_all.at[place.s, place.b]),
                    (gu_ref.at[place.s], gu_all.at[place.s]),
                    (dy_ref, dy_all.at[place.s, place.b]),
                )
            )
        ]
        ends += [
            wire.push(gu_ref.at[place.seq_at(k)], gu_all.at[place.s], place.seq_peer(k))
            for k in range(1, n_seq)
        ]
        dy_work.start()
        for j in range(1, place.half):
            small_work.step(j)
            flag_work.step(j)
        for k in range(1, n_seq):
            cuts[k - 1].wait_recv()
            block = w_ref.at[place.seq_at(-k), place.b]
            ends += [wire.push(block, block, place.bat_peer(m)) for m in range(1, n_bat)]
        for j in range(place.half):
            small_work.collect(j)
        for j in range(1, place.half):
            x_work.step(j)
        for j in range(1, place.half):
            dy_work.step(j)
            dy_work.collect(j - 1)
        dy_work.collect(place.half - 1)
        for work in (small_work, flag_work, x_work, dy_work):
            work.finish()
        for copy in ends:
            copy.wait_recv()
        for copy in own:
            copy.wait()
        wire.drain()

    every = (n_seq, n_bat)
    one = jax.ShapeDtypeStruct(qkv_cut.shape[1:], qkv_cut.dtype)
    gu_one = jax.ShapeDtypeStruct(gu_cut.shape[1:], gu_cut.dtype)
    blocks = (one, w_out, mine, flags, small, gu_one, dy_own)
    leads = (every, (n_bat,), (n_seq,), (n_seq,), every, (n_seq,), every)
    return comm_call(
        kernel,
        [shape_of(lead, block) for lead, block in zip(leads, blocks)],
        [pltpu.VMEM(block.shape, block.dtype) for block in blocks]
        + [pltpu.SemaphoreType.DMA((n_in,))],
        slots,
        1,
        "load_inputs",
        [ANY] * n_in,
    )(qkv_cut, w_out, mine, flags, small, gu_cut, dy_own)


def store_grads(grad_w, grad_wo, grad_gu, small, n_seq, n_bat):
    one = jax.ShapeDtypeStruct(grad_w.shape[2:], grad_w.dtype)
    wo_one = jax.ShapeDtypeStruct(grad_wo.shape[1:], grad_wo.dtype)
    gu_one = jax.ShapeDtypeStruct(grad_gu.shape[1:], grad_gu.dtype)
    small_one = jax.ShapeDtypeStruct(small.shape[2:], small.dtype)
    slots = 2 * n_seq * n_bat + 2 * n_seq + n_bat

    def kernel(*refs):
        w_ref, wo_ref, gu_ref, small_ref = refs[:4]
        w_out_ref, wo_out_ref, gu_out_ref, small_out_ref = refs[4:8]
        w_sum, w_got, wo_sum, wo_got, gu_buf, cut_buf = refs[8:14]
        small_scratch = refs[14:19]
        w_sems, sems, send_sems, recv_sems = refs[19:]
        place = Place(n_seq, n_bat)
        place.greet(all_seq=True)
        wire = Wire(send_sems, recv_sems)
        small_work = FullScatter(
            place, wire, small_ref, small_out_ref, *small_scratch
        )
        small_work.start()
        got, loads = {}, {}
        for i in list(range(1, n_seq)) + [0]:
            to_seq = place.seq_at(i)
            for k in range(1, n_bat):
                got[i, k] = wire.push(
                    w_ref.at[to_seq, place.bat_at(k)], w_got.at[i, k - 1], place.bat_peer(k)
                )
            loads[i] = pltpu.make_async_copy(
                w_ref.at[to_seq, place.b], w_sum.at[i], w_sems.at[i]
            )
            loads[i].start()
        wo_pushed = [
            wire.push(wo_ref.at[place.bat_at(k)], wo_got.at[k - 1], place.bat_peer(k))
            for k in range(1, n_bat)
        ]
        wo_load = pltpu.make_async_copy(wo_ref.at[place.b], wo_sum, sems.at[0])
        wo_load.start()
        ends = [
            wire.push(gu_ref.at[place.seq_at(k)], gu_out_ref.at[place.s], place.seq_peer(k))
            for k in range(1, n_seq)
        ]
        gu_own = keep_own(gu_ref.at[place.s], gu_out_ref.at[place.s], gu_buf, sems.at[1])
        order = small_work.order()
        for j in order:
            small_work.pair(j)
        for i in list(range(1, n_seq)) + [0]:
            loads[i].wait()
            for k in range(1, n_bat):
                got[i, k].wait_recv()
            add_into(w_sum.at[i], *[w_got.at[i, k] for k in range(n_bat - 1)])
            if i:
                ends.append(
                    wire.push(w_sum.at[i], w_out_ref.at[place.s], place.seq_peer(i))
                )
        w_own = pltpu.make_async_copy(w_sum.at[0], w_out_ref.at[place.s], sems.at[2])
        w_own.start()
        for j in order:
            small_work.merge(j)
        wo_load.wait()
        for copy in wo_pushed:
            copy.wait_recv()
        add_into(wo_sum, *[wo_got.at[k] for k in range(n_bat - 1)])
        wo_out_ref[...] = wo_sum[...].astype(F32)
        small_work.finish()
        for copy in ends:
            copy.wait_recv()
        gu_own.wait()
        w_own.wait()
        wire.drain()

    vmem = pl.BlockSpec(memory_space=pltpu.VMEM)
    return comm_call(
        kernel,
        [
            shape_of((n_seq,), one),
            jax.ShapeDtypeStruct(wo_one.shape, F32),
            shape_of((n_seq,), gu_one),
            small_one,
        ],
        [
            pltpu.VMEM((n_seq,) + one.shape, one.dtype),
            pltpu.VMEM((n_seq, n_bat - 1) + one.shape, one.dtype),
            pltpu.VMEM(wo_one.shape, wo_one.dtype),
            pltpu.VMEM((n_bat - 1,) + wo_one.shape, wo_one.dtype),
            pltpu.VMEM(gu_one.shape, gu_one.dtype),
            pltpu.VMEM(one.shape, one.dtype),
        ]
        + FullScatter.scratch(n_seq, n_bat, small_one)
        + [pltpu.SemaphoreType.DMA((n_seq,)), pltpu.SemaphoreType.DMA((3,))],
        slots,
        8,
        "store_grads",
        [ANY] * 4,
        [ANY, vmem, ANY, vmem],
    )(grad_w, grad_wo, grad_gu, small)


def shards(
    tokens,
    lengths,
    key_mask,
    top_experts,
    attn_gain,
    query_gain,
    key_gain,
    mlp_gain,
    w_query,
    w_key,
    w_value,
    w_out,
    w_router,
    expert_gate,
    expert_up,
    expert_down,
    cotangent,
):
    n_seq = lax.axis_size("seq")
    n_bat = lax.axis_size("batch")
    seq = lax.axis_index("seq")
    bat = lax.axis_index("batch")
    rows, span, dim = tokens.shape
    own = rows * span
    col = n_seq * own
    length = n_seq * span
    shard = w_query.shape[0]
    wide = dim // n_seq
    heads = wide // HEAD
    local_experts, depth, hidden_units = expert_gate.shape
    part = hidden_units // n_seq
    experts = local_experts * n_bat

    mine = tokens.reshape(own, dim)
    dy_own = cotangent.reshape(own, dim)
    small = jnp.concatenate(
        [w_router.T, jnp.stack([attn_gain, query_gain, key_gain, mlp_gain])], axis=0
    )
    positions_own = seq * span + jnp.arange(span, dtype=jnp.int32)
    flags = pack((positions_own[None, :] < lengths[:, None]) & (key_mask == 1))
    units = local_experts * part
    fused = (
        n_bat == 4
        and part % 128 == 0
        and own == 128
        and shard % 32 == 0
        and n_seq == 8
        and shard == 64
        and experts == 8
        and n_seq * n_bat * own * dim <= 8 * 1024 * 1024
    )
    if fused:
        w_qkv, w_o, x_col, flag_col, small_all = load_first(
            (w_query, w_key, w_value), w_out, mine, flags, pack(small), rows, n_seq, n_bat
        )
    else:
        qkv_cut = jnp.stack([w_query, w_key, w_value]).reshape(3, shard, n_seq, wide)
        qkv_cut = jnp.transpose(qkv_cut, (2, 1, 0, 3)).reshape(n_seq, shard, 3 * wide)
        gu_cut = jnp.stack([expert_gate, expert_up]).reshape(2, local_experts, depth, n_seq, part)
        gu_cut = jnp.transpose(gu_cut, (3, 2, 0, 1, 4)).reshape(n_seq, depth, 2 * units)
        w_qkv, w_o, x_col, flag_col, small_all, w_gu, dy_all = load_inputs(
            qkv_cut, w_out, mine, flags, pack(small), gu_cut, dy_own, n_seq, n_bat
        )
        w_gu = w_gu.reshape(dim, 2 * units)
        dy_all = dy_all.reshape(-1, dim)
        x_col = jnp.transpose(x_col.reshape(n_seq, rows, span, dim), (1, 0, 2, 3))
    w_qkv = w_qkv.reshape(dim, 3 * wide)
    w_o = w_o.reshape(wide, dim)
    w_down = expert_down.reshape(local_experts * part, dim)
    small_all = unpack(small_all, (n_seq, n_bat), small.shape)
    small_all = jnp.transpose(small_all, (2, 0, 1, 3)).reshape(-1, dim)
    router = small_all[:experts].T.astype(BF)
    gain_attn, gain_mlp = small_all[experts], small_all[experts + 3]
    gain_q = lax.dynamic_slice_in_dim(small_all[experts + 1], seq * wide, wide)
    gain_k = lax.dynamic_slice_in_dim(small_all[experts + 2], seq * wide, wide)
    usable = unpack(flag_col, (n_seq,), key_mask.shape)
    usable = jnp.transpose(usable, (1, 0, 2)).reshape(rows, length)

    expert_ids = jnp.arange(experts, dtype=jnp.int32)
    chosen_t = jnp.any(top_experts.reshape(own, -1).T[None] == expert_ids[:, None, None], axis=1)
    chosen_t = chosen_t.astype(F32)
    cos_part, sin_part = rotary_tables(jnp.arange(length, dtype=jnp.int32))
    cos_wide = jnp.concatenate([cos_part, cos_part], axis=1)
    sin_wide = jnp.concatenate([-sin_part, sin_part], axis=1)
    gain_q, gain_k = gain_q[None, :], gain_k[None, :]
    hidden, qkv, q, k, v, mixed, stats, mixed_out, *extra = attend_forward(
        x_col.reshape(col, dim), w_qkv, gain_attn[None, :], usable, w_o, gain_q, gain_k,
        cos_wide, sin_wide, n_seq, n_bat, rows,
        (dy_own, mine, gain_mlp[None, :], small_all[:experts], chosen_t) if fused else None,
    )
    if not fused:
        x_own = mine.astype(F32)
        residual = x_own + mixed_out.astype(F32)
        scale_r = rms_scale(residual)
        normed = (residual * scale_r * gain_mlp).astype(BF)
        router_probs = jax.nn.softmax(dot(normed, router), axis=-1)
        chosen = chosen_t.T
        gates = router_probs * chosen

    if fused:
        dy_all, residual, normed, probs_t, gates_t = extra
        normed_all, weighted, grad_pre, gate_terms, w_gu = experts_forward(
            normed, gates_t, dy_all, expert_gate, expert_up, w_down, n_seq, n_bat
        )
        w_gu = w_gu.reshape(dim, 2 * units)
        grad_residual, grad_o, small_grads, grad_gate, grad_up, grad_down = experts_backward(
            grad_pre,
            weighted,
            w_gu,
            gate_terms,
            normed_all.reshape(-1, dim),
            dy_all.reshape(-1, dim),
            residual,
            dy_own,
            gain_mlp[None, :],
            small_all[:experts],
            probs_t,
            chosen_t,
            local_experts,
            n_seq,
            n_bat,
        )
        grad_down = grad_down.reshape(local_experts, part, dim)
    else:
        normed_all, gates_all = gather_all([normed, pack(gates.T)], n_seq, n_bat, 4, "gather_normed")
        normed_all = normed_all.reshape(-1, dim)
        gates_all = unpack(gates_all, (n_seq, n_bat), (experts, own))
        gates_all = jnp.transpose(gates_all, (0, 1, 3, 2)).reshape(-1, experts)
        first_expert = bat * local_experts
        gates_here = lax.dynamic_slice_in_dim(gates_all, first_expert, local_experts, 1)
        gates_wide = jnp.repeat(gates_here, part, axis=1)
        pre = dot(normed_all, w_gu)
        gate_pre, up_pre = pre[:, :units], pre[:, units:]
        sig = jax.nn.sigmoid(gate_pre)
        silu = gate_pre * sig
        active = (silu * up_pre).astype(BF).astype(F32)
        weighted = (active * gates_wide).astype(BF)
        mixture = dot(weighted, w_down).astype(BF)
        mixture = mixture.reshape(n_seq, n_bat, own, dim)
        back = dot_t(dy_all, w_down)
        gate_terms = jnp.sum((active * back).reshape(-1, local_experts, part), axis=-1)
        grad_active = back * gates_wide
        grad_gate_pre = (grad_active * up_pre * sig * (1.0 + gate_pre * (1.0 - sig))).astype(BF)
        grad_up_pre = (grad_active * silu).astype(BF)
        grad_pre = jnp.concatenate([grad_gate_pre, grad_up_pre], axis=1)
        grad_down = t_dot(weighted, dy_all)
        grad_gu = t_dot(normed_all, grad_pre).astype(BF)
        grad_normed = dot_t(grad_pre, w_gu).astype(BF)
        gate_terms = gate_terms.reshape(n_seq, n_bat, own, local_experts)
        grad_gates = lax.dynamic_update_slice_in_dim(
            jnp.zeros((n_seq, n_bat, experts, own), F32),
            jnp.transpose(gate_terms, (0, 1, 3, 2)),
            first_expert,
            2,
        )
        grad_gates = jax.vmap(jax.vmap(pack))(grad_gates)
        grad_normed = grad_normed.reshape(n_seq, n_bat, own, dim)
        grad_normed, grad_gates, mixture = scatter_blocks(
            grad_normed, grad_gates, mixture, n_seq, n_bat
        )
        grad_normed = grad_normed.astype(F32)
        grad_gates = unpack(grad_gates, (), (experts, own)).T
        output = (residual + mixture.astype(F32)).astype(BF)
        grad_down = grad_down.reshape(local_experts, part, dim)

    if not fused:
        grad_chosen = grad_gates * chosen
        grad_logits = router_probs * (
            grad_chosen - jnp.sum(router_probs * grad_chosen, axis=-1, keepdims=True)
        )
        grad_router = lax.dot_general(
            normed.astype(F32), grad_logits, (((0,), (0,)), ((), ())), precision=HIGHEST
        )
        grad_normed = grad_normed + lax.dot_general(
            grad_logits, router.astype(F32), (((1,), (1,)), ((), ())), precision=HIGHEST
        )
        grad_resid, gain_mlp_terms = rms_back(residual, scale_r, gain_mlp, grad_normed)
        grad_residual = dy_own.astype(F32) + grad_resid
        grad_o = grad_residual.astype(BF)

    grad_w_o, grad_w, grad_gains, grad_hidden, *extra = attend_backward(
        grad_o, q, k, v, mixed, qkv, stats, hidden, usable, w_o, w_qkv, gain_q, gain_k,
        cos_wide, sin_wide, n_seq, n_bat,
        (weighted, w_down, mine, grad_residual, gain_attn[None, :], small_grads) if fused else None,
    )
    grad_w_o = grad_w_o.reshape(n_bat, shard, dim)
    grad_w = grad_w.reshape(n_seq, n_bat, shard, 3 * wide)
    if not fused:
        grad_hidden = grad_hidden.astype(F32)
        grad_x, gain_attn_terms = rms_back(x_own, rms_scale(x_own), gain_attn, grad_hidden)
        grad_tokens = (grad_residual + grad_x).astype(BF)

        zeros = jnp.zeros((dim,), F32)
        small_grads = jnp.concatenate(
            [
                grad_router.T,
                jnp.stack(
                    [
                        jnp.sum(gain_attn_terms, axis=0),
                        lax.dynamic_update_slice_in_dim(zeros, grad_gains[0], seq * wide, 0),
                        lax.dynamic_update_slice_in_dim(zeros, grad_gains[1], seq * wide, 0),
                        jnp.sum(gain_mlp_terms, axis=0),
                    ]
                ),
            ],
            axis=0,
        )
        small_grads = jnp.transpose(small_grads.reshape(-1, n_seq, n_bat, shard), (1, 2, 0, 3))
        small_grads = jax.vmap(jax.vmap(pack))(small_grads)

    if fused:
        *grad_w, grad_w_o, small_grads, mixture = store_last(
            grad_w, grad_w_o, extra[1], extra[0], n_seq, n_bat
        )
        output, grad_tokens, *grad_w, grad_w_o, grad_gate, grad_up, grad_down = finish(
            residual, mixture, [grad_hidden, *grad_w, grad_w_o, grad_gate, grad_up, grad_down]
        )
        small_grads = lax.dynamic_slice_in_dim(small_grads, lax.rem(bat, 2) * shard, shard, 1)
    else:
        grad_gu = grad_gu.reshape(n_seq, depth, -1)
        grad_w, grad_w_o, grad_gu, small_grads = store_grads(
            grad_w, grad_w_o, grad_gu, small_grads, n_seq, n_bat
        )
        grad_w = grad_w.astype(F32).reshape(n_seq, shard, 3, wide)
        grad_w = jnp.transpose(grad_w, (2, 1, 0, 3)).reshape(3, shard, dim)
        grad_gu = grad_gu.reshape(n_seq, depth, 2, local_experts, part)
        grad_gu = jnp.transpose(grad_gu, (2, 3, 1, 0, 4)).reshape(2, local_experts, depth, hidden_units)
        grad_gu = grad_gu.astype(F32)
        grad_gate, grad_up = grad_gu[0], grad_gu[1]
        small_grads = unpack(small_grads, (), (experts + 4, shard))

    return (
        output.reshape(rows, span, dim),
        grad_tokens.reshape(rows, span, dim),
        small_grads[experts],
        small_grads[experts + 1],
        small_grads[experts + 2],
        small_grads[experts + 3],
        grad_w[0],
        grad_w[1],
        grad_w[2],
        grad_w_o,
        small_grads[:experts].T,
        grad_gate,
        grad_up,
        grad_down,
    )


def solution(mesh):
    tok = P("batch", "seq", None)
    vec = P(("seq", "batch"))
    mat = P(("seq", "batch"), None)
    in_specs = (tok, P("batch"), P("batch", "seq"), tok) + (vec,) * 4 + (mat,) * 5 + (tok,) * 4
    out_specs = (tok, tok) + (vec,) * 4 + (mat,) * 5 + (tok,) * 3
    return jax.shard_map(shards, mesh=mesh, in_specs=in_specs, out_specs=out_specs, check_vma=False)
```

```python
import functools

import jax
import jax.numpy as jnp
from jax import lax
from jax.experimental import pallas as pl
from jax.experimental.pallas import tpu as pltpu
from jax.sharding import PartitionSpec as P

HEAD = 128
EPS = 1e-05
HIGHEST = lax.Precision.HIGHEST
NEGATIVE = -1e30
BF = jnp.bfloat16
F32 = jnp.float32


def dot(a, b):
    return jnp.dot(a, b, preferred_element_type=F32)


def dot_t(a, b):
    return lax.dot_general(a, b, (((1,), (1,)), ((), ())), preferred_element_type=F32)


def t_dot(a, b):
    return lax.dot_general(a, b, (((0,), (0,)), ((), ())), preferred_element_type=F32)


def rms_scale(v):
    return lax.rsqrt(jnp.mean(v * v, axis=-1, keepdims=True) + EPS)


def rms_back(v, scale, gain, grad):
    normal = v * scale
    weighted = grad * gain
    mean = jnp.mean(weighted * normal, axis=-1, keepdims=True)
    return scale * (weighted - normal * mean), grad * normal


def rotary_tables(positions):
    half_head = HEAD // 2
    frequency = 10000.0 ** (-2.0 * jnp.arange(half_head, dtype=F32) / HEAD)
    angles = positions.astype(F32)[:, None] * frequency[None, :]
    return jnp.cos(angles), jnp.sin(angles)


ANY = pl.BlockSpec(memory_space=pl.ANY)
VMEM_LIMIT = 67043328


class Place:
    def __init__(self, n_seq, n_bat):
        self.n_seq, self.n_bat, self.half = n_seq, n_bat, n_seq // 2
        self.s = lax.axis_index("seq")
        self.b = lax.axis_index("batch")
        self.core = lax.rem(self.s, 2)
        self.z = lax.div(self.s, 2)
        self.twin_s = self.s + 1 - 2 * self.core
        self.bat_x = self.b + 1 - 2 * lax.rem(self.b, 2)
        self.bat_y = lax.rem(self.b + 2, 4)
        self.bat_d = lax.rem(self.bat_x + 2, 4)

    def chip(self, i):
        return 2 * i + self.core

    def chip_twin(self, i):
        return 2 * i + 1 - self.core

    def chip_peer(self, i):
        return {"seq": self.chip(lax.rem(i + self.half, self.half)), "batch": self.b}

    def origin(self, m):
        return self.z if m == 0 else self.origin_of(m)

    def origin_of(self, m):
        last = self.half - 1
        upper = lax.div(2 * self.z, self.half)
        mirrored = self.z + upper * (last - 2 * self.z)
        place = m - 1 + lax.div(m - mirrored + last, self.half)
        return place + upper * (last - 2 * place)

    def seq_at(self, k):
        return lax.rem(self.s + (k + self.n_seq), self.n_seq)

    def twin_at(self, k):
        return lax.rem(self.twin_s + (k + self.n_seq), self.n_seq)

    def bat_at(self, k):
        return lax.rem(self.b + (k + self.n_bat), self.n_bat)

    def seq_peer(self, k):
        return {"seq": self.seq_at(k), "batch": self.b}

    def bat_peer(self, k):
        return {"seq": self.s, "batch": self.bat_at(k)}

    def x_peer(self):
        return {"seq": self.s, "batch": self.bat_x}

    def y_peer(self):
        return {"seq": self.s, "batch": self.bat_y}

    def twin(self):
        return {"seq": self.twin_s, "batch": self.b}

    def greet(self, all_seq=False, batch=True):
        steps = range(1, self.n_seq) if all_seq else range(2, self.n_seq, 2)
        peers = [self.seq_peer(k) for k in steps]
        if not all_seq:
            peers.append(self.twin())
        if batch:
            peers += [self.bat_peer(k) for k in range(1, self.n_bat)]
        barrier = pltpu.get_barrier_semaphore()
        for peer in peers:
            pl.semaphore_signal(
                barrier, inc=1, device_id=peer, device_id_type=pl.DeviceIdType.MESH
            )
        pl.semaphore_wait(barrier, len(peers))


class Wire:
    def __init__(self, send_sems, recv_sems):
        self.send_sems, self.recv_sems = send_sems, recv_sems
        self.copies, self.used = [], 0

    def reserve(self, count):
        first = self.used
        self.used += count
        return first

    def make(self, src, dst, peer, send_slot, recv_slot):
        return pltpu.make_async_remote_copy(
            src_ref=src,
            dst_ref=dst,
            send_sem=self.send_sems.at[send_slot],
            recv_sem=self.recv_sems.at[recv_slot],
            device_id=peer,
            device_id_type=pl.DeviceIdType.MESH,
        )

    def push(self, src, dst, peer):
        slot = self.reserve(1)
        copy = self.make(src, dst, peer, slot, slot)
        copy.start()
        self.copies.append((copy, None))
        return copy

    def push_if(self, there, copy):
        pl.when(there)(copy.start)
        self.copies.append((copy, there))

    def settle(self, copy):
        copy.wait_send()
        self.copies = [other for other in self.copies if other[0] is not copy]

    def drain(self):
        for copy, there in self.copies:
            if there is None:
                copy.wait_send()
            else:
                pl.when(there)(copy.wait_send)


class Line:
    def __init__(self, place, wire, src, at):
        self.place, self.wire, self.src, self.at = place, wire, src, at
        self.base = wire.reserve(place.half + 2)
        self.sends = 0

    def copy(self, src, origin, peer):
        return self.wire.make(
            src, self.at(origin), peer, self.base + self.sends, self.base + origin
        )

    def send(self, there, src, origin, to):
        copy = self.copy(src, origin, self.place.chip_peer(to))
        self.sends += 1
        self.wire.push_if(there, copy)

    def start(self):
        place = self.place
        self.send(place.z < place.half - 1, self.src, place.z, place.z + 1)
        self.send(place.z > 0, self.src, place.z, place.z - 1)

    def step(self, m):
        place = self.place
        origin = place.origin(m)
        self.copy(self.at(origin), origin, place.chip_peer(place.z)).wait_recv()
        from_left = lax.div(place.z - origin - 1 + place.half, place.half)
        to = place.z + 2 * from_left - 1
        self.send((to >= 0) & (to < place.half), self.at(origin), origin, to)
        return origin


class SeqGather:
    def __init__(self, place, wire, src, out):
        self.place, self.wire, self.src, self.out = place, wire, src, out
        self.late = []

    def start(self):
        place = self.place
        self.line = Line(place, self.wire, self.src, lambda i: self.out.at[place.chip(i)])
        self.line.start()
        self.late.append(self.wire.push(self.src, self.out.at[place.s], place.twin()))

    def step(self, j):
        block = self.out.at[self.place.chip(self.line.step(j))]
        self.late.append(self.wire.push(block, block, self.place.twin()))

    def finish(self):
        for copy in self.late:
            copy.wait_recv()


class FullGather:
    def __init__(self, place, wire, src, out):
        self.place, self.wire, self.src, self.out = place, wire, src, out
        self.late = []
        self.across = {}

    def spread(self, j, block):
        place = self.place
        self.across[j] = [
            self.wire.push(block, self.out.at[place.seq_at(-2 * j), place.b], place.bat_peer(k))
            for k in range(1, place.n_bat)
        ]

    def start(self):
        place, mine = self.place, self.out.at[self.place.s, self.place.b]
        self.line = [
            self.wire.push(self.src, mine, place.seq_peer(2 * j)) for j in range(1, place.half)
        ]
        self.spread(0, self.src)
        self.late.append(self.wire.push(self.src, mine, place.twin()))

    def step(self, j):
        self.line[j - 1].wait_recv()
        block = self.out.at[self.place.seq_at(-2 * j), self.place.b]
        self.spread(j, block)
        self.late.append(self.wire.push(block, block, self.place.twin()))

    def collect(self, j):
        place = self.place
        for k in range(1, place.n_bat):
            self.across[j][k - 1].wait_recv()
            block = self.out.at[place.seq_at(-2 * j), place.bat_at(-k)]
            self.late.append(self.wire.push(block, block, place.twin()))

    def finish(self):
        for copy in self.late:
            copy.wait_recv()


def keep_own(src, dst, buffer, sem):
    first = pltpu.make_async_copy(src, buffer, sem)
    first.start()
    first.wait()
    second = pltpu.make_async_copy(buffer, dst, sem)
    second.start()
    return second


def comm_call(
    kernel, outs, scratch, slots, collective_id, name, in_specs, out_specs=None, aliases=None
):
    return pl.pallas_call(
        kernel,
        out_shape=outs,
        in_specs=in_specs,
        out_specs=out_specs if out_specs is not None else jax.tree.map(lambda _: ANY, outs),
        scratch_shapes=list(scratch)
        + [pltpu.SemaphoreType.DMA((slots,)), pltpu.SemaphoreType.DMA((slots,))],
        compiler_params=pltpu.CompilerParams(
            collective_id=collective_id, has_side_effects=True, vmem_limit_bytes=VMEM_LIMIT
        ),
        name=name,
        input_output_aliases=aliases or {},
    )


def shape_of(lead, block):
    return jax.ShapeDtypeStruct(tuple(lead) + block.shape, block.dtype)


def gather_all(blocks, n_seq, n_bat, collective_id, name):
    count = len(blocks)

    def kernel(*refs):
        srcs, outs = refs[:count], refs[count : 2 * count]
        buffers = refs[2 * count : 3 * count]
        own_sems, send_sems, recv_sems = refs[3 * count :]
        place = Place(n_seq, n_bat)
        place.greet()
        wire = Wire(send_sems, recv_sems)
        gathers = [FullGather(place, wire, *pair) for pair in zip(srcs, outs)]
        for gather in gathers:
            gather.start()
        own = [
            keep_own(srcs[i], outs[i].at[place.s, place.b], buffers[i], own_sems.at[i])
            for i in range(count)
        ]
        for j in range(1, place.half):
            for gather in gathers:
                gather.step(j)
            for gather in gathers:
                gather.collect(j - 1)
        for gather in gathers:
            gather.collect(place.half - 1)
        for gather in gathers:
            gather.finish()
        for copy in own:
            copy.wait()
        wire.drain()

    return comm_call(
        kernel,
        [shape_of((n_seq, n_bat), block) for block in blocks],
        [pltpu.VMEM(block.shape, block.dtype) for block in blocks]
        + [pltpu.SemaphoreType.DMA((count,))],
        n_seq * n_bat * count,
        collective_id,
        name,
        [ANY] * count,
    )(*blocks)


def add_into(target, *others):
    rows = target.shape[0]
    step = min(rows, 16)

    def body(i, carry):
        at = pl.ds(pl.multiple_of(i * step, step), step)
        total = target[at, :].astype(F32)
        for other in others:
            total = total + other[at, :].astype(F32)
        target[at, :] = total.astype(target.dtype)
        return carry

    lax.fori_loop(0, rows // step, body, 0)


class FullScatter:
    def __init__(self, place, wire, parts, out, mine, twin, across, line, sems, pick=None):
        self.place, self.wire, self.out = place, wire, out
        self.mine, self.twin, self.across, self.line = mine, twin, across, line
        self.sems = sems
        self.pick = pick or (lambda i, j: parts.at[i, j])

    @staticmethod
    def scratch(n_seq, n_bat, block):
        half = n_seq // 2
        return [
            pltpu.VMEM((half, n_bat) + block.shape, block.dtype),
            pltpu.VMEM((half, n_bat) + block.shape, block.dtype),
            pltpu.VMEM((half, n_bat) + block.shape, block.dtype),
            pltpu.VMEM((half,) + block.shape, block.dtype),
            pltpu.SemaphoreType.DMA((half, n_bat)),
        ]

    def order(self):
        return list(range(1, self.place.half)) + [0]

    def start(self):
        place = self.place
        self.from_twin, self.loads, self.from_bat, self.from_seq = {}, {}, {}, {}
        for j in self.order():
            for k in list(range(1, place.n_bat)) + [0]:
                to_bat = place.bat_at(k)
                self.from_twin[j, k] = self.wire.push(
                    self.pick(place.twin_at(2 * j), to_bat), self.twin.at[j, k], place.twin()
                )
                load = pltpu.make_async_copy(
                    self.pick(place.seq_at(2 * j), to_bat),
                    self.mine.at[j, k],
                    self.sems.at[j, k],
                )
                load.start()
                self.loads[j, k] = load

    def pair(self, j):
        place = self.place
        for k in list(range(1, place.n_bat)) + [0]:
            self.from_twin[j, k].wait_recv()
            self.loads[j, k].wait()
            add_into(self.mine.at[j, k], self.twin.at[j, k])
        for k in range(1, place.n_bat):
            self.from_bat[j, k] = self.wire.push(
                self.mine.at[j, k], self.across.at[j, k], place.bat_peer(k)
            )

    def merge(self, j):
        place = self.place
        for k in range(1, place.n_bat):
            self.from_bat[j, k].wait_recv()
        add_into(self.mine.at[j, 0], *[self.across.at[j, k] for k in range(1, place.n_bat)])
        if j:
            self.from_seq[j] = self.wire.push(
                self.mine.at[j, 0], self.line.at[j], place.seq_peer(2 * j)
            )

    def finish(self):
        for j in range(1, self.place.half):
            self.from_seq[j].wait_recv()
        add_into(self.mine.at[0, 0], *[self.line.at[j] for j in range(1, self.place.half)])
        self.out[...] = self.mine[0, 0]


def scatter_all(parts, n_seq, n_bat, collective_id, name):
    blocks = [jax.ShapeDtypeStruct(part.shape[2:], part.dtype) for part in parts]
    count = len(parts)

    def kernel(*refs):
        ins, outs = refs[:count], refs[count : 2 * count]
        rest = refs[2 * count :]
        send_sems, recv_sems = rest[-2:]
        place = Place(n_seq, n_bat)
        place.greet()
        wire = Wire(send_sems, recv_sems)
        works = [
            FullScatter(place, wire, ins[i], outs[i], *rest[5 * i : 5 * i + 5])
            for i in range(count)
        ]
        for work in works:
            work.start()
        order = works[0].order()
        for at, j in enumerate(order):
            for work in works:
                work.pair(j)
            if at:
                for work in works:
                    work.merge(order[at - 1])
        for work in works:
            work.merge(order[-1])
        for work in works:
            work.finish()
        wire.drain()

    scratch = []
    for block in blocks:
        scratch += FullScatter.scratch(n_seq, n_bat, block)
    slots = count * (n_seq * n_bat)
    vmem = pl.BlockSpec(memory_space=pltpu.VMEM)
    return comm_call(
        kernel,
        blocks,
        scratch,
        slots,
        collective_id,
        name,
        [ANY] * count,
        [vmem] * count,
    )(*parts)


def pack(values):
    flat = values.astype(F32).reshape(-1)
    tiles = -(-flat.shape[0] // 1024)
    return jnp.pad(flat, (0, tiles * 1024 - flat.shape[0])).reshape(tiles * 8, 128)


def unpack(tiles, lead, shape):
    size = 1
    for extent in shape:
        size *= extent
    return tiles.reshape(tuple(lead) + (-1,))[..., :size].reshape(tuple(lead) + tuple(shape))


def scatter_blocks(grad_normed, grad_gates, mixture, n_seq, n_bat):
    dim = grad_normed.shape[-1]
    pieces = 1
    while n_seq * n_bat * grad_normed.shape[2] * (dim // pieces) * 4 > 36 * 1024 * 1024:
        pieces *= 2
    size = dim // pieces
    grads, mixtures = [], []
    for i in range(pieces):
        at = slice(i * size, (i + 1) * size)
        parts = [grad_normed[..., at]] + ([grad_gates] if i == 0 else [])
        done = scatter_all(parts, n_seq, n_bat, 16 + 2 * i, "scatter_normed")
        grads.append(done[0])
        if i == 0:
            gates = done[1]
        done = scatter_all([mixture[..., at]], n_seq, n_bat, 17 + 2 * i, "scatter_mixture")
        mixtures.append(done[0])
    return jnp.concatenate(grads, axis=-1), gates, jnp.concatenate(mixtures, axis=-1)


class SeqScatter:
    def __init__(self, place, wire, full, twin, line):
        self.place, self.wire = place, wire
        self.full, self.twin, self.line = full, twin, line
        self.order = list(range(1, place.half)) + [0]

    @staticmethod
    def scratch(rows, n_seq, block):
        lead = ((rows, n_seq), (rows, n_seq // 2), (rows, n_seq // 2))
        return [pltpu.VMEM(extent + block.shape, block.dtype) for extent in lead]

    def start(self):
        place = self.place
        self.from_seq = {}
        self.from_twin = {
            j: self.wire.push(self.full.at[place.twin_at(2 * j)], self.twin.at[j], place.twin())
            for j in self.order
        }

    def pass_on(self, first=0, last=None):
        place = self.place
        for j in self.order[first:last]:
            self.from_twin[j].wait_recv()
            block = self.full.at[place.seq_at(2 * j)]
            add_into(block, self.twin.at[j])
            if j:
                self.from_seq[j] = self.wire.push(block, self.line.at[j], place.seq_peer(2 * j))

    def total(self):
        for copy in self.from_seq.values():
            copy.wait_recv()
        total = self.full[self.place.s].astype(F32)
        for j in range(1, self.place.half):
            total = total + self.line[j].astype(F32)
        return total

    def finish(self, out, at):
        for copy in self.from_seq.values():
            copy.wait_recv()
        own = self.full.at[self.place.s]
        add_into(own, *[self.line.at[j] for j in range(1, self.place.half)])
        out[at, :] = own[...]


def turn(v, cos_wide, sin_wide):
    return v * cos_wide + pltpu.roll(v, HEAD // 2, axis=1) * sin_wide


class Exchange:
    def __init__(self, place, wire, local, got):
        self.local, self.got, self.count = local, got, place.n_seq - 1
        self.copies = [
            wire.push(local, got.at[k - 1], place.seq_peer(k)) for k in range(1, place.n_seq)
        ]

    def total(self):
        for copy in self.copies:
            copy.wait_recv()
        total = self.local[...]
        for k in range(self.count):
            total = total + self.got[k]
        return total


def in_two(v):
    high = v.astype(BF)
    return high, (v - high.astype(F32)).astype(BF)


def lane_sums(v):
    ones = jnp.ones((8, v.shape[1]), BF)
    high, low = in_two(v)
    return (dot_t(ones, high) + dot_t(ones, low))[0:1]


def allowed_block(use, first, count, keys):
    at_query = first + lax.broadcasted_iota(jnp.int32, (count, keys), 0)
    at_key = lax.broadcasted_iota(jnp.int32, (count, keys), 1)
    return (at_key == at_query) | ((at_key < at_query) & (use > 0))


STEP = 128


def head_gain(place, gains_ref, which, wide, h):
    first = pl.multiple_of(place.s * wide + h * HEAD, HEAD)
    return gains_ref[1 + which : 2 + which, pl.ds(first, HEAD)]


def attend_forward(
    x_col, w_qkv, usable, w_o, gains, cos_wide, sin_wide, n_seq, n_bat, rows, side=None
):
    col, dim = x_col.shape
    three = w_qkv.shape[1]
    wide = three // 3
    heads = wide // HEAD
    length = col // rows
    span = length // n_seq
    own = rows * span
    steps = length // STEP
    chunk = min(256, length)
    scale = HEAD ** (-0.5)
    block = jax.ShapeDtypeStruct((span, dim), BF)

    def kernel(*refs):
        (x_ref, w_ref, use_ref, wo_ref, gains_ref, cos_ref, sin_ref) = refs[:7]
        refs = refs[7:]
        if side is not None:
            dy_ref, own_ref, router_ref, chosen_ref = refs[:4]
            refs = refs[4:]
        hid_ref, qkv_ref, q_ref, k_ref, v_ref, mix_ref, stat_ref, out_ref = refs[:8]
        refs = refs[8:]
        if side is not None:
            dy_all, res_ref, normed_ref, probs_ref, gates_ref = refs[:5]
            dy_keep, dy_sem = refs[-4:-2]
            refs = refs[5:-4] + refs[-2:]
        local, got, full, twin, line, send_sems, recv_sems = refs
        place = Place(n_seq, n_bat)
        place.greet(all_seq=True, batch=side is not None)
        wire = Wire(send_sems, recv_sems)
        dy_works, dy_here = [], [place.chip(place.origin(m)) for m in range(place.half)]

        def dy_spread(m):
            if side is None:
                return
            if m:
                dy_line.step(m)
            src = dy_all.at[dy_here[m], place.b] if m else dy_ref
            work = Across(place, wire, src, lambda i: dy_all.at[dy_here[m], i])
            work.start()
            dy_works.append(work)

        if side is not None:
            dy_line = Line(place, wire, dy_ref, lambda i: dy_all.at[place.chip(i), place.b])
            dy_line.start()
            dy_spread(0)
            dy_own = keep_own(dy_ref, dy_all.at[place.s, place.b], dy_keep, dy_sem)
        def project(n, carry):
            at = pl.ds(pl.multiple_of(n * chunk, chunk), chunk)
            x = x_ref[at, :].astype(F32)
            hidden = (x * rms_scale(x) * gains_ref[0:1, :]).astype(BF)
            hid_ref[at, :] = hidden
            qkv_ref[at, :] = dot(hidden, w_ref[...])
            return carry

        lax.fori_loop(0, col // chunk, project, 0)
        for r in range(rows):
            for c in range(steps):
                at = slice(r * length + c * STEP, r * length + (c + 1) * STEP)
                for which in range(2):
                    v = qkv_ref[at, which * wide : (which + 1) * wide]
                    row = (r * 2 + which) * steps + c
                    local[row : row + 1, :] = lane_sums(v * v)
        for r in range(rows):
            for h in range(heads):
                lanes = slice(2 * wide + h * HEAD, 2 * wide + (h + 1) * HEAD)
                v_ref[r, h] = qkv_ref[r * length : (r + 1) * length, lanes].astype(BF)
        exchange = Exchange(place, wire, local, got)
        dy_spread(1)
        total = exchange.total()
        stat_ref[...] = total
        columns = lax.rsqrt(total / dim + EPS).T
        scatters = [
            SeqScatter(place, wire, full.at[r], twin.at[r], line.at[r]) for r in range(rows)
        ]
        for r in range(rows):
            for c in range(steps):
                inside = slice(c * STEP, (c + 1) * STEP)
                at = slice(r * length + c * STEP, r * length + (c + 1) * STEP)
                for which, target in ((0, q_ref), (1, k_ref)):
                    row = (r * 2 + which) * steps + c
                    factor = columns[:, row : row + 1]
                    for h in range(heads):
                        lanes = slice(which * wide + h * HEAD, which * wide + (h + 1) * HEAD)
                        gain = head_gain(place, gains_ref, which, wide, h)
                        v = qkv_ref[at, lanes] * factor * gain
                        target[r, h, inside, :] = turn(
                            v, cos_ref[inside, :], sin_ref[inside, :]
                        ).astype(BF)
            for c in range(length // chunk):
                keys = (c + 1) * chunk
                allowed = allowed_block(use_ref[r : r + 1, :keys], c * chunk, chunk, keys)
                for h in range(heads):
                    query = q_ref[r, h, c * chunk : keys, :]
                    scores = dot_t(query, k_ref[r, h, :keys, :]) * scale
                    scores = jnp.where(allowed, scores, NEGATIVE)
                    raised = jnp.exp(scores - jnp.max(scores, axis=-1, keepdims=True))
                    probs = raised / jnp.sum(raised, axis=-1, keepdims=True)
                    mixed = dot(probs.astype(BF), v_ref[r, h, :keys, :]).astype(BF)
                    mix_ref[r, c * chunk : keys, h * HEAD : (h + 1) * HEAD] = mixed
                if r and c == 0:
                    scatters[r - 1].pass_on()
                if r == 0 and c == 0 and side is not None:
                    dy_works[0].relay()
                    dy_spread(2)
            full[r] = dot(mix_ref[r], wo_ref[...]).astype(BF).reshape(n_seq, span, dim)
            scatters[r].start()
            if r == 0 and side is not None:
                dy_works[1].relay()
                for m in range(3, place.half):
                    dy_spread(m)
        scatters[-1].pass_on()
        for work in dy_works[2:]:
            work.relay()
        passed = []
        if side is not None:
            dy_own.wait()
        for m, work in enumerate(dy_works):
            work.finish()
            group = dy_all.at[dy_here[m]]
            passed.append(wire.push(group, group, place.twin()))
        for r in range(rows):
            at = slice(r * span, (r + 1) * span)
            if side is None:
                scatters[r].finish(out_ref, at)
                continue
            residual = own_ref[at, :].astype(F32) + scatters[r].total()
            res_ref[at, :] = residual
            normed_ref[at, :] = (residual * rms_scale(residual) * gains_ref[3:4, :]).astype(BF)
        if side is not None:
            out_ref[...] = jnp.zeros_like(out_ref)
            logits = dot_t(router_ref[...].astype(BF), normed_ref[...])
            raised = jnp.exp(logits - jnp.max(logits, axis=0, keepdims=True))
            probs = raised / jnp.sum(raised, axis=0, keepdims=True)
            probs_ref[...] = probs
            gates_ref[...] = probs * chosen_ref[...]
        for copy in passed:
            copy.wait_recv()
        wire.drain()

    vmem = pl.BlockSpec(memory_space=pltpu.VMEM)
    side_in, side_out, side_scratch = [], [], []
    slots = (1 + rows) * n_seq
    if side is not None:
        dy, _, router, _ = side
        side_in = list(side)
        side_out = [
            shape_of((n_seq, n_bat), dy),
            jax.ShapeDtypeStruct((own, dim), F32),
            jax.ShapeDtypeStruct((own, dim), BF),
            jax.ShapeDtypeStruct((router.shape[0], own), F32),
            jax.ShapeDtypeStruct((router.shape[0], own), F32),
        ]
        side_scratch = [pltpu.VMEM(dy.shape, dy.dtype), pltpu.SemaphoreType.DMA]
        slots += 4 * n_seq
    head_block = jax.ShapeDtypeStruct((rows, heads, length, HEAD), BF)
    stats = jax.ShapeDtypeStruct((2 * rows * steps, STEP), F32)
    outs = [
        jax.ShapeDtypeStruct((col, dim), BF),
        jax.ShapeDtypeStruct((col, three), F32),
        head_block,
        head_block,
        head_block,
        jax.ShapeDtypeStruct((rows, length, wide), BF),
        stats,
        jax.ShapeDtypeStruct((own, dim) if side is None else (8, HEAD), BF),
    ]
    return comm_call(
        kernel,
        outs + side_out,
        [pltpu.VMEM(stats.shape, F32), pltpu.VMEM((n_seq - 1,) + stats.shape, F32)]
        + SeqScatter.scratch(rows, n_seq, block)
        + side_scratch,
        slots,
        2,
        "attend_forward",
        [vmem] * 7 + ([ANY] + [vmem] * 3 if side_in else []),
        [vmem] * 8 + ([ANY] + [vmem] * 4 if side_in else []),
    )(x_col, w_qkv, usable, w_o, gains, cos_wide, sin_wide, *side_in)


def attend_backward(
    grad_o, q, k, v, mixed, qkv, stats, hidden, usable, w_o, w_qkv, gains, cos_wide, sin_wide,
    n_seq, n_bat, side=None,
):
    rows, heads, length, _ = q.shape
    own, dim = grad_o.shape
    span = own // rows
    col, three = qkv.shape
    wide = three // 3
    steps = length // STEP
    chunk = min(256, length)
    scale = HEAD ** (-0.5)
    group = n_bat * own

    def kernel(*refs):
        (go_ref, q_ref, k_ref, v_ref, mix_ref, qkv_ref, stat_ref, hid_ref, use_ref, wo_ref,
         w_ref, gains_ref, cos_ref, sin_ref) = refs[:14]
        refs = refs[14:]
        if side:
            weighted_ref, down_ref, own_ref, res_ref, small_in = refs[:5]
            refs = refs[5:]
        gwo_ref, gw_ref, gain_ref, out_ref = refs[:4]
        refs = refs[4:]
        if side:
            mixture_ref, small_ref = refs[:2]
            mix_away, mix_twin, mix_halves, mix_full = refs[-6:-2]
            refs = refs[2:-6] + refs[-2:]
        go_all, gm, dq, dk, dv, dqkv, local, got, hid_buf, hid_sems = refs[:10]
        full, twin, line, send_sems, recv_sems = refs[10:]
        place = Place(n_seq, n_bat)
        place.greet(all_seq=True, batch=bool(side))
        wire = Wire(send_sems, recv_sems)
        gathers = [
            SeqGather(place, wire, go_ref.at[pl.ds(r * span, span)], go_all.at[r])
            for r in range(rows)
        ]
        for gather in gathers:
            gather.start()
        for r in range(rows):
            go_all[r, place.s] = go_ref[r * span : (r + 1) * span, :]
        order = list(range(1, place.half)) + [0]
        works, from_twin = {}, {}

        def mixture_of(i):
            at = pl.ds(pl.multiple_of(i * group, group), group)
            return dot(weighted_ref[at, :], down_ref[...])

        todo = [(gather, m) for gather in gathers for m in range(1, place.half)]

        def forward(count):
            for _ in range(min(count, len(todo))):
                gather, m = todo.pop(0)
                gather.step(m)

        if side:

            def send_mixture(n):
                j = order[n]
                if n >= 2:
                    wire.settle(from_twin[order[n - 2]])
                mix_away[n % 2] = (
                    mixture_of(place.twin_at(2 * j)).astype(BF).reshape(n_bat, own, dim)
                )

            def push_mixture(n):
                j = order[n]
                from_twin[j] = wire.push(mix_away.at[n % 2], mix_twin.at[j], place.twin())

            waiting = None
            send_mixture(0)
            push_mixture(0)
            for n, j in enumerate(order):
                if n + 1 < len(order):
                    send_mixture(n + 1)
                total = mixture_of(place.seq_at(2 * j))
                if n + 1 < len(order):
                    push_mixture(n + 1)
                from_twin[j].wait_recv()
                mix_twin[j] = (
                    (total + mix_twin[j].reshape(group, dim).astype(F32))
                    .astype(BF)
                    .reshape(n_bat, own, dim)
                )
                works[j] = AcrossSum(
                    place, wire, mix_twin.at[j], mix_halves.at[j], mix_full.at[j]
                )
                if waiting is not None:
                    works[waiting].start()
                waiting = j
                forward(1)
            works[waiting].start()
        forward(max(0, len(todo) - (rows - 1) * (place.half - 1)))
        columns = lax.rsqrt(stat_ref[...] / dim + EPS).T
        scatters = [
            SeqScatter(place, wire, full.at[r], twin.at[r], line.at[r]) for r in range(rows)
        ]
        gain_sums = [[jnp.zeros((1, HEAD), F32) for _ in range(heads)] for _ in range(2)]
        middles = [works[j] for j in works]

        def attend(r, c, h):
            keys = (c + 1) * chunk
            now = slice(c * chunk, keys)
            allowed = allowed_block(use_ref[r : r + 1, :keys], c * chunk, chunk, keys)
            lanes = slice(h * HEAD, (h + 1) * HEAD)
            query = q_ref[r, h, now, :]
            key = k_ref[r, h, :keys, :]
            scores = jnp.where(allowed, dot_t(query, key) * scale, NEGATIVE)
            raised = jnp.exp(scores - jnp.max(scores, axis=-1, keepdims=True))
            probs = raised / jnp.sum(raised, axis=-1, keepdims=True)
            low = probs.astype(BF)
            grad_mix = gm[r, now, lanes]
            grad_probs = dot_t(grad_mix, v_ref[r, h, :keys, :])
            row_dot = jnp.sum(low.astype(F32) * grad_probs, axis=-1, keepdims=True)
            grad_scores = (probs * (grad_probs - row_dot)).astype(BF)
            dq[now, lanes] = scale * dot(grad_scores, key)
            dk[:keys, lanes] += scale * t_dot(grad_scores, query)
            dv[:keys, lanes] += t_dot(low, grad_mix)

        def take(r):
            gathers[r].finish()
            gm[r] = dot_t(go_all[r].reshape(length, dim), wo_ref[...]).astype(BF)

        take(0)
        for r in range(rows):
            if r:
                scatters[r - 1].pass_on(0, 1)
            dk[...] = jnp.zeros_like(dk)
            dv[...] = jnp.zeros_like(dv)
            for h in range(heads):
                for c in range(length // chunk):
                    attend(r, c, h)
                    forward(1)
                    if middles:
                        middles.pop(0).middle()
            if r == 0:
                forward(len(todo))
                while middles:
                    middles.pop(0).middle()
            for which, grads in ((0, dq), (1, dk)):
                for c in range(steps):
                    inside = slice(c * STEP, (c + 1) * STEP)
                    at = slice(r * length + c * STEP, r * length + (c + 1) * STEP)
                    row = (r * 2 + which) * steps + c
                    factor = columns[:, row : row + 1]
                    products = None
                    for h in range(heads):
                        lanes = slice(h * HEAD, (h + 1) * HEAD)
                        flat = qkv_ref[at, which * wide + h * HEAD : which * wide + (h + 1) * HEAD]
                        flat = flat * factor
                        back = turn(grads[inside, lanes], cos_ref[inside, :], -sin_ref[inside, :])
                        gain_sums[which][h] = gain_sums[which][h] + jnp.sum(
                            back * flat, axis=0, keepdims=True
                        )
                        weighted = back * head_gain(place, gains_ref, which, wide, h)
                        grads[inside, lanes] = weighted
                        product = weighted * flat
                        products = product if products is None else products + product
                    row = which * steps + c
                    local[r, row : row + 1, :] = lane_sums(products)
            exchange = Exchange(place, wire, local.at[r], got.at[r])
            if r:
                scatters[r - 1].pass_on(1)
            dqkv[r, :, 2 * wide :] = dv[...].astype(BF)
            if r + 1 < rows:
                take(r + 1)
            means = (exchange.total() / dim).T
            for which, grads in ((0, dq), (1, dk)):
                lanes = slice(which * wide, (which + 1) * wide)
                for c in range(steps):
                    inside = slice(c * STEP, (c + 1) * STEP)
                    at = slice(r * length + c * STEP, r * length + (c + 1) * STEP)
                    row = (r * 2 + which) * steps + c
                    factor = columns[:, row : row + 1]
                    mean = means[:, which * steps + c : which * steps + c + 1]
                    flat = qkv_ref[at, lanes] * factor
                    dqkv[r, inside, lanes] = (factor * (grads[inside, :] - flat * mean)).astype(BF)
            full[r] = dot_t(dqkv[r], w_ref[...]).astype(BF).reshape(n_seq, span, dim)
            scatters[r].start()
        for which in range(2):
            for h in range(heads):
                gain_ref[which : which + 1, h * HEAD : (h + 1) * HEAD] = gain_sums[which][h]

        def hidden_load(part):
            slot = lax.rem(part, 2)
            at = pl.ds(pl.multiple_of(part * 256, 256), 256)
            return pltpu.make_async_copy(
                hid_ref.at[:, at], hid_buf.at[slot], hid_sems.at[slot]
            )

        hidden_load(0).start()
        scatters[-1].pass_on()

        def weight_part(part, carry):
            at = pl.ds(pl.multiple_of(part * 256, 256), 256)

            @pl.when(part + 1 < dim // 256)
            def _():
                hidden_load(part + 1).start()

            hidden_load(part).wait()
            held = hid_buf[lax.rem(part, 2)]
            gw_ref[at, :] = t_dot(held, dqkv[...].reshape(col, three)).astype(BF)
            total = t_dot(mix_ref[0], go_all[0, :, :, at].reshape(length, 256))
            for r in range(1, rows):
                total = total + t_dot(mix_ref[r], go_all[r, :, :, at].reshape(length, 256))
            gwo_ref[:, at] = total.astype(BF)
            return carry

        lax.fori_loop(0, dim // 256, weight_part, 0)
        for j in works:
            works[j].finish()
            mixture_ref[j] = mix_twin[j, place.b]
        sums = jnp.zeros((1, dim), F32)
        for r in range(rows):
            at = slice(r * span, (r + 1) * span)
            if not side:
                scatters[r].finish(out_ref, at)
                continue
            x = own_ref[at, :].astype(F32)
            grad, terms = rms_back(x, rms_scale(x), gains_ref[0:1, :], scatters[r].total())
            sums = sums + jnp.sum(terms, axis=0, keepdims=True)
            out_ref[at, :] = (res_ref[at, :] + grad).astype(BF)
        if side:
            small_ref[...] = small_in[...]
            small_ref[8:9, :] = sums
            lanes = pl.ds(pl.multiple_of(place.s * wide, wide), wide)
            for which in range(2):
                small_ref[9 + which : 10 + which, lanes] = gain_ref[which : which + 1, :]
        wire.drain()

    vmem = pl.BlockSpec(memory_space=pltpu.VMEM)
    block = jax.ShapeDtypeStruct((span, dim), BF)
    stat_shape = (2 * steps, STEP)
    side_out, side_scratch = [], []
    if side:
        half = n_seq // 2
        side_out = [
            jax.ShapeDtypeStruct((half, own, dim), BF),
            jax.ShapeDtypeStruct((16, dim), F32),
        ]
        side_scratch = [
            pltpu.VMEM((2, n_bat, own, dim), BF),
            pltpu.VMEM((half, n_bat, own, dim), BF),
            pltpu.VMEM((half, 2, own // 2, dim), BF),
            pltpu.VMEM((half, 2, own, dim), BF),
        ]
    return comm_call(
        kernel,
        [
            jax.ShapeDtypeStruct((wide, dim), BF),
            jax.ShapeDtypeStruct((dim, three), BF),
            jax.ShapeDtypeStruct((2, wide), F32),
            jax.ShapeDtypeStruct((own, dim), BF),
        ]
        + side_out,
        [
            pltpu.VMEM((rows, n_seq, span, dim), BF),
            pltpu.VMEM((rows, length, wide), BF),
            pltpu.VMEM((length, wide), F32),
            pltpu.VMEM((length, wide), F32),
            pltpu.VMEM((length, wide), F32),
            pltpu.VMEM((rows, length, three), BF),
            pltpu.VMEM((rows,) + stat_shape, F32),
            pltpu.VMEM((rows, n_seq - 1) + stat_shape, F32),
            pltpu.VMEM((2, col, 256), BF),
            pltpu.SemaphoreType.DMA((2,)),
        ]
        + SeqScatter.scratch(rows, n_seq, block)
        + side_scratch,
        5 * rows * n_seq + (3 * n_seq if side else 0),
        6,
        "attend_backward",
        [vmem] * 7 + [ANY] + [vmem] * (6 + len(side or ())),
        [vmem] * (4 + len(side_out)),
    )(grad_o, q, k, v, mixed, qkv, stats, hidden, usable, w_o, w_qkv, gains, cos_wide, sin_wide,
      *(side or ()))


class Across:
    def __init__(self, place, wire, src, at):
        self.place, self.wire, self.src, self.at = place, wire, src, at
        self.half = src.shape[0] // 2

    def start(self):
        place, own = self.place, self.at(self.place.b)
        self.to_x = self.wire.push(self.src, own, place.x_peer())
        self.to_y = self.wire.push(self.src, own, place.y_peer())

    def relay(self):
        place, half = self.place, self.half
        self.to_x.wait_recv()
        top = self.at(place.bat_x).at[pl.ds(0, half)]
        self.top = self.wire.push(top, top, place.y_peer())
        self.to_y.wait_recv()
        low = self.at(place.bat_y).at[pl.ds(half, half)]
        self.low = self.wire.push(low, low, place.x_peer())

    def finish(self):
        self.top.wait_recv()
        self.low.wait_recv()


class AcrossSum:
    def __init__(self, place, wire, group, halves, full):
        self.place, self.wire = place, wire
        self.group, self.halves, self.full = group, halves, full
        self.half = halves.shape[1]

    def start(self):
        place, half = self.place, self.half
        far = self.group.at[place.bat_d]
        self.top = self.wire.push(far.at[pl.ds(0, half)], self.halves.at[0], place.x_peer())
        self.low = self.wire.push(far.at[pl.ds(half, half)], self.halves.at[1], place.y_peer())

    def middle(self):
        place, half = self.place, self.half
        self.top.wait_recv()
        add_into(self.group.at[place.bat_y].at[pl.ds(0, half)], self.halves.at[0])
        self.low.wait_recv()
        add_into(self.group.at[place.bat_x].at[pl.ds(half, half)], self.halves.at[1])
        self.y = self.wire.push(self.group.at[place.bat_y], self.full.at[0], place.y_peer())
        self.x = self.wire.push(self.group.at[place.bat_x], self.full.at[1], place.x_peer())

    def finish(self):
        self.y.wait_recv()
        self.x.wait_recv()
        add_into(self.group.at[self.place.b], self.full.at[0], self.full.at[1])


def load_first(weights, w_out, mine, flags, small, rows, n_seq, n_bat):
    shard, dim = weights[0].shape
    wide = dim // n_seq
    own = mine.shape[0]
    span = own // rows
    slots = 15 * n_seq + n_seq * n_bat

    def kernel(*refs):
        parts = refs[:3]
        wo_ref, x_ref, flag_ref, small_ref = refs[3:7]
        w_ref, wo_all, x_col, router_ref, gains_ref, use_ref = refs[7:13]
        buffers = refs[13:16]
        own_sems, cut_sems, x_sems, small_all, flag_col, send_sems, recv_sems = refs[16:]
        place = Place(n_seq, n_bat)
        place.greet(all_seq=True)
        wire = Wire(send_sems, recv_sems)
        small_work = FullGather(place, wire, small_ref, small_all)
        flag_work = SeqGather(place, wire, flag_ref, flag_col)
        x_works = [
            SeqGather(place, wire, x_ref.at[pl.ds(r * span, span)], x_col.at[r])
            for r in range(rows)
        ]
        small_work.start()
        flag_work.start()

        def cut(k):
            return pl.ds(pl.multiple_of(place.seq_at(k) * wide, wide), wide)

        def columns(m):
            return pl.ds(m * wide, wide)

        own_cuts = []
        for m in range(3):
            copy = pltpu.make_async_copy(
                parts[m].at[:, cut(0)], buffers[0].at[:, columns(m)], cut_sems.at[m]
            )
            copy.start()
            own_cuts.append(copy)
        cuts = {}
        for k in range(1, n_seq):
            for m in range(3):
                cuts[k, m] = wire.push(
                    parts[m].at[:, cut(k)],
                    w_ref.at[place.s, place.b, :, columns(m)],
                    place.seq_peer(k),
                )
        wo_work = Across(place, wire, wo_ref, lambda i: wo_all.at[i])
        wo_work.start()
        for work in x_works:
            work.start()
        for copy in own_cuts:
            copy.wait()
        spreads = []

        def spread(src, from_seq):
            work = Across(place, wire, src, lambda i: w_ref.at[from_seq, i])
            work.start()
            spreads.append(work)

        spread(buffers[0], place.s)
        own_w = pltpu.make_async_copy(buffers[0], w_ref.at[place.s, place.b], own_sems.at[0])
        own_w.start()
        copies = [own_w]
        fetched = pltpu.make_async_copy(x_ref, buffers[2], own_sems.at[2])
        fetched.start()
        fetched.wait()
        for r in range(rows):
            copy = pltpu.make_async_copy(
                buffers[2].at[pl.ds(r * span, span)], x_col.at[r, place.s], x_sems.at[r]
            )
            copy.start()
            copies.append(copy)
        copies.append(keep_own(wo_ref, wo_all.at[place.b], buffers[1], own_sems.at[1]))
        flag_col[place.s] = flag_ref[...]
        small_all[place.s, place.b] = small_ref[...]
        for j in range(1, place.half):
            small_work.step(j)
            flag_work.step(j)
        for k in range(1, n_seq):
            for m in range(3):
                cuts[k, m].wait_recv()
            spread(w_ref.at[place.seq_at(-k), place.b], place.seq_at(-k))
        for j in range(place.half):
            small_work.collect(j)
        todo = [(work, m) for work in x_works for m in range(1, place.half)]

        def forward(count):
            for _ in range(min(count, len(todo))):
                work, m = todo.pop(0)
                work.step(m)

        forward(1)
        wo_work.relay()
        for work in spreads:
            work.relay()
            forward(1)
        forward(len(todo))
        wo_work.finish()
        for work in spreads:
            work.finish()
        for work in [small_work, flag_work] + x_works:
            work.finish()
        left = lax.broadcasted_iota(jnp.int32, (8, 128), 1) < 64
        for i in range(n_seq):
            for k in range(0, n_bat, 2):
                one, two = small_all[i, k], small_all[i, k + 1]
                at = slice((i * n_bat + k) * 64, (i * n_bat + k + 2) * 64)
                router_ref[:, at] = jnp.where(left, one, pltpu.roll(two, 64, axis=1))
                gains_ref[:, at] = jnp.where(left, pltpu.roll(one, 64, axis=1), two)
        for i in range(0, n_seq, 2):
            one, two = flag_col[i], flag_col[i + 1]
            use_ref[:, i * 64 : (i + 2) * 64] = jnp.where(left, one, pltpu.roll(two, 64, axis=1))
        for copy in copies:
            copy.wait()
        wire.drain()

    one = jax.ShapeDtypeStruct((shard, 3 * wide), BF)
    x_one = jax.ShapeDtypeStruct((span, dim), BF)
    held = (one, w_out, mine)
    vmem = pl.BlockSpec(memory_space=pltpu.VMEM)
    return comm_call(
        kernel,
        [
            shape_of((n_seq, n_bat), one),
            shape_of((n_bat,), w_out),
            shape_of((rows, n_seq), x_one),
            jax.ShapeDtypeStruct((8, dim), F32),
            jax.ShapeDtypeStruct((8, dim), F32),
            jax.ShapeDtypeStruct((8, n_seq * span), F32),
        ],
        [pltpu.VMEM(block.shape, block.dtype) for block in held]
        + [pltpu.SemaphoreType.DMA((n,)) for n in (3, 3, rows)]
        + [pltpu.VMEM((n_seq, n_bat, 8, 128), F32), pltpu.VMEM((n_seq, 8, 128), F32)],
        slots,
        1,
        "load_first",
        [ANY] * 5 + [vmem] * 2,
        [ANY] * 3 + [vmem] * 3,
    )(*weights, w_out, mine, flags, small)


def pick_units(first, experts, units, part):
    at_expert = lax.broadcasted_iota(jnp.int32, (experts, units), 0)
    at_unit = lax.broadcasted_iota(jnp.int32, (experts, units), 1)
    low = (at_expert - first) * part
    return jnp.where((at_unit >= low) & (at_unit < low + part), 1.0, 0.0).astype(BF)


def experts_forward(normed, gates, dy_all, gate, up, w_down, n_seq, n_bat):
    own, dim = normed.shape
    local_experts, depth, hidden = gate.shape
    units = w_down.shape[0]
    part = hidden // n_seq
    group = n_bat * own
    tokens = n_seq * group
    experts = gates.shape[0]
    slots = 64 + 2 * n_seq * n_bat + 2 * local_experts * n_seq

    def kernel(*refs):
        x_ref, gate_ref, dy_ref, wg_ref, wu_ref, down_ref = refs[:6]
        x_all, weighted_ref, grad_ref, term_ref, gu_ref = refs[6:11]
        gates_all, back, gate_buf, x_buf, dy_buf, keep = refs[11:17]
        own_sems, x_sems, dy_sems, gu_sems, send_sems, recv_sems = refs[17:]
        place = Place(n_seq, n_bat)
        place.greet(all_seq=True)
        wire = Wire(send_sems, recv_sems)
        gate_work = FullGather(place, wire, gate_ref, gates_all)
        gate_work.start()
        gates_all[place.s, place.b] = gate_ref[...]
        line = Line(place, wire, x_ref, lambda i: x_all.at[place.chip(i), place.b])
        line.start()
        works = []
        here = [place.chip(place.origin(m)) for m in range(place.half)]
        there = [place.chip_twin(place.origin(m)) for m in range(place.half)]
        for j in range(place.half):
            at_seq = here[j]
            src = x_ref if j == 0 else x_all.at[at_seq, place.b]
            works.append(
                Across(place, wire, src, lambda i, at_seq=at_seq: x_all.at[at_seq, i])
            )
        works[0].start()
        own = keep_own(x_ref, x_all.at[place.s, place.b], keep, own_sems.at[0])
        selected = pick_units(place.b * local_experts, experts, units, part)
        selected_twice = jnp.concatenate([selected, selected], axis=0)

        def dy_load(g, slot):
            return pltpu.make_async_copy(dy_ref.at[g], dy_buf.at[slot], dy_sems.at[slot])

        def rows_of(g):
            return pl.ds(pl.multiple_of(g * group, group), group)

        def backs(first, count):
            dy_load(first, first % 2).start()
            for g in range(first, first + count):
                if g + 1 < first + count:
                    dy_load(g + 1, (g + 1) % 2).start()
                dy_load(g, g % 2).wait()
                block = dy_buf[g % 2].reshape(group, dim)
                back[g * group : (g + 1) * group, :] = dot_t(block, down_ref[...])

        gu_copies = ([], [])

        def send_units(m, ref, offsets):
            for k in offsets:
                lanes = pl.ds(pl.multiple_of(place.seq_at(k) * part, part), part)
                for e in range(local_experts):
                    src = ref.at[e, :, lanes]
                    dst = gu_ref.at[place.s, :, pl.ds(m * units + e * part, part)]
                    if k:
                        gu_copies[m].append(wire.push(src, dst, place.seq_peer(k)).wait_recv)
                    else:
                        copy = pltpu.make_async_copy(src, dst, gu_sems.at[m, e])
                        copy.start()
                        gu_copies[m].append(copy.wait)

        passed = []

        def hand_over(j):
            at_seq = here[j]
            works[j].finish()
            if j == 0:
                own.wait()
            passed.append(wire.push(x_all.at[at_seq], x_all.at[at_seq], place.twin()))

        loads = {}

        def fetch(g, slot):
            loads[slot] = pltpu.make_async_copy(x_all.at[g], x_buf.at[slot], x_sems.at[slot])
            loads[slot].start()

        def weight(m):
            return gu_ref[:, :, m * units : (m + 1) * units].reshape(dim, units)

        def gate_on(g, slot):
            loads[slot].wait()
            gate_buf[rows_of(g), :] = dot(x_buf[slot].reshape(group, dim), weight(0))

        def units_on(g, slot, gated=False):
            if not gated:
                loads[slot].wait()
            at = rows_of(g)
            block = x_buf[slot].reshape(group, dim)
            gate_pre = gate_buf[at, :] if gated else dot(block, weight(0))
            up_pre = dot(block, weight(1))
            sig = jax.nn.sigmoid(gate_pre)
            silu = gate_pre * sig
            active = (silu * up_pre).astype(BF).astype(F32)
            grad_back = back[at, :]
            product = active * grad_back
            wide_gates = []
            for i in range(n_bat):
                inside = slice(i * x_ref.shape[0], (i + 1) * x_ref.shape[0])
                gates_two = jnp.concatenate(in_two(gates_all[g, i]), axis=0)
                wide_gates.append(t_dot(gates_two, selected_twice))
                high, low = in_two(product[inside, :])
                term_ref[g, i] = dot_t(selected, high) + dot_t(selected, low)
            wide_gate = jnp.concatenate(wide_gates, axis=0)
            weighted_ref[at, :] = (active * wide_gate).astype(BF)
            grad_active = grad_back * wide_gate
            grad_ref[at, :units] = (
                grad_active * up_pre * sig * (1.0 + gate_pre * (1.0 - sig))
            ).astype(BF)
            grad_ref[at, units:] = (grad_active * silu).astype(BF)

        half = place.half
        per = n_seq // half
        offsets = list(range(1, n_seq)) + [0]
        for j in range(1, half):
            backs((j - 1) * per, per)
            gate_work.step(j)
            gate_work.collect(j - 1)
            line.step(j)
            works[j].start()
            works[j - 1].relay()
            if j < half - 1:
                send_units(0, wg_ref, offsets[2 * j - 2 : 2 * j])
            else:
                send_units(0, wg_ref, offsets[2 * j - 2 :])
                send_units(1, wu_ref, offsets)
        backs((half - 1) * per, per)
        gate_work.collect(half - 1)
        gate_work.finish()
        hand_over(0)
        fetch(here[0], 0)
        for wait in gu_copies[0]:
            wait()
        gate_on(here[0], 0)
        passed[0].wait_recv()
        fetch(there[0], 1)
        hand_over(1)
        fetch(here[1], 2)
        gate_on(there[0], 1)
        gate_on(here[1], 2)
        works[half - 1].relay()
        passed[1].wait_recv()
        fetch(there[1], 3)
        gate_on(there[1], 3)
        for wait in gu_copies[1]:
            wait()
        for j in range(half):
            units_on(here[j], (2 * j) % 4, j < 2)
            if j + 2 < half:
                hand_over(j + 2)
                fetch(here[j + 2], (2 * j) % 4)
            units_on(there[j], (2 * j + 1) % 4, j < 2)
            if j + 2 < half:
                passed[j + 2].wait_recv()
                fetch(there[j + 2], (2 * j + 1) % 4)
        wire.drain()

    vmem = pl.BlockSpec(memory_space=pltpu.VMEM)
    return comm_call(
        kernel,
        [
            shape_of((n_seq, n_bat), normed),
            jax.ShapeDtypeStruct((tokens, units), BF),
            jax.ShapeDtypeStruct((tokens, 2 * units), BF),
            shape_of((n_seq, n_bat), gates),
            jax.ShapeDtypeStruct((n_seq, depth, 2 * units), BF),
        ],
        [
            pltpu.VMEM((n_seq, n_bat) + gates.shape, F32),
            pltpu.VMEM((tokens, units), F32),
            pltpu.VMEM((tokens, units), F32),
            pltpu.VMEM((4, n_bat, own, dim), BF),
            pltpu.VMEM((2, n_bat, own, dim), BF),
            pltpu.VMEM((own, dim), BF),
            pltpu.SemaphoreType.DMA((1,)),
            pltpu.SemaphoreType.DMA((4,)),
            pltpu.SemaphoreType.DMA((2,)),
            pltpu.SemaphoreType.DMA((2, local_experts)),
        ],
        slots,
        4,
        "experts_forward",
        [ANY, vmem, ANY, ANY, ANY, vmem],
        [ANY, vmem, vmem, vmem, vmem],
    )(normed, gates, dy_all, gate, up, w_down)


def experts_backward(
    grad_pre, weighted, w_gu, terms, x_all, dy_all, residual, dy_own, gains, router, probs, chosen,
    local_experts, n_seq, n_bat,
):
    own = residual.shape[0]
    tokens, dim = x_all.shape
    units = weighted.shape[1]
    part = units // local_experts
    group = n_bat * own
    depth = dim // n_seq
    hidden = n_seq * part
    half = n_seq // 2
    slots = 128 + 2 * n_seq * n_bat
    block = jax.ShapeDtypeStruct((own, dim), BF)
    term = jax.ShapeDtypeStruct(terms.shape[2:], F32)

    def kernel(*refs):
        grad_ref, weighted_ref, gu_ref, term_in, x_ref, dy_ref = refs[:6]
        res_ref, own_dy_ref, gains_ref, router_ref, probs_ref, chosen_ref = refs[6:12]
        out_ref, low_ref, small_ref, gate_out, up_out, down_out = refs[12:18]
        refs = refs[18:]
        away, twin, halves, full, line = refs[:5]
        columns, sent, got, column_sems, term_out = refs[5:10]
        term_scratch = refs[10:15]
        send_sems, recv_sems = refs[15:]
        place = Place(n_seq, n_bat)
        place.greet(all_seq=True)
        wire = Wire(send_sems, recv_sems)
        term_work = FullScatter(place, wire, term_in, term_out, *term_scratch)
        term_work.start()

        def product(i):
            at = pl.ds(pl.multiple_of(i * group, group), group)
            return dot_t(grad_ref[at, :], gu_ref[...])

        order = list(range(1, half)) + [0]
        from_twin, from_seq, works = {}, {}, {}

        def send(j):
            from_twin[j] = wire.push(away.at[j], twin.at[j], place.twin())

        chunks = list(range(1, n_seq)) + [0]

        def chunk_load(n):
            at = pl.ds(pl.multiple_of(place.seq_at(chunks[n]) * depth, depth), depth)
            return pltpu.make_async_copy(x_ref.at[:, at], columns.at[n % 2], column_sems.at[n % 2])

        def down_load(k):
            slot = lax.rem(k, 2)
            at = pl.ds(pl.multiple_of(k * 256, 256), 256)
            return pltpu.make_async_copy(dy_ref.at[:, at], columns.at[slot], column_sems.at[slot])

        def down_part(first, last):
            down_load(first).start()

            def one(k, carry):
                @pl.when(k + 1 < last)
                def _():
                    down_load(k + 1).start()

                down_load(k).wait()
                at = pl.ds(pl.multiple_of(k * 256, 256), 256)
                down_out[:, at] = t_dot(weighted_ref[...], columns[lax.rem(k, 2)])
                return carry

            lax.fori_loop(first, last, one, 0)

        chunk_load(0).start()

        def pair(j):
            part_sum = product(place.seq_at(2 * j))
            from_twin[j].wait_recv()
            twin[j] = (
                (part_sum + twin[j].reshape(group, dim).astype(F32))
                .astype(BF)
                .reshape(n_bat, own, dim)
            )
            works[j] = AcrossSum(place, wire, twin.at[j], halves.at[j], full.at[j])

        arrivals = []
        done = [0]

        def work_chunks(count):
            for n in range(done[0], min(done[0] + count, len(chunks))):
                done[0] = n + 1
                k = chunks[n]
                if n + 1 < len(chunks):
                    chunk_load(n + 1).start()
                chunk_load(n).wait()
                value = t_dot(columns[n % 2], grad_ref[...]).astype(BF)
                if k == 0:
                    got[place.s] = value
                else:
                    sent[k] = value
                if n:
                    k = chunks[n - 1]
                    arrivals.append(wire.push(sent.at[k], got.at[place.s], place.seq_peer(k)))

        def pass_on(j):
            works[j].finish()
            if j:
                from_seq[j] = wire.push(twin.at[j, place.b], line.at[j], place.seq_peer(2 * j))

        work_chunks(1)
        waiting = None
        for j in order:
            away[j] = product(place.twin_at(2 * j)).astype(BF).reshape(n_bat, own, dim)
            if waiting is not None:
                send(waiting)
            waiting = j
            work_chunks(1)
        first, rest = order[:2], order[2:]
        pair(order[0])
        send(waiting)
        for j in first[1:]:
            pair(j)
            works[first[0]].start()
        works[first[-1]].start()
        for j in rest:
            pair(j)
        term_order = term_work.order()
        for j in term_order:
            term_work.pair(j)
        works[first[0]].middle()
        work_chunks(1)
        for j in first[1:]:
            works[j].middle()
        for j in rest:
            works[j].start()
        for j in first:
            work_chunks(3)
            pass_on(j)
        work_chunks(len(chunks))
        for j in term_order:
            term_work.merge(j)
        for j in rest:
            works[j].middle()
        cut = dim // 512
        down_part(0, cut)
        pass_on(rest[0])
        down_part(cut, 2 * cut)
        for j in rest[1:]:
            pass_on(j)
        for copy in arrivals:
            copy.wait_recv()
        for i in range(n_seq):
            lanes = slice(i * part, (i + 1) * part)
            for e in range(local_experts):
                gate_out[e, :, lanes] = got[i, :, e * part : (e + 1) * part].astype(F32)
                up_out[e, :, lanes] = got[i, :, units + e * part : units + (e + 1) * part].astype(
                    F32
                )
        term_work.finish()
        for j in range(1, half):
            from_seq[j].wait_recv()
        total = twin[0, place.b].astype(F32)
        for j in range(1, half):
            total = total + line[j].astype(F32)
        grad_chosen = term_out[...] * chosen_ref[...]
        probs = probs_ref[...]
        grad_logits = probs * (
            grad_chosen - jnp.sum(probs * grad_chosen, axis=0, keepdims=True)
        )
        small_ref[...] = jnp.zeros_like(small_ref)
        residual = res_ref[...]
        scale = rms_scale(residual)
        normal = residual * scale
        normed = (normal * gains_ref[3:4, :]).astype(BF)
        experts = probs.shape[0]
        logits_two = jnp.concatenate(in_two(grad_logits), axis=0)
        products = dot(logits_two, normed)
        small_ref[0:experts, :] = products[:experts] + products[experts:]
        router = router_ref[...].astype(BF)
        total = total + t_dot(logits_two, jnp.concatenate([router, router], axis=0))
        grad, terms_of = rms_back(residual, scale, gains_ref[3:4, :], total)
        small_ref[experts + 3 : experts + 4, :] = jnp.sum(terms_of, axis=0, keepdims=True)
        grad = own_dy_ref[...].astype(F32) + grad
        out_ref[...] = grad
        low_ref[...] = grad.astype(BF)
        wire.drain()

    vmem = pl.BlockSpec(memory_space=pltpu.VMEM)
    expert = jax.ShapeDtypeStruct((local_experts, depth, hidden), F32)
    return comm_call(
        kernel,
        [
            jax.ShapeDtypeStruct((own, dim), F32),
            jax.ShapeDtypeStruct((own, dim), BF),
            jax.ShapeDtypeStruct((16, dim), F32),
            expert,
            expert,
            jax.ShapeDtypeStruct((units, dim), F32),
        ],
        [
            pltpu.VMEM((half, n_bat, own, dim), BF),
            pltpu.VMEM((half, n_bat, own, dim), BF),
            pltpu.VMEM((half, 2, own // 2, dim), BF),
            pltpu.VMEM((half, 2, own, dim), BF),
            pltpu.VMEM((half, own, dim), BF),
            pltpu.VMEM((2, tokens, 256), BF),
            pltpu.VMEM((n_seq, depth, 2 * units), BF),
            pltpu.VMEM((n_seq, depth, 2 * units), BF),
            pltpu.SemaphoreType.DMA((2,)),
            pltpu.VMEM(term.shape, F32),
        ]
        + FullScatter.scratch(n_seq, n_bat, term),
        slots,
        5,
        "experts_backward",
        [vmem] * 3 + [ANY] * 3 + [vmem] * 6,
        [vmem] * 6,
    )(grad_pre, weighted, w_gu, terms, x_all, dy_all, residual, dy_own, gains, router, probs, chosen)


def store_last(grad_w, grad_wo, small, mixture, n_seq, n_bat):
    one = jax.ShapeDtypeStruct(grad_w.shape[2:], grad_w.dtype)
    shard, three = one.shape
    wide = three // 3
    wo_one = jax.ShapeDtypeStruct(grad_wo.shape[1:], grad_wo.dtype)
    small_one = jax.ShapeDtypeStruct((16, 2 * shard), small.dtype)
    half = n_seq // 2
    dim = wo_one.shape[1]
    slots = 64 + n_seq * n_bat + 5 * n_seq

    def kernel(*refs):
        w_ref, wo_ref, small_ref, mix_ref = refs[:4]
        q_out, k_out, v_out, wo_out, small_out, mix_out = refs[4:10]
        w_sum, w_halves, w_full, w_got, wo_sum, wo_halves, wo_full, line = refs[10:18]
        small_scratch = refs[18:23]
        w_sems, wo_sem, send_sems, recv_sems = refs[23:]
        place = Place(n_seq, n_bat)
        place.greet(all_seq=True)
        wire = Wire(send_sems, recv_sems)

        def pick(i, m):
            tile = i * (n_bat // 2) + lax.div(m, 2)
            return small_ref.at[:, pl.ds(pl.multiple_of(tile * 2 * shard, 128), 2 * shard)]

        small_work = FullScatter(place, wire, small_ref, small_out, *small_scratch, pick)
        small_work.start()
        order = list(range(1, n_seq)) + [0]
        loads = {}
        for k in order:
            loads[k] = pltpu.make_async_copy(
                w_ref.at[place.seq_at(k)], w_sum.at[k], w_sems.at[k]
            )
            loads[k].start()
        wo_load = pltpu.make_async_copy(wo_ref, wo_sum, wo_sem.at[0])
        wo_load.start()
        works = {}
        for k in order:
            loads[k].wait()
            works[k] = AcrossSum(place, wire, w_sum.at[k], w_halves.at[k], w_full.at[k])
            works[k].start()
        wo_load.wait()
        wo_work = AcrossSum(place, wire, wo_sum, wo_halves, wo_full)
        wo_work.start()
        term_order = small_work.order()
        for j in term_order:
            small_work.pair(j)
        mix_line = {
            j: wire.push(mix_ref.at[j], line.at[j], place.seq_peer(2 * j)) for j in range(1, half)
        }
        arrivals = []
        ready = None

        def ship(k):
            if k:
                arrivals.append(
                    wire.push(w_sum.at[k, place.b], w_got.at[place.s], place.seq_peer(k))
                )

        for k in order:
            works[k].middle()
        wo_work.middle()
        for j in term_order:
            small_work.merge(j)
        for k in order:
            works[k].finish()
            if ready is not None:
                ship(ready)
            ready = k
        w_got[place.s] = w_sum[0, place.b]
        wo_work.finish()
        wo_out[...] = wo_sum[place.b].astype(F32)
        small_work.finish()
        for copy in arrivals:
            copy.wait_recv()
        for i in range(n_seq):
            at = slice(i * wide, (i + 1) * wide)
            for m, out in enumerate((q_out, k_out, v_out)):
                out[:, at] = w_got[i, :, m * wide : (m + 1) * wide].astype(F32)
        for copy in mix_line.values():
            copy.wait_recv()
        total = mix_ref[0].astype(F32)
        for j in range(1, half):
            total = total + line[j].astype(F32)
        mix_out[...] = total
        wire.drain()

    vmem = pl.BlockSpec(memory_space=pltpu.VMEM)
    matrix = jax.ShapeDtypeStruct((shard, dim), F32)
    return comm_call(
        kernel,
        [matrix] * 4 + [small_one, jax.ShapeDtypeStruct(mixture.shape[1:], F32)],
        [
            pltpu.VMEM((n_seq, n_bat, shard, three), BF),
            pltpu.VMEM((n_seq, 2, shard // 2, three), BF),
            pltpu.VMEM((n_seq, 2, shard, three), BF),
            pltpu.VMEM((n_seq, shard, three), BF),
            pltpu.VMEM((n_bat, shard, dim), BF),
            pltpu.VMEM((2, shard // 2, dim), BF),
            pltpu.VMEM((2, shard, dim), BF),
            pltpu.VMEM(mixture.shape, BF),
        ]
        + FullScatter.scratch(n_seq, n_bat, small_one)
        + [pltpu.SemaphoreType.DMA((n_seq,)), pltpu.SemaphoreType.DMA((1,))],
        slots,
        8,
        "store_last",
        [ANY] * 3 + [vmem],
        [vmem] * 6,
    )(grad_w, grad_wo, small, mixture)


def finish(residual, mixture, grads):
    count = len(grads)

    def kernel(*refs):
        res_ref, mix_ref = refs[:2]
        ins, out_ref, outs = refs[2 : 2 + count], refs[2 + count], refs[3 + count : 3 + 2 * count]
        buffers, sems = refs[3 + 2 * count : 3 + 3 * count], refs[-1]
        loads = []
        for i in range(count):
            copy = pltpu.make_async_copy(ins[i], buffers[i], sems.at[0, i])
            copy.start()
            loads.append(copy)
        out_ref[...] = (res_ref[...] + mix_ref[...]).astype(BF)
        stores = []
        for i in range(count):
            loads[i].wait()
            copy = pltpu.make_async_copy(buffers[i], outs[i], sems.at[1, i])
            copy.start()
            stores.append(copy)
        for copy in stores:
            copy.wait()

    vmem = pl.BlockSpec(memory_space=pltpu.VMEM)
    return pl.pallas_call(
        kernel,
        out_shape=[jax.ShapeDtypeStruct(residual.shape, BF)]
        + [jax.ShapeDtypeStruct(grad.shape, grad.dtype) for grad in grads],
        in_specs=[vmem] * 2 + [ANY] * count,
        out_specs=[vmem] + [ANY] * count,
        scratch_shapes=[pltpu.VMEM(grad.shape, grad.dtype) for grad in grads]
        + [pltpu.SemaphoreType.DMA((2, count))],
        compiler_params=pltpu.CompilerParams(vmem_limit_bytes=VMEM_LIMIT),
        name="finish",
    )(residual, mixture, *grads)


def load_inputs(qkv_cut, w_out, mine, flags, small, gu_cut, dy_own, n_seq, n_bat):
    n_in = 7
    slots = 4 * n_seq * n_bat + 5 * n_seq + 2 * n_bat

    def kernel(*refs):
        cut_ref, wo_ref, x_ref, flag_ref, small_ref, gu_ref, dy_ref = refs[:n_in]
        w_ref, wo_all, x_col, flag_col, small_all, gu_all, dy_all = refs[n_in : 2 * n_in]
        buffers = refs[2 * n_in : 3 * n_in]
        own_sems, send_sems, recv_sems = refs[3 * n_in :]
        place = Place(n_seq, n_bat)
        place.greet(all_seq=True)
        wire = Wire(send_sems, recv_sems)
        small_work = FullGather(place, wire, small_ref, small_all)
        flag_work = SeqGather(place, wire, flag_ref, flag_col)
        x_work = SeqGather(place, wire, x_ref, x_col)
        dy_work = FullGather(place, wire, dy_ref, dy_all)
        small_work.start()
        flag_work.start()
        cuts = [
            wire.push(cut_ref.at[place.seq_at(k)], w_ref.at[place.s, place.b], place.seq_peer(k))
            for k in range(1, n_seq)
        ]
        ends = [
            wire.push(wo_ref, wo_all.at[place.b], place.bat_peer(k)) for k in range(1, n_bat)
        ]
        ends += [
            wire.push(cut_ref.at[place.s], w_ref.at[place.s, place.b], place.bat_peer(k))
            for k in range(1, n_bat)
        ]
        x_work.start()
        own = [
            keep_own(src, dst, buffers[i], own_sems.at[i])
            for i, (src, dst) in enumerate(
                (
                    (cut_ref.at[place.s], w_ref.at[place.s, place.b]),
                    (wo_ref, wo_all.at[place.b]),
                    (x_ref, x_col.at[place.s]),
                    (flag_ref, flag_col.at[place.s]),
                    (small_ref, small_all.at[place.s, place.b]),
                    (gu_ref.at[place.s], gu_all.at[place.s]),
                    (dy_ref, dy_all.at[place.s, place.b]),
                )
            )
        ]
        ends += [
            wire.push(gu_ref.at[place.seq_at(k)], gu_all.at[place.s], place.seq_peer(k))
            for k in range(1, n_seq)
        ]
        dy_work.start()
        for j in range(1, place.half):
            small_work.step(j)
            flag_work.step(j)
        for k in range(1, n_seq):
            cuts[k - 1].wait_recv()
            block = w_ref.at[place.seq_at(-k), place.b]
            ends += [wire.push(block, block, place.bat_peer(m)) for m in range(1, n_bat)]
        for j in range(place.half):
            small_work.collect(j)
        for j in range(1, place.half):
            x_work.step(j)
        for j in range(1, place.half):
            dy_work.step(j)
            dy_work.collect(j - 1)
        dy_work.collect(place.half - 1)
        for work in (small_work, flag_work, x_work, dy_work):
            work.finish()
        for copy in ends:
            copy.wait_recv()
        for copy in own:
            copy.wait()
        wire.drain()

    every = (n_seq, n_bat)
    one = jax.ShapeDtypeStruct(qkv_cut.shape[1:], qkv_cut.dtype)
    gu_one = jax.ShapeDtypeStruct(gu_cut.shape[1:], gu_cut.dtype)
    blocks = (one, w_out, mine, flags, small, gu_one, dy_own)
    leads = (every, (n_bat,), (n_seq,), (n_seq,), every, (n_seq,), every)
    return comm_call(
        kernel,
        [shape_of(lead, block) for lead, block in zip(leads, blocks)],
        [pltpu.VMEM(block.shape, block.dtype) for block in blocks]
        + [pltpu.SemaphoreType.DMA((n_in,))],
        slots,
        1,
        "load_inputs",
        [ANY] * n_in,
    )(qkv_cut, w_out, mine, flags, small, gu_cut, dy_own)


def store_grads(grad_w, grad_wo, grad_gu, small, n_seq, n_bat):
    one = jax.ShapeDtypeStruct(grad_w.shape[2:], grad_w.dtype)
    wo_one = jax.ShapeDtypeStruct(grad_wo.shape[1:], grad_wo.dtype)
    gu_one = jax.ShapeDtypeStruct(grad_gu.shape[1:], grad_gu.dtype)
    small_one = jax.ShapeDtypeStruct(small.shape[2:], small.dtype)
    slots = 2 * n_seq * n_bat + 2 * n_seq + n_bat

    def kernel(*refs):
        w_ref, wo_ref, gu_ref, small_ref = refs[:4]
        w_out_ref, wo_out_ref, gu_out_ref, small_out_ref = refs[4:8]
        w_sum, w_got, wo_sum, wo_got, gu_buf, cut_buf = refs[8:14]
        small_scratch = refs[14:19]
        w_sems, sems, send_sems, recv_sems = refs[19:]
        place = Place(n_seq, n_bat)
        place.greet(all_seq=True)
        wire = Wire(send_sems, recv_sems)
        small_work = FullScatter(
            place, wire, small_ref, small_out_ref, *small_scratch
        )
        small_work.start()
        got, loads = {}, {}
        for i in list(range(1, n_seq)) + [0]:
            to_seq = place.seq_at(i)
            for k in range(1, n_bat):
                got[i, k] = wire.push(
                    w_ref.at[to_seq, place.bat_at(k)], w_got.at[i, k - 1], place.bat_peer(k)
                )
            loads[i] = pltpu.make_async_copy(
                w_ref.at[to_seq, place.b], w_sum.at[i], w_sems.at[i]
            )
            loads[i].start()
        wo_pushed = [
            wire.push(wo_ref.at[place.bat_at(k)], wo_got.at[k - 1], place.bat_peer(k))
            for k in range(1, n_bat)
        ]
        wo_load = pltpu.make_async_copy(wo_ref.at[place.b], wo_sum, sems.at[0])
        wo_load.start()
        ends = [
            wire.push(gu_ref.at[place.seq_at(k)], gu_out_ref.at[place.s], place.seq_peer(k))
            for k in range(1, n_seq)
        ]
        gu_own = keep_own(gu_ref.at[place.s], gu_out_ref.at[place.s], gu_buf, sems.at[1])
        order = small_work.order()
        for j in order:
            small_work.pair(j)
        for i in list(range(1, n_seq)) + [0]:
            loads[i].wait()
            for k in range(1, n_bat):
                got[i, k].wait_recv()
            add_into(w_sum.at[i], *[w_got.at[i, k] for k in range(n_bat - 1)])
            if i:
                ends.append(
                    wire.push(w_sum.at[i], w_out_ref.at[place.s], place.seq_peer(i))
                )
        w_own = pltpu.make_async_copy(w_sum.at[0], w_out_ref.at[place.s], sems.at[2])
        w_own.start()
        for j in order:
            small_work.merge(j)
        wo_load.wait()
        for copy in wo_pushed:
            copy.wait_recv()
        add_into(wo_sum, *[wo_got.at[k] for k in range(n_bat - 1)])
        wo_out_ref[...] = wo_sum[...].astype(F32)
        small_work.finish()
        for copy in ends:
            copy.wait_recv()
        gu_own.wait()
        w_own.wait()
        wire.drain()

    vmem = pl.BlockSpec(memory_space=pltpu.VMEM)
    return comm_call(
        kernel,
        [
            shape_of((n_seq,), one),
            jax.ShapeDtypeStruct(wo_one.shape, F32),
            shape_of((n_seq,), gu_one),
            small_one,
        ],
        [
            pltpu.VMEM((n_seq,) + one.shape, one.dtype),
            pltpu.VMEM((n_seq, n_bat - 1) + one.shape, one.dtype),
            pltpu.VMEM(wo_one.shape, wo_one.dtype),
            pltpu.VMEM((n_bat - 1,) + wo_one.shape, wo_one.dtype),
            pltpu.VMEM(gu_one.shape, gu_one.dtype),
            pltpu.VMEM(one.shape, one.dtype),
        ]
        + FullScatter.scratch(n_seq, n_bat, small_one)
        + [pltpu.SemaphoreType.DMA((n_seq,)), pltpu.SemaphoreType.DMA((3,))],
        slots,
        8,
        "store_grads",
        [ANY] * 4,
        [ANY, vmem, ANY, vmem],
    )(grad_w, grad_wo, grad_gu, small)


def shards(
    tokens,
    lengths,
    key_mask,
    top_experts,
    attn_gain,
    query_gain,
    key_gain,
    mlp_gain,
    w_query,
    w_key,
    w_value,
    w_out,
    w_router,
    expert_gate,
    expert_up,
    expert_down,
    cotangent,
):
    n_seq = lax.axis_size("seq")
    n_bat = lax.axis_size("batch")
    seq = lax.axis_index("seq")
    bat = lax.axis_index("batch")
    rows, span, dim = tokens.shape
    own = rows * span
    col = n_seq * own
    length = n_seq * span
    shard = w_query.shape[0]
    wide = dim // n_seq
    heads = wide // HEAD
    local_experts, depth, hidden_units = expert_gate.shape
    part = hidden_units // n_seq
    experts = local_experts * n_bat

    mine = tokens.reshape(own, dim)
    dy_own = cotangent.reshape(own, dim)
    small = jnp.concatenate(
        [w_router.T, jnp.stack([attn_gain, query_gain, key_gain, mlp_gain])], axis=0
    )
    positions_own = seq * span + jnp.arange(span, dtype=jnp.int32)
    flags = pack((positions_own[None, :] < lengths[:, None]) & (key_mask == 1))
    units = local_experts * part
    fused = (
        n_bat == 4
        and part % 128 == 0
        and own == 128
        and shard % 32 == 0
        and n_seq == 8
        and shard == 64
        and experts == 8
        and span == 64
        and rows <= 8
        and n_seq * n_bat * own * dim <= 8 * 1024 * 1024
    )
    if fused:
        gains = jnp.stack([attn_gain, query_gain, key_gain, mlp_gain])
        small = jnp.concatenate([w_router.T, jnp.pad(gains, ((0, 4), (0, 0)))], axis=1).astype(F32)
        flags = (positions_own[None, :] < lengths[:, None]) & (key_mask == 1)
        flags = jnp.pad(flags.astype(F32), ((0, 8 - rows), (0, 128 - span)))
        w_qkv, w_o, x_col, router_t, gains, usable = load_first(
            (w_query, w_key, w_value), w_out, mine, flags, small, rows, n_seq, n_bat
        )
    else:
        qkv_cut = jnp.stack([w_query, w_key, w_value]).reshape(3, shard, n_seq, wide)
        qkv_cut = jnp.transpose(qkv_cut, (2, 1, 0, 3)).reshape(n_seq, shard, 3 * wide)
        gu_cut = jnp.stack([expert_gate, expert_up]).reshape(2, local_experts, depth, n_seq, part)
        gu_cut = jnp.transpose(gu_cut, (3, 2, 0, 1, 4)).reshape(n_seq, depth, 2 * units)
        w_qkv, w_o, x_col, flag_col, small_all, w_gu, dy_all = load_inputs(
            qkv_cut, w_out, mine, flags, pack(small), gu_cut, dy_own, n_seq, n_bat
        )
        w_gu = w_gu.reshape(dim, 2 * units)
        dy_all = dy_all.reshape(-1, dim)
        x_col = jnp.transpose(x_col.reshape(n_seq, rows, span, dim), (1, 0, 2, 3))
    w_qkv = w_qkv.reshape(dim, 3 * wide)
    w_o = w_o.reshape(wide, dim)
    w_down = expert_down.reshape(local_experts * part, dim)
    if not fused:
        small_all = unpack(small_all, (n_seq, n_bat), small.shape)
        small_all = jnp.transpose(small_all, (2, 0, 1, 3)).reshape(-1, dim)
        router = small_all[:experts].T.astype(BF)
        gains = small_all[experts:]
        gain_attn, gain_mlp = gains[0], gains[3]
        usable = unpack(flag_col, (n_seq,), key_mask.shape)
        usable = jnp.transpose(usable, (1, 0, 2)).reshape(rows, length)
        router_t = small_all[:experts]

    expert_ids = jnp.arange(experts, dtype=jnp.int32)
    chosen_t = jnp.any(top_experts.reshape(own, -1).T[None] == expert_ids[:, None, None], axis=1)
    chosen_t = chosen_t.astype(F32)
    cos_part, sin_part = rotary_tables(jnp.arange(length, dtype=jnp.int32))
    cos_wide = jnp.concatenate([cos_part, cos_part], axis=1)
    sin_wide = jnp.concatenate([-sin_part, sin_part], axis=1)
    hidden, qkv, q, k, v, mixed, stats, mixed_out, *extra = attend_forward(
        x_col.reshape(col, dim), w_qkv, usable, w_o, gains, cos_wide, sin_wide, n_seq, n_bat, rows,
        (dy_own, mine, router_t, chosen_t) if fused else None,
    )
    if not fused:
        x_own = mine.astype(F32)
        residual = x_own + mixed_out.astype(F32)
        scale_r = rms_scale(residual)
        normed = (residual * scale_r * gain_mlp).astype(BF)
        router_probs = jax.nn.softmax(dot(normed, router), axis=-1)
        chosen = chosen_t.T
        gates = router_probs * chosen

    if fused:
        dy_all, residual, normed, probs_t, gates_t = extra
        normed_all, weighted, grad_pre, gate_terms, w_gu = experts_forward(
            normed, gates_t, dy_all, expert_gate, expert_up, w_down, n_seq, n_bat
        )
        w_gu = w_gu.reshape(dim, 2 * units)
        grad_residual, grad_o, small_grads, grad_gate, grad_up, grad_down = experts_backward(
            grad_pre,
            weighted,
            w_gu,
            gate_terms,
            normed_all.reshape(-1, dim),
            dy_all.reshape(-1, dim),
            residual,
            dy_own,
            gains,
            router_t,
            probs_t,
            chosen_t,
            local_experts,
            n_seq,
            n_bat,
        )
        grad_down = grad_down.reshape(local_experts, part, dim)
    else:
        normed_all, gates_all = gather_all([normed, pack(gates.T)], n_seq, n_bat, 4, "gather_normed")
        normed_all = normed_all.reshape(-1, dim)
        gates_all = unpack(gates_all, (n_seq, n_bat), (experts, own))
        gates_all = jnp.transpose(gates_all, (0, 1, 3, 2)).reshape(-1, experts)
        first_expert = bat * local_experts
        gates_here = lax.dynamic_slice_in_dim(gates_all, first_expert, local_experts, 1)
        gates_wide = jnp.repeat(gates_here, part, axis=1)
        pre = dot(normed_all, w_gu)
        gate_pre, up_pre = pre[:, :units], pre[:, units:]
        sig = jax.nn.sigmoid(gate_pre)
        silu = gate_pre * sig
        active = (silu * up_pre).astype(BF).astype(F32)
        weighted = (active * gates_wide).astype(BF)
        mixture = dot(weighted, w_down).astype(BF)
        mixture = mixture.reshape(n_seq, n_bat, own, dim)
        back = dot_t(dy_all, w_down)
        gate_terms = jnp.sum((active * back).reshape(-1, local_experts, part), axis=-1)
        grad_active = back * gates_wide
        grad_gate_pre = (grad_active * up_pre * sig * (1.0 + gate_pre * (1.0 - sig))).astype(BF)
        grad_up_pre = (grad_active * silu).astype(BF)
        grad_pre = jnp.concatenate([grad_gate_pre, grad_up_pre], axis=1)
        grad_down = t_dot(weighted, dy_all)
        grad_gu = t_dot(normed_all, grad_pre).astype(BF)
        grad_normed = dot_t(grad_pre, w_gu).astype(BF)
        gate_terms = gate_terms.reshape(n_seq, n_bat, own, local_experts)
        grad_gates = lax.dynamic_update_slice_in_dim(
            jnp.zeros((n_seq, n_bat, experts, own), F32),
            jnp.transpose(gate_terms, (0, 1, 3, 2)),
            first_expert,
            2,
        )
        grad_gates = jax.vmap(jax.vmap(pack))(grad_gates)
        grad_normed = grad_normed.reshape(n_seq, n_bat, own, dim)
        grad_normed, grad_gates, mixture = scatter_blocks(
            grad_normed, grad_gates, mixture, n_seq, n_bat
        )
        grad_normed = grad_normed.astype(F32)
        grad_gates = unpack(grad_gates, (), (experts, own)).T
        output = (residual + mixture.astype(F32)).astype(BF)
        grad_down = grad_down.reshape(local_experts, part, dim)

    if not fused:
        grad_chosen = grad_gates * chosen
        grad_logits = router_probs * (
            grad_chosen - jnp.sum(router_probs * grad_chosen, axis=-1, keepdims=True)
        )
        grad_router = lax.dot_general(
            normed.astype(F32), grad_logits, (((0,), (0,)), ((), ())), precision=HIGHEST
        )
        grad_normed = grad_normed + lax.dot_general(
            grad_logits, router.astype(F32), (((1,), (1,)), ((), ())), precision=HIGHEST
        )
        grad_resid, gain_mlp_terms = rms_back(residual, scale_r, gain_mlp, grad_normed)
        grad_residual = dy_own.astype(F32) + grad_resid
        grad_o = grad_residual.astype(BF)

    grad_w_o, grad_w, grad_gains, grad_hidden, *extra = attend_backward(
        grad_o, q, k, v, mixed, qkv, stats, hidden, usable, w_o, w_qkv, gains, cos_wide, sin_wide,
        n_seq, n_bat,
        (weighted, w_down, mine, grad_residual, small_grads) if fused else None,
    )
    grad_w_o = grad_w_o.reshape(n_bat, shard, dim)
    grad_w = grad_w.reshape(n_seq, n_bat, shard, 3 * wide)
    if not fused:
        grad_hidden = grad_hidden.astype(F32)
        grad_x, gain_attn_terms = rms_back(x_own, rms_scale(x_own), gain_attn, grad_hidden)
        grad_tokens = (grad_residual + grad_x).astype(BF)

        zeros = jnp.zeros((dim,), F32)
        small_grads = jnp.concatenate(
            [
                grad_router.T,
                jnp.stack(
                    [
                        jnp.sum(gain_attn_terms, axis=0),
                        lax.dynamic_update_slice_in_dim(zeros, grad_gains[0], seq * wide, 0),
                        lax.dynamic_update_slice_in_dim(zeros, grad_gains[1], seq * wide, 0),
                        jnp.sum(gain_mlp_terms, axis=0),
                    ]
                ),
            ],
            axis=0,
        )
        small_grads = jnp.transpose(small_grads.reshape(-1, n_seq, n_bat, shard), (1, 2, 0, 3))
        small_grads = jax.vmap(jax.vmap(pack))(small_grads)

    if fused:
        *grad_w, grad_w_o, small_grads, mixture = store_last(
            grad_w, grad_w_o, extra[1], extra[0], n_seq, n_bat
        )
        output, grad_tokens, *grad_w, grad_w_o, grad_gate, grad_up, grad_down = finish(
            residual, mixture, [grad_hidden, *grad_w, grad_w_o, grad_gate, grad_up, grad_down]
        )
        small_grads = lax.dynamic_slice_in_dim(small_grads, lax.rem(bat, 2) * shard, shard, 1)
    else:
        grad_gu = grad_gu.reshape(n_seq, depth, -1)
        grad_w, grad_w_o, grad_gu, small_grads = store_grads(
            grad_w, grad_w_o, grad_gu, small_grads, n_seq, n_bat
        )
        grad_w = grad_w.astype(F32).reshape(n_seq, shard, 3, wide)
        grad_w = jnp.transpose(grad_w, (2, 1, 0, 3)).reshape(3, shard, dim)
        grad_gu = grad_gu.reshape(n_seq, depth, 2, local_experts, part)
        grad_gu = jnp.transpose(grad_gu, (2, 3, 1, 0, 4)).reshape(2, local_experts, depth, hidden_units)
        grad_gu = grad_gu.astype(F32)
        grad_gate, grad_up = grad_gu[0], grad_gu[1]
        small_grads = unpack(small_grads, (), (experts + 4, shard))

    return (
        output.reshape(rows, span, dim),
        grad_tokens.reshape(rows, span, dim),
        small_grads[experts],
        small_grads[experts + 1],
        small_grads[experts + 2],
        small_grads[experts + 3],
        grad_w[0],
        grad_w[1],
        grad_w[2],
        grad_w_o,
        small_grads[:experts].T,
        grad_gate,
        grad_up,
        grad_down,
    )


def solution(mesh):
    tok = P("batch", "seq", None)
    vec = P(("seq", "batch"))
    mat = P(("seq", "batch"), None)
    in_specs = (tok, P("batch"), P("batch", "seq"), tok) + (vec,) * 4 + (mat,) * 5 + (tok,) * 4
    out_specs = (tok, tok) + (vec,) * 4 + (mat,) * 5 + (tok,) * 3
    return jax.shard_map(shards, mesh=mesh, in_specs=in_specs, out_specs=out_specs, check_vma=False)
```

```python
import functools

import jax
import jax.numpy as jnp
import numpy as np
from jax import lax
from jax.experimental import pallas as pl
from jax.experimental.pallas import tpu as pltpu
from jax.sharding import PartitionSpec as P

HEAD = 128
EPS = 1e-05
HIGHEST = lax.Precision.HIGHEST
NEGATIVE = -1e30
BF = jnp.bfloat16
F32 = jnp.float32


def dot(a, b):
    return jnp.dot(a, b, preferred_element_type=F32)


def dot_t(a, b):
    return lax.dot_general(a, b, (((1,), (1,)), ((), ())), preferred_element_type=F32)


def t_dot(a, b):
    return lax.dot_general(a, b, (((0,), (0,)), ((), ())), preferred_element_type=F32)


def rms_scale(v):
    return lax.rsqrt(jnp.mean(v * v, axis=-1, keepdims=True) + EPS)


def rms_back(v, scale, gain, grad):
    normal = v * scale
    weighted = grad * gain
    mean = jnp.mean(weighted * normal, axis=-1, keepdims=True)
    return scale * (weighted - normal * mean), grad * normal


def rotary_tables(length):
    half_head = HEAD // 2
    frequency = 10000.0 ** (-2.0 * np.arange(half_head, dtype=np.float32) / HEAD)
    angles = np.arange(length, dtype=np.float32)[:, None] * frequency.astype(np.float32)[None, :]
    cosines, sines = np.cos(angles), np.sin(angles)
    return np.concatenate([cosines, cosines], axis=1), np.concatenate([-sines, sines], axis=1)


ANY = pl.BlockSpec(memory_space=pl.ANY)
VMEM_LIMIT = 67043328


class Place:
    def __init__(self, n_seq, n_bat):
        self.n_seq, self.n_bat, self.half = n_seq, n_bat, n_seq // 2
        self.s = lax.axis_index("seq")
        self.b = lax.axis_index("batch")
        self.core = lax.rem(self.s, 2)
        self.z = lax.div(self.s, 2)
        self.twin_s = self.s + 1 - 2 * self.core
        self.bat_x = self.b + 1 - 2 * lax.rem(self.b, 2)
        self.bat_y = lax.rem(self.b + 2, 4)
        self.bat_d = lax.rem(self.bat_x + 2, 4)

    def chip(self, i):
        return 2 * i + self.core

    def chip_twin(self, i):
        return 2 * i + 1 - self.core

    def chip_peer(self, i):
        return {"seq": self.chip(lax.rem(i + self.half, self.half)), "batch": self.b}

    def origin(self, m):
        return self.z if m == 0 else self.origin_of(m)

    def origin_of(self, m):
        last = self.half - 1
        upper = lax.div(2 * self.z, self.half)
        mirrored = self.z + upper * (last - 2 * self.z)
        place = m - 1 + lax.div(m - mirrored + last, self.half)
        return place + upper * (last - 2 * place)

    def seq_at(self, k):
        return lax.rem(self.s + (k + self.n_seq), self.n_seq)

    def twin_at(self, k):
        return lax.rem(self.twin_s + (k + self.n_seq), self.n_seq)

    def bat_at(self, k):
        return lax.rem(self.b + (k + self.n_bat), self.n_bat)

    def seq_peer(self, k):
        return {"seq": self.seq_at(k), "batch": self.b}

    def bat_peer(self, k):
        return {"seq": self.s, "batch": self.bat_at(k)}

    def x_peer(self):
        return {"seq": self.s, "batch": self.bat_x}

    def y_peer(self):
        return {"seq": self.s, "batch": self.bat_y}

    def twin(self):
        return {"seq": self.twin_s, "batch": self.b}

    def greet(self, all_seq=False, batch=True):
        steps = range(1, self.n_seq) if all_seq else range(2, self.n_seq, 2)
        peers = [self.seq_peer(k) for k in steps]
        if not all_seq:
            peers.append(self.twin())
        if batch:
            peers += [self.bat_peer(k) for k in range(1, self.n_bat)]
        barrier = pltpu.get_barrier_semaphore()
        for peer in peers:
            pl.semaphore_signal(
                barrier, inc=1, device_id=peer, device_id_type=pl.DeviceIdType.MESH
            )
        pl.semaphore_wait(barrier, len(peers))


class Wire:
    def __init__(self, send_sems, recv_sems):
        self.send_sems, self.recv_sems = send_sems, recv_sems
        self.copies, self.used = [], 0

    def reserve(self, count):
        first = self.used
        self.used += count
        return first

    def make(self, src, dst, peer, send_slot, recv_slot):
        return pltpu.make_async_remote_copy(
            src_ref=src,
            dst_ref=dst,
            send_sem=self.send_sems.at[send_slot],
            recv_sem=self.recv_sems.at[recv_slot],
            device_id=peer,
            device_id_type=pl.DeviceIdType.MESH,
        )

    def push(self, src, dst, peer):
        slot = self.reserve(1)
        copy = self.make(src, dst, peer, slot, slot)
        copy.start()
        self.copies.append((copy, None))
        return copy

    def push_if(self, there, copy):
        pl.when(there)(copy.start)
        self.copies.append((copy, there))

    def settle(self, copy):
        copy.wait_send()
        self.copies = [other for other in self.copies if other[0] is not copy]

    def drain(self):
        for copy, there in self.copies:
            if there is None:
                copy.wait_send()
            else:
                pl.when(there)(copy.wait_send)


class Line:
    def __init__(self, place, wire, src, at):
        self.place, self.wire, self.src, self.at = place, wire, src, at
        self.base = wire.reserve(place.half + 2)
        self.sends = 0

    def copy(self, src, origin, peer):
        return self.wire.make(
            src, self.at(origin), peer, self.base + self.sends, self.base + origin
        )

    def send(self, there, src, origin, to):
        copy = self.copy(src, origin, self.place.chip_peer(to))
        self.sends += 1
        self.wire.push_if(there, copy)

    def start(self):
        place = self.place
        self.send(place.z < place.half - 1, self.src, place.z, place.z + 1)
        self.send(place.z > 0, self.src, place.z, place.z - 1)

    def step(self, m):
        place = self.place
        origin = place.origin(m)
        self.copy(self.at(origin), origin, place.chip_peer(place.z)).wait_recv()
        from_left = lax.div(place.z - origin - 1 + place.half, place.half)
        to = place.z + 2 * from_left - 1
        self.send((to >= 0) & (to < place.half), self.at(origin), origin, to)
        return origin


class SeqGather:
    def __init__(self, place, wire, src, out):
        self.place, self.wire, self.src, self.out = place, wire, src, out
        self.late = []

    def start(self):
        place = self.place
        self.line = Line(place, self.wire, self.src, lambda i: self.out.at[place.chip(i)])
        self.line.start()
        self.late.append(self.wire.push(self.src, self.out.at[place.s], place.twin()))

    def step(self, j):
        block = self.out.at[self.place.chip(self.line.step(j))]
        self.late.append(self.wire.push(block, block, self.place.twin()))

    def finish(self):
        for copy in self.late:
            copy.wait_recv()


class FullGather:
    def __init__(self, place, wire, src, out):
        self.place, self.wire, self.src, self.out = place, wire, src, out
        self.late = []
        self.across = {}

    def spread(self, j, block):
        place = self.place
        self.across[j] = [
            self.wire.push(block, self.out.at[place.seq_at(-2 * j), place.b], place.bat_peer(k))
            for k in range(1, place.n_bat)
        ]

    def start(self):
        place, mine = self.place, self.out.at[self.place.s, self.place.b]
        self.line = [
            self.wire.push(self.src, mine, place.seq_peer(2 * j)) for j in range(1, place.half)
        ]
        self.spread(0, self.src)
        self.late.append(self.wire.push(self.src, mine, place.twin()))

    def step(self, j):
        self.line[j - 1].wait_recv()
        block = self.out.at[self.place.seq_at(-2 * j), self.place.b]
        self.spread(j, block)
        self.late.append(self.wire.push(block, block, self.place.twin()))

    def collect(self, j):
        place = self.place
        for k in range(1, place.n_bat):
            self.across[j][k - 1].wait_recv()
            block = self.out.at[place.seq_at(-2 * j), place.bat_at(-k)]
            self.late.append(self.wire.push(block, block, place.twin()))

    def finish(self):
        for copy in self.late:
            copy.wait_recv()


def keep_own(src, dst, buffer, sem):
    first = pltpu.make_async_copy(src, buffer, sem)
    first.start()
    first.wait()
    second = pltpu.make_async_copy(buffer, dst, sem)
    second.start()
    return second


def comm_call(
    kernel, outs, scratch, slots, collective_id, name, in_specs, out_specs=None, aliases=None
):
    return pl.pallas_call(
        kernel,
        out_shape=outs,
        in_specs=in_specs,
        out_specs=out_specs if out_specs is not None else jax.tree.map(lambda _: ANY, outs),
        scratch_shapes=list(scratch)
        + [pltpu.SemaphoreType.DMA((slots,)), pltpu.SemaphoreType.DMA((slots,))],
        compiler_params=pltpu.CompilerParams(
            collective_id=collective_id, has_side_effects=True, vmem_limit_bytes=VMEM_LIMIT
        ),
        name=name,
        input_output_aliases=aliases or {},
    )


def shape_of(lead, block):
    return jax.ShapeDtypeStruct(tuple(lead) + block.shape, block.dtype)


def gather_all(blocks, n_seq, n_bat, collective_id, name):
    count = len(blocks)

    def kernel(*refs):
        srcs, outs = refs[:count], refs[count : 2 * count]
        buffers = refs[2 * count : 3 * count]
        own_sems, send_sems, recv_sems = refs[3 * count :]
        place = Place(n_seq, n_bat)
        place.greet()
        wire = Wire(send_sems, recv_sems)
        gathers = [FullGather(place, wire, *pair) for pair in zip(srcs, outs)]
        for gather in gathers:
            gather.start()
        own = [
            keep_own(srcs[i], outs[i].at[place.s, place.b], buffers[i], own_sems.at[i])
            for i in range(count)
        ]
        for j in range(1, place.half):
            for gather in gathers:
                gather.step(j)
            for gather in gathers:
                gather.collect(j - 1)
        for gather in gathers:
            gather.collect(place.half - 1)
        for gather in gathers:
            gather.finish()
        for copy in own:
            copy.wait()
        wire.drain()

    return comm_call(
        kernel,
        [shape_of((n_seq, n_bat), block) for block in blocks],
        [pltpu.VMEM(block.shape, block.dtype) for block in blocks]
        + [pltpu.SemaphoreType.DMA((count,))],
        n_seq * n_bat * count,
        collective_id,
        name,
        [ANY] * count,
    )(*blocks)


def add_into(target, *others):
    rows = target.shape[0]
    step = min(rows, 16)

    def body(i, carry):
        at = pl.ds(pl.multiple_of(i * step, step), step)
        total = target[at, :].astype(F32)
        for other in others:
            total = total + other[at, :].astype(F32)
        target[at, :] = total.astype(target.dtype)
        return carry

    lax.fori_loop(0, rows // step, body, 0)


class FullScatter:
    def __init__(self, place, wire, parts, out, mine, twin, across, line, sems, pick=None):
        self.place, self.wire, self.out = place, wire, out
        self.mine, self.twin, self.across, self.line = mine, twin, across, line
        self.sems = sems
        self.pick = pick or (lambda i, j: parts.at[i, j])

    @staticmethod
    def scratch(n_seq, n_bat, block):
        half = n_seq // 2
        return [
            pltpu.VMEM((half, n_bat) + block.shape, block.dtype),
            pltpu.VMEM((half, n_bat) + block.shape, block.dtype),
            pltpu.VMEM((half, n_bat) + block.shape, block.dtype),
            pltpu.VMEM((half,) + block.shape, block.dtype),
            pltpu.SemaphoreType.DMA((half, n_bat)),
        ]

    def order(self):
        return list(range(1, self.place.half)) + [0]

    def start(self):
        place = self.place
        self.from_twin, self.loads, self.from_bat, self.from_seq = {}, {}, {}, {}
        for j in self.order():
            for k in list(range(1, place.n_bat)) + [0]:
                to_bat = place.bat_at(k)
                self.from_twin[j, k] = self.wire.push(
                    self.pick(place.twin_at(2 * j), to_bat), self.twin.at[j, k], place.twin()
                )
                load = pltpu.make_async_copy(
                    self.pick(place.seq_at(2 * j), to_bat),
                    self.mine.at[j, k],
                    self.sems.at[j, k],
                )
                load.start()
                self.loads[j, k] = load

    def pair(self, j):
        place = self.place
        for k in list(range(1, place.n_bat)) + [0]:
            self.from_twin[j, k].wait_recv()
            self.loads[j, k].wait()
            add_into(self.mine.at[j, k], self.twin.at[j, k])
        for k in range(1, place.n_bat):
            self.from_bat[j, k] = self.wire.push(
                self.mine.at[j, k], self.across.at[j, k], place.bat_peer(k)
            )

    def merge(self, j):
        place = self.place
        for k in range(1, place.n_bat):
            self.from_bat[j, k].wait_recv()
        add_into(self.mine.at[j, 0], *[self.across.at[j, k] for k in range(1, place.n_bat)])
        if j:
            self.from_seq[j] = self.wire.push(
                self.mine.at[j, 0], self.line.at[j], place.seq_peer(2 * j)
            )

    def finish(self):
        for j in range(1, self.place.half):
            self.from_seq[j].wait_recv()
        add_into(self.mine.at[0, 0], *[self.line.at[j] for j in range(1, self.place.half)])
        self.out[...] = self.mine[0, 0]


def scatter_all(parts, n_seq, n_bat, collective_id, name):
    blocks = [jax.ShapeDtypeStruct(part.shape[2:], part.dtype) for part in parts]
    count = len(parts)

    def kernel(*refs):
        ins, outs = refs[:count], refs[count : 2 * count]
        rest = refs[2 * count :]
        send_sems, recv_sems = rest[-2:]
        place = Place(n_seq, n_bat)
        place.greet()
        wire = Wire(send_sems, recv_sems)
        works = [
            FullScatter(place, wire, ins[i], outs[i], *rest[5 * i : 5 * i + 5])
            for i in range(count)
        ]
        for work in works:
            work.start()
        order = works[0].order()
        for at, j in enumerate(order):
            for work in works:
                work.pair(j)
            if at:
                for work in works:
                    work.merge(order[at - 1])
        for work in works:
            work.merge(order[-1])
        for work in works:
            work.finish()
        wire.drain()

    scratch = []
    for block in blocks:
        scratch += FullScatter.scratch(n_seq, n_bat, block)
    slots = count * (n_seq * n_bat)
    vmem = pl.BlockSpec(memory_space=pltpu.VMEM)
    return comm_call(
        kernel,
        blocks,
        scratch,
        slots,
        collective_id,
        name,
        [ANY] * count,
        [vmem] * count,
    )(*parts)


def pack(values):
    flat = values.astype(F32).reshape(-1)
    tiles = -(-flat.shape[0] // 1024)
    return jnp.pad(flat, (0, tiles * 1024 - flat.shape[0])).reshape(tiles * 8, 128)


def unpack(tiles, lead, shape):
    size = 1
    for extent in shape:
        size *= extent
    return tiles.reshape(tuple(lead) + (-1,))[..., :size].reshape(tuple(lead) + tuple(shape))


def scatter_blocks(grad_normed, grad_gates, mixture, n_seq, n_bat):
    dim = grad_normed.shape[-1]
    pieces = 1
    while n_seq * n_bat * grad_normed.shape[2] * (dim // pieces) * 4 > 36 * 1024 * 1024:
        pieces *= 2
    size = dim // pieces
    grads, mixtures = [], []
    for i in range(pieces):
        at = slice(i * size, (i + 1) * size)
        parts = [grad_normed[..., at]] + ([grad_gates] if i == 0 else [])
        done = scatter_all(parts, n_seq, n_bat, 16 + 2 * i, "scatter_normed")
        grads.append(done[0])
        if i == 0:
            gates = done[1]
        done = scatter_all([mixture[..., at]], n_seq, n_bat, 17 + 2 * i, "scatter_mixture")
        mixtures.append(done[0])
    return jnp.concatenate(grads, axis=-1), gates, jnp.concatenate(mixtures, axis=-1)


class SeqScatter:
    def __init__(self, place, wire, full, twin, line):
        self.place, self.wire = place, wire
        self.full, self.twin, self.line = full, twin, line
        self.order = list(range(1, place.half)) + [0]

    @staticmethod
    def scratch(rows, n_seq, block):
        lead = ((rows, n_seq), (rows, n_seq // 2), (rows, n_seq // 2))
        return [pltpu.VMEM(extent + block.shape, block.dtype) for extent in lead]

    def start(self):
        place = self.place
        self.from_seq = {}
        self.from_twin = {
            j: self.wire.push(self.full.at[place.twin_at(2 * j)], self.twin.at[j], place.twin())
            for j in self.order
        }

    def pass_on(self, first=0, last=None):
        place = self.place
        for j in self.order[first:last]:
            self.from_twin[j].wait_recv()
            block = self.full.at[place.seq_at(2 * j)]
            add_into(block, self.twin.at[j])
            if j:
                self.from_seq[j] = self.wire.push(block, self.line.at[j], place.seq_peer(2 * j))

    def total(self):
        for copy in self.from_seq.values():
            copy.wait_recv()
        total = self.full[self.place.s].astype(F32)
        for j in range(1, self.place.half):
            total = total + self.line[j].astype(F32)
        return total

    def finish(self, out, at):
        for copy in self.from_seq.values():
            copy.wait_recv()
        own = self.full.at[self.place.s]
        add_into(own, *[self.line.at[j] for j in range(1, self.place.half)])
        out[at, :] = own[...]


def turn(v, cos_wide, sin_wide):
    return v * cos_wide + pltpu.roll(v, HEAD // 2, axis=1) * sin_wide


class Exchange:
    def __init__(self, place, wire, local, got):
        self.local, self.got, self.count = local, got, place.n_seq - 1
        self.copies = [
            wire.push(local, got.at[k - 1], place.seq_peer(k)) for k in range(1, place.n_seq)
        ]

    def total(self):
        for copy in self.copies:
            copy.wait_recv()
        total = self.local[...]
        for k in range(self.count):
            total = total + self.got[k]
        return total


def in_two(v):
    high = v.astype(BF)
    return high, (v - high.astype(F32)).astype(BF)


def lane_sums(v):
    ones = jnp.ones((8, v.shape[1]), BF)
    high, low = in_two(v)
    return (dot_t(ones, high) + dot_t(ones, low))[0:1]


def allowed_block(use, first, count, keys):
    at_query = first + lax.broadcasted_iota(jnp.int32, (count, keys), 0)
    at_key = lax.broadcasted_iota(jnp.int32, (count, keys), 1)
    return (at_key == at_query) | ((at_key < at_query) & (use > 0))


STEP = 128


def head_gain(place, gains_ref, which, wide, h):
    first = pl.multiple_of(place.s * wide + h * HEAD, HEAD)
    return gains_ref[1 + which : 2 + which, pl.ds(first, HEAD)]


def attend_forward(
    x_col, w_qkv, usable, w_o, gains, cos_wide, sin_wide, n_seq, n_bat, rows, side=None
):
    col, dim = x_col.shape
    three = w_qkv.shape[1]
    wide = three // 3
    heads = wide // HEAD
    length = col // rows
    span = length // n_seq
    own = rows * span
    steps = length // STEP
    chunk = min(256, length)
    scale = HEAD ** (-0.5)
    block = jax.ShapeDtypeStruct((span, dim), BF)

    def kernel(*refs):
        (x_ref, w_ref, use_ref, wo_ref, gains_ref, cos_ref, sin_ref) = refs[:7]
        refs = refs[7:]
        if side is not None:
            dy_ref, own_ref, router_ref, chosen_ref = refs[:4]
            refs = refs[4:]
        hid_ref, qkv_ref, q_ref, k_ref, v_ref, mix_ref, stat_ref, out_ref = refs[:8]
        refs = refs[8:]
        if side is not None:
            dy_all, res_ref, normed_ref, probs_ref, gates_ref = refs[:5]
            dy_keep, dy_sem = refs[-4:-2]
            refs = refs[5:-4] + refs[-2:]
        local, got, full, twin, line, send_sems, recv_sems = refs
        place = Place(n_seq, n_bat)
        place.greet(all_seq=True, batch=side is not None)
        wire = Wire(send_sems, recv_sems)
        dy_works, dy_here = [], [place.chip(place.origin(m)) for m in range(place.half)]

        def dy_spread(m):
            if side is None:
                return
            if m:
                dy_line.step(m)
            src = dy_all.at[dy_here[m], place.b] if m else dy_ref
            work = Across(place, wire, src, lambda i: dy_all.at[dy_here[m], i])
            work.start()
            dy_works.append(work)

        if side is not None:
            dy_line = Line(place, wire, dy_ref, lambda i: dy_all.at[place.chip(i), place.b])
            dy_line.start()
            dy_spread(0)
            dy_own = keep_own(dy_ref, dy_all.at[place.s, place.b], dy_keep, dy_sem)
        def project(n, carry):
            at = pl.ds(pl.multiple_of(n * chunk, chunk), chunk)
            x = x_ref[at, :].astype(F32)
            hidden = (x * rms_scale(x) * gains_ref[0:1, :]).astype(BF)
            hid_ref[at, :] = hidden
            qkv_ref[at, :] = dot(hidden, w_ref[...])
            return carry

        lax.fori_loop(0, col // chunk, project, 0)
        for r in range(rows):
            for c in range(steps):
                at = slice(r * length + c * STEP, r * length + (c + 1) * STEP)
                for which in range(2):
                    v = qkv_ref[at, which * wide : (which + 1) * wide]
                    row = (r * 2 + which) * steps + c
                    local[row : row + 1, :] = lane_sums(v * v)
        for r in range(rows):
            for h in range(heads):
                lanes = slice(2 * wide + h * HEAD, 2 * wide + (h + 1) * HEAD)
                v_ref[r, h] = qkv_ref[r * length : (r + 1) * length, lanes].astype(BF)
        exchange = Exchange(place, wire, local, got)
        dy_spread(1)
        total = exchange.total()
        stat_ref[...] = total
        columns = lax.rsqrt(total / dim + EPS).T
        scatters = [
            SeqScatter(place, wire, full.at[r], twin.at[r], line.at[r]) for r in range(rows)
        ]
        for r in range(rows):
            for c in range(steps):
                inside = slice(c * STEP, (c + 1) * STEP)
                at = slice(r * length + c * STEP, r * length + (c + 1) * STEP)
                for which, target in ((0, q_ref), (1, k_ref)):
                    row = (r * 2 + which) * steps + c
                    factor = columns[:, row : row + 1]
                    for h in range(heads):
                        lanes = slice(which * wide + h * HEAD, which * wide + (h + 1) * HEAD)
                        gain = head_gain(place, gains_ref, which, wide, h)
                        v = qkv_ref[at, lanes] * factor * gain
                        target[r, h, inside, :] = turn(
                            v, cos_ref[inside, :], sin_ref[inside, :]
                        ).astype(BF)
            for c in range(length // chunk):
                keys = (c + 1) * chunk
                allowed = allowed_block(use_ref[r : r + 1, :keys], c * chunk, chunk, keys)
                for h in range(heads):
                    query = q_ref[r, h, c * chunk : keys, :]
                    scores = dot_t(query, k_ref[r, h, :keys, :]) * scale
                    scores = jnp.where(allowed, scores, NEGATIVE)
                    raised = jnp.exp(scores - jnp.max(scores, axis=-1, keepdims=True))
                    probs = raised / jnp.sum(raised, axis=-1, keepdims=True)
                    mixed = dot(probs.astype(BF), v_ref[r, h, :keys, :]).astype(BF)
                    mix_ref[r, c * chunk : keys, h * HEAD : (h + 1) * HEAD] = mixed
                if r and c == 0:
                    scatters[r - 1].pass_on()
                if r == 0 and c == 0 and side is not None:
                    dy_works[0].relay()
                    dy_spread(2)
            full[r] = dot(mix_ref[r], wo_ref[...]).astype(BF).reshape(n_seq, span, dim)
            scatters[r].start()
            if r == 0 and side is not None:
                dy_works[1].relay()
                for m in range(3, place.half):
                    dy_spread(m)
        scatters[-1].pass_on()
        for work in dy_works[2:]:
            work.relay()
        passed = []
        if side is not None:
            dy_own.wait()
        for m, work in enumerate(dy_works):
            work.finish()
            group = dy_all.at[dy_here[m]]
            passed.append(wire.push(group, group, place.twin()))
        for r in range(rows):
            at = slice(r * span, (r + 1) * span)
            if side is None:
                scatters[r].finish(out_ref, at)
                continue
            residual = own_ref[at, :].astype(F32) + scatters[r].total()
            res_ref[at, :] = residual
            normed_ref[at, :] = (residual * rms_scale(residual) * gains_ref[3:4, :]).astype(BF)
        if side is not None:
            out_ref[...] = jnp.zeros_like(out_ref)
            logits = dot_t(router_ref[...].astype(BF), normed_ref[...])
            raised = jnp.exp(logits - jnp.max(logits, axis=0, keepdims=True))
            probs = raised / jnp.sum(raised, axis=0, keepdims=True)
            probs_ref[...] = probs
            gates_ref[...] = probs * chosen_ref[...]
        for copy in passed:
            copy.wait_recv()
        wire.drain()

    vmem = pl.BlockSpec(memory_space=pltpu.VMEM)
    side_in, side_out, side_scratch = [], [], []
    slots = (1 + rows) * n_seq
    if side is not None:
        dy, _, router, _ = side
        side_in = list(side)
        side_out = [
            shape_of((n_seq, n_bat), dy),
            jax.ShapeDtypeStruct((own, dim), F32),
            jax.ShapeDtypeStruct((own, dim), BF),
            jax.ShapeDtypeStruct((router.shape[0], own), F32),
            jax.ShapeDtypeStruct((router.shape[0], own), F32),
        ]
        side_scratch = [pltpu.VMEM(dy.shape, dy.dtype), pltpu.SemaphoreType.DMA]
        slots += 4 * n_seq
    head_block = jax.ShapeDtypeStruct((rows, heads, length, HEAD), BF)
    stats = jax.ShapeDtypeStruct((2 * rows * steps, STEP), F32)
    outs = [
        jax.ShapeDtypeStruct((col, dim), BF),
        jax.ShapeDtypeStruct((col, three), F32),
        head_block,
        head_block,
        head_block,
        jax.ShapeDtypeStruct((rows, length, wide), BF),
        stats,
        jax.ShapeDtypeStruct((own, dim) if side is None else (8, HEAD), BF),
    ]
    return comm_call(
        kernel,
        outs + side_out,
        [pltpu.VMEM(stats.shape, F32), pltpu.VMEM((n_seq - 1,) + stats.shape, F32)]
        + SeqScatter.scratch(rows, n_seq, block)
        + side_scratch,
        slots,
        2,
        "attend_forward",
        [vmem] * 7 + ([ANY] + [vmem] * 3 if side_in else []),
        [vmem] * 8 + ([ANY] + [vmem] * 4 if side_in else []),
    )(x_col, w_qkv, usable, w_o, gains, cos_wide, sin_wide, *side_in)


def attend_backward(
    grad_o, q, k, v, mixed, qkv, stats, hidden, usable, w_o, w_qkv, gains, cos_wide, sin_wide,
    n_seq, n_bat, side=None,
):
    rows, heads, length, _ = q.shape
    own, dim = grad_o.shape
    span = own // rows
    col, three = qkv.shape
    wide = three // 3
    steps = length // STEP
    chunk = min(256, length)
    scale = HEAD ** (-0.5)
    group = n_bat * own

    def kernel(*refs):
        (go_ref, q_ref, k_ref, v_ref, mix_ref, qkv_ref, stat_ref, hid_ref, use_ref, wo_ref,
         w_ref, gains_ref, cos_ref, sin_ref) = refs[:14]
        refs = refs[14:]
        if side:
            weighted_ref, down_ref, own_ref, res_ref, small_in = refs[:5]
            refs = refs[5:]
        gwo_ref, gw_ref, gain_ref, out_ref = refs[:4]
        refs = refs[4:]
        if side:
            mixture_ref, small_ref = refs[:2]
            mix_away, mix_twin, mix_halves, mix_full = refs[-6:-2]
            refs = refs[2:-6] + refs[-2:]
        go_all, gm, dq, dk, dv, dqkv, local, got, hid_buf, hid_sems = refs[:10]
        full, twin, line, send_sems, recv_sems = refs[10:]
        place = Place(n_seq, n_bat)
        place.greet(all_seq=True, batch=bool(side))
        wire = Wire(send_sems, recv_sems)
        gathers = [
            SeqGather(place, wire, go_ref.at[pl.ds(r * span, span)], go_all.at[r])
            for r in range(rows)
        ]
        for gather in gathers:
            gather.start()
        for r in range(rows):
            go_all[r, place.s] = go_ref[r * span : (r + 1) * span, :]
        order = list(range(1, place.half)) + [0]
        works, from_twin = {}, {}

        def mixture_of(i):
            at = pl.ds(pl.multiple_of(i * group, group), group)
            return dot(weighted_ref[at, :], down_ref[...])

        todo = [(gather, m) for gather in gathers for m in range(1, place.half)]

        def forward(count):
            for _ in range(min(count, len(todo))):
                gather, m = todo.pop(0)
                gather.step(m)

        if side:

            def send_mixture(n):
                j = order[n]
                if n >= 2:
                    wire.settle(from_twin[order[n - 2]])
                mix_away[n % 2] = (
                    mixture_of(place.twin_at(2 * j)).astype(BF).reshape(n_bat, own, dim)
                )

            def push_mixture(n):
                j = order[n]
                from_twin[j] = wire.push(mix_away.at[n % 2], mix_twin.at[j], place.twin())

            waiting = None
            send_mixture(0)
            push_mixture(0)
            for n, j in enumerate(order):
                if n + 1 < len(order):
                    send_mixture(n + 1)
                total = mixture_of(place.seq_at(2 * j))
                if n + 1 < len(order):
                    push_mixture(n + 1)
                from_twin[j].wait_recv()
                mix_twin[j] = (
                    (total + mix_twin[j].reshape(group, dim).astype(F32))
                    .astype(BF)
                    .reshape(n_bat, own, dim)
                )
                works[j] = AcrossSum(
                    place, wire, mix_twin.at[j], mix_halves.at[j], mix_full.at[j]
                )
                if waiting is not None:
                    works[waiting].start()
                waiting = j
                forward(1)
            works[waiting].start()
        forward(max(0, len(todo) - (rows - 1) * (place.half - 1)))
        columns = lax.rsqrt(stat_ref[...] / dim + EPS).T
        scatters = [
            SeqScatter(place, wire, full.at[r], twin.at[r], line.at[r]) for r in range(rows)
        ]
        gain_sums = [[jnp.zeros((1, HEAD), F32) for _ in range(heads)] for _ in range(2)]
        middles = [works[j] for j in works]

        def attend(r, c, h):
            keys = (c + 1) * chunk
            now = slice(c * chunk, keys)
            allowed = allowed_block(use_ref[r : r + 1, :keys], c * chunk, chunk, keys)
            lanes = slice(h * HEAD, (h + 1) * HEAD)
            query = q_ref[r, h, now, :]
            key = k_ref[r, h, :keys, :]
            scores = jnp.where(allowed, dot_t(query, key) * scale, NEGATIVE)
            raised = jnp.exp(scores - jnp.max(scores, axis=-1, keepdims=True))
            probs = raised / jnp.sum(raised, axis=-1, keepdims=True)
            low = probs.astype(BF)
            grad_mix = gm[r, now, lanes]
            grad_probs = dot_t(grad_mix, v_ref[r, h, :keys, :])
            row_dot = jnp.sum(low.astype(F32) * grad_probs, axis=-1, keepdims=True)
            grad_scores = (probs * (grad_probs - row_dot)).astype(BF)
            dq[now, lanes] = scale * dot(grad_scores, key)
            dk[:keys, lanes] += scale * t_dot(grad_scores, query)
            dv[:keys, lanes] += t_dot(low, grad_mix)

        def take(r):
            gathers[r].finish()
            gm[r] = dot_t(go_all[r].reshape(length, dim), wo_ref[...]).astype(BF)

        take(0)
        for r in range(rows):
            if r:
                scatters[r - 1].pass_on(0, 1)
            dk[...] = jnp.zeros_like(dk)
            dv[...] = jnp.zeros_like(dv)
            for h in range(heads):
                for c in range(length // chunk):
                    attend(r, c, h)
                    forward(1)
                    if middles:
                        middles.pop(0).middle()
            if r == 0:
                forward(len(todo))
                while middles:
                    middles.pop(0).middle()
            for which, grads in ((0, dq), (1, dk)):
                for c in range(steps):
                    inside = slice(c * STEP, (c + 1) * STEP)
                    at = slice(r * length + c * STEP, r * length + (c + 1) * STEP)
                    row = (r * 2 + which) * steps + c
                    factor = columns[:, row : row + 1]
                    products = None
                    for h in range(heads):
                        lanes = slice(h * HEAD, (h + 1) * HEAD)
                        flat = qkv_ref[at, which * wide + h * HEAD : which * wide + (h + 1) * HEAD]
                        flat = flat * factor
                        back = turn(grads[inside, lanes], cos_ref[inside, :], -sin_ref[inside, :])
                        gain_sums[which][h] = gain_sums[which][h] + jnp.sum(
                            back * flat, axis=0, keepdims=True
                        )
                        weighted = back * head_gain(place, gains_ref, which, wide, h)
                        grads[inside, lanes] = weighted
                        product = weighted * flat
                        products = product if products is None else products + product
                    row = which * steps + c
                    local[r, row : row + 1, :] = lane_sums(products)
            exchange = Exchange(place, wire, local.at[r], got.at[r])
            if r:
                scatters[r - 1].pass_on(1)
            dqkv[r, :, 2 * wide :] = dv[...].astype(BF)
            if r + 1 < rows:
                take(r + 1)
            means = (exchange.total() / dim).T
            for which, grads in ((0, dq), (1, dk)):
                lanes = slice(which * wide, (which + 1) * wide)
                for c in range(steps):
                    inside = slice(c * STEP, (c + 1) * STEP)
                    at = slice(r * length + c * STEP, r * length + (c + 1) * STEP)
                    row = (r * 2 + which) * steps + c
                    factor = columns[:, row : row + 1]
                    mean = means[:, which * steps + c : which * steps + c + 1]
                    flat = qkv_ref[at, lanes] * factor
                    dqkv[r, inside, lanes] = (factor * (grads[inside, :] - flat * mean)).astype(BF)
            full[r] = dot_t(dqkv[r], w_ref[...]).astype(BF).reshape(n_seq, span, dim)
            scatters[r].start()
        for which in range(2):
            for h in range(heads):
                gain_ref[which : which + 1, h * HEAD : (h + 1) * HEAD] = gain_sums[which][h]

        def hidden_load(part):
            slot = lax.rem(part, 2)
            at = pl.ds(pl.multiple_of(part * 256, 256), 256)
            return pltpu.make_async_copy(
                hid_ref.at[:, at], hid_buf.at[slot], hid_sems.at[slot]
            )

        hidden_load(0).start()
        scatters[-1].pass_on()

        def weight_part(part, carry):
            at = pl.ds(pl.multiple_of(part * 256, 256), 256)

            @pl.when(part + 1 < dim // 256)
            def _():
                hidden_load(part + 1).start()

            hidden_load(part).wait()
            held = hid_buf[lax.rem(part, 2)]
            gw_ref[at, :] = t_dot(held, dqkv[...].reshape(col, three)).astype(BF)
            total = t_dot(mix_ref[0], go_all[0, :, :, at].reshape(length, 256))
            for r in range(1, rows):
                total = total + t_dot(mix_ref[r], go_all[r, :, :, at].reshape(length, 256))
            gwo_ref[:, at] = total.astype(BF)
            return carry

        lax.fori_loop(0, dim // 256, weight_part, 0)
        for j in works:
            works[j].finish()
            mixture_ref[j] = mix_twin[j, place.b]
        sums = jnp.zeros((1, dim), F32)
        for r in range(rows):
            at = slice(r * span, (r + 1) * span)
            if not side:
                scatters[r].finish(out_ref, at)
                continue
            x = own_ref[at, :].astype(F32)
            grad, terms = rms_back(x, rms_scale(x), gains_ref[0:1, :], scatters[r].total())
            sums = sums + jnp.sum(terms, axis=0, keepdims=True)
            out_ref[at, :] = (res_ref[at, :] + grad).astype(BF)
        if side:
            small_ref[...] = small_in[...]
            small_ref[8:9, :] = sums
            lanes = pl.ds(pl.multiple_of(place.s * wide, wide), wide)
            for which in range(2):
                small_ref[9 + which : 10 + which, lanes] = gain_ref[which : which + 1, :]
        wire.drain()

    vmem = pl.BlockSpec(memory_space=pltpu.VMEM)
    block = jax.ShapeDtypeStruct((span, dim), BF)
    stat_shape = (2 * steps, STEP)
    side_out, side_scratch = [], []
    if side:
        half = n_seq // 2
        side_out = [
            jax.ShapeDtypeStruct((half, own, dim), BF),
            jax.ShapeDtypeStruct((16, dim), F32),
        ]
        side_scratch = [
            pltpu.VMEM((2, n_bat, own, dim), BF),
            pltpu.VMEM((half, n_bat, own, dim), BF),
            pltpu.VMEM((half, 2, own // 2, dim), BF),
            pltpu.VMEM((half, 2, own, dim), BF),
        ]
    return comm_call(
        kernel,
        [
            jax.ShapeDtypeStruct((wide, dim), BF),
            jax.ShapeDtypeStruct((dim, three), BF),
            jax.ShapeDtypeStruct((2, wide), F32),
            jax.ShapeDtypeStruct((own, dim), BF),
        ]
        + side_out,
        [
            pltpu.VMEM((rows, n_seq, span, dim), BF),
            pltpu.VMEM((rows, length, wide), BF),
            pltpu.VMEM((length, wide), F32),
            pltpu.VMEM((length, wide), F32),
            pltpu.VMEM((length, wide), F32),
            pltpu.VMEM((rows, length, three), BF),
            pltpu.VMEM((rows,) + stat_shape, F32),
            pltpu.VMEM((rows, n_seq - 1) + stat_shape, F32),
            pltpu.VMEM((2, col, 256), BF),
            pltpu.SemaphoreType.DMA((2,)),
        ]
        + SeqScatter.scratch(rows, n_seq, block)
        + side_scratch,
        5 * rows * n_seq + (3 * n_seq if side else 0),
        6,
        "attend_backward",
        [vmem] * 7 + [ANY] + [vmem] * (6 + len(side or ())),
        [vmem] * (4 + len(side_out)),
    )(grad_o, q, k, v, mixed, qkv, stats, hidden, usable, w_o, w_qkv, gains, cos_wide, sin_wide,
      *(side or ()))


class Across:
    def __init__(self, place, wire, src, at):
        self.place, self.wire, self.src, self.at = place, wire, src, at
        self.half = src.shape[0] // 2

    def start(self):
        place, own = self.place, self.at(self.place.b)
        self.to_x = self.wire.push(self.src, own, place.x_peer())
        self.to_y = self.wire.push(self.src, own, place.y_peer())

    def relay(self):
        place, half = self.place, self.half
        self.to_x.wait_recv()
        top = self.at(place.bat_x).at[pl.ds(0, half)]
        self.top = self.wire.push(top, top, place.y_peer())
        self.to_y.wait_recv()
        low = self.at(place.bat_y).at[pl.ds(half, half)]
        self.low = self.wire.push(low, low, place.x_peer())

    def finish(self):
        self.top.wait_recv()
        self.low.wait_recv()


class AcrossSum:
    def __init__(self, place, wire, group, halves, full):
        self.place, self.wire = place, wire
        self.group, self.halves, self.full = group, halves, full
        self.half = halves.shape[1]

    def start(self):
        place, half = self.place, self.half
        far = self.group.at[place.bat_d]
        self.top = self.wire.push(far.at[pl.ds(0, half)], self.halves.at[0], place.x_peer())
        self.low = self.wire.push(far.at[pl.ds(half, half)], self.halves.at[1], place.y_peer())

    def middle(self):
        place, half = self.place, self.half
        self.top.wait_recv()
        add_into(self.group.at[place.bat_y].at[pl.ds(0, half)], self.halves.at[0])
        self.low.wait_recv()
        add_into(self.group.at[place.bat_x].at[pl.ds(half, half)], self.halves.at[1])
        self.y = self.wire.push(self.group.at[place.bat_y], self.full.at[0], place.y_peer())
        self.x = self.wire.push(self.group.at[place.bat_x], self.full.at[1], place.x_peer())

    def finish(self):
        self.y.wait_recv()
        self.x.wait_recv()
        add_into(self.group.at[self.place.b], self.full.at[0], self.full.at[1])


def load_first(weights, w_out, mine, flags, small, rows, n_seq, n_bat):
    shard, dim = weights[0].shape
    wide = dim // n_seq
    own = mine.shape[0]
    span = own // rows
    slots = 15 * n_seq + n_seq * n_bat

    def kernel(*refs):
        parts = refs[:3]
        wo_ref, x_ref, flag_ref, small_ref = refs[3:7]
        w_ref, wo_all, x_col, router_ref, gains_ref, use_ref = refs[7:13]
        buffers = refs[13:16]
        own_sems, cut_sems, x_sems, small_all, flag_col, send_sems, recv_sems = refs[16:]
        place = Place(n_seq, n_bat)
        place.greet(all_seq=True)
        wire = Wire(send_sems, recv_sems)
        small_work = FullGather(place, wire, small_ref, small_all)
        flag_work = SeqGather(place, wire, flag_ref, flag_col)
        x_works = [
            SeqGather(place, wire, x_ref.at[pl.ds(r * span, span)], x_col.at[r])
            for r in range(rows)
        ]
        small_work.start()
        flag_work.start()

        def cut(k):
            return pl.ds(pl.multiple_of(place.seq_at(k) * wide, wide), wide)

        def columns(m):
            return pl.ds(m * wide, wide)

        own_cuts = []
        for m in range(3):
            copy = pltpu.make_async_copy(
                parts[m].at[:, cut(0)], buffers[0].at[:, columns(m)], cut_sems.at[m]
            )
            copy.start()
            own_cuts.append(copy)
        cuts = {}
        for k in range(1, n_seq):
            for m in range(3):
                cuts[k, m] = wire.push(
                    parts[m].at[:, cut(k)],
                    w_ref.at[place.s, place.b, :, columns(m)],
                    place.seq_peer(k),
                )
        wo_work = Across(place, wire, wo_ref, lambda i: wo_all.at[i])
        wo_work.start()
        for work in x_works:
            work.start()
        for copy in own_cuts:
            copy.wait()
        spreads = []

        def spread(src, from_seq):
            work = Across(place, wire, src, lambda i: w_ref.at[from_seq, i])
            work.start()
            spreads.append(work)

        spread(buffers[0], place.s)
        own_w = pltpu.make_async_copy(buffers[0], w_ref.at[place.s, place.b], own_sems.at[0])
        own_w.start()
        copies = [own_w]
        fetched = pltpu.make_async_copy(x_ref, buffers[2], own_sems.at[2])
        fetched.start()
        fetched.wait()
        for r in range(rows):
            copy = pltpu.make_async_copy(
                buffers[2].at[pl.ds(r * span, span)], x_col.at[r, place.s], x_sems.at[r]
            )
            copy.start()
            copies.append(copy)
        copies.append(keep_own(wo_ref, wo_all.at[place.b], buffers[1], own_sems.at[1]))
        flag_col[place.s] = flag_ref[...]
        small_all[place.s, place.b] = small_ref[...]
        for j in range(1, place.half):
            small_work.step(j)
            flag_work.step(j)
        for k in range(1, n_seq):
            for m in range(3):
                cuts[k, m].wait_recv()
            spread(w_ref.at[place.seq_at(-k), place.b], place.seq_at(-k))
        for j in range(place.half):
            small_work.collect(j)
        todo = [(work, m) for work in x_works for m in range(1, place.half)]

        def forward(count):
            for _ in range(min(count, len(todo))):
                work, m = todo.pop(0)
                work.step(m)

        forward(1)
        wo_work.relay()
        for work in spreads:
            work.relay()
            forward(1)
        forward(len(todo))
        wo_work.finish()
        for work in spreads:
            work.finish()
        for work in [small_work, flag_work] + x_works:
            work.finish()
        left = lax.broadcasted_iota(jnp.int32, (8, 128), 1) < 64
        for i in range(n_seq):
            for k in range(0, n_bat, 2):
                one, two = small_all[i, k], small_all[i, k + 1]
                at = slice((i * n_bat + k) * 64, (i * n_bat + k + 2) * 64)
                router_ref[:, at] = jnp.where(left, one, pltpu.roll(two, 64, axis=1))
                gains_ref[:, at] = jnp.where(left, pltpu.roll(one, 64, axis=1), two)
        for i in range(0, n_seq, 2):
            one, two = flag_col[i], flag_col[i + 1]
            use_ref[:, i * 64 : (i + 2) * 64] = jnp.where(left, one, pltpu.roll(two, 64, axis=1))
        for copy in copies:
            copy.wait()
        wire.drain()

    one = jax.ShapeDtypeStruct((shard, 3 * wide), BF)
    x_one = jax.ShapeDtypeStruct((span, dim), BF)
    held = (one, w_out, mine)
    vmem = pl.BlockSpec(memory_space=pltpu.VMEM)
    return comm_call(
        kernel,
        [
            shape_of((n_seq, n_bat), one),
            shape_of((n_bat,), w_out),
            shape_of((rows, n_seq), x_one),
            jax.ShapeDtypeStruct((8, dim), F32),
            jax.ShapeDtypeStruct((8, dim), F32),
            jax.ShapeDtypeStruct((8, n_seq * span), F32),
        ],
        [pltpu.VMEM(block.shape, block.dtype) for block in held]
        + [pltpu.SemaphoreType.DMA((n,)) for n in (3, 3, rows)]
        + [pltpu.VMEM((n_seq, n_bat, 8, 128), F32), pltpu.VMEM((n_seq, 8, 128), F32)],
        slots,
        1,
        "load_first",
        [ANY] * 5 + [vmem] * 2,
        [ANY] * 3 + [vmem] * 3,
    )(*weights, w_out, mine, flags, small)


def pick_units(first, experts, units, part):
    at_expert = lax.broadcasted_iota(jnp.int32, (experts, units), 0)
    at_unit = lax.broadcasted_iota(jnp.int32, (experts, units), 1)
    low = (at_expert - first) * part
    return jnp.where((at_unit >= low) & (at_unit < low + part), 1.0, 0.0).astype(BF)


def experts_forward(normed, gates, dy_all, gate, up, w_down, n_seq, n_bat):
    own, dim = normed.shape
    local_experts, depth, hidden = gate.shape
    units = w_down.shape[0]
    part = hidden // n_seq
    group = n_bat * own
    tokens = n_seq * group
    experts = gates.shape[0]
    slots = 64 + 2 * n_seq * n_bat + 2 * local_experts * n_seq

    def kernel(*refs):
        x_ref, gate_ref, dy_ref, wg_ref, wu_ref, down_ref = refs[:6]
        x_all, weighted_ref, grad_ref, term_ref, gu_ref = refs[6:11]
        gates_all, back, gate_buf, x_buf, dy_buf, keep = refs[11:17]
        own_sems, x_sems, dy_sems, gu_sems, send_sems, recv_sems = refs[17:]
        place = Place(n_seq, n_bat)
        place.greet(all_seq=True)
        wire = Wire(send_sems, recv_sems)
        gate_work = FullGather(place, wire, gate_ref, gates_all)
        gate_work.start()
        gates_all[place.s, place.b] = gate_ref[...]
        line = Line(place, wire, x_ref, lambda i: x_all.at[place.chip(i), place.b])
        line.start()
        works = []
        here = [place.chip(place.origin(m)) for m in range(place.half)]
        there = [place.chip_twin(place.origin(m)) for m in range(place.half)]
        for j in range(place.half):
            at_seq = here[j]
            src = x_ref if j == 0 else x_all.at[at_seq, place.b]
            works.append(
                Across(place, wire, src, lambda i, at_seq=at_seq: x_all.at[at_seq, i])
            )
        works[0].start()
        own = keep_own(x_ref, x_all.at[place.s, place.b], keep, own_sems.at[0])
        selected = pick_units(place.b * local_experts, experts, units, part)
        selected_twice = jnp.concatenate([selected, selected], axis=0)

        def dy_load(g, slot):
            return pltpu.make_async_copy(dy_ref.at[g], dy_buf.at[slot], dy_sems.at[slot])

        def rows_of(g):
            return pl.ds(pl.multiple_of(g * group, group), group)

        def backs(first, count):
            dy_load(first, first % 2).start()
            for g in range(first, first + count):
                if g + 1 < first + count:
                    dy_load(g + 1, (g + 1) % 2).start()
                dy_load(g, g % 2).wait()
                block = dy_buf[g % 2].reshape(group, dim)
                back[g * group : (g + 1) * group, :] = dot_t(block, down_ref[...])

        gu_copies = ([], [])

        def send_units(m, ref, offsets):
            for k in offsets:
                lanes = pl.ds(pl.multiple_of(place.seq_at(k) * part, part), part)
                for e in range(local_experts):
                    src = ref.at[e, :, lanes]
                    dst = gu_ref.at[place.s, :, pl.ds(m * units + e * part, part)]
                    if k:
                        gu_copies[m].append(wire.push(src, dst, place.seq_peer(k)).wait_recv)
                    else:
                        copy = pltpu.make_async_copy(src, dst, gu_sems.at[m, e])
                        copy.start()
                        gu_copies[m].append(copy.wait)

        passed = []

        def hand_over(j):
            at_seq = here[j]
            works[j].finish()
            if j == 0:
                own.wait()
            passed.append(wire.push(x_all.at[at_seq], x_all.at[at_seq], place.twin()))

        loads = {}

        def fetch(g, slot):
            loads[slot] = pltpu.make_async_copy(x_all.at[g], x_buf.at[slot], x_sems.at[slot])
            loads[slot].start()

        def weight(m):
            return gu_ref[:, :, m * units : (m + 1) * units].reshape(dim, units)

        def gate_on(g, slot):
            loads[slot].wait()
            gate_buf[rows_of(g), :] = dot(x_buf[slot].reshape(group, dim), weight(0))

        def units_on(g, slot, gated=False):
            if not gated:
                loads[slot].wait()
            at = rows_of(g)
            block = x_buf[slot].reshape(group, dim)
            gate_pre = gate_buf[at, :] if gated else dot(block, weight(0))
            up_pre = dot(block, weight(1))
            sig = jax.nn.sigmoid(gate_pre)
            silu = gate_pre * sig
            active = (silu * up_pre).astype(BF).astype(F32)
            grad_back = back[at, :]
            product = active * grad_back
            wide_gates = []
            for i in range(n_bat):
                inside = slice(i * x_ref.shape[0], (i + 1) * x_ref.shape[0])
                gates_two = jnp.concatenate(in_two(gates_all[g, i]), axis=0)
                wide_gates.append(t_dot(gates_two, selected_twice))
                high, low = in_two(product[inside, :])
                term_ref[g, i] = dot_t(selected, high) + dot_t(selected, low)
            wide_gate = jnp.concatenate(wide_gates, axis=0)
            weighted_ref[at, :] = (active * wide_gate).astype(BF)
            grad_active = grad_back * wide_gate
            grad_ref[at, :units] = (
                grad_active * up_pre * sig * (1.0 + gate_pre * (1.0 - sig))
            ).astype(BF)
            grad_ref[at, units:] = (grad_active * silu).astype(BF)

        half = place.half
        per = n_seq // half
        offsets = list(range(1, n_seq)) + [0]
        for j in range(1, half):
            backs((j - 1) * per, per)
            gate_work.step(j)
            gate_work.collect(j - 1)
            line.step(j)
            works[j].start()
            works[j - 1].relay()
            if j < half - 1:
                send_units(0, wg_ref, offsets[2 * j - 2 : 2 * j])
            else:
                send_units(0, wg_ref, offsets[2 * j - 2 :])
                send_units(1, wu_ref, offsets)
        backs((half - 1) * per, per)
        gate_work.collect(half - 1)
        gate_work.finish()
        hand_over(0)
        fetch(here[0], 0)
        for wait in gu_copies[0]:
            wait()
        gate_on(here[0], 0)
        passed[0].wait_recv()
        fetch(there[0], 1)
        hand_over(1)
        fetch(here[1], 2)
        gate_on(there[0], 1)
        gate_on(here[1], 2)
        works[half - 1].relay()
        passed[1].wait_recv()
        fetch(there[1], 3)
        gate_on(there[1], 3)
        for wait in gu_copies[1]:
            wait()
        for j in range(half):
            units_on(here[j], (2 * j) % 4, j < 2)
            if j + 2 < half:
                hand_over(j + 2)
                fetch(here[j + 2], (2 * j) % 4)
            units_on(there[j], (2 * j + 1) % 4, j < 2)
            if j + 2 < half:
                passed[j + 2].wait_recv()
                fetch(there[j + 2], (2 * j + 1) % 4)
        wire.drain()

    vmem = pl.BlockSpec(memory_space=pltpu.VMEM)
    return comm_call(
        kernel,
        [
            shape_of((n_seq, n_bat), normed),
            jax.ShapeDtypeStruct((tokens, units), BF),
            jax.ShapeDtypeStruct((tokens, 2 * units), BF),
            shape_of((n_seq, n_bat), gates),
            jax.ShapeDtypeStruct((n_seq, depth, 2 * units), BF),
        ],
        [
            pltpu.VMEM((n_seq, n_bat) + gates.shape, F32),
            pltpu.VMEM((tokens, units), F32),
            pltpu.VMEM((tokens, units), F32),
            pltpu.VMEM((4, n_bat, own, dim), BF),
            pltpu.VMEM((2, n_bat, own, dim), BF),
            pltpu.VMEM((own, dim), BF),
            pltpu.SemaphoreType.DMA((1,)),
            pltpu.SemaphoreType.DMA((4,)),
            pltpu.SemaphoreType.DMA((2,)),
            pltpu.SemaphoreType.DMA((2, local_experts)),
        ],
        slots,
        4,
        "experts_forward",
        [ANY, vmem, ANY, ANY, ANY, vmem],
        [ANY, vmem, vmem, vmem, vmem],
    )(normed, gates, dy_all, gate, up, w_down)


def experts_backward(
    grad_pre, weighted, w_gu, terms, x_all, dy_all, residual, dy_own, gains, router, probs, chosen,
    local_experts, n_seq, n_bat,
):
    own = residual.shape[0]
    tokens, dim = x_all.shape
    units = weighted.shape[1]
    part = units // local_experts
    group = n_bat * own
    depth = dim // n_seq
    hidden = n_seq * part
    half = n_seq // 2
    slots = 128 + 2 * n_seq * n_bat
    block = jax.ShapeDtypeStruct((own, dim), BF)
    term = jax.ShapeDtypeStruct(terms.shape[2:], F32)

    def kernel(*refs):
        grad_ref, weighted_ref, gu_ref, term_in, x_ref, dy_ref = refs[:6]
        res_ref, own_dy_ref, gains_ref, router_ref, probs_ref, chosen_ref = refs[6:12]
        out_ref, low_ref, small_ref, gate_out, up_out, down_out = refs[12:18]
        refs = refs[18:]
        away, twin, halves, full, line = refs[:5]
        columns, sent, got, column_sems, term_out = refs[5:10]
        term_scratch = refs[10:15]
        send_sems, recv_sems = refs[15:]
        place = Place(n_seq, n_bat)
        place.greet(all_seq=True)
        wire = Wire(send_sems, recv_sems)
        term_work = FullScatter(place, wire, term_in, term_out, *term_scratch)
        term_work.start()

        def product(i):
            at = pl.ds(pl.multiple_of(i * group, group), group)
            return dot_t(grad_ref[at, :], gu_ref[...])

        order = list(range(1, half)) + [0]
        from_twin, from_seq, works = {}, {}, {}

        def send(j):
            from_twin[j] = wire.push(away.at[j], twin.at[j], place.twin())

        chunks = list(range(1, n_seq)) + [0]

        def chunk_load(n):
            at = pl.ds(pl.multiple_of(place.seq_at(chunks[n]) * depth, depth), depth)
            return pltpu.make_async_copy(x_ref.at[:, at], columns.at[n % 2], column_sems.at[n % 2])

        def down_load(k):
            slot = lax.rem(k, 2)
            at = pl.ds(pl.multiple_of(k * 256, 256), 256)
            return pltpu.make_async_copy(dy_ref.at[:, at], columns.at[slot], column_sems.at[slot])

        def down_part(first, last):
            down_load(first).start()

            def one(k, carry):
                @pl.when(k + 1 < last)
                def _():
                    down_load(k + 1).start()

                down_load(k).wait()
                at = pl.ds(pl.multiple_of(k * 256, 256), 256)
                down_out[:, at] = t_dot(weighted_ref[...], columns[lax.rem(k, 2)])
                return carry

            lax.fori_loop(first, last, one, 0)

        chunk_load(0).start()

        def pair(j):
            part_sum = product(place.seq_at(2 * j))
            from_twin[j].wait_recv()
            twin[j] = (
                (part_sum + twin[j].reshape(group, dim).astype(F32))
                .astype(BF)
                .reshape(n_bat, own, dim)
            )
            works[j] = AcrossSum(place, wire, twin.at[j], halves.at[j], full.at[j])

        arrivals = []
        done = [0]

        def work_chunks(count):
            for n in range(done[0], min(done[0] + count, len(chunks))):
                done[0] = n + 1
                k = chunks[n]
                if n + 1 < len(chunks):
                    chunk_load(n + 1).start()
                chunk_load(n).wait()
                if n:
                    last = chunks[n - 1]
                    arrivals.append(
                        wire.push(sent.at[last], got.at[place.s], place.seq_peer(last))
                    )
                value = t_dot(columns[n % 2], grad_ref[...]).astype(BF)
                if k == 0:
                    got[place.s] = value
                else:
                    sent[k] = value

        def pass_on(j):
            works[j].finish()
            if j:
                from_seq[j] = wire.push(twin.at[j, place.b], line.at[j], place.seq_peer(2 * j))

        work_chunks(1)
        waiting = None
        for j in order:
            away[j] = product(place.twin_at(2 * j)).astype(BF).reshape(n_bat, own, dim)
            if waiting is not None:
                send(waiting)
            waiting = j
            work_chunks(1)
        first, rest = order[:2], order[2:]
        pair(order[0])
        send(waiting)
        for j in first[1:]:
            pair(j)
            works[first[0]].start()
        works[first[-1]].start()
        for j in rest:
            pair(j)
        term_order = term_work.order()
        for j in term_order:
            term_work.pair(j)
        works[first[0]].middle()
        work_chunks(1)
        for j in first[1:]:
            works[j].middle()
        for j in rest:
            works[j].start()
        for j in first:
            work_chunks(3)
            pass_on(j)
        work_chunks(len(chunks))
        for j in term_order:
            term_work.merge(j)
        for j in rest:
            works[j].middle()
        cut = dim // 512
        down_part(0, cut)
        pass_on(rest[0])
        down_part(cut, 2 * cut)
        for j in rest[1:]:
            pass_on(j)
        for copy in arrivals:
            copy.wait_recv()
        for i in range(n_seq):
            lanes = slice(i * part, (i + 1) * part)
            for e in range(local_experts):
                gate_out[e, :, lanes] = got[i, :, e * part : (e + 1) * part].astype(F32)
                up_out[e, :, lanes] = got[i, :, units + e * part : units + (e + 1) * part].astype(
                    F32
                )
        term_work.finish()
        for j in range(1, half):
            from_seq[j].wait_recv()
        total = twin[0, place.b].astype(F32)
        for j in range(1, half):
            total = total + line[j].astype(F32)
        grad_chosen = term_out[...] * chosen_ref[...]
        probs = probs_ref[...]
        grad_logits = probs * (
            grad_chosen - jnp.sum(probs * grad_chosen, axis=0, keepdims=True)
        )
        small_ref[...] = jnp.zeros_like(small_ref)
        residual = res_ref[...]
        scale = rms_scale(residual)
        normal = residual * scale
        normed = (normal * gains_ref[3:4, :]).astype(BF)
        experts = probs.shape[0]
        logits_two = jnp.concatenate(in_two(grad_logits), axis=0)
        products = dot(logits_two, normed)
        small_ref[0:experts, :] = products[:experts] + products[experts:]
        router = router_ref[...].astype(BF)
        total = total + t_dot(logits_two, jnp.concatenate([router, router], axis=0))
        grad, terms_of = rms_back(residual, scale, gains_ref[3:4, :], total)
        small_ref[experts + 3 : experts + 4, :] = jnp.sum(terms_of, axis=0, keepdims=True)
        grad = own_dy_ref[...].astype(F32) + grad
        out_ref[...] = grad
        low_ref[...] = grad.astype(BF)
        wire.drain()

    vmem = pl.BlockSpec(memory_space=pltpu.VMEM)
    expert = jax.ShapeDtypeStruct((local_experts, depth, hidden), F32)
    return comm_call(
        kernel,
        [
            jax.ShapeDtypeStruct((own, dim), F32),
            jax.ShapeDtypeStruct((own, dim), BF),
            jax.ShapeDtypeStruct((16, dim), F32),
            expert,
            expert,
            jax.ShapeDtypeStruct((units, dim), F32),
        ],
        [
            pltpu.VMEM((half, n_bat, own, dim), BF),
            pltpu.VMEM((half, n_bat, own, dim), BF),
            pltpu.VMEM((half, 2, own // 2, dim), BF),
            pltpu.VMEM((half, 2, own, dim), BF),
            pltpu.VMEM((half, own, dim), BF),
            pltpu.VMEM((2, tokens, 256), BF),
            pltpu.VMEM((n_seq, depth, 2 * units), BF),
            pltpu.VMEM((n_seq, depth, 2 * units), BF),
            pltpu.SemaphoreType.DMA((2,)),
            pltpu.VMEM(term.shape, F32),
        ]
        + FullScatter.scratch(n_seq, n_bat, term),
        slots,
        5,
        "experts_backward",
        [vmem] * 3 + [ANY] * 3 + [vmem] * 6,
        [vmem] * 6,
    )(grad_pre, weighted, w_gu, terms, x_all, dy_all, residual, dy_own, gains, router, probs, chosen)


def store_last(grad_w, grad_wo, small, mixture, n_seq, n_bat):
    one = jax.ShapeDtypeStruct(grad_w.shape[2:], grad_w.dtype)
    shard, three = one.shape
    wide = three // 3
    wo_one = jax.ShapeDtypeStruct(grad_wo.shape[1:], grad_wo.dtype)
    small_one = jax.ShapeDtypeStruct((16, 2 * shard), small.dtype)
    half = n_seq // 2
    dim = wo_one.shape[1]
    slots = 64 + n_seq * n_bat + 5 * n_seq

    def kernel(*refs):
        w_ref, wo_ref, small_ref, mix_ref = refs[:4]
        q_out, k_out, v_out, wo_out, small_out, mix_out = refs[4:10]
        w_sum, w_halves, w_full, w_got, wo_sum, wo_halves, wo_full, line = refs[10:18]
        small_scratch = refs[18:23]
        w_sems, wo_sem, send_sems, recv_sems = refs[23:]
        place = Place(n_seq, n_bat)
        place.greet(all_seq=True)
        wire = Wire(send_sems, recv_sems)

        def pick(i, m):
            tile = i * (n_bat // 2) + lax.div(m, 2)
            return small_ref.at[:, pl.ds(pl.multiple_of(tile * 2 * shard, 128), 2 * shard)]

        small_work = FullScatter(place, wire, small_ref, small_out, *small_scratch, pick)
        small_work.start()
        order = list(range(1, n_seq)) + [0]
        loads = {}
        for k in order:
            loads[k] = pltpu.make_async_copy(
                w_ref.at[place.seq_at(k)], w_sum.at[k], w_sems.at[k]
            )
            loads[k].start()
        wo_load = pltpu.make_async_copy(wo_ref, wo_sum, wo_sem.at[0])
        wo_load.start()
        works = {}
        for k in order:
            loads[k].wait()
            works[k] = AcrossSum(place, wire, w_sum.at[k], w_halves.at[k], w_full.at[k])
            works[k].start()
        wo_load.wait()
        wo_work = AcrossSum(place, wire, wo_sum, wo_halves, wo_full)
        wo_work.start()
        term_order = small_work.order()
        for j in term_order:
            small_work.pair(j)
        mix_line = {
            j: wire.push(mix_ref.at[j], line.at[j], place.seq_peer(2 * j)) for j in range(1, half)
        }
        arrivals = []
        ready = None

        def ship(k):
            if k:
                arrivals.append(
                    wire.push(w_sum.at[k, place.b], w_got.at[place.s], place.seq_peer(k))
                )

        for k in order:
            works[k].middle()
        wo_work.middle()
        for j in term_order:
            small_work.merge(j)
        for k in order:
            works[k].finish()
            if ready is not None:
                ship(ready)
            ready = k
        w_got[place.s] = w_sum[0, place.b]
        wo_work.finish()
        wo_out[...] = wo_sum[place.b].astype(F32)
        small_work.finish()
        for copy in arrivals:
            copy.wait_recv()
        for i in range(n_seq):
            at = slice(i * wide, (i + 1) * wide)
            for m, out in enumerate((q_out, k_out, v_out)):
                out[:, at] = w_got[i, :, m * wide : (m + 1) * wide].astype(F32)
        for copy in mix_line.values():
            copy.wait_recv()
        total = mix_ref[0].astype(F32)
        for j in range(1, half):
            total = total + line[j].astype(F32)
        mix_out[...] = total
        wire.drain()

    vmem = pl.BlockSpec(memory_space=pltpu.VMEM)
    matrix = jax.ShapeDtypeStruct((shard, dim), F32)
    return comm_call(
        kernel,
        [matrix] * 4 + [small_one, jax.ShapeDtypeStruct(mixture.shape[1:], F32)],
        [
            pltpu.VMEM((n_seq, n_bat, shard, three), BF),
            pltpu.VMEM((n_seq, 2, shard // 2, three), BF),
            pltpu.VMEM((n_seq, 2, shard, three), BF),
            pltpu.VMEM((n_seq, shard, three), BF),
            pltpu.VMEM((n_bat, shard, dim), BF),
            pltpu.VMEM((2, shard // 2, dim), BF),
            pltpu.VMEM((2, shard, dim), BF),
            pltpu.VMEM(mixture.shape, BF),
        ]
        + FullScatter.scratch(n_seq, n_bat, small_one)
        + [pltpu.SemaphoreType.DMA((n_seq,)), pltpu.SemaphoreType.DMA((1,))],
        slots,
        8,
        "store_last",
        [ANY] * 3 + [vmem],
        [vmem] * 6,
    )(grad_w, grad_wo, small, mixture)


def finish(residual, mixture, grads):
    count = len(grads)
    pieces = []
    for i in sorted(range(count), key=lambda i: -grads[i].size):
        large = grads[i].size >= 1 << 18 and grads[i].ndim == 3
        pieces += [(i, k) for k in range(grads[i].shape[0])] if large else [(i, None)]

    def kernel(*refs):
        res_ref, mix_ref = refs[:2]
        ins, out_ref, outs = refs[2 : 2 + count], refs[2 + count], refs[3 + count : 3 + 2 * count]
        refs = refs[3 + 2 * count :]
        buffers, res_buf, mix_buf, out_buf, sems, own_sems = refs[:count], *refs[count:]

        def piece(group, n):
            i, k = pieces[n]
            return group[i] if k is None else group[i].at[k]

        loads = []
        for n in range(len(pieces)):
            copy = pltpu.make_async_copy(piece(ins, n), piece(buffers, n), sems.at[0, n])
            copy.start()
            loads.append(copy)
            if n == 0:
                first = pltpu.make_async_copy(res_ref, res_buf, own_sems.at[0])
                second = pltpu.make_async_copy(mix_ref, mix_buf, own_sems.at[1])
                first.start()
                second.start()
        stores = []
        for n, load in enumerate(loads):
            load.wait()
            copy = pltpu.make_async_copy(piece(buffers, n), piece(outs, n), sems.at[1, n])
            copy.start()
            stores.append(copy)
            if n == 0:
                first.wait()
                second.wait()
                out_buf[...] = (res_buf[...] + mix_buf[...]).astype(BF)
            if n == 1:
                copy = pltpu.make_async_copy(out_buf, out_ref, own_sems.at[2])
                copy.start()
                stores.append(copy)
        for copy in stores:
            copy.wait()

    return pl.pallas_call(
        kernel,
        out_shape=[jax.ShapeDtypeStruct(residual.shape, BF)]
        + [jax.ShapeDtypeStruct(grad.shape, grad.dtype) for grad in grads],
        in_specs=[ANY] * (2 + count),
        out_specs=[ANY] * (1 + count),
        scratch_shapes=[pltpu.VMEM(grad.shape, grad.dtype) for grad in grads]
        + [
            pltpu.VMEM(residual.shape, F32),
            pltpu.VMEM(residual.shape, F32),
            pltpu.VMEM(residual.shape, BF),
            pltpu.SemaphoreType.DMA((2, len(pieces))),
            pltpu.SemaphoreType.DMA((3,)),
        ],
        compiler_params=pltpu.CompilerParams(vmem_limit_bytes=VMEM_LIMIT),
        name="finish",
    )(residual, mixture, *grads)


def load_inputs(qkv_cut, w_out, mine, flags, small, gu_cut, dy_own, n_seq, n_bat):
    n_in = 7
    slots = 4 * n_seq * n_bat + 5 * n_seq + 2 * n_bat

    def kernel(*refs):
        cut_ref, wo_ref, x_ref, flag_ref, small_ref, gu_ref, dy_ref = refs[:n_in]
        w_ref, wo_all, x_col, flag_col, small_all, gu_all, dy_all = refs[n_in : 2 * n_in]
        buffers = refs[2 * n_in : 3 * n_in]
        own_sems, send_sems, recv_sems = refs[3 * n_in :]
        place = Place(n_seq, n_bat)
        place.greet(all_seq=True)
        wire = Wire(send_sems, recv_sems)
        small_work = FullGather(place, wire, small_ref, small_all)
        flag_work = SeqGather(place, wire, flag_ref, flag_col)
        x_work = SeqGather(place, wire, x_ref, x_col)
        dy_work = FullGather(place, wire, dy_ref, dy_all)
        small_work.start()
        flag_work.start()
        cuts = [
            wire.push(cut_ref.at[place.seq_at(k)], w_ref.at[place.s, place.b], place.seq_peer(k))
            for k in range(1, n_seq)
        ]
        ends = [
            wire.push(wo_ref, wo_all.at[place.b], place.bat_peer(k)) for k in range(1, n_bat)
        ]
        ends += [
            wire.push(cut_ref.at[place.s], w_ref.at[place.s, place.b], place.bat_peer(k))
            for k in range(1, n_bat)
        ]
        x_work.start()
        own = [
            keep_own(src, dst, buffers[i], own_sems.at[i])
            for i, (src, dst) in enumerate(
                (
                    (cut_ref.at[place.s], w_ref.at[place.s, place.b]),
                    (wo_ref, wo_all.at[place.b]),
                    (x_ref, x_col.at[place.s]),
                    (flag_ref, flag_col.at[place.s]),
                    (small_ref, small_all.at[place.s, place.b]),
                    (gu_ref.at[place.s], gu_all.at[place.s]),
                    (dy_ref, dy_all.at[place.s, place.b]),
                )
            )
        ]
        ends += [
            wire.push(gu_ref.at[place.seq_at(k)], gu_all.at[place.s], place.seq_peer(k))
            for k in range(1, n_seq)
        ]
        dy_work.start()
        for j in range(1, place.half):
            small_work.step(j)
            flag_work.step(j)
        for k in range(1, n_seq):
            cuts[k - 1].wait_recv()
            block = w_ref.at[place.seq_at(-k), place.b]
            ends += [wire.push(block, block, place.bat_peer(m)) for m in range(1, n_bat)]
        for j in range(place.half):
            small_work.collect(j)
        for j in range(1, place.half):
            x_work.step(j)
        for j in range(1, place.half):
            dy_work.step(j)
            dy_work.collect(j - 1)
        dy_work.collect(place.half - 1)
        for work in (small_work, flag_work, x_work, dy_work):
            work.finish()
        for copy in ends:
            copy.wait_recv()
        for copy in own:
            copy.wait()
        wire.drain()

    every = (n_seq, n_bat)
    one = jax.ShapeDtypeStruct(qkv_cut.shape[1:], qkv_cut.dtype)
    gu_one = jax.ShapeDtypeStruct(gu_cut.shape[1:], gu_cut.dtype)
    blocks = (one, w_out, mine, flags, small, gu_one, dy_own)
    leads = (every, (n_bat,), (n_seq,), (n_seq,), every, (n_seq,), every)
    return comm_call(
        kernel,
        [shape_of(lead, block) for lead, block in zip(leads, blocks)],
        [pltpu.VMEM(block.shape, block.dtype) for block in blocks]
        + [pltpu.SemaphoreType.DMA((n_in,))],
        slots,
        1,
        "load_inputs",
        [ANY] * n_in,
    )(qkv_cut, w_out, mine, flags, small, gu_cut, dy_own)


def store_grads(grad_w, grad_wo, grad_gu, small, n_seq, n_bat):
    one = jax.ShapeDtypeStruct(grad_w.shape[2:], grad_w.dtype)
    wo_one = jax.ShapeDtypeStruct(grad_wo.shape[1:], grad_wo.dtype)
    gu_one = jax.ShapeDtypeStruct(grad_gu.shape[1:], grad_gu.dtype)
    small_one = jax.ShapeDtypeStruct(small.shape[2:], small.dtype)
    slots = 2 * n_seq * n_bat + 2 * n_seq + n_bat

    def kernel(*refs):
        w_ref, wo_ref, gu_ref, small_ref = refs[:4]
        w_out_ref, wo_out_ref, gu_out_ref, small_out_ref = refs[4:8]
        w_sum, w_got, wo_sum, wo_got, gu_buf, cut_buf = refs[8:14]
        small_scratch = refs[14:19]
        w_sems, sems, send_sems, recv_sems = refs[19:]
        place = Place(n_seq, n_bat)
        place.greet(all_seq=True)
        wire = Wire(send_sems, recv_sems)
        small_work = FullScatter(
            place, wire, small_ref, small_out_ref, *small_scratch
        )
        small_work.start()
        got, loads = {}, {}
        for i in list(range(1, n_seq)) + [0]:
            to_seq = place.seq_at(i)
            for k in range(1, n_bat):
                got[i, k] = wire.push(
                    w_ref.at[to_seq, place.bat_at(k)], w_got.at[i, k - 1], place.bat_peer(k)
                )
            loads[i] = pltpu.make_async_copy(
                w_ref.at[to_seq, place.b], w_sum.at[i], w_sems.at[i]
            )
            loads[i].start()
        wo_pushed = [
            wire.push(wo_ref.at[place.bat_at(k)], wo_got.at[k - 1], place.bat_peer(k))
            for k in range(1, n_bat)
        ]
        wo_load = pltpu.make_async_copy(wo_ref.at[place.b], wo_sum, sems.at[0])
        wo_load.start()
        ends = [
            wire.push(gu_ref.at[place.seq_at(k)], gu_out_ref.at[place.s], place.seq_peer(k))
            for k in range(1, n_seq)
        ]
        gu_own = keep_own(gu_ref.at[place.s], gu_out_ref.at[place.s], gu_buf, sems.at[1])
        order = small_work.order()
        for j in order:
            small_work.pair(j)
        for i in list(range(1, n_seq)) + [0]:
            loads[i].wait()
            for k in range(1, n_bat):
                got[i, k].wait_recv()
            add_into(w_sum.at[i], *[w_got.at[i, k] for k in range(n_bat - 1)])
            if i:
                ends.append(
                    wire.push(w_sum.at[i], w_out_ref.at[place.s], place.seq_peer(i))
                )
        w_own = pltpu.make_async_copy(w_sum.at[0], w_out_ref.at[place.s], sems.at[2])
        w_own.start()
        for j in order:
            small_work.merge(j)
        wo_load.wait()
        for copy in wo_pushed:
            copy.wait_recv()
        add_into(wo_sum, *[wo_got.at[k] for k in range(n_bat - 1)])
        wo_out_ref[...] = wo_sum[...].astype(F32)
        small_work.finish()
        for copy in ends:
            copy.wait_recv()
        gu_own.wait()
        w_own.wait()
        wire.drain()

    vmem = pl.BlockSpec(memory_space=pltpu.VMEM)
    return comm_call(
        kernel,
        [
            shape_of((n_seq,), one),
            jax.ShapeDtypeStruct(wo_one.shape, F32),
            shape_of((n_seq,), gu_one),
            small_one,
        ],
        [
            pltpu.VMEM((n_seq,) + one.shape, one.dtype),
            pltpu.VMEM((n_seq, n_bat - 1) + one.shape, one.dtype),
            pltpu.VMEM(wo_one.shape, wo_one.dtype),
            pltpu.VMEM((n_bat - 1,) + wo_one.shape, wo_one.dtype),
            pltpu.VMEM(gu_one.shape, gu_one.dtype),
            pltpu.VMEM(one.shape, one.dtype),
        ]
        + FullScatter.scratch(n_seq, n_bat, small_one)
        + [pltpu.SemaphoreType.DMA((n_seq,)), pltpu.SemaphoreType.DMA((3,))],
        slots,
        8,
        "store_grads",
        [ANY] * 4,
        [ANY, vmem, ANY, vmem],
    )(grad_w, grad_wo, grad_gu, small)


def shards(
    tokens,
    lengths,
    key_mask,
    top_experts,
    attn_gain,
    query_gain,
    key_gain,
    mlp_gain,
    w_query,
    w_key,
    w_value,
    w_out,
    w_router,
    expert_gate,
    expert_up,
    expert_down,
    cotangent,
):
    n_seq = lax.axis_size("seq")
    n_bat = lax.axis_size("batch")
    seq = lax.axis_index("seq")
    bat = lax.axis_index("batch")
    rows, span, dim = tokens.shape
    own = rows * span
    col = n_seq * own
    length = n_seq * span
    shard = w_query.shape[0]
    wide = dim // n_seq
    heads = wide // HEAD
    local_experts, depth, hidden_units = expert_gate.shape
    part = hidden_units // n_seq
    experts = local_experts * n_bat

    mine = tokens.reshape(own, dim)
    dy_own = cotangent.reshape(own, dim)
    small = jnp.concatenate(
        [w_router.T, jnp.stack([attn_gain, query_gain, key_gain, mlp_gain])], axis=0
    )
    positions_own = seq * span + jnp.arange(span, dtype=jnp.int32)
    flags = pack((positions_own[None, :] < lengths[:, None]) & (key_mask == 1))
    units = local_experts * part
    fused = (
        n_bat == 4
        and part % 128 == 0
        and own == 128
        and shard % 32 == 0
        and n_seq == 8
        and shard == 64
        and experts == 8
        and span == 64
        and rows <= 8
        and n_seq * n_bat * own * dim <= 8 * 1024 * 1024
    )
    if fused:
        gains = jnp.stack([attn_gain, query_gain, key_gain, mlp_gain])
        small = jnp.concatenate([w_router.T, jnp.pad(gains, ((0, 4), (0, 0)))], axis=1).astype(F32)
        flags = (positions_own[None, :] < lengths[:, None]) & (key_mask == 1)
        flags = jnp.pad(flags.astype(F32), ((0, 8 - rows), (0, 128 - span)))
        w_qkv, w_o, x_col, router_t, gains, usable = load_first(
            (w_query, w_key, w_value), w_out, mine, flags, small, rows, n_seq, n_bat
        )
    else:
        qkv_cut = jnp.stack([w_query, w_key, w_value]).reshape(3, shard, n_seq, wide)
        qkv_cut = jnp.transpose(qkv_cut, (2, 1, 0, 3)).reshape(n_seq, shard, 3 * wide)
        gu_cut = jnp.stack([expert_gate, expert_up]).reshape(2, local_experts, depth, n_seq, part)
        gu_cut = jnp.transpose(gu_cut, (3, 2, 0, 1, 4)).reshape(n_seq, depth, 2 * units)
        w_qkv, w_o, x_col, flag_col, small_all, w_gu, dy_all = load_inputs(
            qkv_cut, w_out, mine, flags, pack(small), gu_cut, dy_own, n_seq, n_bat
        )
        w_gu = w_gu.reshape(dim, 2 * units)
        dy_all = dy_all.reshape(-1, dim)
        x_col = jnp.transpose(x_col.reshape(n_seq, rows, span, dim), (1, 0, 2, 3))
    w_qkv = w_qkv.reshape(dim, 3 * wide)
    w_o = w_o.reshape(wide, dim)
    w_down = expert_down.reshape(local_experts * part, dim)
    if not fused:
        small_all = unpack(small_all, (n_seq, n_bat), small.shape)
        small_all = jnp.transpose(small_all, (2, 0, 1, 3)).reshape(-1, dim)
        router = small_all[:experts].T.astype(BF)
        gains = small_all[experts:]
        gain_attn, gain_mlp = gains[0], gains[3]
        usable = unpack(flag_col, (n_seq,), key_mask.shape)
        usable = jnp.transpose(usable, (1, 0, 2)).reshape(rows, length)
        router_t = small_all[:experts]

    expert_ids = jnp.arange(experts, dtype=jnp.int32)
    chosen_t = jnp.any(top_experts.reshape(own, -1).T[None] == expert_ids[:, None, None], axis=1)
    chosen_t = chosen_t.astype(F32)
    cos_wide, sin_wide = rotary_tables(length)
    hidden, qkv, q, k, v, mixed, stats, mixed_out, *extra = attend_forward(
        x_col.reshape(col, dim), w_qkv, usable, w_o, gains, cos_wide, sin_wide, n_seq, n_bat, rows,
        (dy_own, mine, router_t, chosen_t) if fused else None,
    )
    if not fused:
        x_own = mine.astype(F32)
        residual = x_own + mixed_out.astype(F32)
        scale_r = rms_scale(residual)
        normed = (residual * scale_r * gain_mlp).astype(BF)
        router_probs = jax.nn.softmax(dot(normed, router), axis=-1)
        chosen = chosen_t.T
        gates = router_probs * chosen

    if fused:
        dy_all, residual, normed, probs_t, gates_t = extra
        normed_all, weighted, grad_pre, gate_terms, w_gu = experts_forward(
            normed, gates_t, dy_all, expert_gate, expert_up, w_down, n_seq, n_bat
        )
        w_gu = w_gu.reshape(dim, 2 * units)
        grad_residual, grad_o, small_grads, grad_gate, grad_up, grad_down = experts_backward(
            grad_pre,
            weighted,
            w_gu,
            gate_terms,
            normed_all.reshape(-1, dim),
            dy_all.reshape(-1, dim),
            residual,
            dy_own,
            gains,
            router_t,
            probs_t,
            chosen_t,
            local_experts,
            n_seq,
            n_bat,
        )
        grad_down = grad_down.reshape(local_experts, part, dim)
    else:
        normed_all, gates_all = gather_all([normed, pack(gates.T)], n_seq, n_bat, 4, "gather_normed")
        normed_all = normed_all.reshape(-1, dim)
        gates_all = unpack(gates_all, (n_seq, n_bat), (experts, own))
        gates_all = jnp.transpose(gates_all, (0, 1, 3, 2)).reshape(-1, experts)
        first_expert = bat * local_experts
        gates_here = lax.dynamic_slice_in_dim(gates_all, first_expert, local_experts, 1)
        gates_wide = jnp.repeat(gates_here, part, axis=1)
        pre = dot(normed_all, w_gu)
        gate_pre, up_pre = pre[:, :units], pre[:, units:]
        sig = jax.nn.sigmoid(gate_pre)
        silu = gate_pre * sig
        active = (silu * up_pre).astype(BF).astype(F32)
        weighted = (active * gates_wide).astype(BF)
        mixture = dot(weighted, w_down).astype(BF)
        mixture = mixture.reshape(n_seq, n_bat, own, dim)
        back = dot_t(dy_all, w_down)
        gate_terms = jnp.sum((active * back).reshape(-1, local_experts, part), axis=-1)
        grad_active = back * gates_wide
        grad_gate_pre = (grad_active * up_pre * sig * (1.0 + gate_pre * (1.0 - sig))).astype(BF)
        grad_up_pre = (grad_active * silu).astype(BF)
        grad_pre = jnp.concatenate([grad_gate_pre, grad_up_pre], axis=1)
        grad_down = t_dot(weighted, dy_all)
        grad_gu = t_dot(normed_all, grad_pre).astype(BF)
        grad_normed = dot_t(grad_pre, w_gu).astype(BF)
        gate_terms = gate_terms.reshape(n_seq, n_bat, own, local_experts)
        grad_gates = lax.dynamic_update_slice_in_dim(
            jnp.zeros((n_seq, n_bat, experts, own), F32),
            jnp.transpose(gate_terms, (0, 1, 3, 2)),
            first_expert,
            2,
        )
        grad_gates = jax.vmap(jax.vmap(pack))(grad_gates)
        grad_normed = grad_normed.reshape(n_seq, n_bat, own, dim)
        grad_normed, grad_gates, mixture = scatter_blocks(
            grad_normed, grad_gates, mixture, n_seq, n_bat
        )
        grad_normed = grad_normed.astype(F32)
        grad_gates = unpack(grad_gates, (), (experts, own)).T
        output = (residual + mixture.astype(F32)).astype(BF)
        grad_down = grad_down.reshape(local_experts, part, dim)

    if not fused:
        grad_chosen = grad_gates * chosen
        grad_logits = router_probs * (
            grad_chosen - jnp.sum(router_probs * grad_chosen, axis=-1, keepdims=True)
        )
        grad_router = lax.dot_general(
            normed.astype(F32), grad_logits, (((0,), (0,)), ((), ())), precision=HIGHEST
        )
        grad_normed = grad_normed + lax.dot_general(
            grad_logits, router.astype(F32), (((1,), (1,)), ((), ())), precision=HIGHEST
        )
        grad_resid, gain_mlp_terms = rms_back(residual, scale_r, gain_mlp, grad_normed)
        grad_residual = dy_own.astype(F32) + grad_resid
        grad_o = grad_residual.astype(BF)

    grad_w_o, grad_w, grad_gains, grad_hidden, *extra = attend_backward(
        grad_o, q, k, v, mixed, qkv, stats, hidden, usable, w_o, w_qkv, gains, cos_wide, sin_wide,
        n_seq, n_bat,
        (weighted, w_down, mine, grad_residual, small_grads) if fused else None,
    )
    grad_w_o = grad_w_o.reshape(n_bat, shard, dim)
    grad_w = grad_w.reshape(n_seq, n_bat, shard, 3 * wide)
    if not fused:
        grad_hidden = grad_hidden.astype(F32)
        grad_x, gain_attn_terms = rms_back(x_own, rms_scale(x_own), gain_attn, grad_hidden)
        grad_tokens = (grad_residual + grad_x).astype(BF)

        zeros = jnp.zeros((dim,), F32)
        small_grads = jnp.concatenate(
            [
                grad_router.T,
                jnp.stack(
                    [
                        jnp.sum(gain_attn_terms, axis=0),
                        lax.dynamic_update_slice_in_dim(zeros, grad_gains[0], seq * wide, 0),
                        lax.dynamic_update_slice_in_dim(zeros, grad_gains[1], seq * wide, 0),
                        jnp.sum(gain_mlp_terms, axis=0),
                    ]
                ),
            ],
            axis=0,
        )
        small_grads = jnp.transpose(small_grads.reshape(-1, n_seq, n_bat, shard), (1, 2, 0, 3))
        small_grads = jax.vmap(jax.vmap(pack))(small_grads)

    if fused:
        *grad_w, grad_w_o, small_grads, mixture = store_last(
            grad_w, grad_w_o, extra[1], extra[0], n_seq, n_bat
        )
        output, grad_tokens, *grad_w, grad_w_o, grad_gate, grad_up, grad_down = finish(
            residual, mixture, [grad_hidden, *grad_w, grad_w_o, grad_gate, grad_up, grad_down]
        )
        small_grads = lax.dynamic_slice_in_dim(small_grads, lax.rem(bat, 2) * shard, shard, 1)
    else:
        grad_gu = grad_gu.reshape(n_seq, depth, -1)
        grad_w, grad_w_o, grad_gu, small_grads = store_grads(
            grad_w, grad_w_o, grad_gu, small_grads, n_seq, n_bat
        )
        grad_w = grad_w.astype(F32).reshape(n_seq, shard, 3, wide)
        grad_w = jnp.transpose(grad_w, (2, 1, 0, 3)).reshape(3, shard, dim)
        grad_gu = grad_gu.reshape(n_seq, depth, 2, local_experts, part)
        grad_gu = jnp.transpose(grad_gu, (2, 3, 1, 0, 4)).reshape(2, local_experts, depth, hidden_units)
        grad_gu = grad_gu.astype(F32)
        grad_gate, grad_up = grad_gu[0], grad_gu[1]
        small_grads = unpack(small_grads, (), (experts + 4, shard))

    return (
        output.reshape(rows, span, dim),
        grad_tokens.reshape(rows, span, dim),
        small_grads[experts],
        small_grads[experts + 1],
        small_grads[experts + 2],
        small_grads[experts + 3],
        grad_w[0],
        grad_w[1],
        grad_w[2],
        grad_w_o,
        small_grads[:experts].T,
        grad_gate,
        grad_up,
        grad_down,
    )


def solution(mesh):
    tok = P("batch", "seq", None)
    vec = P(("seq", "batch"))
    mat = P(("seq", "batch"), None)
    in_specs = (tok, P("batch"), P("batch", "seq"), tok) + (vec,) * 4 + (mat,) * 5 + (tok,) * 4
    out_specs = (tok, tok) + (vec,) * 4 + (mat,) * 5 + (tok,) * 3
    return jax.shard_map(shards, mesh=mesh, in_specs=in_specs, out_specs=out_specs, check_vma=False)
```

```python
import functools

import jax
import jax.numpy as jnp
import numpy as np
from jax import lax
from jax.experimental import pallas as pl
from jax.experimental.pallas import tpu as pltpu
from jax.sharding import PartitionSpec as P

HEAD = 128
EPS = 1e-05
HIGHEST = lax.Precision.HIGHEST
NEGATIVE = -1e30
BF = jnp.bfloat16
F32 = jnp.float32


def dot(a, b):
    return jnp.dot(a, b, preferred_element_type=F32)


def dot_t(a, b):
    return lax.dot_general(a, b, (((1,), (1,)), ((), ())), preferred_element_type=F32)


def t_dot(a, b):
    return lax.dot_general(a, b, (((0,), (0,)), ((), ())), preferred_element_type=F32)


def rms_scale(v):
    return lax.rsqrt(jnp.mean(v * v, axis=-1, keepdims=True) + EPS)


def rms_back(v, scale, gain, grad):
    normal = v * scale
    weighted = grad * gain
    mean = jnp.mean(weighted * normal, axis=-1, keepdims=True)
    return scale * (weighted - normal * mean), grad * normal


def rotary_tables(length):
    half_head = HEAD // 2
    frequency = 10000.0 ** (-2.0 * np.arange(half_head, dtype=np.float32) / HEAD)
    angles = np.arange(length, dtype=np.float32)[:, None] * frequency.astype(np.float32)[None, :]
    cosines, sines = np.cos(angles), np.sin(angles)
    return np.concatenate([cosines, cosines], axis=1), np.concatenate([-sines, sines], axis=1)


ANY = pl.BlockSpec(memory_space=pl.ANY)
VMEM_LIMIT = 67043328


class Place:
    def __init__(self, n_seq, n_bat):
        self.n_seq, self.n_bat, self.half = n_seq, n_bat, n_seq // 2
        self.s = lax.axis_index("seq")
        self.b = lax.axis_index("batch")
        self.core = lax.rem(self.s, 2)
        self.z = lax.div(self.s, 2)
        self.twin_s = self.s + 1 - 2 * self.core
        self.bat_x = self.b + 1 - 2 * lax.rem(self.b, 2)
        self.bat_y = lax.rem(self.b + 2, 4)
        self.bat_d = lax.rem(self.bat_x + 2, 4)

    def chip(self, i):
        return 2 * i + self.core

    def chip_twin(self, i):
        return 2 * i + 1 - self.core

    def chip_peer(self, i):
        return {"seq": self.chip(lax.rem(i + self.half, self.half)), "batch": self.b}

    def origin(self, m):
        return self.z if m == 0 else self.origin_of(m)

    def origin_of(self, m):
        last = self.half - 1
        upper = lax.div(2 * self.z, self.half)
        mirrored = self.z + upper * (last - 2 * self.z)
        place = m - 1 + lax.div(m - mirrored + last, self.half)
        return place + upper * (last - 2 * place)

    def seq_at(self, k):
        return lax.rem(self.s + (k + self.n_seq), self.n_seq)

    def twin_at(self, k):
        return lax.rem(self.twin_s + (k + self.n_seq), self.n_seq)

    def bat_at(self, k):
        return lax.rem(self.b + (k + self.n_bat), self.n_bat)

    def seq_peer(self, k):
        return {"seq": self.seq_at(k), "batch": self.b}

    def bat_peer(self, k):
        return {"seq": self.s, "batch": self.bat_at(k)}

    def x_peer(self):
        return {"seq": self.s, "batch": self.bat_x}

    def y_peer(self):
        return {"seq": self.s, "batch": self.bat_y}

    def twin(self):
        return {"seq": self.twin_s, "batch": self.b}

    def greet(self, all_seq=False, batch=True):
        steps = range(1, self.n_seq) if all_seq else range(2, self.n_seq, 2)
        peers = [self.seq_peer(k) for k in steps]
        if not all_seq:
            peers.append(self.twin())
        if batch:
            peers += [self.bat_peer(k) for k in range(1, self.n_bat)]
        barrier = pltpu.get_barrier_semaphore()
        for peer in peers:
            pl.semaphore_signal(
                barrier, inc=1, device_id=peer, device_id_type=pl.DeviceIdType.MESH
            )
        pl.semaphore_wait(barrier, len(peers))


class Wire:
    def __init__(self, send_sems, recv_sems):
        self.send_sems, self.recv_sems = send_sems, recv_sems
        self.copies, self.used = [], 0

    def reserve(self, count):
        first = self.used
        self.used += count
        return first

    def make(self, src, dst, peer, send_slot, recv_slot):
        return pltpu.make_async_remote_copy(
            src_ref=src,
            dst_ref=dst,
            send_sem=self.send_sems.at[send_slot],
            recv_sem=self.recv_sems.at[recv_slot],
            device_id=peer,
            device_id_type=pl.DeviceIdType.MESH,
        )

    def push(self, src, dst, peer):
        slot = self.reserve(1)
        copy = self.make(src, dst, peer, slot, slot)
        copy.start()
        self.copies.append((copy, None))
        return copy

    def push_if(self, there, copy):
        pl.when(there)(copy.start)
        self.copies.append((copy, there))

    def settle(self, copy):
        copy.wait_send()
        self.copies = [other for other in self.copies if other[0] is not copy]

    def drain(self):
        for copy, there in self.copies:
            if there is None:
                copy.wait_send()
            else:
                pl.when(there)(copy.wait_send)


class Line:
    def __init__(self, place, wire, src, at):
        self.place, self.wire, self.src, self.at = place, wire, src, at
        self.base = wire.reserve(place.half + 2)
        self.sends = 0

    def copy(self, src, origin, peer):
        return self.wire.make(
            src, self.at(origin), peer, self.base + self.sends, self.base + origin
        )

    def send(self, there, src, origin, to):
        copy = self.copy(src, origin, self.place.chip_peer(to))
        self.sends += 1
        self.wire.push_if(there, copy)

    def start(self):
        place = self.place
        self.send(place.z < place.half - 1, self.src, place.z, place.z + 1)
        self.send(place.z > 0, self.src, place.z, place.z - 1)

    def step(self, m):
        place = self.place
        origin = place.origin(m)
        self.copy(self.at(origin), origin, place.chip_peer(place.z)).wait_recv()
        from_left = lax.div(place.z - origin - 1 + place.half, place.half)
        to = place.z + 2 * from_left - 1
        self.send((to >= 0) & (to < place.half), self.at(origin), origin, to)
        return origin


class SeqGather:
    def __init__(self, place, wire, src, out):
        self.place, self.wire, self.src, self.out = place, wire, src, out
        self.late = []

    def start(self):
        place = self.place
        self.line = Line(place, self.wire, self.src, lambda i: self.out.at[place.chip(i)])
        self.line.start()
        self.late.append(self.wire.push(self.src, self.out.at[place.s], place.twin()))

    def step(self, j):
        block = self.out.at[self.place.chip(self.line.step(j))]
        self.late.append(self.wire.push(block, block, self.place.twin()))

    def finish(self):
        for copy in self.late:
            copy.wait_recv()


class FullGather:
    def __init__(self, place, wire, src, out):
        self.place, self.wire, self.src, self.out = place, wire, src, out
        self.late = []
        self.across = {}

    def spread(self, j, block):
        place = self.place
        self.across[j] = [
            self.wire.push(block, self.out.at[place.seq_at(-2 * j), place.b], place.bat_peer(k))
            for k in range(1, place.n_bat)
        ]

    def start(self):
        place, mine = self.place, self.out.at[self.place.s, self.place.b]
        self.line = [
            self.wire.push(self.src, mine, place.seq_peer(2 * j)) for j in range(1, place.half)
        ]
        self.spread(0, self.src)
        self.late.append(self.wire.push(self.src, mine, place.twin()))

    def step(self, j):
        self.line[j - 1].wait_recv()
        block = self.out.at[self.place.seq_at(-2 * j), self.place.b]
        self.spread(j, block)
        self.late.append(self.wire.push(block, block, self.place.twin()))

    def collect(self, j):
        place = self.place
        for k in range(1, place.n_bat):
            self.across[j][k - 1].wait_recv()
            block = self.out.at[place.seq_at(-2 * j), place.bat_at(-k)]
            self.late.append(self.wire.push(block, block, place.twin()))

    def finish(self):
        for copy in self.late:
            copy.wait_recv()


def keep_own(src, dst, buffer, sem):
    first = pltpu.make_async_copy(src, buffer, sem)
    first.start()
    first.wait()
    second = pltpu.make_async_copy(buffer, dst, sem)
    second.start()
    return second


def comm_call(
    kernel, outs, scratch, slots, collective_id, name, in_specs, out_specs=None, aliases=None
):
    return pl.pallas_call(
        kernel,
        out_shape=outs,
        in_specs=in_specs,
        out_specs=out_specs if out_specs is not None else jax.tree.map(lambda _: ANY, outs),
        scratch_shapes=list(scratch)
        + [pltpu.SemaphoreType.DMA((slots,)), pltpu.SemaphoreType.DMA((slots,))],
        compiler_params=pltpu.CompilerParams(
            collective_id=collective_id, has_side_effects=True, vmem_limit_bytes=VMEM_LIMIT
        ),
        name=name,
        input_output_aliases=aliases or {},
    )


def shape_of(lead, block):
    return jax.ShapeDtypeStruct(tuple(lead) + block.shape, block.dtype)


def gather_all(blocks, n_seq, n_bat, collective_id, name):
    count = len(blocks)

    def kernel(*refs):
        srcs, outs = refs[:count], refs[count : 2 * count]
        buffers = refs[2 * count : 3 * count]
        own_sems, send_sems, recv_sems = refs[3 * count :]
        place = Place(n_seq, n_bat)
        place.greet()
        wire = Wire(send_sems, recv_sems)
        gathers = [FullGather(place, wire, *pair) for pair in zip(srcs, outs)]
        for gather in gathers:
            gather.start()
        own = [
            keep_own(srcs[i], outs[i].at[place.s, place.b], buffers[i], own_sems.at[i])
            for i in range(count)
        ]
        for j in range(1, place.half):
            for gather in gathers:
                gather.step(j)
            for gather in gathers:
                gather.collect(j - 1)
        for gather in gathers:
            gather.collect(place.half - 1)
        for gather in gathers:
            gather.finish()
        for copy in own:
            copy.wait()
        wire.drain()

    return comm_call(
        kernel,
        [shape_of((n_seq, n_bat), block) for block in blocks],
        [pltpu.VMEM(block.shape, block.dtype) for block in blocks]
        + [pltpu.SemaphoreType.DMA((count,))],
        n_seq * n_bat * count,
        collective_id,
        name,
        [ANY] * count,
    )(*blocks)


def add_into(target, *others):
    rows = target.shape[0]
    step = min(rows, 16)

    def body(i, carry):
        at = pl.ds(pl.multiple_of(i * step, step), step)
        total = target[at, :].astype(F32)
        for other in others:
            total = total + other[at, :].astype(F32)
        target[at, :] = total.astype(target.dtype)
        return carry

    lax.fori_loop(0, rows // step, body, 0)


class FullScatter:
    def __init__(self, place, wire, parts, out, mine, twin, across, line, sems, pick=None):
        self.place, self.wire, self.out = place, wire, out
        self.mine, self.twin, self.across, self.line = mine, twin, across, line
        self.sems = sems
        self.pick = pick or (lambda i, j: parts.at[i, j])

    @staticmethod
    def scratch(n_seq, n_bat, block):
        half = n_seq // 2
        return [
            pltpu.VMEM((half, n_bat) + block.shape, block.dtype),
            pltpu.VMEM((half, n_bat) + block.shape, block.dtype),
            pltpu.VMEM((half, n_bat) + block.shape, block.dtype),
            pltpu.VMEM((half,) + block.shape, block.dtype),
            pltpu.SemaphoreType.DMA((half, n_bat)),
        ]

    def order(self):
        return list(range(1, self.place.half)) + [0]

    def start(self):
        place = self.place
        self.from_twin, self.loads, self.from_bat, self.from_seq = {}, {}, {}, {}
        for j in self.order():
            for k in list(range(1, place.n_bat)) + [0]:
                to_bat = place.bat_at(k)
                self.from_twin[j, k] = self.wire.push(
                    self.pick(place.twin_at(2 * j), to_bat), self.twin.at[j, k], place.twin()
                )
                load = pltpu.make_async_copy(
                    self.pick(place.seq_at(2 * j), to_bat),
                    self.mine.at[j, k],
                    self.sems.at[j, k],
                )
                load.start()
                self.loads[j, k] = load

    def pair(self, j):
        place = self.place
        for k in list(range(1, place.n_bat)) + [0]:
            self.from_twin[j, k].wait_recv()
            self.loads[j, k].wait()
            add_into(self.mine.at[j, k], self.twin.at[j, k])
        for k in range(1, place.n_bat):
            self.from_bat[j, k] = self.wire.push(
                self.mine.at[j, k], self.across.at[j, k], place.bat_peer(k)
            )

    def merge(self, j):
        place = self.place
        for k in range(1, place.n_bat):
            self.from_bat[j, k].wait_recv()
        add_into(self.mine.at[j, 0], *[self.across.at[j, k] for k in range(1, place.n_bat)])
        if j:
            self.from_seq[j] = self.wire.push(
                self.mine.at[j, 0], self.line.at[j], place.seq_peer(2 * j)
            )

    def finish(self):
        for j in range(1, self.place.half):
            self.from_seq[j].wait_recv()
        add_into(self.mine.at[0, 0], *[self.line.at[j] for j in range(1, self.place.half)])
        self.out[...] = self.mine[0, 0]


def scatter_all(parts, n_seq, n_bat, collective_id, name):
    blocks = [jax.ShapeDtypeStruct(part.shape[2:], part.dtype) for part in parts]
    count = len(parts)

    def kernel(*refs):
        ins, outs = refs[:count], refs[count : 2 * count]
        rest = refs[2 * count :]
        send_sems, recv_sems = rest[-2:]
        place = Place(n_seq, n_bat)
        place.greet()
        wire = Wire(send_sems, recv_sems)
        works = [
            FullScatter(place, wire, ins[i], outs[i], *rest[5 * i : 5 * i + 5])
            for i in range(count)
        ]
        for work in works:
            work.start()
        order = works[0].order()
        for at, j in enumerate(order):
            for work in works:
                work.pair(j)
            if at:
                for work in works:
                    work.merge(order[at - 1])
        for work in works:
            work.merge(order[-1])
        for work in works:
            work.finish()
        wire.drain()

    scratch = []
    for block in blocks:
        scratch += FullScatter.scratch(n_seq, n_bat, block)
    slots = count * (n_seq * n_bat)
    vmem = pl.BlockSpec(memory_space=pltpu.VMEM)
    return comm_call(
        kernel,
        blocks,
        scratch,
        slots,
        collective_id,
        name,
        [ANY] * count,
        [vmem] * count,
    )(*parts)


def pack(values):
    flat = values.astype(F32).reshape(-1)
    tiles = -(-flat.shape[0] // 1024)
    return jnp.pad(flat, (0, tiles * 1024 - flat.shape[0])).reshape(tiles * 8, 128)


def unpack(tiles, lead, shape):
    size = 1
    for extent in shape:
        size *= extent
    return tiles.reshape(tuple(lead) + (-1,))[..., :size].reshape(tuple(lead) + tuple(shape))


def scatter_blocks(grad_normed, grad_gates, mixture, n_seq, n_bat):
    dim = grad_normed.shape[-1]
    pieces = 1
    while n_seq * n_bat * grad_normed.shape[2] * (dim // pieces) * 4 > 36 * 1024 * 1024:
        pieces *= 2
    size = dim // pieces
    grads, mixtures = [], []
    for i in range(pieces):
        at = slice(i * size, (i + 1) * size)
        parts = [grad_normed[..., at]] + ([grad_gates] if i == 0 else [])
        done = scatter_all(parts, n_seq, n_bat, 16 + 2 * i, "scatter_normed")
        grads.append(done[0])
        if i == 0:
            gates = done[1]
        done = scatter_all([mixture[..., at]], n_seq, n_bat, 17 + 2 * i, "scatter_mixture")
        mixtures.append(done[0])
    return jnp.concatenate(grads, axis=-1), gates, jnp.concatenate(mixtures, axis=-1)


class SeqScatter:
    def __init__(self, place, wire, full, twin, line):
        self.place, self.wire = place, wire
        self.full, self.twin, self.line = full, twin, line
        self.order = list(range(1, place.half)) + [0]

    @staticmethod
    def scratch(rows, n_seq, block):
        lead = ((rows, n_seq), (rows, n_seq // 2), (rows, n_seq // 2))
        return [pltpu.VMEM(extent + block.shape, block.dtype) for extent in lead]

    def start(self):
        place = self.place
        self.from_seq = {}
        self.from_twin = {
            j: self.wire.push(self.full.at[place.twin_at(2 * j)], self.twin.at[j], place.twin())
            for j in self.order
        }

    def pass_on(self, first=0, last=None):
        place = self.place
        for j in self.order[first:last]:
            self.from_twin[j].wait_recv()
            block = self.full.at[place.seq_at(2 * j)]
            add_into(block, self.twin.at[j])
            if j:
                self.from_seq[j] = self.wire.push(block, self.line.at[j], place.seq_peer(2 * j))

    def total(self):
        for copy in self.from_seq.values():
            copy.wait_recv()
        total = self.full[self.place.s].astype(F32)
        for j in range(1, self.place.half):
            total = total + self.line[j].astype(F32)
        return total

    def finish(self, out, at):
        for copy in self.from_seq.values():
            copy.wait_recv()
        own = self.full.at[self.place.s]
        add_into(own, *[self.line.at[j] for j in range(1, self.place.half)])
        out[at, :] = own[...]


def turn(v, cos_wide, sin_wide):
    return v * cos_wide + pltpu.roll(v, HEAD // 2, axis=1) * sin_wide


class Exchange:
    def __init__(self, place, wire, local, got):
        self.local, self.got, self.count = local, got, place.n_seq - 1
        self.copies = [
            wire.push(local, got.at[k - 1], place.seq_peer(k)) for k in range(1, place.n_seq)
        ]

    def total(self):
        for copy in self.copies:
            copy.wait_recv()
        total = self.local[...]
        for k in range(self.count):
            total = total + self.got[k]
        return total


def in_two(v):
    high = v.astype(BF)
    return high, (v - high.astype(F32)).astype(BF)


def lane_sums(v):
    ones = jnp.ones((8, v.shape[1]), BF)
    high, low = in_two(v)
    return (dot_t(ones, high) + dot_t(ones, low))[0:1]


def allowed_block(use, first, count, keys):
    at_query = first + lax.broadcasted_iota(jnp.int32, (count, keys), 0)
    at_key = lax.broadcasted_iota(jnp.int32, (count, keys), 1)
    return (at_key == at_query) | ((at_key < at_query) & (use > 0))


STEP = 128


def head_gain(place, gains_ref, which, wide, h):
    first = pl.multiple_of(place.s * wide + h * HEAD, HEAD)
    return gains_ref[1 + which : 2 + which, pl.ds(first, HEAD)]


def attend_forward(
    x_col, w_qkv, usable, w_o, gains, cos_wide, sin_wide, n_seq, n_bat, rows, side=None
):
    col, dim = x_col.shape
    three = w_qkv.shape[1]
    wide = three // 3
    heads = wide // HEAD
    length = col // rows
    span = length // n_seq
    own = rows * span
    steps = length // STEP
    chunk = min(256, length)
    scale = HEAD ** (-0.5)
    block = jax.ShapeDtypeStruct((span, dim), BF)

    def kernel(*refs):
        (x_ref, w_ref, use_ref, wo_ref, gains_ref, cos_ref, sin_ref) = refs[:7]
        refs = refs[7:]
        if side is not None:
            dy_ref, own_ref, router_ref, chosen_ref = refs[:4]
            refs = refs[4:]
        hid_ref, qkv_ref, q_ref, k_ref, v_ref, mix_ref, stat_ref, out_ref = refs[:8]
        refs = refs[8:]
        if side is not None:
            dy_all, res_ref, normed_ref, probs_ref, gates_ref = refs[:5]
            dy_keep, dy_sem = refs[-4:-2]
            refs = refs[5:-4] + refs[-2:]
        local, got, full, twin, line, send_sems, recv_sems = refs
        place = Place(n_seq, n_bat)
        place.greet(all_seq=True, batch=side is not None)
        wire = Wire(send_sems, recv_sems)
        dy_works, dy_here = [], [place.chip(place.origin(m)) for m in range(place.half)]

        def dy_spread(m):
            if side is None:
                return
            if m:
                dy_line.step(m)
            src = dy_all.at[dy_here[m], place.b] if m else dy_ref
            work = Across(place, wire, src, lambda i: dy_all.at[dy_here[m], i])
            work.start()
            dy_works.append(work)

        if side is not None:
            dy_line = Line(place, wire, dy_ref, lambda i: dy_all.at[place.chip(i), place.b])
            dy_line.start()
            dy_spread(0)
            dy_own = keep_own(dy_ref, dy_all.at[place.s, place.b], dy_keep, dy_sem)
        def project(n, carry):
            at = pl.ds(pl.multiple_of(n * chunk, chunk), chunk)
            x = x_ref[at, :].astype(F32)
            hidden = (x * rms_scale(x) * gains_ref[0:1, :]).astype(BF)
            hid_ref[at, :] = hidden
            qkv_ref[at, :] = dot(hidden, w_ref[...])
            return carry

        lax.fori_loop(0, col // chunk, project, 0)
        for r in range(rows):
            for c in range(steps):
                at = slice(r * length + c * STEP, r * length + (c + 1) * STEP)
                for which in range(2):
                    v = qkv_ref[at, which * wide : (which + 1) * wide]
                    row = (r * 2 + which) * steps + c
                    local[row : row + 1, :] = lane_sums(v * v)
        for r in range(rows):
            for h in range(heads):
                lanes = slice(2 * wide + h * HEAD, 2 * wide + (h + 1) * HEAD)
                v_ref[r, h] = qkv_ref[r * length : (r + 1) * length, lanes].astype(BF)
        exchange = Exchange(place, wire, local, got)
        dy_spread(1)
        total = exchange.total()
        stat_ref[...] = total
        columns = lax.rsqrt(total / dim + EPS).T
        scatters = [
            SeqScatter(place, wire, full.at[r], twin.at[r], line.at[r]) for r in range(rows)
        ]
        for r in range(rows):
            for c in range(steps):
                inside = slice(c * STEP, (c + 1) * STEP)
                at = slice(r * length + c * STEP, r * length + (c + 1) * STEP)
                for which, target in ((0, q_ref), (1, k_ref)):
                    row = (r * 2 + which) * steps + c
                    factor = columns[:, row : row + 1]
                    for h in range(heads):
                        lanes = slice(which * wide + h * HEAD, which * wide + (h + 1) * HEAD)
                        gain = head_gain(place, gains_ref, which, wide, h)
                        v = qkv_ref[at, lanes] * factor * gain
                        target[r, h, inside, :] = turn(
                            v, cos_ref[inside, :], sin_ref[inside, :]
                        ).astype(BF)
            for c in range(length // chunk):
                keys = (c + 1) * chunk
                allowed = allowed_block(use_ref[r : r + 1, :keys], c * chunk, chunk, keys)
                for h in range(heads):
                    query = q_ref[r, h, c * chunk : keys, :]
                    scores = dot_t(query, k_ref[r, h, :keys, :]) * scale
                    scores = jnp.where(allowed, scores, NEGATIVE)
                    raised = jnp.exp(scores - jnp.max(scores, axis=-1, keepdims=True))
                    probs = raised / jnp.sum(raised, axis=-1, keepdims=True)
                    mixed = dot(probs.astype(BF), v_ref[r, h, :keys, :]).astype(BF)
                    mix_ref[r, c * chunk : keys, h * HEAD : (h + 1) * HEAD] = mixed
                if r and c == 0:
                    scatters[r - 1].pass_on()
                if r == 0 and c == 0 and side is not None:
                    dy_works[0].relay()
                    dy_spread(2)
            full[r] = dot(mix_ref[r], wo_ref[...]).astype(BF).reshape(n_seq, span, dim)
            scatters[r].start()
            if r == 0 and side is not None:
                dy_works[1].relay()
                for m in range(3, place.half):
                    dy_spread(m)
        scatters[-1].pass_on()
        for work in dy_works[2:]:
            work.relay()
        passed = []
        if side is not None:
            dy_own.wait()
        for m, work in enumerate(dy_works):
            work.finish()
            group = dy_all.at[dy_here[m]]
            passed.append(wire.push(group, group, place.twin()))
        for r in range(rows):
            at = slice(r * span, (r + 1) * span)
            if side is None:
                scatters[r].finish(out_ref, at)
                continue
            residual = own_ref[at, :].astype(F32) + scatters[r].total()
            res_ref[at, :] = residual
            normed_ref[at, :] = (residual * rms_scale(residual) * gains_ref[3:4, :]).astype(BF)
        if side is not None:
            out_ref[...] = jnp.zeros_like(out_ref)
            logits = dot_t(router_ref[...].astype(BF), normed_ref[...])
            raised = jnp.exp(logits - jnp.max(logits, axis=0, keepdims=True))
            probs = raised / jnp.sum(raised, axis=0, keepdims=True)
            probs_ref[...] = probs
            gates_ref[...] = probs * chosen_ref[...]
        for copy in passed:
            copy.wait_recv()
        wire.drain()

    vmem = pl.BlockSpec(memory_space=pltpu.VMEM)
    side_in, side_out, side_scratch = [], [], []
    slots = (1 + rows) * n_seq
    if side is not None:
        dy, _, router, _ = side
        side_in = list(side)
        side_out = [
            shape_of((n_seq, n_bat), dy),
            jax.ShapeDtypeStruct((own, dim), F32),
            jax.ShapeDtypeStruct((own, dim), BF),
            jax.ShapeDtypeStruct((router.shape[0], own), F32),
            jax.ShapeDtypeStruct((router.shape[0], own), F32),
        ]
        side_scratch = [pltpu.VMEM(dy.shape, dy.dtype), pltpu.SemaphoreType.DMA]
        slots += 4 * n_seq
    head_block = jax.ShapeDtypeStruct((rows, heads, length, HEAD), BF)
    stats = jax.ShapeDtypeStruct((2 * rows * steps, STEP), F32)
    outs = [
        jax.ShapeDtypeStruct((col, dim), BF),
        jax.ShapeDtypeStruct((col, three), F32),
        head_block,
        head_block,
        head_block,
        jax.ShapeDtypeStruct((rows, length, wide), BF),
        stats,
        jax.ShapeDtypeStruct((own, dim) if side is None else (8, HEAD), BF),
    ]
    return comm_call(
        kernel,
        outs + side_out,
        [pltpu.VMEM(stats.shape, F32), pltpu.VMEM((n_seq - 1,) + stats.shape, F32)]
        + SeqScatter.scratch(rows, n_seq, block)
        + side_scratch,
        slots,
        2,
        "attend_forward",
        [vmem] * 7 + ([ANY] + [vmem] * 3 if side_in else []),
        [vmem] * 8 + ([ANY] + [vmem] * 4 if side_in else []),
    )(x_col, w_qkv, usable, w_o, gains, cos_wide, sin_wide, *side_in)


def attend_backward(
    grad_o, q, k, v, mixed, qkv, stats, hidden, usable, w_o, w_qkv, gains, cos_wide, sin_wide,
    n_seq, n_bat, side=None,
):
    rows, heads, length, _ = q.shape
    own, dim = grad_o.shape
    span = own // rows
    col, three = qkv.shape
    wide = three // 3
    steps = length // STEP
    chunk = min(256, length)
    scale = HEAD ** (-0.5)
    group = n_bat * own

    def kernel(*refs):
        (go_ref, q_ref, k_ref, v_ref, mix_ref, qkv_ref, stat_ref, hid_ref, use_ref, wo_ref,
         w_ref, gains_ref, cos_ref, sin_ref) = refs[:14]
        refs = refs[14:]
        if side:
            weighted_ref, down_ref, own_ref, res_ref, small_in = refs[:5]
            refs = refs[5:]
        gwo_ref, gw_ref, gain_ref, out_ref = refs[:4]
        refs = refs[4:]
        if side:
            mixture_ref, small_ref = refs[:2]
            mix_away, mix_twin, mix_halves, mix_full = refs[-6:-2]
            refs = refs[2:-6] + refs[-2:]
        go_all, gm, dq, dk, dv, dqkv, local, got, hid_buf, hid_sems = refs[:10]
        full, twin, line, send_sems, recv_sems = refs[10:]
        place = Place(n_seq, n_bat)
        place.greet(all_seq=True, batch=bool(side))
        wire = Wire(send_sems, recv_sems)
        gathers = [
            SeqGather(place, wire, go_ref.at[pl.ds(r * span, span)], go_all.at[r])
            for r in range(rows)
        ]
        for gather in gathers:
            gather.start()
        for r in range(rows):
            go_all[r, place.s] = go_ref[r * span : (r + 1) * span, :]
        order = list(range(1, place.half)) + [0]
        works, from_twin = {}, {}

        def mixture_of(i):
            at = pl.ds(pl.multiple_of(i * group, group), group)
            return dot(weighted_ref[at, :], down_ref[...])

        todo = [(gather, m) for gather in gathers for m in range(1, place.half)]

        def forward(count):
            for _ in range(min(count, len(todo))):
                gather, m = todo.pop(0)
                gather.step(m)

        if side:

            def send_mixture(n):
                j = order[n]
                if n >= 2:
                    wire.settle(from_twin[order[n - 2]])
                mix_away[n % 2] = (
                    mixture_of(place.twin_at(2 * j)).astype(BF).reshape(n_bat, own, dim)
                )

            def push_mixture(n):
                j = order[n]
                from_twin[j] = wire.push(mix_away.at[n % 2], mix_twin.at[j], place.twin())

            waiting = None
            send_mixture(0)
            push_mixture(0)
            for n, j in enumerate(order):
                if n + 1 < len(order):
                    send_mixture(n + 1)
                total = mixture_of(place.seq_at(2 * j))
                if n + 1 < len(order):
                    push_mixture(n + 1)
                from_twin[j].wait_recv()
                mix_twin[j] = (
                    (total + mix_twin[j].reshape(group, dim).astype(F32))
                    .astype(BF)
                    .reshape(n_bat, own, dim)
                )
                works[j] = AcrossSum(
                    place, wire, mix_twin.at[j], mix_halves.at[j], mix_full.at[j]
                )
                if waiting is not None:
                    works[waiting].start()
                waiting = j
                forward(1)
            works[waiting].start()
        forward(max(0, len(todo) - (rows - 1) * (place.half - 1)))
        columns = lax.rsqrt(stat_ref[...] / dim + EPS).T
        scatters = [
            SeqScatter(place, wire, full.at[r], twin.at[r], line.at[r]) for r in range(rows)
        ]
        gain_sums = [[jnp.zeros((1, HEAD), F32) for _ in range(heads)] for _ in range(2)]
        middles = [works[j] for j in works]

        def attend(r, c, h):
            keys = (c + 1) * chunk
            now = slice(c * chunk, keys)
            allowed = allowed_block(use_ref[r : r + 1, :keys], c * chunk, chunk, keys)
            lanes = slice(h * HEAD, (h + 1) * HEAD)
            query = q_ref[r, h, now, :]
            key = k_ref[r, h, :keys, :]
            scores = jnp.where(allowed, dot_t(query, key) * scale, NEGATIVE)
            raised = jnp.exp(scores - jnp.max(scores, axis=-1, keepdims=True))
            probs = raised / jnp.sum(raised, axis=-1, keepdims=True)
            low = probs.astype(BF)
            grad_mix = gm[r, now, lanes]
            grad_probs = dot_t(grad_mix, v_ref[r, h, :keys, :])
            row_dot = jnp.sum(low.astype(F32) * grad_probs, axis=-1, keepdims=True)
            grad_scores = (probs * (grad_probs - row_dot)).astype(BF)
            dq[now, lanes] = scale * dot(grad_scores, key)
            dk[:keys, lanes] += scale * t_dot(grad_scores, query)
            dv[:keys, lanes] += t_dot(low, grad_mix)

        def take(r):
            gathers[r].finish()
            gm[r] = dot_t(go_all[r].reshape(length, dim), wo_ref[...]).astype(BF)

        take(0)
        for r in range(rows):
            if r:
                scatters[r - 1].pass_on(0, 1)
            dk[...] = jnp.zeros_like(dk)
            dv[...] = jnp.zeros_like(dv)
            for h in range(heads):
                for c in range(length // chunk):
                    attend(r, c, h)
                    forward(1)
                    if middles:
                        middles.pop(0).middle()
            if r == 0:
                forward(len(todo))
                while middles:
                    middles.pop(0).middle()
            for which, grads in ((0, dq), (1, dk)):
                for c in range(steps):
                    inside = slice(c * STEP, (c + 1) * STEP)
                    at = slice(r * length + c * STEP, r * length + (c + 1) * STEP)
                    row = (r * 2 + which) * steps + c
                    factor = columns[:, row : row + 1]
                    products = None
                    for h in range(heads):
                        lanes = slice(h * HEAD, (h + 1) * HEAD)
                        flat = qkv_ref[at, which * wide + h * HEAD : which * wide + (h + 1) * HEAD]
                        flat = flat * factor
                        back = turn(grads[inside, lanes], cos_ref[inside, :], -sin_ref[inside, :])
                        gain_sums[which][h] = gain_sums[which][h] + jnp.sum(
                            back * flat, axis=0, keepdims=True
                        )
                        weighted = back * head_gain(place, gains_ref, which, wide, h)
                        grads[inside, lanes] = weighted
                        product = weighted * flat
                        products = product if products is None else products + product
                    row = which * steps + c
                    local[r, row : row + 1, :] = lane_sums(products)
            exchange = Exchange(place, wire, local.at[r], got.at[r])
            if r:
                scatters[r - 1].pass_on(1)
            dqkv[r, :, 2 * wide :] = dv[...].astype(BF)
            if r + 1 < rows:
                take(r + 1)
            means = (exchange.total() / dim).T
            for which, grads in ((0, dq), (1, dk)):
                lanes = slice(which * wide, (which + 1) * wide)
                for c in range(steps):
                    inside = slice(c * STEP, (c + 1) * STEP)
                    at = slice(r * length + c * STEP, r * length + (c + 1) * STEP)
                    row = (r * 2 + which) * steps + c
                    factor = columns[:, row : row + 1]
                    mean = means[:, which * steps + c : which * steps + c + 1]
                    flat = qkv_ref[at, lanes] * factor
                    dqkv[r, inside, lanes] = (factor * (grads[inside, :] - flat * mean)).astype(BF)
            full[r] = dot_t(dqkv[r], w_ref[...]).astype(BF).reshape(n_seq, span, dim)
            scatters[r].start()
        for which in range(2):
            for h in range(heads):
                gain_ref[which : which + 1, h * HEAD : (h + 1) * HEAD] = gain_sums[which][h]

        def hidden_load(part):
            slot = lax.rem(part, 2)
            at = pl.ds(pl.multiple_of(part * 256, 256), 256)
            return pltpu.make_async_copy(
                hid_ref.at[:, at], hid_buf.at[slot], hid_sems.at[slot]
            )

        hidden_load(0).start()
        scatters[-1].pass_on()

        def weight_part(part, carry):
            at = pl.ds(pl.multiple_of(part * 256, 256), 256)

            @pl.when(part + 1 < dim // 256)
            def _():
                hidden_load(part + 1).start()

            hidden_load(part).wait()
            held = hid_buf[lax.rem(part, 2)]
            gw_ref[at, :] = t_dot(held, dqkv[...].reshape(col, three)).astype(BF)
            total = t_dot(mix_ref[0], go_all[0, :, :, at].reshape(length, 256))
            for r in range(1, rows):
                total = total + t_dot(mix_ref[r], go_all[r, :, :, at].reshape(length, 256))
            gwo_ref[:, at] = total.astype(BF)
            return carry

        lax.fori_loop(0, dim // 256, weight_part, 0)
        for j in works:
            works[j].finish()
            mixture_ref[j] = mix_twin[j, place.b]
        sums = jnp.zeros((1, dim), F32)
        for r in range(rows):
            at = slice(r * span, (r + 1) * span)
            if not side:
                scatters[r].finish(out_ref, at)
                continue
            x = own_ref[at, :].astype(F32)
            grad, terms = rms_back(x, rms_scale(x), gains_ref[0:1, :], scatters[r].total())
            sums = sums + jnp.sum(terms, axis=0, keepdims=True)
            out_ref[at, :] = (res_ref[at, :] + grad).astype(BF)
        if side:
            small_ref[...] = small_in[...]
            small_ref[8:9, :] = sums
            lanes = pl.ds(pl.multiple_of(place.s * wide, wide), wide)
            for which in range(2):
                small_ref[9 + which : 10 + which, lanes] = gain_ref[which : which + 1, :]
        wire.drain()

    vmem = pl.BlockSpec(memory_space=pltpu.VMEM)
    block = jax.ShapeDtypeStruct((span, dim), BF)
    stat_shape = (2 * steps, STEP)
    side_out, side_scratch = [], []
    if side:
        half = n_seq // 2
        side_out = [
            jax.ShapeDtypeStruct((half, own, dim), BF),
            jax.ShapeDtypeStruct((16, dim), F32),
        ]
        side_scratch = [
            pltpu.VMEM((2, n_bat, own, dim), BF),
            pltpu.VMEM((half, n_bat, own, dim), BF),
            pltpu.VMEM((half, 2, own // 2, dim), BF),
            pltpu.VMEM((half, 2, own, dim), BF),
        ]
    return comm_call(
        kernel,
        [
            jax.ShapeDtypeStruct((wide, dim), BF),
            jax.ShapeDtypeStruct((dim, three), BF),
            jax.ShapeDtypeStruct((2, wide), F32),
            jax.ShapeDtypeStruct((own, dim), BF),
        ]
        + side_out,
        [
            pltpu.VMEM((rows, n_seq, span, dim), BF),
            pltpu.VMEM((rows, length, wide), BF),
            pltpu.VMEM((length, wide), F32),
            pltpu.VMEM((length, wide), F32),
            pltpu.VMEM((length, wide), F32),
            pltpu.VMEM((rows, length, three), BF),
            pltpu.VMEM((rows,) + stat_shape, F32),
            pltpu.VMEM((rows, n_seq - 1) + stat_shape, F32),
            pltpu.VMEM((2, col, 256), BF),
            pltpu.SemaphoreType.DMA((2,)),
        ]
        + SeqScatter.scratch(rows, n_seq, block)
        + side_scratch,
        5 * rows * n_seq + (3 * n_seq if side else 0),
        6,
        "attend_backward",
        [vmem] * 7 + [ANY] + [vmem] * (6 + len(side or ())),
        [vmem] * (4 + len(side_out)),
    )(grad_o, q, k, v, mixed, qkv, stats, hidden, usable, w_o, w_qkv, gains, cos_wide, sin_wide,
      *(side or ()))


class Across:
    def __init__(self, place, wire, src, at):
        self.place, self.wire, self.src, self.at = place, wire, src, at
        self.half = src.shape[0] // 2

    def start(self):
        place, own = self.place, self.at(self.place.b)
        self.to_x = self.wire.push(self.src, own, place.x_peer())
        self.to_y = self.wire.push(self.src, own, place.y_peer())

    def relay(self):
        place, half = self.place, self.half
        self.to_x.wait_recv()
        top = self.at(place.bat_x).at[pl.ds(0, half)]
        self.top = self.wire.push(top, top, place.y_peer())
        self.to_y.wait_recv()
        low = self.at(place.bat_y).at[pl.ds(half, half)]
        self.low = self.wire.push(low, low, place.x_peer())

    def finish(self):
        self.top.wait_recv()
        self.low.wait_recv()


class AcrossSum:
    def __init__(self, place, wire, group, halves, full):
        self.place, self.wire = place, wire
        self.group, self.halves, self.full = group, halves, full
        self.half = halves.shape[1]

    def start(self):
        place, half = self.place, self.half
        far = self.group.at[place.bat_d]
        self.top = self.wire.push(far.at[pl.ds(0, half)], self.halves.at[0], place.x_peer())
        self.low = self.wire.push(far.at[pl.ds(half, half)], self.halves.at[1], place.y_peer())

    def middle(self):
        place, half = self.place, self.half
        self.top.wait_recv()
        add_into(self.group.at[place.bat_y].at[pl.ds(0, half)], self.halves.at[0])
        self.low.wait_recv()
        add_into(self.group.at[place.bat_x].at[pl.ds(half, half)], self.halves.at[1])
        self.y = self.wire.push(self.group.at[place.bat_y], self.full.at[0], place.y_peer())
        self.x = self.wire.push(self.group.at[place.bat_x], self.full.at[1], place.x_peer())

    def finish(self):
        self.y.wait_recv()
        self.x.wait_recv()
        add_into(self.group.at[self.place.b], self.full.at[0], self.full.at[1])


def load_first(weights, w_out, mine, flags, small, rows, n_seq, n_bat):
    shard, dim = weights[0].shape
    wide = dim // n_seq
    own = mine.shape[0]
    span = own // rows
    slots = 15 * n_seq + n_seq * n_bat

    def kernel(*refs):
        parts = refs[:3]
        wo_ref, x_ref, flag_ref, small_ref = refs[3:7]
        w_ref, wo_all, x_col, router_ref, gains_ref, use_ref = refs[7:13]
        buffers = refs[13:16]
        own_sems, cut_sems, x_sems, small_all, flag_col, send_sems, recv_sems = refs[16:]
        place = Place(n_seq, n_bat)
        place.greet(all_seq=True)
        wire = Wire(send_sems, recv_sems)
        small_work = FullGather(place, wire, small_ref, small_all)
        flag_work = SeqGather(place, wire, flag_ref, flag_col)
        x_works = [
            SeqGather(place, wire, x_ref.at[pl.ds(r * span, span)], x_col.at[r])
            for r in range(rows)
        ]
        small_work.start()
        flag_work.start()

        def cut(k):
            return pl.ds(pl.multiple_of(place.seq_at(k) * wide, wide), wide)

        def columns(m):
            return pl.ds(m * wide, wide)

        own_cuts = []
        for m in range(3):
            copy = pltpu.make_async_copy(
                parts[m].at[:, cut(0)], buffers[0].at[:, columns(m)], cut_sems.at[m]
            )
            copy.start()
            own_cuts.append(copy)
        cuts = {}
        for k in range(1, n_seq):
            for m in range(3):
                cuts[k, m] = wire.push(
                    parts[m].at[:, cut(k)],
                    w_ref.at[place.s, place.b, :, columns(m)],
                    place.seq_peer(k),
                )
        wo_work = Across(place, wire, wo_ref, lambda i: wo_all.at[i])
        wo_work.start()
        for work in x_works:
            work.start()
        for copy in own_cuts:
            copy.wait()
        spreads = []

        def spread(src, from_seq):
            work = Across(place, wire, src, lambda i: w_ref.at[from_seq, i])
            work.start()
            spreads.append(work)

        spread(buffers[0], place.s)
        own_w = pltpu.make_async_copy(buffers[0], w_ref.at[place.s, place.b], own_sems.at[0])
        own_w.start()
        copies = [own_w]
        fetched = pltpu.make_async_copy(x_ref, buffers[2], own_sems.at[2])
        fetched.start()
        fetched.wait()
        for r in range(rows):
            copy = pltpu.make_async_copy(
                buffers[2].at[pl.ds(r * span, span)], x_col.at[r, place.s], x_sems.at[r]
            )
            copy.start()
            copies.append(copy)
        copies.append(keep_own(wo_ref, wo_all.at[place.b], buffers[1], own_sems.at[1]))
        flag_col[place.s] = flag_ref[...]
        small_all[place.s, place.b] = small_ref[...]
        for j in range(1, place.half):
            small_work.step(j)
            flag_work.step(j)
        for k in range(1, n_seq):
            for m in range(3):
                cuts[k, m].wait_recv()
            spread(w_ref.at[place.seq_at(-k), place.b], place.seq_at(-k))
        for j in range(place.half):
            small_work.collect(j)
        todo = [(work, m) for work in x_works for m in range(1, place.half)]

        def forward(count):
            for _ in range(min(count, len(todo))):
                work, m = todo.pop(0)
                work.step(m)

        forward(1)
        wo_work.relay()
        for work in spreads:
            work.relay()
            forward(1)
        forward(len(todo))
        wo_work.finish()
        for work in spreads:
            work.finish()
        for work in [small_work, flag_work] + x_works:
            work.finish()
        left = lax.broadcasted_iota(jnp.int32, (8, 128), 1) < 64
        for i in range(n_seq):
            for k in range(0, n_bat, 2):
                one, two = small_all[i, k], small_all[i, k + 1]
                at = slice((i * n_bat + k) * 64, (i * n_bat + k + 2) * 64)
                router_ref[:, at] = jnp.where(left, one, pltpu.roll(two, 64, axis=1))
                gains_ref[:, at] = jnp.where(left, pltpu.roll(one, 64, axis=1), two)
        for i in range(0, n_seq, 2):
            one, two = flag_col[i], flag_col[i + 1]
            use_ref[:, i * 64 : (i + 2) * 64] = jnp.where(left, one, pltpu.roll(two, 64, axis=1))
        for copy in copies:
            copy.wait()
        wire.drain()

    one = jax.ShapeDtypeStruct((shard, 3 * wide), BF)
    x_one = jax.ShapeDtypeStruct((span, dim), BF)
    held = (one, w_out, mine)
    vmem = pl.BlockSpec(memory_space=pltpu.VMEM)
    return comm_call(
        kernel,
        [
            shape_of((n_seq, n_bat), one),
            shape_of((n_bat,), w_out),
            shape_of((rows, n_seq), x_one),
            jax.ShapeDtypeStruct((8, dim), F32),
            jax.ShapeDtypeStruct((8, dim), F32),
            jax.ShapeDtypeStruct((8, n_seq * span), F32),
        ],
        [pltpu.VMEM(block.shape, block.dtype) for block in held]
        + [pltpu.SemaphoreType.DMA((n,)) for n in (3, 3, rows)]
        + [pltpu.VMEM((n_seq, n_bat, 8, 128), F32), pltpu.VMEM((n_seq, 8, 128), F32)],
        slots,
        1,
        "load_first",
        [ANY] * 5 + [vmem] * 2,
        [ANY] * 3 + [vmem] * 3,
    )(*weights, w_out, mine, flags, small)


def pick_units(first, experts, units, part):
    at_expert = lax.broadcasted_iota(jnp.int32, (experts, units), 0)
    at_unit = lax.broadcasted_iota(jnp.int32, (experts, units), 1)
    low = (at_expert - first) * part
    return jnp.where((at_unit >= low) & (at_unit < low + part), 1.0, 0.0).astype(BF)


def experts_forward(normed, gates, dy_all, gate, up, w_down, n_seq, n_bat):
    own, dim = normed.shape
    local_experts, depth, hidden = gate.shape
    units = w_down.shape[0]
    part = hidden // n_seq
    group = n_bat * own
    tokens = n_seq * group
    experts = gates.shape[0]
    slots = 64 + 2 * n_seq * n_bat + 2 * local_experts * n_seq

    def kernel(*refs):
        x_ref, gate_ref, dy_ref, wg_ref, wu_ref, down_ref = refs[:6]
        x_all, weighted_ref, grad_ref, term_ref, gu_ref = refs[6:11]
        gates_all, back, gate_buf, x_buf, dy_buf, keep = refs[11:17]
        own_sems, x_sems, dy_sems, gu_sems, send_sems, recv_sems = refs[17:]
        place = Place(n_seq, n_bat)
        place.greet(all_seq=True)
        wire = Wire(send_sems, recv_sems)
        gate_work = FullGather(place, wire, gate_ref, gates_all)
        gate_work.start()
        gates_all[place.s, place.b] = gate_ref[...]
        line = Line(place, wire, x_ref, lambda i: x_all.at[place.chip(i), place.b])
        line.start()
        works = []
        here = [place.chip(place.origin(m)) for m in range(place.half)]
        there = [place.chip_twin(place.origin(m)) for m in range(place.half)]
        for j in range(place.half):
            at_seq = here[j]
            src = x_ref if j == 0 else x_all.at[at_seq, place.b]
            works.append(
                Across(place, wire, src, lambda i, at_seq=at_seq: x_all.at[at_seq, i])
            )
        works[0].start()
        own = keep_own(x_ref, x_all.at[place.s, place.b], keep, own_sems.at[0])
        selected = pick_units(place.b * local_experts, experts, units, part)
        selected_twice = jnp.concatenate([selected, selected], axis=0)

        def dy_load(g, slot):
            return pltpu.make_async_copy(dy_ref.at[g], dy_buf.at[slot], dy_sems.at[slot])

        def rows_of(g):
            return pl.ds(pl.multiple_of(g * group, group), group)

        def backs(first, count):
            dy_load(first, first % 2).start()
            for g in range(first, first + count):
                if g + 1 < first + count:
                    dy_load(g + 1, (g + 1) % 2).start()
                dy_load(g, g % 2).wait()
                block = dy_buf[g % 2].reshape(group, dim)
                back[g * group : (g + 1) * group, :] = dot_t(block, down_ref[...])

        gu_copies = ([], [])

        def send_units(m, ref, offsets):
            for k in offsets:
                lanes = pl.ds(pl.multiple_of(place.seq_at(k) * part, part), part)
                for e in range(local_experts):
                    src = ref.at[e, :, lanes]
                    dst = gu_ref.at[place.s, :, pl.ds(m * units + e * part, part)]
                    if k:
                        gu_copies[m].append(wire.push(src, dst, place.seq_peer(k)).wait_recv)
                    else:
                        copy = pltpu.make_async_copy(src, dst, gu_sems.at[m, e])
                        copy.start()
                        gu_copies[m].append(copy.wait)

        passed = []

        def hand_over(j):
            at_seq = here[j]
            works[j].finish()
            if j == 0:
                own.wait()
            passed.append(wire.push(x_all.at[at_seq], x_all.at[at_seq], place.twin()))

        loads = {}

        def fetch(g, slot):
            loads[slot] = pltpu.make_async_copy(x_all.at[g], x_buf.at[slot], x_sems.at[slot])
            loads[slot].start()

        def weight(m):
            return gu_ref[:, :, m * units : (m + 1) * units].reshape(dim, units)

        def gate_on(g, slot):
            loads[slot].wait()
            gate_buf[rows_of(g), :] = dot(x_buf[slot].reshape(group, dim), weight(0))

        def units_on(g, slot, gated=False):
            if not gated:
                loads[slot].wait()
            at = rows_of(g)
            block = x_buf[slot].reshape(group, dim)
            gate_pre = gate_buf[at, :] if gated else dot(block, weight(0))
            up_pre = dot(block, weight(1))
            sig = jax.nn.sigmoid(gate_pre)
            silu = gate_pre * sig
            active = (silu * up_pre).astype(BF).astype(F32)
            grad_back = back[at, :]
            product = active * grad_back
            wide_gates = []
            for i in range(n_bat):
                inside = slice(i * x_ref.shape[0], (i + 1) * x_ref.shape[0])
                gates_two = jnp.concatenate(in_two(gates_all[g, i]), axis=0)
                wide_gates.append(t_dot(gates_two, selected_twice))
                high, low = in_two(product[inside, :])
                term_ref[g, i] = dot_t(selected, high) + dot_t(selected, low)
            wide_gate = jnp.concatenate(wide_gates, axis=0)
            weighted_ref[at, :] = (active * wide_gate).astype(BF)
            grad_active = grad_back * wide_gate
            grad_ref[at, :units] = (
                grad_active * up_pre * sig * (1.0 + gate_pre * (1.0 - sig))
            ).astype(BF)
            grad_ref[at, units:] = (grad_active * silu).astype(BF)

        half = place.half
        per = n_seq // half
        offsets = list(range(1, n_seq)) + [0]
        for j in range(1, half):
            backs((j - 1) * per, per)
            gate_work.step(j)
            gate_work.collect(j - 1)
            line.step(j)
            works[j].start()
            works[j - 1].relay()
            if j < half - 1:
                send_units(0, wg_ref, offsets[2 * j - 2 : 2 * j])
            else:
                send_units(0, wg_ref, offsets[2 * j - 2 :])
                send_units(1, wu_ref, offsets)
        backs((half - 1) * per, per)
        gate_work.collect(half - 1)
        gate_work.finish()
        hand_over(0)
        fetch(here[0], 0)
        for wait in gu_copies[0]:
            wait()
        gate_on(here[0], 0)
        passed[0].wait_recv()
        fetch(there[0], 1)
        hand_over(1)
        fetch(here[1], 2)
        gate_on(there[0], 1)
        gate_on(here[1], 2)
        works[half - 1].relay()
        passed[1].wait_recv()
        fetch(there[1], 3)
        gate_on(there[1], 3)
        for wait in gu_copies[1]:
            wait()
        for j in range(half):
            units_on(here[j], (2 * j) % 4, j < 2)
            if j + 2 < half:
                hand_over(j + 2)
                fetch(here[j + 2], (2 * j) % 4)
            units_on(there[j], (2 * j + 1) % 4, j < 2)
            if j + 2 < half:
                passed[j + 2].wait_recv()
                fetch(there[j + 2], (2 * j + 1) % 4)
        wire.drain()

    vmem = pl.BlockSpec(memory_space=pltpu.VMEM)
    return comm_call(
        kernel,
        [
            shape_of((n_seq, n_bat), normed),
            jax.ShapeDtypeStruct((tokens, units), BF),
            jax.ShapeDtypeStruct((tokens, 2 * units), BF),
            shape_of((n_seq, n_bat), gates),
            jax.ShapeDtypeStruct((n_seq, depth, 2 * units), BF),
        ],
        [
            pltpu.VMEM((n_seq, n_bat) + gates.shape, F32),
            pltpu.VMEM((tokens, units), F32),
            pltpu.VMEM((tokens, units), F32),
            pltpu.VMEM((4, n_bat, own, dim), BF),
            pltpu.VMEM((2, n_bat, own, dim), BF),
            pltpu.VMEM((own, dim), BF),
            pltpu.SemaphoreType.DMA((1,)),
            pltpu.SemaphoreType.DMA((4,)),
            pltpu.SemaphoreType.DMA((2,)),
            pltpu.SemaphoreType.DMA((2, local_experts)),
        ],
        slots,
        4,
        "experts_forward",
        [ANY, vmem, ANY, ANY, ANY, vmem],
        [ANY, vmem, vmem, vmem, vmem],
    )(normed, gates, dy_all, gate, up, w_down)


def experts_backward(
    grad_pre, weighted, w_gu, terms, x_all, dy_all, residual, dy_own, gains, router, probs, chosen,
    local_experts, n_seq, n_bat,
):
    own = residual.shape[0]
    tokens, dim = x_all.shape
    units = weighted.shape[1]
    part = units // local_experts
    group = n_bat * own
    depth = dim // n_seq
    hidden = n_seq * part
    half = n_seq // 2
    slots = 128 + 2 * n_seq * n_bat
    block = jax.ShapeDtypeStruct((own, dim), BF)
    term = jax.ShapeDtypeStruct(terms.shape[2:], F32)

    def kernel(*refs):
        grad_ref, weighted_ref, gu_ref, term_in, x_ref, dy_ref = refs[:6]
        res_ref, own_dy_ref, gains_ref, router_ref, probs_ref, chosen_ref = refs[6:12]
        out_ref, low_ref, small_ref, gate_out, up_out, down_out = refs[12:18]
        refs = refs[18:]
        away, twin, halves, full, line = refs[:5]
        columns, sent, got, column_sems, term_out = refs[5:10]
        term_scratch = refs[10:15]
        send_sems, recv_sems = refs[15:]
        place = Place(n_seq, n_bat)
        place.greet(all_seq=True)
        wire = Wire(send_sems, recv_sems)
        term_work = FullScatter(place, wire, term_in, term_out, *term_scratch)
        term_work.start()

        def product(i):
            at = pl.ds(pl.multiple_of(i * group, group), group)
            return dot_t(grad_ref[at, :], gu_ref[...])

        order = list(range(1, half)) + [0]
        from_twin, from_seq, works = {}, {}, {}

        def send(j):
            from_twin[j] = wire.push(away.at[j], twin.at[j], place.twin())

        chunks = list(range(1, n_seq)) + [0]

        def chunk_load(n):
            at = pl.ds(pl.multiple_of(place.seq_at(chunks[n]) * depth, depth), depth)
            return pltpu.make_async_copy(x_ref.at[:, at], columns.at[n % 2], column_sems.at[n % 2])

        def down_load(k):
            slot = lax.rem(k, 2)
            at = pl.ds(pl.multiple_of(k * 256, 256), 256)
            return pltpu.make_async_copy(dy_ref.at[:, at], columns.at[slot], column_sems.at[slot])

        def down_part(first, last):
            down_load(first).start()

            def one(k, carry):
                @pl.when(k + 1 < last)
                def _():
                    down_load(k + 1).start()

                down_load(k).wait()
                at = pl.ds(pl.multiple_of(k * 256, 256), 256)
                down_out[:, at] = t_dot(weighted_ref[...], columns[lax.rem(k, 2)])
                return carry

            lax.fori_loop(first, last, one, 0)

        chunk_load(0).start()

        def pair(j):
            part_sum = product(place.seq_at(2 * j))
            from_twin[j].wait_recv()
            twin[j] = (
                (part_sum + twin[j].reshape(group, dim).astype(F32))
                .astype(BF)
                .reshape(n_bat, own, dim)
            )
            works[j] = AcrossSum(place, wire, twin.at[j], halves.at[j], full.at[j])

        arrivals = []
        done = [0]

        def work_chunks(count):
            for n in range(done[0], min(done[0] + count, len(chunks))):
                done[0] = n + 1
                k = chunks[n]
                if n + 1 < len(chunks):
                    chunk_load(n + 1).start()
                chunk_load(n).wait()
                if n:
                    last = chunks[n - 1]
                    arrivals.append(
                        wire.push(sent.at[last], got.at[place.s], place.seq_peer(last))
                    )
                value = t_dot(columns[n % 2], grad_ref[...]).astype(BF)
                if k == 0:
                    got[place.s] = value
                else:
                    sent[k] = value

        def pass_on(j):
            works[j].finish()
            if j:
                from_seq[j] = wire.push(twin.at[j, place.b], line.at[j], place.seq_peer(2 * j))

        work_chunks(1)
        waiting = None
        for j in order:
            away[j] = product(place.twin_at(2 * j)).astype(BF).reshape(n_bat, own, dim)
            if waiting is not None:
                send(waiting)
            waiting = j
            work_chunks(1)
        first, rest = order[:2], order[2:]
        pair(order[0])
        send(waiting)
        for j in first[1:]:
            pair(j)
            works[first[0]].start()
        works[first[-1]].start()
        for j in rest:
            pair(j)
        term_order = term_work.order()
        for j in term_order:
            term_work.pair(j)
        works[first[0]].middle()
        work_chunks(1)
        for j in first[1:]:
            works[j].middle()
        for j in rest:
            works[j].start()
        for j in first:
            work_chunks(3)
            pass_on(j)
        work_chunks(len(chunks))
        for j in term_order:
            term_work.merge(j)
        for j in rest:
            works[j].middle()
        cut = dim // 512
        down_part(0, cut)
        pass_on(rest[0])
        down_part(cut, 2 * cut)
        for j in rest[1:]:
            pass_on(j)
        for copy in arrivals:
            copy.wait_recv()
        for i in range(n_seq):
            lanes = slice(i * part, (i + 1) * part)
            for e in range(local_experts):
                gate_out[e, :, lanes] = got[i, :, e * part : (e + 1) * part].astype(F32)
                up_out[e, :, lanes] = got[i, :, units + e * part : units + (e + 1) * part].astype(
                    F32
                )
        term_work.finish()
        for j in range(1, half):
            from_seq[j].wait_recv()
        total = twin[0, place.b].astype(F32)
        for j in range(1, half):
            total = total + line[j].astype(F32)
        grad_chosen = term_out[...] * chosen_ref[...]
        probs = probs_ref[...]
        grad_logits = probs * (
            grad_chosen - jnp.sum(probs * grad_chosen, axis=0, keepdims=True)
        )
        small_ref[...] = jnp.zeros_like(small_ref)
        residual = res_ref[...]
        scale = rms_scale(residual)
        normal = residual * scale
        normed = (normal * gains_ref[3:4, :]).astype(BF)
        experts = probs.shape[0]
        logits_two = jnp.concatenate(in_two(grad_logits), axis=0)
        products = dot(logits_two, normed)
        small_ref[0:experts, :] = products[:experts] + products[experts:]
        router = router_ref[...].astype(BF)
        total = total + t_dot(logits_two, jnp.concatenate([router, router], axis=0))
        grad, terms_of = rms_back(residual, scale, gains_ref[3:4, :], total)
        small_ref[experts + 3 : experts + 4, :] = jnp.sum(terms_of, axis=0, keepdims=True)
        grad = own_dy_ref[...].astype(F32) + grad
        out_ref[...] = grad
        low_ref[...] = grad.astype(BF)
        wire.drain()

    vmem = pl.BlockSpec(memory_space=pltpu.VMEM)
    expert = jax.ShapeDtypeStruct((local_experts, depth, hidden), F32)
    return comm_call(
        kernel,
        [
            jax.ShapeDtypeStruct((own, dim), F32),
            jax.ShapeDtypeStruct((own, dim), BF),
            jax.ShapeDtypeStruct((16, dim), F32),
            expert,
            expert,
            jax.ShapeDtypeStruct((units, dim), F32),
        ],
        [
            pltpu.VMEM((half, n_bat, own, dim), BF),
            pltpu.VMEM((half, n_bat, own, dim), BF),
            pltpu.VMEM((half, 2, own // 2, dim), BF),
            pltpu.VMEM((half, 2, own, dim), BF),
            pltpu.VMEM((half, own, dim), BF),
            pltpu.VMEM((2, tokens, 256), BF),
            pltpu.VMEM((n_seq, depth, 2 * units), BF),
            pltpu.VMEM((n_seq, depth, 2 * units), BF),
            pltpu.SemaphoreType.DMA((2,)),
            pltpu.VMEM(term.shape, F32),
        ]
        + FullScatter.scratch(n_seq, n_bat, term),
        slots,
        5,
        "experts_backward",
        [vmem] * 3 + [ANY] * 3 + [vmem] * 6,
        [vmem] * 6,
    )(grad_pre, weighted, w_gu, terms, x_all, dy_all, residual, dy_own, gains, router, probs, chosen)


def store_last(grad_w, grad_wo, small, mixture, n_seq, n_bat):
    one = jax.ShapeDtypeStruct(grad_w.shape[2:], grad_w.dtype)
    shard, three = one.shape
    wide = three // 3
    wo_one = jax.ShapeDtypeStruct(grad_wo.shape[1:], grad_wo.dtype)
    small_one = jax.ShapeDtypeStruct((16, 2 * shard), small.dtype)
    half = n_seq // 2
    dim = wo_one.shape[1]
    slots = 64 + n_seq * n_bat + 5 * n_seq

    def kernel(*refs):
        w_ref, wo_ref, small_ref, mix_ref = refs[:4]
        q_out, k_out, v_out, wo_out, small_out, mix_out = refs[4:10]
        w_sum, w_halves, w_full, w_got, wo_sum, wo_halves, wo_full, line = refs[10:18]
        small_scratch = refs[18:23]
        w_sems, wo_sem, send_sems, recv_sems = refs[23:]
        place = Place(n_seq, n_bat)
        place.greet(all_seq=True)
        wire = Wire(send_sems, recv_sems)

        def pick(i, m):
            tile = i * (n_bat // 2) + lax.div(m, 2)
            return small_ref.at[:, pl.ds(pl.multiple_of(tile * 2 * shard, 128), 2 * shard)]

        small_work = FullScatter(place, wire, small_ref, small_out, *small_scratch, pick)
        small_work.start()
        order = list(range(1, n_seq)) + [0]
        loads = {}
        for k in order:
            loads[k] = pltpu.make_async_copy(
                w_ref.at[place.seq_at(k)], w_sum.at[k], w_sems.at[k]
            )
            loads[k].start()
        wo_load = pltpu.make_async_copy(wo_ref, wo_sum, wo_sem.at[0])
        wo_load.start()
        works = {}
        for k in order:
            loads[k].wait()
            works[k] = AcrossSum(place, wire, w_sum.at[k], w_halves.at[k], w_full.at[k])
            works[k].start()
        wo_load.wait()
        wo_work = AcrossSum(place, wire, wo_sum, wo_halves, wo_full)
        wo_work.start()
        term_order = small_work.order()
        for j in term_order:
            small_work.pair(j)
        mix_line = {
            j: wire.push(mix_ref.at[j], line.at[j], place.seq_peer(2 * j)) for j in range(1, half)
        }
        arrivals = []
        ready = None

        def ship(k):
            if k:
                arrivals.append(
                    wire.push(w_sum.at[k, place.b], w_got.at[place.s], place.seq_peer(k))
                )

        for k in order:
            works[k].middle()
        wo_work.middle()
        for j in term_order:
            small_work.merge(j)
        for k in order:
            works[k].finish()
            if ready is not None:
                ship(ready)
            ready = k
        w_got[place.s] = w_sum[0, place.b]
        wo_work.finish()
        wo_out[...] = wo_sum[place.b].astype(F32)
        small_work.finish()
        for copy in arrivals:
            copy.wait_recv()
        for i in range(n_seq):
            at = slice(i * wide, (i + 1) * wide)
            for m, out in enumerate((q_out, k_out, v_out)):
                out[:, at] = w_got[i, :, m * wide : (m + 1) * wide].astype(F32)
        for copy in mix_line.values():
            copy.wait_recv()
        total = mix_ref[0].astype(F32)
        for j in range(1, half):
            total = total + line[j].astype(F32)
        mix_out[...] = total
        wire.drain()

    vmem = pl.BlockSpec(memory_space=pltpu.VMEM)
    matrix = jax.ShapeDtypeStruct((shard, dim), F32)
    return comm_call(
        kernel,
        [matrix] * 4 + [small_one, jax.ShapeDtypeStruct(mixture.shape[1:], F32)],
        [
            pltpu.VMEM((n_seq, n_bat, shard, three), BF),
            pltpu.VMEM((n_seq, 2, shard // 2, three), BF),
            pltpu.VMEM((n_seq, 2, shard, three), BF),
            pltpu.VMEM((n_seq, shard, three), BF),
            pltpu.VMEM((n_bat, shard, dim), BF),
            pltpu.VMEM((2, shard // 2, dim), BF),
            pltpu.VMEM((2, shard, dim), BF),
            pltpu.VMEM(mixture.shape, BF),
        ]
        + FullScatter.scratch(n_seq, n_bat, small_one)
        + [pltpu.SemaphoreType.DMA((n_seq,)), pltpu.SemaphoreType.DMA((1,))],
        slots,
        8,
        "store_last",
        [ANY] * 3 + [vmem],
        [vmem] * 6,
    )(grad_w, grad_wo, small, mixture)


def finish(residual, mixture, grads):
    count = len(grads)
    pieces = []
    for i in sorted(range(count), key=lambda i: -grads[i].size):
        large = grads[i].size >= 1 << 18 and grads[i].ndim == 3
        pieces += [(i, k) for k in range(grads[i].shape[0])] if large else [(i, None)]

    def kernel(*refs):
        res_ref, mix_ref = refs[:2]
        ins, out_ref, outs = refs[2 : 2 + count], refs[2 + count], refs[3 + count : 3 + 2 * count]
        refs = refs[3 + 2 * count :]
        buffers, res_buf, mix_buf, out_buf, sems, own_sems = refs[:count], *refs[count:]

        def piece(group, n):
            i, k = pieces[n]
            return group[i] if k is None else group[i].at[k]

        loads = []
        for n in range(len(pieces)):
            copy = pltpu.make_async_copy(piece(ins, n), piece(buffers, n), sems.at[0, n])
            copy.start()
            loads.append(copy)
            if n == 0:
                first = pltpu.make_async_copy(res_ref, res_buf, own_sems.at[0])
                second = pltpu.make_async_copy(mix_ref, mix_buf, own_sems.at[1])
                first.start()
                second.start()
        stores = []
        for n, load in enumerate(loads):
            load.wait()
            copy = pltpu.make_async_copy(piece(buffers, n), piece(outs, n), sems.at[1, n])
            copy.start()
            stores.append(copy)
            if n == 0:
                first.wait()
                second.wait()
                out_buf[...] = (res_buf[...] + mix_buf[...]).astype(BF)
            if n == 1:
                copy = pltpu.make_async_copy(out_buf, out_ref, own_sems.at[2])
                copy.start()
                stores.append(copy)
        for copy in stores:
            copy.wait()

    return pl.pallas_call(
        kernel,
        out_shape=[jax.ShapeDtypeStruct(residual.shape, BF)]
        + [jax.ShapeDtypeStruct(grad.shape, grad.dtype) for grad in grads],
        in_specs=[ANY] * (2 + count),
        out_specs=[ANY] * (1 + count),
        scratch_shapes=[pltpu.VMEM(grad.shape, grad.dtype) for grad in grads]
        + [
            pltpu.VMEM(residual.shape, F32),
            pltpu.VMEM(residual.shape, F32),
            pltpu.VMEM(residual.shape, BF),
            pltpu.SemaphoreType.DMA((2, len(pieces))),
            pltpu.SemaphoreType.DMA((3,)),
        ],
        compiler_params=pltpu.CompilerParams(vmem_limit_bytes=VMEM_LIMIT),
        name="finish",
    )(residual, mixture, *grads)


def load_inputs(qkv_cut, w_out, mine, flags, small, gu_cut, dy_own, n_seq, n_bat):
    n_in = 7
    slots = 4 * n_seq * n_bat + 5 * n_seq + 2 * n_bat

    def kernel(*refs):
        cut_ref, wo_ref, x_ref, flag_ref, small_ref, gu_ref, dy_ref = refs[:n_in]
        w_ref, wo_all, x_col, flag_col, small_all, gu_all, dy_all = refs[n_in : 2 * n_in]
        buffers = refs[2 * n_in : 3 * n_in]
        own_sems, send_sems, recv_sems = refs[3 * n_in :]
        place = Place(n_seq, n_bat)
        place.greet(all_seq=True)
        wire = Wire(send_sems, recv_sems)
        small_work = FullGather(place, wire, small_ref, small_all)
        flag_work = SeqGather(place, wire, flag_ref, flag_col)
        x_work = SeqGather(place, wire, x_ref, x_col)
        dy_work = FullGather(place, wire, dy_ref, dy_all)
        small_work.start()
        flag_work.start()
        cuts = [
            wire.push(cut_ref.at[place.seq_at(k)], w_ref.at[place.s, place.b], place.seq_peer(k))
            for k in range(1, n_seq)
        ]
        ends = [
            wire.push(wo_ref, wo_all.at[place.b], place.bat_peer(k)) for k in range(1, n_bat)
        ]
        ends += [
            wire.push(cut_ref.at[place.s], w_ref.at[place.s, place.b], place.bat_peer(k))
            for k in range(1, n_bat)
        ]
        x_work.start()
        own = [
            keep_own(src, dst, buffers[i], own_sems.at[i])
            for i, (src, dst) in enumerate(
                (
                    (cut_ref.at[place.s], w_ref.at[place.s, place.b]),
                    (wo_ref, wo_all.at[place.b]),
                    (x_ref, x_col.at[place.s]),
                    (flag_ref, flag_col.at[place.s]),
                    (small_ref, small_all.at[place.s, place.b]),
                    (gu_ref.at[place.s], gu_all.at[place.s]),
                    (dy_ref, dy_all.at[place.s, place.b]),
                )
            )
        ]
        ends += [
            wire.push(gu_ref.at[place.seq_at(k)], gu_all.at[place.s], place.seq_peer(k))
            for k in range(1, n_seq)
        ]
        dy_work.start()
        for j in range(1, place.half):
            small_work.step(j)
            flag_work.step(j)
        for k in range(1, n_seq):
            cuts[k - 1].wait_recv()
            block = w_ref.at[place.seq_at(-k), place.b]
            ends += [wire.push(block, block, place.bat_peer(m)) for m in range(1, n_bat)]
        for j in range(place.half):
            small_work.collect(j)
        for j in range(1, place.half):
            x_work.step(j)
        for j in range(1, place.half):
            dy_work.step(j)
            dy_work.collect(j - 1)
        dy_work.collect(place.half - 1)
        for work in (small_work, flag_work, x_work, dy_work):
            work.finish()
        for copy in ends:
            copy.wait_recv()
        for copy in own:
            copy.wait()
        wire.drain()

    every = (n_seq, n_bat)
    one = jax.ShapeDtypeStruct(qkv_cut.shape[1:], qkv_cut.dtype)
    gu_one = jax.ShapeDtypeStruct(gu_cut.shape[1:], gu_cut.dtype)
    blocks = (one, w_out, mine, flags, small, gu_one, dy_own)
    leads = (every, (n_bat,), (n_seq,), (n_seq,), every, (n_seq,), every)
    return comm_call(
        kernel,
        [shape_of(lead, block) for lead, block in zip(leads, blocks)],
        [pltpu.VMEM(block.shape, block.dtype) for block in blocks]
        + [pltpu.SemaphoreType.DMA((n_in,))],
        slots,
        1,
        "load_inputs",
        [ANY] * n_in,
    )(qkv_cut, w_out, mine, flags, small, gu_cut, dy_own)


def store_grads(grad_w, grad_wo, grad_gu, small, n_seq, n_bat):
    one = jax.ShapeDtypeStruct(grad_w.shape[2:], grad_w.dtype)
    wo_one = jax.ShapeDtypeStruct(grad_wo.shape[1:], grad_wo.dtype)
    gu_one = jax.ShapeDtypeStruct(grad_gu.shape[1:], grad_gu.dtype)
    small_one = jax.ShapeDtypeStruct(small.shape[2:], small.dtype)
    slots = 2 * n_seq * n_bat + 2 * n_seq + n_bat

    def kernel(*refs):
        w_ref, wo_ref, gu_ref, small_ref = refs[:4]
        w_out_ref, wo_out_ref, gu_out_ref, small_out_ref = refs[4:8]
        w_sum, w_got, wo_sum, wo_got, gu_buf, cut_buf = refs[8:14]
        small_scratch = refs[14:19]
        w_sems, sems, send_sems, recv_sems = refs[19:]
        place = Place(n_seq, n_bat)
        place.greet(all_seq=True)
        wire = Wire(send_sems, recv_sems)
        small_work = FullScatter(
            place, wire, small_ref, small_out_ref, *small_scratch
        )
        small_work.start()
        got, loads = {}, {}
        for i in list(range(1, n_seq)) + [0]:
            to_seq = place.seq_at(i)
            for k in range(1, n_bat):
                got[i, k] = wire.push(
                    w_ref.at[to_seq, place.bat_at(k)], w_got.at[i, k - 1], place.bat_peer(k)
                )
            loads[i] = pltpu.make_async_copy(
                w_ref.at[to_seq, place.b], w_sum.at[i], w_sems.at[i]
            )
            loads[i].start()
        wo_pushed = [
            wire.push(wo_ref.at[place.bat_at(k)], wo_got.at[k - 1], place.bat_peer(k))
            for k in range(1, n_bat)
        ]
        wo_load = pltpu.make_async_copy(wo_ref.at[place.b], wo_sum, sems.at[0])
        wo_load.start()
        ends = [
            wire.push(gu_ref.at[place.seq_at(k)], gu_out_ref.at[place.s], place.seq_peer(k))
            for k in range(1, n_seq)
        ]
        gu_own = keep_own(gu_ref.at[place.s], gu_out_ref.at[place.s], gu_buf, sems.at[1])
        order = small_work.order()
        for j in order:
            small_work.pair(j)
        for i in list(range(1, n_seq)) + [0]:
            loads[i].wait()
            for k in range(1, n_bat):
                got[i, k].wait_recv()
            add_into(w_sum.at[i], *[w_got.at[i, k] for k in range(n_bat - 1)])
            if i:
                ends.append(
                    wire.push(w_sum.at[i], w_out_ref.at[place.s], place.seq_peer(i))
                )
        w_own = pltpu.make_async_copy(w_sum.at[0], w_out_ref.at[place.s], sems.at[2])
        w_own.start()
        for j in order:
            small_work.merge(j)
        wo_load.wait()
        for copy in wo_pushed:
            copy.wait_recv()
        add_into(wo_sum, *[wo_got.at[k] for k in range(n_bat - 1)])
        wo_out_ref[...] = wo_sum[...].astype(F32)
        small_work.finish()
        for copy in ends:
            copy.wait_recv()
        gu_own.wait()
        w_own.wait()
        wire.drain()

    vmem = pl.BlockSpec(memory_space=pltpu.VMEM)
    return comm_call(
        kernel,
        [
            shape_of((n_seq,), one),
            jax.ShapeDtypeStruct(wo_one.shape, F32),
            shape_of((n_seq,), gu_one),
            small_one,
        ],
        [
            pltpu.VMEM((n_seq,) + one.shape, one.dtype),
            pltpu.VMEM((n_seq, n_bat - 1) + one.shape, one.dtype),
            pltpu.VMEM(wo_one.shape, wo_one.dtype),
            pltpu.VMEM((n_bat - 1,) + wo_one.shape, wo_one.dtype),
            pltpu.VMEM(gu_one.shape, gu_one.dtype),
            pltpu.VMEM(one.shape, one.dtype),
        ]
        + FullScatter.scratch(n_seq, n_bat, small_one)
        + [pltpu.SemaphoreType.DMA((n_seq,)), pltpu.SemaphoreType.DMA((3,))],
        slots,
        8,
        "store_grads",
        [ANY] * 4,
        [ANY, vmem, ANY, vmem],
    )(grad_w, grad_wo, grad_gu, small)


def shards(
    tokens,
    lengths,
    key_mask,
    top_experts,
    attn_gain,
    query_gain,
    key_gain,
    mlp_gain,
    w_query,
    w_key,
    w_value,
    w_out,
    w_router,
    expert_gate,
    expert_up,
    expert_down,
    cotangent,
):
    n_seq = lax.axis_size("seq")
    n_bat = lax.axis_size("batch")
    seq = lax.axis_index("seq")
    bat = lax.axis_index("batch")
    rows, span, dim = tokens.shape
    own = rows * span
    col = n_seq * own
    length = n_seq * span
    shard = w_query.shape[0]
    wide = dim // n_seq
    heads = wide // HEAD
    local_experts, depth, hidden_units = expert_gate.shape
    part = hidden_units // n_seq
    experts = local_experts * n_bat

    mine = tokens.reshape(own, dim)
    dy_own = cotangent.reshape(own, dim)
    small = jnp.concatenate(
        [w_router.T, jnp.stack([attn_gain, query_gain, key_gain, mlp_gain])], axis=0
    )
    positions_own = seq * span + jnp.arange(span, dtype=jnp.int32)
    flags = pack((positions_own[None, :] < lengths[:, None]) & (key_mask == 1))
    units = local_experts * part
    fused = (
        n_bat == 4
        and part % 128 == 0
        and own == 128
        and shard % 32 == 0
        and n_seq == 8
        and shard == 64
        and experts == 8
        and span == 64
        and rows <= 8
        and n_seq * n_bat * own * dim <= 8 * 1024 * 1024
    )
    if fused:
        gains = jnp.stack([attn_gain, query_gain, key_gain, mlp_gain])
        small = jnp.concatenate([w_router.T, jnp.pad(gains, ((0, 4), (0, 0)))], axis=1).astype(F32)
        flags = (positions_own[None, :] < lengths[:, None]) & (key_mask == 1)
        flags = jnp.pad(flags.astype(F32), ((0, 8 - rows), (0, 128 - span)))
        w_qkv, w_o, x_col, router_t, gains, usable = load_first(
            (w_query, w_key, w_value), w_out, mine, flags, small, rows, n_seq, n_bat
        )
    else:
        qkv_cut = jnp.stack([w_query, w_key, w_value]).reshape(3, shard, n_seq, wide)
        qkv_cut = jnp.transpose(qkv_cut, (2, 1, 0, 3)).reshape(n_seq, shard, 3 * wide)
        gu_cut = jnp.stack([expert_gate, expert_up]).reshape(2, local_experts, depth, n_seq, part)
        gu_cut = jnp.transpose(gu_cut, (3, 2, 0, 1, 4)).reshape(n_seq, depth, 2 * units)
        w_qkv, w_o, x_col, flag_col, small_all, w_gu, dy_all = load_inputs(
            qkv_cut, w_out, mine, flags, pack(small), gu_cut, dy_own, n_seq, n_bat
        )
        w_gu = w_gu.reshape(dim, 2 * units)
        dy_all = dy_all.reshape(-1, dim)
        x_col = jnp.transpose(x_col.reshape(n_seq, rows, span, dim), (1, 0, 2, 3))
    w_qkv = w_qkv.reshape(dim, 3 * wide)
    w_o = w_o.reshape(wide, dim)
    w_down = expert_down.reshape(local_experts * part, dim)
    if not fused:
        small_all = unpack(small_all, (n_seq, n_bat), small.shape)
        small_all = jnp.transpose(small_all, (2, 0, 1, 3)).reshape(-1, dim)
        router = small_all[:experts].T.astype(BF)
        gains = small_all[experts:]
        gain_attn, gain_mlp = gains[0], gains[3]
        usable = unpack(flag_col, (n_seq,), key_mask.shape)
        usable = jnp.transpose(usable, (1, 0, 2)).reshape(rows, length)
        router_t = small_all[:experts]

    expert_ids = jnp.arange(experts, dtype=jnp.int32)
    named = top_experts.reshape(own, -1).T[None] == expert_ids[:, None, None]
    chosen_t = jnp.sum(named.astype(F32), axis=1)
    cos_wide, sin_wide = rotary_tables(length)
    hidden, qkv, q, k, v, mixed, stats, mixed_out, *extra = attend_forward(
        x_col.reshape(col, dim), w_qkv, usable, w_o, gains, cos_wide, sin_wide, n_seq, n_bat, rows,
        (dy_own, mine, router_t, chosen_t) if fused else None,
    )
    if not fused:
        x_own = mine.astype(F32)
        residual = x_own + mixed_out.astype(F32)
        scale_r = rms_scale(residual)
        normed = (residual * scale_r * gain_mlp).astype(BF)
        router_probs = jax.nn.softmax(dot(normed, router), axis=-1)
        chosen = chosen_t.T
        gates = router_probs * chosen

    if fused:
        dy_all, residual, normed, probs_t, gates_t = extra
        normed_all, weighted, grad_pre, gate_terms, w_gu = experts_forward(
            normed, gates_t, dy_all, expert_gate, expert_up, w_down, n_seq, n_bat
        )
        w_gu = w_gu.reshape(dim, 2 * units)
        grad_residual, grad_o, small_grads, grad_gate, grad_up, grad_down = experts_backward(
            grad_pre,
            weighted,
            w_gu,
            gate_terms,
            normed_all.reshape(-1, dim),
            dy_all.reshape(-1, dim),
            residual,
            dy_own,
            gains,
            router_t,
            probs_t,
            chosen_t,
            local_experts,
            n_seq,
            n_bat,
        )
        grad_down = grad_down.reshape(local_experts, part, dim)
    else:
        normed_all, gates_all = gather_all([normed, pack(gates.T)], n_seq, n_bat, 4, "gather_normed")
        normed_all = normed_all.reshape(-1, dim)
        gates_all = unpack(gates_all, (n_seq, n_bat), (experts, own))
        gates_all = jnp.transpose(gates_all, (0, 1, 3, 2)).reshape(-1, experts)
        first_expert = bat * local_experts
        gates_here = lax.dynamic_slice_in_dim(gates_all, first_expert, local_experts, 1)
        gates_wide = jnp.repeat(gates_here, part, axis=1)
        pre = dot(normed_all, w_gu)
        gate_pre, up_pre = pre[:, :units], pre[:, units:]
        sig = jax.nn.sigmoid(gate_pre)
        silu = gate_pre * sig
        active = (silu * up_pre).astype(BF).astype(F32)
        weighted = (active * gates_wide).astype(BF)
        mixture = dot(weighted, w_down).astype(BF)
        mixture = mixture.reshape(n_seq, n_bat, own, dim)
        back = dot_t(dy_all, w_down)
        gate_terms = jnp.sum((active * back).reshape(-1, local_experts, part), axis=-1)
        grad_active = back * gates_wide
        grad_gate_pre = (grad_active * up_pre * sig * (1.0 + gate_pre * (1.0 - sig))).astype(BF)
        grad_up_pre = (grad_active * silu).astype(BF)
        grad_pre = jnp.concatenate([grad_gate_pre, grad_up_pre], axis=1)
        grad_down = t_dot(weighted, dy_all)
        grad_gu = t_dot(normed_all, grad_pre).astype(BF)
        grad_normed = dot_t(grad_pre, w_gu).astype(BF)
        gate_terms = gate_terms.reshape(n_seq, n_bat, own, local_experts)
        grad_gates = lax.dynamic_update_slice_in_dim(
            jnp.zeros((n_seq, n_bat, experts, own), F32),
            jnp.transpose(gate_terms, (0, 1, 3, 2)),
            first_expert,
            2,
        )
        grad_gates = jax.vmap(jax.vmap(pack))(grad_gates)
        grad_normed = grad_normed.reshape(n_seq, n_bat, own, dim)
        grad_normed, grad_gates, mixture = scatter_blocks(
            grad_normed, grad_gates, mixture, n_seq, n_bat
        )
        grad_normed = grad_normed.astype(F32)
        grad_gates = unpack(grad_gates, (), (experts, own)).T
        output = (residual + mixture.astype(F32)).astype(BF)
        grad_down = grad_down.reshape(local_experts, part, dim)

    if not fused:
        grad_chosen = grad_gates * chosen
        grad_logits = router_probs * (
            grad_chosen - jnp.sum(router_probs * grad_chosen, axis=-1, keepdims=True)
        )
        grad_router = lax.dot_general(
            normed.astype(F32), grad_logits, (((0,), (0,)), ((), ())), precision=HIGHEST
        )
        grad_normed = grad_normed + lax.dot_general(
            grad_logits, router.astype(F32), (((1,), (1,)), ((), ())), precision=HIGHEST
        )
        grad_resid, gain_mlp_terms = rms_back(residual, scale_r, gain_mlp, grad_normed)
        grad_residual = dy_own.astype(F32) + grad_resid
        grad_o = grad_residual.astype(BF)

    grad_w_o, grad_w, grad_gains, grad_hidden, *extra = attend_backward(
        grad_o, q, k, v, mixed, qkv, stats, hidden, usable, w_o, w_qkv, gains, cos_wide, sin_wide,
        n_seq, n_bat,
        (weighted, w_down, mine, grad_residual, small_grads) if fused else None,
    )
    grad_w_o = grad_w_o.reshape(n_bat, shard, dim)
    grad_w = grad_w.reshape(n_seq, n_bat, shard, 3 * wide)
    if not fused:
        grad_hidden = grad_hidden.astype(F32)
        grad_x, gain_attn_terms = rms_back(x_own, rms_scale(x_own), gain_attn, grad_hidden)
        grad_tokens = (grad_residual + grad_x).astype(BF)

        zeros = jnp.zeros((dim,), F32)
        small_grads = jnp.concatenate(
            [
                grad_router.T,
                jnp.stack(
                    [
                        jnp.sum(gain_attn_terms, axis=0),
                        lax.dynamic_update_slice_in_dim(zeros, grad_gains[0], seq * wide, 0),
                        lax.dynamic_update_slice_in_dim(zeros, grad_gains[1], seq * wide, 0),
                        jnp.sum(gain_mlp_terms, axis=0),
                    ]
                ),
            ],
            axis=0,
        )
        small_grads = jnp.transpose(small_grads.reshape(-1, n_seq, n_bat, shard), (1, 2, 0, 3))
        small_grads = jax.vmap(jax.vmap(pack))(small_grads)

    if fused:
        *grad_w, grad_w_o, small_grads, mixture = store_last(
            grad_w, grad_w_o, extra[1], extra[0], n_seq, n_bat
        )
        output, grad_tokens, *grad_w, grad_w_o, grad_gate, grad_up, grad_down = finish(
            residual, mixture, [grad_hidden, *grad_w, grad_w_o, grad_gate, grad_up, grad_down]
        )
        small_grads = lax.dynamic_slice_in_dim(small_grads, lax.rem(bat, 2) * shard, shard, 1)
    else:
        grad_gu = grad_gu.reshape(n_seq, depth, -1)
        grad_w, grad_w_o, grad_gu, small_grads = store_grads(
            grad_w, grad_w_o, grad_gu, small_grads, n_seq, n_bat
        )
        grad_w = grad_w.astype(F32).reshape(n_seq, shard, 3, wide)
        grad_w = jnp.transpose(grad_w, (2, 1, 0, 3)).reshape(3, shard, dim)
        grad_gu = grad_gu.reshape(n_seq, depth, 2, local_experts, part)
        grad_gu = jnp.transpose(grad_gu, (2, 3, 1, 0, 4)).reshape(2, local_experts, depth, hidden_units)
        grad_gu = grad_gu.astype(F32)
        grad_gate, grad_up = grad_gu[0], grad_gu[1]
        small_grads = unpack(small_grads, (), (experts + 4, shard))

    return (
        output.reshape(rows, span, dim),
        grad_tokens.reshape(rows, span, dim),
        small_grads[experts],
        small_grads[experts + 1],
        small_grads[experts + 2],
        small_grads[experts + 3],
        grad_w[0],
        grad_w[1],
        grad_w[2],
        grad_w_o,
        small_grads[:experts].T,
        grad_gate,
        grad_up,
        grad_down,
    )


def solution(mesh):
    tok = P("batch", "seq", None)
    vec = P(("seq", "batch"))
    mat = P(("seq", "batch"), None)
    in_specs = (tok, P("batch"), P("batch", "seq"), tok) + (vec,) * 4 + (mat,) * 5 + (tok,) * 4
    out_specs = (tok, tok) + (vec,) * 4 + (mat,) * 5 + (tok,) * 3
    return jax.shard_map(shards, mesh=mesh, in_specs=in_specs, out_specs=out_specs, check_vma=False)
```
